32 devices in a mesh: dp: 8 (over y, x, core), mp: 4 (over z).
Axes of the slice: x: 2, y: 2, z: 4, core: 2. Of those that a mesh axis runs over, the one named last changes fastest.
Arguments:
- tokens: bfloat16 [2048, 2048], P('dp'), may hold values from -6 to 6
- lengths: int32 [8, 4], P('dp'), may hold values from 0 to 256, as said below
- ln_gain: float32 [2048], replicated, may hold values from 0.5 to 1.5
- ln_bias: float32 [2048], replicated, may hold values from -3 to 3
- w_query: bfloat16 [2048, 2048], P(None, 'mp'), may hold values from -0.125 to 0.125
- b_query: float32 [2048], P('mp'), may hold values from -3 to 3
- w_key: bfloat16 [2048, 2048], P(None, 'mp'), may hold values from -0.125 to 0.125
- b_key: float32 [2048], P('mp'), may hold values from -3 to 3
- w_value: bfloat16 [2048, 2048], P(None, 'mp'), may hold values from -0.125 to 0.125
- b_value: float32 [2048], P('mp'), may hold values from -3 to 3
- w_out: bfloat16 [2048, 2048], P('mp'), may hold values from -0.375 to 0.375
- w_up: bfloat16 [2048, 8192], P(None, 'mp'), may hold values from -0.125 to 0.125
- b_up: float32 [8192], P('mp'), may hold values from -3 to 3
- w_down: bfloat16 [8192, 2048], P('mp'), may hold values from -0.0625 to 0.0625
- out_bias: float32 [2048], replicated, may hold values from -3 to 3
- cotangent: bfloat16 [2048, 2048], P('dp'), may hold values from -6 to 6
Outputs:
- mixed: bfloat16 [2048, 2048], P('dp')
- grad_tokens: bfloat16 [2048, 2048], P('dp')
- grad_ln_gain: float32 [2048], P('dp')
- grad_ln_bias: float32 [2048], P('dp')
- grad_w_query: float32 [2048, 2048], P('dp', 'mp')
- grad_b_query: float32 [2048], P('mp')
- grad_w_key: float32 [2048, 2048], P('dp', 'mp')
- grad_b_key: float32 [2048], P('mp')
- grad_w_value: float32 [2048, 2048], P('dp', 'mp')
- grad_b_value: float32 [2048], P('mp')
- grad_w_out: float32 [2048, 2048], P('mp', 'dp')
- grad_w_up: float32 [2048, 8192], P('dp', 'mp')
- grad_b_up: float32 [8192], P('mp')
- grad_w_down: float32 [8192, 2048], P('mp', 'dp')
- grad_out_bias: float32 [2048], P('dp')
The draws below stay inside these ranges and needn't reach their ends.
Inputs may be any that keep to these rules, and one draw needn't show every extreme that they name: `lengths`: row g lists the sequences that the group g of 256 slots packs, used slots first, each used length at least 64, unused slots 0; a row sums to 256 or less; some row holds a single sequence of 256.
All inputs are finite; a program needn't handle non-finite values.
Results may differ from the reference program's by a relative error of at most 0.015.
Values may be sent and summed in bfloat16 or wider, within the bound.
A program may use at most 192 MiB of HBM per device.

```python
import jax
import jax.numpy as jnp
from jax import lax

D = 2048
HEADS = 32
HD = 64
ROT = 32
FF = 8192
TOK_DEV = 256
MIN_LEN = 64
SLOTS = 4
TOKENS = 2048
N_DP = 8


def draw_lengths(key, part):
    k_power, k_power2, k_jitter, k_fill, k_single = jax.random.split(key, 5)
    span = (TOK_DEV // MIN_LEN).bit_length() - 1
    power = jnp.minimum(jax.random.randint(k_power, (N_DP, SLOTS), 0, span + 1), jax.random.randint(k_power2, (N_DP, SLOTS), 0, span + 1))
    base_len = MIN_LEN * 2 ** power
    jitter = jax.random.randint(k_jitter, (N_DP, SLOTS), 0, MIN_LEN)
    length = jnp.minimum(base_len + jitter, TOK_DEV).astype(jnp.int32)
    target = jax.random.randint(k_fill, (N_DP, 1), TOK_DEV // 2, TOK_DEV + 1).astype(jnp.int32)
    length = jnp.concatenate([jnp.minimum(length[:, :1], target), length[:, 1:]], axis=1)
    ends = jnp.cumsum(length, axis=1)
    length = jnp.where(ends <= target, length, 0)
    chosen = jax.random.randint(k_single, (), 0, N_DP)
    single = jnp.concatenate([jnp.full((1,), TOK_DEV, jnp.int32), jnp.zeros((SLOTS - 1,), jnp.int32)])
    picked = jnp.arange(N_DP, dtype=jnp.int32)[:, None] == chosen
    return jnp.where(picked, single[None, :], length).astype(jnp.int32)


def strengthened(values, key, source, target, parts, factor):
    def block_of(axis_at):
        return (jnp.arange(values.shape[axis_at]) // (values.shape[axis_at] // parts)).reshape((-1,) + (1,) * (values.ndim - 1 - axis_at))

    near = jax.random.permutation(key, parts)[block_of(target)]
    other_side = (block_of(target) + parts // 2) % parts
    return jnp.where((block_of(source) == near) | (block_of(source) == other_side), factor * values, values)


def block_levels(rng, shape, shards, smallest, high):
    gain, own = 1.0, jax.random.fold_in(rng, 6)
    for axis_at, shards_of in shards:
        heights = jnp.exp(jax.random.uniform(jax.random.fold_in(own, axis_at), (shards_of,), jnp.float32, smallest / len(shards), high / len(shards)))
        gain = gain * jnp.repeat(heights, shape[axis_at] // shards_of).reshape([-1 if axis == axis_at else 1 for axis in range(len(shape))])
    return gain


def noise(stream_key, dims, deviation, reach, shards=(), kind=jnp.bfloat16):
    gain = block_levels(stream_key, dims, shards, -0.22, 0.18) if shards else 1.0
    values = jax.random.normal(stream_key, dims, jnp.float32) * deviation * gain
    return jnp.minimum(jnp.maximum(values, -reach), reach).astype(kind)


def bell_draw_with(stream_key, dims, deviation, bound, shards, heavy, kind=jnp.bfloat16):
    values = deviation * jax.random.normal(stream_key, dims, jnp.float32)
    if shards:
        values = values * block_levels(stream_key, dims, shards, -0.22, 0.18)
    return jnp.clip(strengthened(values, jax.random.fold_in(stream_key, 3), *heavy), -bound, bound).astype(kind)


def setup_inputs(seed: int = 0) -> dict:
    arg_keys = jax.random.split(jax.random.key(seed), 17)
    return {
        "tokens": noise(arg_keys[0], (TOKENS, D), 1.0, 6.0, ((0, 8),)),
        "lengths": draw_lengths(jax.random.fold_in(arg_keys[16], 71), 0),
        "ln_gain": jnp.clip(1.0 + 0.1 * jax.random.normal(arg_keys[2], (D,), jnp.float32), 0.5, 1.5),
        "ln_bias": noise(arg_keys[3], (D,), 0.3, 3.0, (), jnp.float32),
        "w_query": noise(arg_keys[4], (D, D), D ** -0.5, 0.125, ((1, 4),)),
        "b_query": noise(arg_keys[5], (D,), 0.3, 3.0, ((0, 4),), jnp.float32),
        "w_key": noise(arg_keys[6], (D, D), D ** -0.5, 0.125, ((1, 4),)),
        "b_key": noise(arg_keys[7], (D,), 0.3, 3.0, ((0, 4),), jnp.float32),
        "w_value": noise(arg_keys[8], (D, D), D ** -0.5, 0.125, ((1, 4),)),
        "b_value": noise(arg_keys[9], (D,), 0.3, 3.0, ((0, 4),), jnp.float32),
        "w_out": noise(arg_keys[10], (D, D), (D // 8) ** -0.5, 0.375, ((0, 4),)),
        "w_up": noise(arg_keys[11], (D, FF), D ** -0.5, 0.125, ((1, 4),)),
        "b_up": noise(arg_keys[12], (FF,), 0.3, 3.0, ((0, 4),), jnp.float32),
        "w_down": noise(arg_keys[13], (FF, D), FF ** -0.5, 0.0625, ((0, 4),)),
        "out_bias": noise(arg_keys[14], (D,), 0.3, 3.0, (), jnp.float32),
        "cotangent": bell_draw_with(arg_keys[15], (TOKENS, D), 1.0, 6.0, ((0, 8),), (0, 1, 8, 2.0)),
    }


@jax.custom_vjp
def low(v):
    return lax.optimization_barrier(v.astype(jnp.bfloat16)).astype(jnp.float32)

@jax.custom_vjp
def low_back(v):
    return v

def low_keep(v):
    return (low(v), None)

def low_pass(kept, grad):
    return (grad,)

def back_keep(v):
    return (v, None)

def back_low(kept, grad):
    return (low(grad),)
low.defvjp(low_keep, low_pass)
low_back.defvjp(back_keep, back_low)
EPSILON = 1e-05
HIGH = lax.Precision.HIGHEST

def layer_norm(inputs, gain_vec, shift_vec):
    center = inputs - lax.optimization_barrier(jnp.mean(inputs, axis=-1, keepdims=True))
    spread = lax.optimization_barrier(jnp.mean(center * center, axis=-1, keepdims=True))
    return center * lax.rsqrt(spread + EPSILON) * gain_vec + shift_vec

def token_layout(lens_row, tok_count):
    ends = jnp.cumsum(lens_row).astype(jnp.int32)
    starts_at = (ends - lens_row).astype(jnp.int32)
    places = jnp.arange(tok_count, dtype=jnp.int32)
    inside = (places[:, None] >= starts_at[None, :]) & (places[:, None] < ends[None, :])
    inside_int = inside.astype(jnp.int32)
    numbers = jnp.arange(1, lens_row.shape[0] + 1, dtype=jnp.int32)
    segment = (lax.optimization_barrier(jnp.sum(inside_int * numbers[None, :], axis=1)) - 1).astype(jnp.int32)
    offset = (places - lax.optimization_barrier(jnp.sum(inside_int * starts_at[None, :], axis=1))).astype(jnp.int32)
    return (segment, offset, segment >= 0)

def rotary_tables(offset):
    freq = 10000.0 ** (-jnp.arange(0, ROT, 2, dtype=jnp.float32) / ROT)
    angle = offset.astype(jnp.float32)[:, None] * freq[None, :]
    return (jnp.cos(angle)[:, None, :], jnp.sin(angle)[:, None, :])

def rotate(field, cosine, sine):
    half = cosine.shape[-1]
    first = field[..., :half]
    second = field[..., half:2 * half]
    return jnp.concatenate([first * cosine - second * sine, second * cosine + first * sine, field[..., 2 * half:]], axis=-1)

def attend_rows(turned_q, turned_k, values, segment, first_row, block_rows):
    rows_q = lax.dynamic_slice_in_dim(turned_q, first_row, block_rows, 0)
    seg_rows = lax.dynamic_slice_in_dim(segment, first_row, block_rows, 0)
    scores = jnp.einsum('qhd,khd->hqk', rows_q, turned_k, precision=HIGH) * 0.125
    scores = low_back(scores)
    place_rows = first_row + jnp.arange(block_rows, dtype=jnp.int32)
    place_cols = jnp.arange(turned_k.shape[0], dtype=jnp.int32)
    allowed = (seg_rows[:, None] == segment[None, :]) & (place_cols[None, :] <= place_rows[:, None])
    masked = jnp.where(allowed[None], scores, -1e+30)
    row_top = lax.optimization_barrier(jnp.max(masked, axis=-1, keepdims=True))
    expo = jnp.exp(masked - row_top)
    probs = expo / lax.optimization_barrier(jnp.sum(expo, axis=-1, keepdims=True))
    return jnp.einsum('hqk,khd->qhd', low(probs), values, precision=HIGH)

def device_pass(tokens_row, lens_row, params):
    ln_gain, ln_bias, w_query, b_query, w_key, b_key, w_value, b_value, w_out, w_up, b_up, w_down, out_bias = params
    tok_count = tokens_row.shape[0]
    segment, offset, is_valid = token_layout(lens_row, tok_count)
    cosine, sine = rotary_tables(offset)
    normed = low(layer_norm(tokens_row, ln_gain, ln_bias))

    def project(weight, offset_vec):
        return low_back(jnp.dot(normed, weight, precision=HIGH, preferred_element_type=jnp.float32) + offset_vec)
    queries = project(w_query, b_query).reshape(tok_count, HEADS, HD)
    key_rows = project(w_key, b_key).reshape(tok_count, HEADS, HD)
    turned_q = low(rotate(queries, cosine, sine))
    turned_k = low(rotate(key_rows, cosine, sine))
    values = low(project(w_value, b_value).reshape(tok_count, HEADS, HD))
    block_rows = min(512, tok_count)
    firsts = jnp.arange(0, tok_count, block_rows, dtype=jnp.int32)
    attend = jax.checkpoint(attend_rows, static_argnums=(5,))
    attended = lax.map(lambda first_row: attend(turned_q, turned_k, values, segment, first_row, block_rows), firsts)
    attended = low(low_back(attended.reshape(tok_count, D)))
    branch_attn = jnp.dot(attended, w_out, precision=HIGH, preferred_element_type=jnp.float32)
    upward = project(w_up, b_up)
    activated = low(jax.nn.gelu(upward, approximate=True))
    branch_mlp = jnp.dot(activated, w_down, precision=HIGH, preferred_element_type=jnp.float32)
    return tokens_row + jnp.where(is_valid[:, None], branch_attn + branch_mlp + out_bias, 0.0)

def reference(tokens, lengths, ln_gain, ln_bias, w_query, b_query, w_key, b_key, w_value, b_value, w_out, w_up, b_up, w_down, out_bias, cotangent):
    params = tuple((member.astype(jnp.float32) for member in (ln_gain, ln_bias, w_query, b_query, w_key, b_key, w_value, b_value, w_out, w_up, b_up, w_down, out_bias)))
    tokens_f = tokens.astype(jnp.float32).reshape(N_DP, TOK_DEV, D)
    per_device = jax.checkpoint(device_pass)

    def forward(tok_all, param_set):
        return lax.map(lambda pair_item: per_device(pair_item[0], pair_item[1], param_set), (tok_all, lengths))
    result, pull = jax.vjp(forward, tokens_f, params)
    grad_all, grad_params = pull(cotangent.astype(jnp.float32).reshape(N_DP, TOK_DEV, D))
    mixed = result.reshape(TOKENS, D).astype(jnp.bfloat16)
    grad_tokens = grad_all.reshape(TOKENS, D).astype(jnp.bfloat16)
    return (mixed, grad_tokens, grad_params[0], grad_params[1], grad_params[2], grad_params[3], grad_params[4], grad_params[5], grad_params[6], grad_params[7], grad_params[8], grad_params[9], grad_params[10], grad_params[11], grad_params[12])
```

```python
import jax
import jax.numpy as jnp
from jax import lax
from jax.sharding import PartitionSpec as P

HD = 64
ROT = 32
EPSILON = 1e-05


def token_layout(lens_row, tok_count):
    ends = jnp.cumsum(lens_row)
    starts_at = ends - lens_row
    places = jnp.arange(tok_count, dtype=jnp.int32)
    inside = (places[:, None] >= starts_at[None, :]) & (places[:, None] < ends[None, :])
    inside_int = inside.astype(jnp.int32)
    numbers = jnp.arange(1, lens_row.shape[0] + 1, dtype=jnp.int32)
    segment = jnp.sum(inside_int * numbers[None, :], axis=1) - 1
    offset = places - jnp.sum(inside_int * starts_at[None, :], axis=1)
    return (segment, offset, segment >= 0)


def rotary_tables(offset):
    freq = 10000.0 ** (-jnp.arange(0, ROT, 2, dtype=jnp.float32) / ROT)
    angle = offset.astype(jnp.float32)[:, None] * freq[None, :]
    return (jnp.cos(angle)[:, None, :], jnp.sin(angle)[:, None, :])


def rotate(field, cosine, sine):
    half = cosine.shape[-1]
    first = field[..., :half]
    second = field[..., half : 2 * half]
    return jnp.concatenate(
        [first * cosine - second * sine, second * cosine + first * sine, field[..., 2 * half :]],
        axis=-1,
    )


def dot(left, right, dims):
    return lax.dot_general(left, right, (dims, ((), ())), preferred_element_type=jnp.float32)


def span(bits):
    out = [0]
    for bit in bits:
        out = out + [value | bit for value in out]
    return out


def make_body(n_dp, n_mp):
    low_bits = [1 << i for i in range(n_dp.bit_length() - 1)]
    rest = low_bits[1:]
    half = len(rest) // 2
    first_bits, second_bits = rest[:half], rest[half:]
    core_bits = low_bits[:1]

    def swap(value, mask):
        return lax.ppermute(value, "dp", [(i, i ^ mask) for i in range(n_dp)])

    def gather(value, bits):
        pieces = [value]
        for bit in bits:
            pieces = pieces + [swap(piece, bit) for piece in pieces]
        return pieces

    def to_others(blocks):
        me = lax.axis_index("mp")
        received = []
        for delta in range(1, n_mp):
            block = lax.dynamic_index_in_dim(blocks, lax.rem(me + delta, n_mp), 0, keepdims=False)
            received.append(
                lax.ppermute(block, "mp", [(i, (i + delta) % n_mp) for i in range(n_mp)])
            )
        own = lax.dynamic_index_in_dim(blocks, me, 0, keepdims=False)
        return own, received

    def share_rows(block):
        me = lax.axis_index("mp")
        out = jnp.zeros((n_mp,) + block.shape, block.dtype)
        out = lax.dynamic_update_index_in_dim(out, block, me, 0)
        for delta in range(1, n_mp):
            other = lax.ppermute(block, "mp", [(i, (i + delta) % n_mp) for i in range(n_mp)])
            out = lax.dynamic_update_index_in_dim(out, other, lax.rem(me - delta + n_mp, n_mp), 0)
        return out.reshape((-1,) + block.shape[1:])

    def body(
        tokens,
        lengths,
        ln_gain,
        ln_bias,
        w_query,
        b_query,
        w_key,
        b_key,
        w_value,
        b_value,
        w_out,
        w_up,
        b_up,
        w_down,
        out_bias,
        cotangent,
    ):
        tok_count, width = tokens.shape
        local_width = w_query.shape[1]
        head_count = local_width // HD
        me = lax.axis_index("dp")
        zed = lax.axis_index("mp")
        own_cols = width // n_dp
        segment, offset, is_valid = token_layout(lengths[0], tok_count)
        cosine, sine = rotary_tables(offset)
        tokens_f = tokens.astype(jnp.float32)
        center = tokens_f - jnp.mean(tokens_f, axis=-1, keepdims=True)
        spread = jnp.mean(center * center, axis=-1, keepdims=True)
        inv_dev = lax.rsqrt(spread + EPSILON)
        standard = center * inv_dev
        normed_low = (standard * ln_gain + ln_bias).astype(jnp.bfloat16)
        grad_low = jnp.where(is_valid[:, None], cotangent, jnp.zeros_like(cotangent))

        def columns_for(value, owner):
            return lax.dynamic_slice_in_dim(value, owner * own_cols, own_cols, 1)

        def exchange_side(value, gather_bits, reduce_bits):
            pieces = []
            for offset_j in span(gather_bits):
                block = jnp.concatenate(
                    [columns_for(value, me ^ (offset_j ^ m)) for m in span(reduce_bits)], axis=1
                )
                pieces.append(swap(block, offset_j) if offset_j else block)
            return jnp.concatenate(pieces, axis=0)

        bits_n = (first_bits + core_bits, second_bits)
        bits_g = (second_bits + core_bits, first_bits)
        side_g = exchange_side(grad_low, *bits_g)
        side_n = exchange_side(normed_low, *bits_n)

        def weight_grad(pieces, side, reduce_bits, rows_first):
            many = jnp.concatenate(pieces, axis=0)
            total = None
            for at, m in enumerate(span(reduce_bits)):
                part = side[:, at * own_cols : (at + 1) * own_cols]
                if rows_first:
                    product = dot(part, many, ((0,), (0,)))
                else:
                    product = dot(many, part, ((0,), (0,)))
                if m == 0:
                    total = product
                else:
                    total = total + swap(product.astype(jnp.bfloat16), m).astype(jnp.float32)
            return total

        upward = dot(normed_low, w_up, ((1,), (0,))) + b_up
        activated, act_back = jax.vjp(lambda u: jax.nn.gelu(u, approximate=True), upward)
        activated_low = activated.astype(jnp.bfloat16)
        many_act = gather(activated_low, bits_g[0])
        act_grad = dot(grad_low, w_down, ((1,), (1,)))
        up_grad = act_back(act_grad)[0].astype(jnp.bfloat16)
        many_up = gather(up_grad, bits_n[0])
        grad_down = weight_grad(many_act, side_g, bits_g[1], False)
        grad_up = weight_grad(many_up, side_n, bits_n[1], True)

        def project(weight, offset_vec):
            return dot(normed_low, weight, ((1,), (0,))) + offset_vec

        queries = project(w_query, b_query).reshape(tok_count, head_count, HD)
        key_rows = project(w_key, b_key).reshape(tok_count, head_count, HD)
        turned_q, turn_q_back = jax.vjp(lambda field: rotate(field, cosine, sine), queries)
        turned_k, turn_k_back = jax.vjp(lambda field: rotate(field, cosine, sine), key_rows)
        query_low = turned_q.astype(jnp.bfloat16)
        key_low = turned_k.astype(jnp.bfloat16)
        value_low = (
            project(w_value, b_value).reshape(tok_count, head_count, HD).astype(jnp.bfloat16)
        )
        scores = (
            jnp.einsum("qhd,khd->hqk", query_low, key_low, preferred_element_type=jnp.float32)
            * 0.125
        )
        places = jnp.arange(tok_count, dtype=jnp.int32)
        allowed = (segment[:, None] == segment[None, :]) & (places[None, :] <= places[:, None])
        masked = jnp.where(allowed[None], scores, -1e30)
        row_top = jnp.max(masked, axis=-1, keepdims=True)
        expo = jnp.exp(masked - row_top)
        totals = jnp.sum(expo, axis=-1, keepdims=True)
        probs_f = expo / totals
        probs = probs_f.astype(jnp.bfloat16)
        attended_low = (
            jnp.einsum("hqk,khd->qhd", probs, value_low, preferred_element_type=jnp.float32)
            .reshape(tok_count, local_width)
            .astype(jnp.bfloat16)
        )
        many_att = gather(attended_low, bits_g[0])
        partial_out = dot(attended_low, w_out, ((1,), (0,))) + dot(
            activated_low, w_down, ((1,), (0,))
        )
        att_grad = (
            dot(grad_low, w_out, ((1,), (1,)))
            .astype(jnp.bfloat16)
            .reshape(tok_count, head_count, HD)
        )
        prob_grad = jnp.einsum(
            "qhd,khd->hqk", att_grad, value_low, preferred_element_type=jnp.float32
        )
        row_delta = jnp.sum(probs_f * prob_grad, axis=-1, keepdims=True)
        score_grad = (probs_f * (prob_grad - row_delta)).astype(jnp.bfloat16)
        q_grad = (
            jnp.einsum("hqk,khd->qhd", score_grad, key_low, preferred_element_type=jnp.float32)
            * 0.125
        )
        k_grad = (
            jnp.einsum("hqk,qhd->khd", score_grad, query_low, preferred_element_type=jnp.float32)
            * 0.125
        )
        v_grad = jnp.einsum("hqk,qhd->khd", probs, att_grad, preferred_element_type=jnp.float32)
        query_grad = turn_q_back(q_grad)[0].reshape(tok_count, local_width).astype(jnp.bfloat16)
        key_grad = turn_k_back(k_grad)[0].reshape(tok_count, local_width).astype(jnp.bfloat16)
        value_grad = v_grad.reshape(tok_count, local_width).astype(jnp.bfloat16)
        qkv_grad = jnp.concatenate([query_grad, key_grad, value_grad], axis=1)
        many_qkv = gather(qkv_grad, bits_n[0])
        grad_qkv = weight_grad(many_qkv, side_n, bits_n[1], True)
        grad_outproj = weight_grad(many_att, side_g, bits_g[1], False)
        normed_grad = (
            dot(up_grad, w_up, ((1,), (1,)))
            + dot(query_grad, w_query, ((1,), (1,)))
            + dot(key_grad, w_key, ((1,), (1,)))
            + dot(value_grad, w_value, ((1,), (1,)))
        )

        rows = tok_count // n_mp

        def my_rows(value):
            return lax.dynamic_slice_in_dim(value, zed * rows, rows, 0)

        def sum_rows(value):
            own = my_rows(value)
            blocks = value.astype(jnp.bfloat16).reshape(n_mp, rows, width)
            for other in to_others(blocks)[1]:
                own = own + other.astype(jnp.float32)
            return own

        total = sum_rows(partial_out)
        mixed_rows = (
            my_rows(tokens_f) + jnp.where(my_rows(is_valid)[:, None], total + out_bias, 0.0)
        ).astype(jnp.bfloat16)
        mixed = share_rows(mixed_rows)

        grads = sum_rows(normed_grad) * ln_gain
        xhat = my_rows(standard)
        back = my_rows(inv_dev) * (
            grads
            - jnp.mean(grads, axis=-1, keepdims=True)
            - xhat * jnp.mean(grads * xhat, axis=-1, keepdims=True)
        )
        grad_tokens = share_rows(
            (my_rows(cotangent).astype(jnp.float32) + back).astype(jnp.bfloat16)
        )

        def sum_over_dp(value):
            for bit in low_bits:
                value = value + swap(value, bit)
            return value

        vectors = jnp.concatenate(
            [
                jnp.sum(normed_grad * standard, axis=0),
                jnp.sum(normed_grad, axis=0),
                jnp.sum(grad_low.astype(jnp.float32), axis=0),
                jnp.sum(up_grad.astype(jnp.float32), axis=0),
                jnp.sum(qkv_grad.astype(jnp.float32), axis=0),
            ]
        )
        vectors = sum_over_dp(vectors)
        norms = vectors[: 2 * width]
        for bit in [1 << i for i in range(n_mp.bit_length() - 1)]:
            norms = norms + lax.ppermute(norms, "mp", [(i, i ^ bit) for i in range(n_mp)])

        def shard(value):
            return lax.dynamic_slice_in_dim(value, me * own_cols, own_cols, 0)

        sent_gain = shard(norms[:width])
        sent_shift = shard(norms[width:])
        sent_bias = shard(vectors[2 * width : 3 * width])
        hidden = w_up.shape[1]
        bias_up = vectors[3 * width : 3 * width + hidden]
        bias_q, bias_k, bias_v = jnp.split(vectors[3 * width + hidden :], 3)
        sent_q, sent_k, sent_v = jnp.split(grad_qkv, 3, axis=1)
        return (
            mixed,
            grad_tokens,
            sent_gain,
            sent_shift,
            sent_q,
            bias_q,
            sent_k,
            bias_k,
            sent_v,
            bias_v,
            grad_outproj,
            grad_up,
            bias_up,
            grad_down,
            sent_bias,
        )

    return body


def solution(mesh):
    in_specs = (
        P("dp", None),
        P("dp", None),
        P(),
        P(),
        P(None, "mp"),
        P("mp"),
        P(None, "mp"),
        P("mp"),
        P(None, "mp"),
        P("mp"),
        P("mp", None),
        P(None, "mp"),
        P("mp"),
        P("mp", None),
        P(),
        P("dp", None),
    )
    out_specs = (
        P("dp", None),
        P("dp", None),
        P("dp"),
        P("dp"),
        P("dp", "mp"),
        P("mp"),
        P("dp", "mp"),
        P("mp"),
        P("dp", "mp"),
        P("mp"),
        P("mp", "dp"),
        P("dp", "mp"),
        P("mp"),
        P("mp", "dp"),
        P("dp"),
    )
    body = make_body(mesh.shape["dp"], mesh.shape["mp"])
    return jax.shard_map(body, mesh=mesh, in_specs=in_specs, out_specs=out_specs, check_vma=False)
```

```python
import functools
import math

import jax
import jax.numpy as jnp
from jax import lax
from jax.experimental import pallas as pl
from jax.experimental.pallas import tpu as pltpu
from jax.sharding import PartitionSpec as P

HD = 64
ROT = 32
EPSILON = 1e-05
GROUP = 8
CORE, XBIT, YBIT = 1, 2, 4
BLK = 256
F32 = jnp.float32
BF16 = jnp.bfloat16
MESH = pl.DeviceIdType.MESH
GELU_A = math.sqrt(2.0 / math.pi)
GELU_B = 0.044715


def nn(left, right):
    return lax.dot_general(left, right, (((1,), (0,)), ((), ())), preferred_element_type=F32)


def nt(left, right):
    return lax.dot_general(left, right, (((1,), (1,)), ((), ())), preferred_element_type=F32)


def tn(left, right):
    return lax.dot_general(left, right, (((0,), (0,)), ((), ())), preferred_element_type=F32)


def flip(index, mask):
    for bit in (1, 2, 4):
        if mask & bit:
            index = index + bit * (1 - 2 * ((index // bit) % 2))
    return index


def mult(value, by):
    return pl.multiple_of(value, by)


N_JS = (0, XBIT, CORE, XBIT | CORE)
N_MS = (0, YBIT)
G_JS = (0, YBIT, CORE, YBIT | CORE)
G_MS = (0, XBIT)


def layer_kernel(
    n_chunks,
    g_chunks,
    lens,
    tok_h,
    cot_h,
    gain,
    shift,
    bq,
    bk,
    bv,
    bup,
    obias,
    wq_h,
    wk_h,
    wv_h,
    wo_h,
    wu_h,
    wd_h,
    mixed_h,
    gtok_h,
    gradn_h,
    gradg_h,
    vec_o,
    tok,
    gout,
    normed,
    turned_n,
    wq,
    wk,
    wv,
    wo,
    wu,
    wd,
    bn,
    bg,
    side_n,
    side_g,
    rsn_s,
    rsn_r,
    rsg_s,
    rsg_r,
    act,
    dact,
    gqkv,
    att,
    q_s,
    k_s,
    v_s,
    ga_s,
    amask,
    rot_c,
    rot_a,
    rot_b,
    stat_m,
    stat_i,
    stage_n,
    stage_g,
    zpart,
    zr1,
    zr2,
    zs2,
    zout,
    vz,
    vzr,
    vd,
    vdr,
    gsum,
    bsum,
    bsum_r,
    cot_rows,
    in_sem,
    wu_sem,
    wd_sem,
    sn_ss,
    sn_rs,
    sg_ss,
    sg_rs,
    bn_ss,
    bn_rs,
    bg_ss,
    bg_rs,
    rn_ss,
    rn_rs,
    rg_ss,
    rg_rs,
    z_ss,
    z_rs,
    vz_ss,
    vz_rs,
    vd_ss,
    vd_rs,
    bs_ss,
    bs_rs,
    on_sem,
    og_sem,
    oz_sem,
):
    toks, width = tok.shape
    hidden = wu.shape[1]
    heads_w = wq.shape[1]
    n_qkv = 3 * heads_w // BLK
    n_att = heads_w // BLK
    n_hid = hidden // BLK
    n_own = width // BLK
    dp = lax.axis_index("dp")
    zed = lax.axis_index("mp")
    inner = lax.rem(dp, GROUP)
    outer = dp - inner
    half = toks // 2
    quarter = toks // 4

    def peer(mask):
        return (outer + flip(inner, mask), zed)

    def zpeer(mask):
        return (dp, zed + mask * (1 - 2 * ((zed // mask) % 2)))

    def remote(src, dst, ssem, rsem, where):
        return pltpu.make_async_remote_copy(
            src_ref=src,
            dst_ref=dst,
            send_sem=ssem,
            recv_sem=rsem,
            device_id=where,
            device_id_type=MESH,
        )

    loads = [
        pltpu.make_async_copy(src, dst, in_sem.at[i])
        for i, (src, dst) in enumerate(
            ((cot_h, gout), (tok_h, tok), (wq_h, wq), (wk_h, wk), (wv_h, wv), (wo_h, wo))
        )
    ]
    for load in loads:
        load.start()

    def wu_load(c):
        cols = pl.ds(mult(c * BLK, BLK), BLK)
        return pltpu.make_async_copy(wu_h.at[:, cols], wu.at[:, cols], wu_sem.at[c])

    def wd_load(c):
        rows = pl.ds(mult(c * BLK, BLK), BLK)
        return pltpu.make_async_copy(wd_h.at[rows, :], wd.at[rows, :], wd_sem.at[c])

    @pl.loop(0, n_hid)
    def _(c):
        wu_load(c).start()

    @pl.loop(0, n_hid)
    def _(c):
        wd_load(c).start()

    b0 = lax.rem(zed, 2)
    b1 = (zed // 2) % 2
    keep_half = mult(b0 * half, half)
    send_half = mult((1 - b0) * half, half)
    keep_q = mult(b1 * quarter, quarter)
    send_q = mult((1 - b1) * quarter, quarter)
    my_rows = mult(b0 * half + b1 * quarter, quarter)
    cot_load = pltpu.make_async_copy(cot_h.at[pl.ds(my_rows, quarter), :], cot_rows, in_sem.at[6])
    cot_load.start()

    barrier = pltpu.get_barrier_semaphore()
    for mask in range(1, GROUP):
        pl.semaphore_signal(barrier, inc=1, device_id=peer(mask), device_id_type=MESH)
    for mask in (1, 2):
        pl.semaphore_signal(barrier, inc=1, device_id=zpeer(mask), device_id_type=MESH)

    ends = []
    total_len = 0
    for j in range(lens.shape[1]):
        total_len = total_len + lens[0, j]
        ends.append(total_len)

    def segment_of(place):
        number = jnp.zeros_like(place)
        start_of = jnp.zeros_like(place)
        for j, end in enumerate(ends):
            start = end - lens[0, j]
            inside = ((place >= start) & (place < end)).astype(jnp.int32)
            number = number + inside * (j + 1)
            start_of = start_of + inside * start
        return number, start_of

    place_r = lax.broadcasted_iota(jnp.int32, (toks, toks), 0)
    place_c = lax.broadcasted_iota(jnp.int32, (toks, toks), 1)
    seg_r, _ = segment_of(place_r)
    seg_c, _ = segment_of(place_c)
    allowed = (seg_r == seg_c) & (place_c <= place_r)
    amask[...] = jnp.where(allowed, 0.0, -1e30)

    loads[0].wait()
    gsum[...] = jnp.zeros_like(gsum)
    step_rows = 32

    @pl.loop(0, toks // step_rows)
    def _(r):
        first = r * step_rows
        rows = pl.ds(mult(first, step_rows), step_rows)
        place = first + lax.broadcasted_iota(jnp.int32, (step_rows, width), 0)
        value = jnp.where(place < total_len, gout[rows, :].astype(F32), 0.0)
        gout[rows, :] = value.astype(BF16)
        gsum[0:1, :] = gsum[0:1, :] + jnp.sum(value, axis=0, keepdims=True)

    pl.semaphore_wait(barrier, GROUP + 1)

    def side_g_copy(i, m):
        owner = flip(inner, G_JS[i] ^ G_MS[m])
        return remote(
            gout.at[:, pl.ds(mult(owner * BLK, BLK), BLK)],
            side_g.at[m, pl.ds(i * toks, toks), :],
            sg_ss.at[i - 1, m],
            sg_rs.at[i - 1, m],
            peer(G_JS[i]),
        )

    def side_n_copy(i, m):
        owner = flip(inner, N_JS[i] ^ N_MS[m])
        return remote(
            turned_n.at[owner],
            side_n.at[m, :, pl.ds(i * toks, toks)],
            sn_ss.at[i - 1, m],
            sn_rs.at[i - 1, m],
            peer(N_JS[i]),
        )

    for i in (1, 3, 2):
        for m in (0, 1):
            side_g_copy(i, m).start()

    loads[1].wait()

    @pl.loop(0, toks // step_rows)
    def _(r):
        rows = pl.ds(mult(r * step_rows, step_rows), step_rows)
        value = tok[rows, :].astype(F32)
        mean = jnp.sum(value, axis=1, keepdims=True) * (1.0 / width)
        center = value - mean
        spread = jnp.sum(center * center, axis=1, keepdims=True) * (1.0 / width)
        inv = lax.rsqrt(spread + EPSILON)
        normed[rows, :] = (center * inv * gain[...] + shift[...]).astype(BF16)
        stat_m[rows, :] = jnp.broadcast_to(mean, (step_rows, 128))
        stat_i[rows, :] = jnp.broadcast_to(inv, (step_rows, 128))

    @pl.loop(0, n_own)
    def _(o):
        turned_n[o] = normed[:, pl.ds(mult(o * BLK, BLK), BLK)].T

    for i in (1, 3, 2):
        for m in (0, 1):
            side_n_copy(i, m).start()
    for m in (0, 1):
        owner_g = mult(flip(inner, G_MS[m]) * BLK, BLK)
        side_g[m, 0:toks, :] = gout[:, pl.ds(owner_g, BLK)]
        side_n[m, :, 0:toks] = turned_n[flip(inner, N_MS[m])]

    lane = lax.broadcasted_iota(jnp.int32, (toks, 128), 1)
    slot = lax.broadcasted_iota(jnp.int32, (toks, 128), 0)
    _, start_of = segment_of(slot)
    in_head = lane % HD
    order = (in_head % (ROT // 2)).astype(F32)
    freq = jnp.exp(order * (-2.0 / ROT * math.log(10000.0)))
    angle = (slot - start_of).astype(F32) * freq
    cosine, sine = jnp.cos(angle), jnp.sin(angle)
    rot_c[...] = jnp.where(in_head < ROT, cosine, 1.0)
    rot_a[...] = jnp.where(in_head < ROT // 2, -sine, 0.0)
    rot_b[...] = jnp.where((in_head >= ROT // 2) & (in_head < ROT), sine, 0.0)

    def rotate(value, sign):
        left = pltpu.roll(value, 128 - ROT // 2, 1)
        right = pltpu.roll(value, ROT // 2, 1)
        return value * rot_c[...] + sign * (left * rot_a[...] + right * rot_b[...])

    for load in loads[2:6]:
        load.wait()

    @pl.loop(0, heads_w // BLK)
    def _(n):
        cols = pl.ds(mult(n * BLK, BLK), BLK)
        query = nn(normed[...], wq[:, cols]) + bq[:, cols]
        keys = nn(normed[...], wk[:, cols]) + bk[:, cols]
        for part in range(BLK // 128):
            at = pl.ds(mult(n * BLK + part * 128, 128), 128)
            lanes = slice(part * 128, part * 128 + 128)
            q_s[:, at] = (rotate(query[:, lanes], 1.0) * 0.125).astype(BF16)
            k_s[:, at] = rotate(keys[:, lanes], 1.0).astype(BF16)
        v_s[:, cols] = (nn(normed[...], wv[:, cols]) + bv[:, cols]).astype(BF16)
        ga_s[:, cols] = nt(gout[...], wo[cols, :]).astype(BF16)

    def bn_copy(s, k):
        src = bn.at[s, pl.ds(toks if k == 2 else 0, toks), :]
        slot_at = (1, 2, 3)[k]
        return remote(
            src,
            bn.at[s, pl.ds(slot_at * toks, toks), :],
            bn_ss.at[s, k],
            bn_rs.at[s, k],
            peer((XBIT, CORE, CORE)[k]),
        )

    def bg_copy(s, k):
        src = bg.at[s, :, pl.ds(toks if k == 2 else 0, toks)]
        slot_at = (1, 2, 3)[k]
        return remote(
            src,
            bg.at[s, :, pl.ds(slot_at * toks, toks)],
            bg_ss.at[s, k],
            bg_rs.at[s, k],
            peer((YBIT, CORE, CORE)[k]),
        )

    low_lane = lax.broadcasted_iota(jnp.int32, (1, 128), 1) < HD
    head_mask = (jnp.where(low_lane, 1.0, 0.0).astype(BF16), jnp.where(low_lane, 0.0, 1.0).astype(BF16))
    low_full = lax.broadcasted_iota(jnp.int32, (toks, 128), 1) < HD

    @pl.loop(0, n_att)
    def _(n):
        for part in range(BLK // 128):
            at = pl.ds(mult(n * BLK + part * 128, 128), 128)
            lanes = slice(part * 128, part * 128 + 128)
            qp, kp, vp, gp = q_s[:, at], k_s[:, at], v_s[:, at], ga_s[:, at]
            results = []
            for h in range(2):
                scores = nt(qp * head_mask[h], kp) + amask[...]
                top = jnp.max(scores, axis=1, keepdims=True)
                expo = jnp.exp(scores - top)
                probs = expo * (1.0 / jnp.sum(expo, axis=1, keepdims=True))
                probs_low = probs.astype(BF16)
                out = nn(probs_low, vp)
                prob_grad = nt(gp * head_mask[h], vp)
                delta = jnp.sum(probs * prob_grad, axis=1, keepdims=True)
                score_grad = (probs * (prob_grad - delta)).astype(BF16)
                results.append(
                    (out, nn(score_grad, kp), tn(score_grad, qp), tn(probs_low, gp))
                )
            out, dq, dk, dv = (
                jnp.where(low_full, first, second) for first, second in zip(*results)
            )
            att[:, at] = out.astype(BF16)
            bg[n, lanes, 0:toks] = out.astype(BF16).T
            dq = rotate(dq * 0.125, -1.0).astype(BF16)
            dk = rotate(dk, -1.0).astype(BF16)
            dv = dv.astype(BF16)
            for kind, value in enumerate((dq, dk, dv)):
                bn[n + kind * n_att, 0:toks, lanes] = value
                gqkv[:, pl.ds(mult(kind * heads_w + n * BLK + part * 128, 128), 128)] = value
        for k in (0, 1):
            bg_copy(n, k).start()
            for kind in range(3):
                bn_copy(n + kind * n_att, k).start()

    @pl.loop(0, n_hid)
    def _(c):
        cols = pl.ds(mult(c * BLK, BLK), BLK)
        wu_load(c).wait()
        up = nn(normed[...], wu[:, cols]) + bup[:, cols]
        square = up * up
        tanh = jnp.tanh(GELU_A * up * (1.0 + GELU_B * square))
        active = (0.5 * up * (1.0 + tanh)).astype(BF16)
        act[:, cols] = active
        dact[:, cols] = (
            0.5 * (1.0 + tanh)
            + 0.5 * up * (1.0 - tanh * tanh) * (GELU_A * (1.0 + 3.0 * GELU_B * square))
        ).astype(BF16)
        bg[n_att + c, :, 0:toks] = active.T
        for k in (0, 1):
            bg_copy(n_att + c, k).start()

    def z_copy(t, which):
        if which == 0:
            return remote(
                zpart.at[t, pl.ds(send_half, half), :],
                zr1.at[t],
                z_ss.at[t, 0],
                z_rs.at[t, 0],
                zpeer(1),
            )
        if which == 1:
            return remote(zs2.at[t], zr2.at[t], z_ss.at[t, 1], z_rs.at[t, 1], zpeer(2))
        if which == 2:
            rows = pl.ds(my_rows, quarter)
            where = zpeer(2)
        else:
            rows = pl.ds(keep_half, half)
            where = zpeer(1)
        return remote(
            zout.at[t, rows, :], zout.at[t, rows, :], z_ss.at[t, which], z_rs.at[t, which], where
        )

    def z_second(t):
        z_copy(t, 0).wait_recv()

        @pl.loop(0, quarter // 16)
        def _(r):
            at = r * 16
            mine = zpart[t, pl.ds(mult(keep_half + send_q + at, 16), 16), :].astype(F32)
            other = zr1[t, pl.ds(mult(send_q + at, 16), 16), :].astype(F32)
            zs2[t, pl.ds(mult(at, 16), 16), :] = (mine + other).astype(BF16)

        z_copy(t, 1).start()

    def z_sum(t, at):
        mine = zpart[t, pl.ds(mult(my_rows + at, 16), 16), :].astype(F32)
        other = zr1[t, pl.ds(mult(keep_q + at, 16), 16), :].astype(F32)
        far = zr2[t, pl.ds(mult(at, 16), 16), :].astype(F32)
        return mine + other + far

    @pl.loop(0, n_hid)
    def _(c):
        wd_load(c).wait()

    @pl.loop(0, n_own)
    def _(n):
        cols = pl.ds(mult(n * BLK, BLK), BLK)
        zpart[0, :, cols] = (nn(act[...], wd[:, cols]) + nn(att[...], wo[:, cols])).astype(BF16)

    z_copy(0, 0).start()

    @pl.loop(0, n_hid)
    def _(c):
        cols = pl.ds(mult(c * BLK, BLK), BLK)
        grad = (nt(gout[...], wd[cols, :]) * dact[:, cols].astype(F32)).astype(BF16)
        dact[:, cols] = grad
        bn[n_qkv + c, 0:toks, :] = grad
        for k in (0, 1):
            bn_copy(n_qkv + c, k).start()

    vz[...] = jnp.zeros_like(vz)

    @pl.loop(0, n_own)
    def _(n):
        cols = pl.ds(mult(n * BLK, BLK), BLK)
        grad = nt(dact[...], wu[cols, :])
        for kind, weight in enumerate((wq, wk, wv)):
            grad = grad + nt(gqkv[:, kind * heads_w : (kind + 1) * heads_w], weight[cols, :])
        zpart[1, :, cols] = grad.astype(BF16)
        for part in range(BLK // 128):
            lanes = slice(part * 128, part * 128 + 128)
            at = pl.ds(mult(n * BLK + part * 128, 128), 128)
            piece = grad[:, lanes]
            standard = (tok[:, at].astype(F32) - stat_m[...]) * stat_i[...]
            vz[0, n, 0:1, lanes] = jnp.sum(piece * standard, axis=0, keepdims=True)
            vz[0, n, 1:2, lanes] = jnp.sum(piece, axis=0, keepdims=True)

    z_copy(1, 0).start()

    def vz_copy(t):
        return remote(vz.at[t], vzr.at[t], vz_ss.at[t], vz_rs.at[t], zpeer((1, 2)[t]))

    def vd_copy(mask):
        return remote(
            vd.at[flip(inner, mask)],
            vdr.at[mask],
            vd_ss.at[mask],
            vd_rs.at[mask],
            peer(mask),
        )

    bs_copy = remote(bsum, bsum_r, bs_ss, bs_rs, peer(YBIT))
    vz_copy(0).start()

    def rn_copy(s):
        return remote(rsn_s.at[s], rsn_r.at[s], rn_ss.at[s], rn_rs.at[s], peer(YBIT))

    def rg_copy(s):
        return remote(rsg_s.at[s], rsg_r.at[s], rg_ss.at[s], rg_rs.at[s], peer(XBIT))

    for i in (1, 2, 3):
        for m in (0, 1):
            side_g_copy(i, m).wait_recv()
            side_n_copy(i, m).wait_recv()
    bsum[...] = jnp.zeros_like(bsum)

    def mixed_rows():
        z_copy(0, 1).wait_recv()

        @pl.loop(0, quarter // 16)
        def _(r):
            at = r * 16
            rows = pl.ds(mult(my_rows + at, 16), 16)
            place = my_rows + at + lax.broadcasted_iota(jnp.int32, (16, width), 0)
            branch = jnp.where(place < total_len, z_sum(0, at) + obias[...], 0.0)
            zout[0, rows, :] = (tok[rows, :].astype(F32) + branch).astype(BF16)

        z_copy(0, 2).start()

    def grad_rows():
        z_copy(1, 1).wait_recv()
        cot_load.wait()

        @pl.loop(0, quarter // 16)
        def _(r):
            at = r * 16
            rows = pl.ds(mult(my_rows + at, 16), 16)
            inv = stat_i[rows, 0:1]
            standard = (tok[rows, :].astype(F32) - stat_m[rows, 0:1]) * inv
            grad = z_sum(1, at) * gain[...]
            first = jnp.sum(grad, axis=1, keepdims=True) * (1.0 / width)
            second = jnp.sum(grad * standard, axis=1, keepdims=True) * (1.0 / width)
            back = inv * (grad - first - standard * second)
            raw = cot_rows[pl.ds(mult(at, 16), 16), :].astype(F32)
            zout[1, rows, :] = (raw + back).astype(BF16)

        z_copy(1, 2).start()

    def z_last(t):
        z_copy(t, 2).wait_recv()
        z_copy(t, 3).start()

    def vec_second():
        vz_copy(0).wait_recv()
        vz[1] = vz[0] + vzr[0]
        vz_copy(1).start()

    def vec_spread():
        vz_copy(1).wait_recv()
        vd[...] = vz[1] + vzr[1]
        for owner in range(n_own):
            vd[owner, 2:3, :] = gsum[0:1, owner * BLK : owner * BLK + BLK]
        for mask in range(1, GROUP):
            vd_copy(mask).start()

    ones_row = jnp.ones((8, 4 * toks), BF16)

    @pl.loop(0, n_chunks + 1)
    def _(s):
        @pl.when(s < n_chunks)
        def _():
            bn_copy(s, 0).wait_recv()
            bn_copy(s, 2).start()

        @pl.when(s < g_chunks)
        def _():
            bg_copy(s, 0).wait_recv()
            bg_copy(s, 2).start()

        @pl.when(s > 0)
        def _():
            p = s - 1
            bn_copy(p, 1).wait_recv()
            bn_copy(p, 2).wait_recv()
            rsn_s[p] = nn(side_n[1], bn[p]).astype(BF16)
            rn_copy(p).start()
            bsum[pl.ds(p, 1), :] = nn(ones_row, bn[p])[0:1, :]

        @pl.when((s > 0) & (s <= g_chunks))
        def _():
            p = s - 1
            bg_copy(p, 1).wait_recv()
            bg_copy(p, 2).wait_recv()
            rsg_s[p] = nn(bg[p], side_g[1]).astype(BF16)
            rg_copy(p).start()

        @pl.when(s == 5)
        def _():
            z_second(0)
            vec_second()

        @pl.when(s == 9)
        def _():
            z_second(1)
            mixed_rows()
            vec_spread()

    bs_copy.start()

    def out_n(s):
        return pltpu.make_async_copy(
            stage_n.at[lax.rem(s, 2)],
            gradn_h.at[:, pl.ds(mult(s * BLK, BLK), BLK)],
            on_sem.at[lax.rem(s, 2)],
        )

    def out_g(s):
        return pltpu.make_async_copy(
            stage_g.at[lax.rem(s, 2)],
            gradg_h.at[pl.ds(mult(s * BLK, BLK), BLK), :],
            og_sem.at[lax.rem(s, 2)],
        )

    @pl.loop(0, n_chunks)
    def _(s):
        @pl.when(s >= 2)
        def _():
            out_n(s - 2).wait()

        mine = nn(side_n[0], bn[s])
        rn_copy(s).wait_recv()
        stage_n[lax.rem(s, 2)] = mine + rsn_r[s].astype(F32)
        out_n(s).start()

        @pl.when(s == 0)
        def _():
            z_last(0)

        @pl.when(s == 1)
        def _():
            grad_rows()

        @pl.when(s < g_chunks)
        def _():
            @pl.when(s >= 2)
            def _():
                out_g(s - 2).wait()

            mine_g = nn(bg[s], side_g[0])
            rg_copy(s).wait_recv()
            stage_g[lax.rem(s, 2)] = mine_g + rsg_r[s].astype(F32)
            out_g(s).start()

        @pl.when(s == 6)
        def _():
            z_last(1)

    bs_copy.wait_recv()
    sums = vd[inner]
    for mask in range(1, GROUP):
        vd_copy(mask).wait_recv()
        sums = sums + vdr[mask]
    vec_o[0:8, :] = sums
    vec_o[8:, :] = bsum[...] + bsum_r[...]

    z_outs = []
    for t, out_h in enumerate((mixed_h, gtok_h)):
        z_copy(t, 3).wait_recv()
        z_outs.append(pltpu.make_async_copy(zout.at[t], out_h, oz_sem.at[t]))
        z_outs[t].start()

    for i in (1, 2, 3):
        for m in (0, 1):
            side_g_copy(i, m).wait_send()
            side_n_copy(i, m).wait_send()

    @pl.loop(0, n_chunks)
    def _(s):
        for k in range(3):
            bn_copy(s, k).wait_send()
        rn_copy(s).wait_send()

    @pl.loop(0, g_chunks)
    def _(s):
        for k in range(3):
            bg_copy(s, k).wait_send()
        rg_copy(s).wait_send()

    for t in (0, 1):
        for which in range(4):
            z_copy(t, which).wait_send()
        vz_copy(t).wait_send()
    for mask in range(1, GROUP):
        vd_copy(mask).wait_send()
    bs_copy.wait_send()
    for back in (2, 1):
        out_n(n_chunks - back).wait()
        out_g(g_chunks - back).wait()
    for out in z_outs:
        out.wait()


def layer(tokens, lengths, ln_gain, ln_bias, w_query, b_query, w_key, b_key, w_value, b_value, w_out, w_up, b_up, w_down, out_bias, cotangent):
    toks, width = tokens.shape
    heads_w = w_query.shape[1]
    hidden = w_up.shape[1]
    n_chunks = (3 * heads_w + hidden) // BLK
    g_chunks = (heads_w + hidden) // BLK
    n_own = width // BLK
    n_vec = -(-n_chunks // 8) * 8
    half, quarter = toks // 2, toks // 4
    dma = pltpu.SemaphoreType.DMA
    vmem = pltpu.VMEM
    scratch = [
        vmem((toks, width), BF16),
        vmem((toks, width), BF16),
        vmem((toks, width), BF16),
        vmem((n_own, BLK, toks), BF16),
        vmem(w_query.shape, BF16),
        vmem(w_key.shape, BF16),
        vmem(w_value.shape, BF16),
        vmem(w_out.shape, BF16),
        vmem(w_up.shape, BF16),
        vmem(w_down.shape, BF16),
        vmem((n_chunks, 4 * toks, BLK), BF16),
        vmem((g_chunks, BLK, 4 * toks), BF16),
        vmem((2, BLK, 4 * toks), BF16),
        vmem((2, 4 * toks, BLK), BF16),
        vmem((n_chunks, BLK, BLK), BF16),
        vmem((n_chunks, BLK, BLK), BF16),
        vmem((g_chunks, BLK, BLK), BF16),
        vmem((g_chunks, BLK, BLK), BF16),
        vmem((toks, hidden), BF16),
        vmem((toks, hidden), BF16),
        vmem((toks, 3 * heads_w), BF16),
        vmem((toks, heads_w), BF16),
        vmem((toks, heads_w), BF16),
        vmem((toks, heads_w), BF16),
        vmem((toks, heads_w), BF16),
        vmem((toks, heads_w), BF16),
        vmem((toks, toks), F32),
        vmem((toks, 128), F32),
        vmem((toks, 128), F32),
        vmem((toks, 128), F32),
        vmem((toks, 128), F32),
        vmem((toks, 128), F32),
        vmem((2, BLK, BLK), F32),
        vmem((2, BLK, BLK), F32),
        vmem((2, toks, width), BF16),
        vmem((2, half, width), BF16),
        vmem((2, quarter, width), BF16),
        vmem((2, quarter, width), BF16),
        vmem((2, toks, width), BF16),
        vmem((2, n_own, 8, BLK), F32),
        vmem((2, n_own, 8, BLK), F32),
        vmem((n_own, 8, BLK), F32),
        vmem((GROUP, 8, BLK), F32),
        vmem((8, width), F32),
        vmem((n_vec, BLK), F32),
        vmem((n_vec, BLK), F32),
        vmem((quarter, width), BF16),
        dma((7,)),
        dma((hidden // BLK,)),
        dma((hidden // BLK,)),
        dma((3, 2)),
        dma((3, 2)),
        dma((3, 2)),
        dma((3, 2)),
        dma((n_chunks, 3)),
        dma((n_chunks, 3)),
        dma((g_chunks, 3)),
        dma((g_chunks, 3)),
        dma((n_chunks,)),
        dma((n_chunks,)),
        dma((g_chunks,)),
        dma((g_chunks,)),
        dma((2, 4)),
        dma((2, 4)),
        dma((2,)),
        dma((2,)),
        dma((GROUP,)),
        dma((GROUP,)),
        dma,
        dma,
        dma((2,)),
        dma((2,)),
        dma((2,)),
    ]
    anyspace = pl.BlockSpec(memory_space=pl.ANY)
    local = pl.BlockSpec(memory_space=pltpu.VMEM)
    row = lambda value: value.reshape(1, -1)
    mixed, grad_tokens, grad_n, grad_g, vec = pl.pallas_call(
        functools.partial(layer_kernel, n_chunks, g_chunks),
        out_shape=(
            jax.ShapeDtypeStruct((toks, width), BF16),
            jax.ShapeDtypeStruct((toks, width), BF16),
            jax.ShapeDtypeStruct((BLK, n_chunks * BLK), F32),
            jax.ShapeDtypeStruct((g_chunks * BLK, BLK), F32),
            jax.ShapeDtypeStruct((8 + n_vec, BLK), F32),
        ),
        in_specs=[pl.BlockSpec(memory_space=pltpu.SMEM), anyspace, anyspace]
        + [local] * 7
        + [anyspace] * 6,
        out_specs=(anyspace, anyspace, anyspace, anyspace, local),
        scratch_shapes=scratch,
        compiler_params=pltpu.CompilerParams(
            collective_id=0, has_side_effects=True, vmem_limit_bytes=67043328
        ),
    )(
        lengths,
        tokens,
        cotangent,
        row(ln_gain),
        row(ln_bias),
        row(b_query),
        row(b_key),
        row(b_value),
        row(b_up),
        row(out_bias),
        w_query,
        w_key,
        w_value,
        w_out,
        w_up,
        w_down,
    )
    sent_q = grad_n[:, :heads_w]
    sent_k = grad_n[:, heads_w : 2 * heads_w]
    sent_v = grad_n[:, 2 * heads_w : 3 * heads_w]
    sent_up = grad_n[:, 3 * heads_w :]
    per = heads_w // BLK
    bias = vec[8 : 8 + n_chunks]
    return (
        mixed,
        grad_tokens,
        vec[0],
        vec[1],
        sent_q,
        bias[:per].reshape(-1),
        sent_k,
        bias[per : 2 * per].reshape(-1),
        sent_v,
        bias[2 * per : 3 * per].reshape(-1),
        grad_g[:heads_w],
        sent_up,
        bias[3 * per :].reshape(-1),
        grad_g[heads_w:],
        vec[2],
    )


def make_body(n_dp, n_mp):
    outer = n_dp // GROUP

    def order(value, axis):
        if outer == 1:
            return value
        shape = value.shape
        split = shape[:axis] + (outer, GROUP, shape[axis] // n_dp) + shape[axis + 1 :]
        return jnp.swapaxes(value.reshape(split), axis, axis + 1).reshape(shape)

    def restore(value, axis):
        if outer == 1:
            return value
        shape = value.shape
        split = shape[:axis] + (GROUP, outer, shape[axis] // n_dp) + shape[axis + 1 :]
        return jnp.swapaxes(value.reshape(split), axis, axis + 1).reshape(shape)

    groups = [[o * GROUP + i for o in range(outer)] for i in range(GROUP)]

    def scatter(value, axis):
        if outer == 1:
            return value
        return lax.psum_scatter(
            value, "dp", scatter_dimension=axis, axis_index_groups=groups, tiled=True
        )

    def total(value):
        if outer == 1:
            return value
        return lax.psum(value, "dp", axis_index_groups=groups)

    def body(tokens, lengths, ln_gain, ln_bias, w_query, b_query, w_key, b_key, w_value, b_value, w_out, w_up, b_up, w_down, out_bias, cotangent):
        found = layer(
            order(tokens, 1),
            lengths,
            order(ln_gain, 0),
            order(ln_bias, 0),
            order(w_query, 0),
            b_query,
            order(w_key, 0),
            b_key,
            order(w_value, 0),
            b_value,
            order(w_out, 1),
            order(w_up, 0),
            b_up,
            order(w_down, 1),
            order(out_bias, 0),
            order(cotangent, 1),
        )
        (mixed, grad_tokens, gain, shift, g_q, b_q, g_k, b_k, g_v, b_v, g_out, g_up, b_u, g_down, b_out) = found
        return (
            restore(mixed, 1),
            restore(grad_tokens, 1),
            scatter(gain, 0),
            scatter(shift, 0),
            scatter(g_q, 0),
            total(b_q),
            scatter(g_k, 0),
            total(b_k),
            scatter(g_v, 0),
            total(b_v),
            scatter(g_out, 1),
            scatter(g_up, 0),
            total(b_u),
            scatter(g_down, 1),
            scatter(b_out, 0),
        )

    return body


def solution(mesh):
    in_specs = (
        P("dp", None),
        P("dp", None),
        P(),
        P(),
        P(None, "mp"),
        P("mp"),
        P(None, "mp"),
        P("mp"),
        P(None, "mp"),
        P("mp"),
        P("mp", None),
        P(None, "mp"),
        P("mp"),
        P("mp", None),
        P(),
        P("dp", None),
    )
    out_specs = (
        P("dp", None),
        P("dp", None),
        P("dp"),
        P("dp"),
        P("dp", "mp"),
        P("mp"),
        P("dp", "mp"),
        P("mp"),
        P("dp", "mp"),
        P("mp"),
        P("mp", "dp"),
        P("dp", "mp"),
        P("mp"),
        P("mp", "dp"),
        P("dp"),
    )
    body = make_body(mesh.shape["dp"], mesh.shape["mp"])
    return jax.shard_map(body, mesh=mesh, in_specs=in_specs, out_specs=out_specs, check_vma=False)
```

```python
import functools
import math

import jax
import jax.numpy as jnp
from jax import lax
from jax.experimental import pallas as pl
from jax.experimental.pallas import tpu as pltpu
from jax.sharding import PartitionSpec as P

HD = 64
ROT = 32
EPSILON = 1e-05
GROUP = 8
CORE, XBIT, YBIT = 1, 2, 4
BLK = 256
N_MP = 4
Z_PARTS = 4
F32 = jnp.float32
BF16 = jnp.bfloat16
MESH = pl.DeviceIdType.MESH
MAIN_VMEM = 46 * 2**20
GELU_A = math.sqrt(2.0 / math.pi)
GELU_B = 0.044715


def nn(left, right):
    return lax.dot_general(left, right, (((1,), (0,)), ((), ())), preferred_element_type=F32)


def nt(left, right):
    return lax.dot_general(left, right, (((1,), (1,)), ((), ())), preferred_element_type=F32)


def tn(left, right):
    return lax.dot_general(left, right, (((0,), (0,)), ((), ())), preferred_element_type=F32)


def flip(index, mask):
    for bit in (1, 2, 4):
        if mask & bit:
            index = index + bit * (1 - 2 * ((index // bit) % 2))
    return index


def mult(value, by):
    return pl.multiple_of(value, by)


N_JS = (0, XBIT, CORE, XBIT | CORE)
N_MS = (0, YBIT)
G_JS = (0, YBIT, CORE, YBIT | CORE)
G_MS = (0, XBIT)


def layer_kernel(
    n_chunks,
    g_chunks,
    lens,
    tok_h,
    cot_h,
    gain,
    shift,
    bq,
    bk,
    bv,
    bup,
    obias,
    wq_h,
    wk_h,
    wv_h,
    wo_h,
    wu_h,
    wd_h,
    bn,
    bg,
    rsn_r,
    rsg_r,
    zout,
    vec_o,
    tok,
    gout,
    normed,
    turned_n,
    wq,
    wk,
    wv,
    wo,
    wu,
    wd,
    side_n,
    side_g,
    rsn_s,
    rsg_s,
    act,
    dact,
    gqkv,
    att,
    q_s,
    k_s,
    v_s,
    ga_s,
    amask,
    rot_c,
    rot_a,
    rot_b,
    stat_m,
    stat_i,
    zpart,
    zfar,
    znear,
    zmid,
    vz,
    vzr,
    vd,
    vdr,
    gsum,
    bsum,
    bsum_r,
    cot_rows,
    in_sem,
    wu_sem,
    wd_sem,
    sn_ss,
    sn_rs,
    sg_ss,
    sg_rs,
    bn_ss,
    bn_rs,
    bg_ss,
    bg_rs,
    rn_ss,
    rn_rs,
    rg_ss,
    rg_rs,
    zf_ss,
    zf_rs,
    zn_ss,
    zn_rs,
    zm_ss,
    zm_rs,
    zo_ss,
    zo_rs,
    zw_ss,
    zw_rs,
    vz_ss,
    vz_rs,
    vd_ss,
    vd_rs,
    bs_ss,
    bs_rs,
):
    toks, width = tok.shape
    hidden = wu.shape[1]
    heads_w = wq.shape[1]
    n_qkv = 3 * heads_w // BLK
    n_att = heads_w // BLK
    n_hid = hidden // BLK
    n_own = width // BLK
    dp = lax.axis_index("dp")
    zed = lax.axis_index("mp")
    inner = lax.rem(dp, GROUP)
    outer = dp - inner
    half = toks // 2
    piece_cols = width // Z_PARTS
    piece_rows = half // Z_PARTS

    def peer(mask):
        return (outer + flip(inner, mask), zed)

    middle = (zed == 1) | (zed == 2)
    end_of_line = (zed == 0) | (zed == 3)
    side_of_line = zed // 2
    beside = (dp, zed + 1 - 2 * lax.rem(zed, 2))
    across = (dp, 3 - zed)
    near_rows = mult(side_of_line * half, half)
    far_rows = mult((1 - side_of_line) * half, half)

    def zpeer(step):
        return (dp, lax.rem(zed + step, N_MP))

    def remote(src, dst, ssem, rsem, where):
        return pltpu.make_async_remote_copy(
            src_ref=src,
            dst_ref=dst,
            send_sem=ssem,
            recv_sem=rsem,
            device_id=where,
            device_id_type=MESH,
        )

    loads = [
        pltpu.make_async_copy(src, dst, in_sem.at[i])
        for i, (src, dst) in enumerate(
            ((cot_h, gout), (tok_h, tok), (wq_h, wq), (wk_h, wk), (wv_h, wv), (wo_h, wo))
        )
    ]
    for load in loads:
        load.start()

    def wu_load(c):
        cols = pl.ds(mult(c * BLK, BLK), BLK)
        return pltpu.make_async_copy(wu_h.at[:, cols], wu.at[:, cols], wu_sem.at[c])

    def wd_load(c):
        rows = pl.ds(mult(c * BLK, BLK), BLK)
        return pltpu.make_async_copy(wd_h.at[rows, :], wd.at[rows, :], wd_sem.at[c])

    @pl.loop(0, n_hid)
    def _(c):
        wu_load(c).start()

    @pl.loop(0, n_hid)
    def _(c):
        wd_load(c).start()

    cot_load = pltpu.make_async_copy(cot_h.at[pl.ds(near_rows, half), :], cot_rows, in_sem.at[6])
    cot_load.start()

    barrier = pltpu.get_barrier_semaphore()
    for mask in range(1, GROUP):
        pl.semaphore_signal(barrier, inc=1, device_id=peer(mask), device_id_type=MESH)
    for step in range(1, N_MP):
        pl.semaphore_signal(barrier, inc=1, device_id=zpeer(step), device_id_type=MESH)

    ends = []
    total_len = 0
    for j in range(lens.shape[1]):
        total_len = total_len + lens[0, j]
        ends.append(total_len)

    def segment_of(place):
        number = jnp.zeros_like(place)
        start_of = jnp.zeros_like(place)
        for j, end in enumerate(ends):
            start = end - lens[0, j]
            inside = ((place >= start) & (place < end)).astype(jnp.int32)
            number = number + inside * (j + 1)
            start_of = start_of + inside * start
        return number, start_of

    place_r = lax.broadcasted_iota(jnp.int32, (toks, toks), 0)
    place_c = lax.broadcasted_iota(jnp.int32, (toks, toks), 1)
    seg_r, _ = segment_of(place_r)
    seg_c, _ = segment_of(place_c)
    allowed = (seg_r == seg_c) & (place_c <= place_r)
    amask[...] = jnp.where(allowed, 0.0, -1e30)

    loads[0].wait()
    gsum[...] = jnp.zeros_like(gsum)
    step_rows = 32

    @pl.loop(0, toks // step_rows)
    def _(r):
        first = r * step_rows
        rows = pl.ds(mult(first, step_rows), step_rows)
        place = first + lax.broadcasted_iota(jnp.int32, (step_rows, width), 0)
        value = jnp.where(place < total_len, gout[rows, :].astype(F32), 0.0)
        gout[rows, :] = value.astype(BF16)
        gsum[0:1, :] = gsum[0:1, :] + jnp.sum(value, axis=0, keepdims=True)

    def side_g_copy(i, m):
        owner = flip(inner, G_JS[i] ^ G_MS[m])
        return remote(
            gout.at[:, pl.ds(mult(owner * BLK, BLK), BLK)],
            side_g.at[pl.ds(i * toks, toks), pl.ds(m * BLK, BLK)],
            sg_ss,
            sg_rs.at[i - 1, m],
            peer(G_JS[i]),
        )

    def side_n_copy(i, m):
        owner = flip(inner, N_JS[i] ^ N_MS[m])
        return remote(
            turned_n.at[owner],
            side_n.at[m, :, pl.ds(i * toks, toks)],
            sn_ss,
            sn_rs.at[i - 1, m],
            peer(N_JS[i]),
        )

    loads[1].wait()

    @pl.loop(0, toks // step_rows)
    def _(r):
        rows = pl.ds(mult(r * step_rows, step_rows), step_rows)
        value = tok[rows, :].astype(F32)
        mean = jnp.sum(value, axis=1, keepdims=True) * (1.0 / width)
        center = value - mean
        spread = jnp.sum(center * center, axis=1, keepdims=True) * (1.0 / width)
        inv = lax.rsqrt(spread + EPSILON)
        normed[rows, :] = (center * inv * gain[...] + shift[...]).astype(BF16)
        stat_m[rows, :] = jnp.broadcast_to(mean, (step_rows, 128))
        stat_i[rows, :] = jnp.broadcast_to(inv, (step_rows, 128))

    pl.semaphore_wait(barrier, GROUP - 1 + N_MP - 1)
    for i in (1, 3, 2):
        for m in (0, 1):
            side_g_copy(i, m).start()

    @pl.loop(0, n_own)
    def _(o):
        turned_n[o] = normed[:, pl.ds(mult(o * BLK, BLK), BLK)].T

    for i in (1, 3, 2):
        for m in (0, 1):
            side_n_copy(i, m).start()
    for m in (0, 1):
        owner_g = mult(flip(inner, G_MS[m]) * BLK, BLK)
        side_g[0:toks, m * BLK : m * BLK + BLK] = gout[:, pl.ds(owner_g, BLK)]
        side_n[m, :, 0:toks] = turned_n[flip(inner, N_MS[m])]

    lane = lax.broadcasted_iota(jnp.int32, (toks, 128), 1)
    slot = lax.broadcasted_iota(jnp.int32, (toks, 128), 0)
    _, start_of = segment_of(slot)
    in_head = lane % HD
    order = (in_head % (ROT // 2)).astype(F32)
    freq = jnp.exp(order * (-2.0 / ROT * math.log(10000.0)))
    angle = (slot - start_of).astype(F32) * freq
    cosine, sine = jnp.cos(angle), jnp.sin(angle)
    rot_c[...] = jnp.where(in_head < ROT, cosine, 1.0)
    rot_a[...] = jnp.where(in_head < ROT // 2, -sine, 0.0)
    rot_b[...] = jnp.where((in_head >= ROT // 2) & (in_head < ROT), sine, 0.0)

    def rotate(value, sign):
        left = pltpu.roll(value, 128 - ROT // 2, 1)
        right = pltpu.roll(value, ROT // 2, 1)
        return value * rot_c[...] + sign * (left * rot_a[...] + right * rot_b[...])

    for load in loads[2:6]:
        load.wait()

    @pl.loop(0, heads_w // BLK)
    def _(n):
        cols = pl.ds(mult(n * BLK, BLK), BLK)
        query = nn(normed[...], wq[:, cols]) + bq[:, cols]
        keys = nn(normed[...], wk[:, cols]) + bk[:, cols]
        for part in range(BLK // 128):
            at = pl.ds(mult(n * BLK + part * 128, 128), 128)
            lanes = slice(part * 128, part * 128 + 128)
            q_s[:, at] = (rotate(query[:, lanes], 1.0) * 0.125).astype(BF16)
            k_s[:, at] = rotate(keys[:, lanes], 1.0).astype(BF16)
        v_s[:, cols] = (nn(normed[...], wv[:, cols]) + bv[:, cols]).astype(BF16)
        ga_s[:, cols] = nt(gout[...], wo[cols, :]).astype(BF16)

    def bn_copy(s, k):
        src = bn.at[s, pl.ds(toks if k == 2 else 0, toks), :]
        slot_at = (1, 2, 3)[k]
        return remote(
            src,
            bn.at[s, pl.ds(slot_at * toks, toks), :],
            bn_ss,
            bn_rs.at[s, min(k, 1)],
            peer((XBIT, CORE, CORE)[k]),
        )

    def bg_copy(s, k):
        src = bg.at[s, :, pl.ds(toks if k == 2 else 0, toks)]
        slot_at = (1, 2, 3)[k]
        return remote(
            src,
            bg.at[s, :, pl.ds(slot_at * toks, toks)],
            bg_ss,
            bg_rs.at[s, min(k, 1)],
            peer((YBIT, CORE, CORE)[k]),
        )

    low_lane = lax.broadcasted_iota(jnp.int32, (1, 128), 1) < HD
    head_mask = (jnp.where(low_lane, 1.0, 0.0).astype(BF16), jnp.where(low_lane, 0.0, 1.0).astype(BF16))
    low_full = lax.broadcasted_iota(jnp.int32, (toks, 128), 1) < HD

    @pl.loop(0, n_att)
    def _(n):
        for part in range(BLK // 128):
            at = pl.ds(mult(n * BLK + part * 128, 128), 128)
            lanes = slice(part * 128, part * 128 + 128)
            qp, kp, vp, gp = q_s[:, at], k_s[:, at], v_s[:, at], ga_s[:, at]
            results = []
            for h in range(2):
                scores = nt(qp * head_mask[h], kp) + amask[...]
                top = jnp.max(scores, axis=1, keepdims=True)
                expo = jnp.exp(scores - top)
                probs = expo * (1.0 / jnp.sum(expo, axis=1, keepdims=True))
                probs_low = probs.astype(BF16)
                out = nn(probs_low, vp)
                prob_grad = nt(gp * head_mask[h], vp)
                delta = jnp.sum(probs * prob_grad, axis=1, keepdims=True)
                score_grad = (probs * (prob_grad - delta)).astype(BF16)
                results.append(
                    (out, nn(score_grad, kp), tn(score_grad, qp), tn(probs_low, gp))
                )
            out, dq, dk, dv = (
                jnp.where(low_full, first, second) for first, second in zip(*results)
            )
            att[:, at] = out.astype(BF16)
            bg[n, lanes, 0:toks] = out.astype(BF16).T
            dq = rotate(dq * 0.125, -1.0).astype(BF16)
            dk = rotate(dk, -1.0).astype(BF16)
            dv = dv.astype(BF16)
            for kind, value in enumerate((dq, dk, dv)):
                bn[n + kind * n_att, 0:toks, lanes] = value
                gqkv[:, pl.ds(mult(kind * heads_w + n * BLK + part * 128, 128), 128)] = value
        for k in (0, 1):
            bg_copy(n, k).start()
            for kind in range(3):
                bn_copy(n + kind * n_att, k).start()

    @pl.loop(0, n_hid)
    def _(c):
        cols = pl.ds(mult(c * BLK, BLK), BLK)
        wu_load(c).wait()
        up = nn(normed[...], wu[:, cols]) + bup[:, cols]
        square = up * up
        tanh = jnp.tanh(GELU_A * up * (1.0 + GELU_B * square))
        active = (0.5 * up * (1.0 + tanh)).astype(BF16)
        act[:, cols] = active
        dact[:, cols] = (
            0.5 * (1.0 + tanh)
            + 0.5 * up * (1.0 - tanh * tanh) * (GELU_A * (1.0 + 3.0 * GELU_B * square))
        ).astype(BF16)
        bg[n_att + c, :, 0:toks] = active.T
        for k in (0, 1):
            bg_copy(n_att + c, k).start()

    def piece(t, g, first_row):
        if t == 0:
            return pl.ds(first_row, half), pl.ds(mult(g * piece_cols, piece_cols), piece_cols)
        return pl.ds(mult(first_row + g * piece_rows, piece_rows), piece_rows), pl.ds(0, width)

    def z_far(t, g):
        rows, cols = piece(t, g, far_rows)
        to_rows, _ = piece(t, g, 0)
        return remote(
            zpart.at[t, rows, cols],
            zfar.at[t, to_rows, cols],
            zf_ss,
            zf_rs.at[t * Z_PARTS + g],
            beside,
        )

    def z_near(t, g):
        rows, cols = piece(t, g, near_rows)
        to_rows, _ = piece(t, g, 0)
        return remote(
            zpart.at[t, rows, cols],
            znear.at[t, to_rows, cols],
            zn_ss,
            zn_rs.at[t * Z_PARTS + g],
            beside,
        )

    def z_mid(t, g):
        rows, cols = piece(t, g, far_rows)
        to_rows, _ = piece(t, g, 0)
        return remote(
            zpart.at[t, rows, cols],
            zmid.at[t, to_rows, cols],
            zm_ss,
            zm_rs.at[t * Z_PARTS + g],
            across,
        )

    def z_done(t, g, where):
        rows, cols = piece(t, g, near_rows)
        return remote(
            zout.at[t, rows, cols], zout.at[t, rows, cols], zo_ss, zo_rs.at[t * Z_PARTS + g], where
        )

    def z_pass(t, g):
        rows, cols = piece(t, g, far_rows)
        return remote(
            zout.at[t, rows, cols], zout.at[t, rows, cols], zw_ss, zw_rs.at[t * Z_PARTS + g], beside
        )

    def z_send(t, g):
        @pl.when(end_of_line)
        def _():
            z_far(t, g).start()
            z_near(t, g).start()

    def by_rows(t, body):
        count = 16 if t == 0 else piece_rows // 2

        @pl.loop(0, (half if t == 0 else piece_rows) // count)
        def _(r):
            body(r * count, count)

    def z_first(t, g):
        z_far(t, g).wait_recv()
        cols = piece(t, g, 0)[1]
        first = 0 if t == 0 else g * piece_rows

        def add(at, count):
            mine = pl.ds(mult(far_rows + first + at, count), count)
            other = pl.ds(mult(first + at, count), count)
            zpart[t, mine, cols] = (
                zpart[t, mine, cols].astype(F32) + zfar[t, other, cols].astype(F32)
            ).astype(BF16)

        by_rows(t, add)
        z_mid(t, g).start()

    def z_second(t, g):
        z_near(t, g).wait_recv()
        z_mid(t, g).wait_recv()
        if t == 1:
            @pl.when(g == 0)
            def _():
                cot_load.wait()
        cols = piece(t, g, 0)[1]
        first = 0 if t == 0 else g * piece_rows

        def finish(at, count):
            rows = pl.ds(mult(near_rows + first + at, count), count)
            there = pl.ds(mult(first + at, count), count)
            total = (
                zpart[t, rows, cols].astype(F32)
                + znear[t, there, cols].astype(F32)
                + zmid[t, there, cols].astype(F32)
            )
            base = tok[rows, cols].astype(F32)
            if t == 0:
                place = near_rows + at + lax.broadcasted_iota(jnp.int32, total.shape, 0)
                branch = jnp.where(place < total_len, total + obias[:, cols], 0.0)
                zout[t, rows, cols] = (base + branch).astype(BF16)
            else:
                inv = stat_i[rows, 0:1]
                standard = (base - stat_m[rows, 0:1]) * inv
                grad = total * gain[...]
                mean_g = jnp.sum(grad, axis=1, keepdims=True) * (1.0 / width)
                mean_x = jnp.sum(grad * standard, axis=1, keepdims=True) * (1.0 / width)
                back = inv * (grad - mean_g - standard * mean_x)
                zout[t, rows, cols] = (cot_rows[there, :].astype(F32) + back).astype(BF16)

        by_rows(t, finish)
        z_done(t, g, beside).start()
        z_done(t, g, across).start()

    def z_third(t, g):
        z_done(t, g, across).wait_recv()
        z_pass(t, g).start()

    def z_steps(first, second, third):
        for number, step in ((first, z_first), (second, z_second), (third, z_third)):
            for t in (0, 1):
                low = t * Z_PARTS

                @pl.when(middle & (number >= low) & (number < low + Z_PARTS))
                def _(number=number, step=step, t=t, low=low):
                    step(t, number - low)

    @pl.loop(0, n_hid)
    def _(c):
        wd_load(c).wait()

    @pl.loop(0, n_own)
    def _(n):
        cols = pl.ds(mult(n * BLK, BLK), BLK)
        zpart[0, :, cols] = (nn(act[...], wd[:, cols]) + nn(att[...], wo[:, cols])).astype(BF16)

        @pl.when(lax.rem(n, n_own // Z_PARTS) == n_own // Z_PARTS - 1)
        def _():
            z_send(0, n // (n_own // Z_PARTS))

    @pl.loop(0, n_hid)
    def _(c):
        cols = pl.ds(mult(c * BLK, BLK), BLK)
        grad = (nt(gout[...], wd[cols, :]) * dact[:, cols].astype(F32)).astype(BF16)
        dact[:, cols] = grad
        bn[n_qkv + c, 0:toks, :] = grad
        for k in (0, 1):
            bn_copy(n_qkv + c, k).start()

    z_steps(0, -1, -1)

    vz[...] = jnp.zeros_like(vz)

    @pl.loop(0, n_own)
    def _(n):
        cols = pl.ds(mult(n * BLK, BLK), BLK)
        grad = nt(dact[...], wu[cols, :])
        for kind, weight in enumerate((wq, wk, wv)):
            grad = grad + nt(gqkv[:, kind * heads_w : (kind + 1) * heads_w], weight[cols, :])
        zpart[1, :, cols] = grad.astype(BF16)
        for part in range(BLK // 128):
            lanes = slice(part * 128, part * 128 + 128)
            at = pl.ds(mult(n * BLK + part * 128, 128), 128)
            piece = grad[:, lanes]
            standard = (tok[:, at].astype(F32) - stat_m[...]) * stat_i[...]
            vz[n, 0:1, lanes] = jnp.sum(piece * standard, axis=0, keepdims=True)
            vz[n, 1:2, lanes] = jnp.sum(piece, axis=0, keepdims=True)

    def vz_copy(step):
        return remote(vz, vzr.at[step], vz_ss, vz_rs.at[step], zpeer(step))

    for step in range(1, N_MP):
        vz_copy(step).start()
    for g in range(Z_PARTS):
        z_send(1, g)

    def vd_copy(mask):
        return remote(
            vd.at[flip(inner, mask)],
            vdr.at[mask],
            vd_ss,
            vd_rs.at[mask],
            peer(mask),
        )

    bs_copy = remote(bsum, bsum_r, bs_ss, bs_rs, peer(YBIT))

    def rn_copy(s):
        return remote(rsn_s.at[s], rsn_r.at[s], rn_ss, rn_rs.at[s], peer(YBIT))

    def rg_copy(s):
        return remote(rsg_s.at[s], rsg_r.at[s], rg_ss, rg_rs.at[s], peer(XBIT))

    for i in (1, 2, 3):
        for m in (0, 1):
            side_g_copy(i, m).wait_recv()
            side_n_copy(i, m).wait_recv()
    bsum[...] = jnp.zeros_like(bsum)

    def vec_spread():
        total = vz[...]
        for step in range(1, N_MP):
            vz_copy(step).wait_recv()
            total = total + vzr[step]
        vd[...] = total
        for owner in range(n_own):
            vd[owner, 2:3, :] = gsum[0:1, owner * BLK : owner * BLK + BLK]
        for mask in range(1, GROUP):
            vd_copy(mask).start()

    z_steps(1, 0, -1)
    def pair_n(p):
        return bn.at[p, pl.ds(2 * toks, 2 * toks), :]

    def pair_g(p):
        return bg.at[p, :, pl.ds(2 * toks, 2 * toks)]

    ones_row = jnp.ones((8, 4 * toks), BF16)

    @pl.loop(0, n_chunks + 1)
    def _(s):
        @pl.when(s < n_chunks)
        def _():
            bn_copy(s, 0).wait_recv()
            bn_copy(s, 2).start()

        @pl.when(s < g_chunks)
        def _():
            bg_copy(s, 0).wait_recv()
            bg_copy(s, 2).start()

        @pl.when(s > 0)
        def _():
            p = s - 1
            pltpu.make_async_copy(pair_n(p), pair_n(p), bn_rs.at[p, 1]).wait()
            both = nn(side_n[...].reshape(2 * BLK, 4 * toks), bn[p])
            rsn_s[p] = both[BLK:, :].astype(BF16)
            rn_copy(p).start()
            bsum[pl.ds(p, 1), :] = nn(ones_row, bn[p])[0:1, :]
            bn[p, 2 * toks : 3 * toks, :] = both[:BLK, :].astype(BF16)

        @pl.when((s > 0) & (s <= g_chunks))
        def _():
            p = s - 1
            pltpu.make_async_copy(pair_g(p), pair_g(p), bg_rs.at[p, 1]).wait()
            both = nn(bg[p], side_g[...])
            rsg_s[p] = both[:, BLK:].astype(BF16)
            rg_copy(p).start()
            bg[p, :, 2 * toks : 3 * toks] = both[:, :BLK].astype(BF16)

        @pl.when((s >= 6) & (lax.rem(s, 2) == 0))
        def _():
            e = (s - 6) // 2
            z_steps(2 + e, 1 + e, e - 1)

    bs_copy.start()
    vec_spread()
    for numbers in ((7, 6, 4), (8, 7, 5), (8, 8, 6), (8, 8, 7)):
        z_steps(*numbers)

    bs_copy.wait_recv()
    sums = vd[inner]
    for mask in range(1, GROUP):
        vd_copy(mask).wait_recv()
        sums = sums + vdr[mask]
    vec_o[0:8, :] = sums
    vec_o[8:, :] = bsum[...] + bsum_r[...]

    @pl.loop(0, n_chunks)
    def _(s):
        rn_copy(s).wait_recv()

    @pl.loop(0, g_chunks)
    def _(s):
        rg_copy(s).wait_recv()

    def sent(ref, sem):
        pltpu.make_async_copy(ref, ref, sem).wait()

    sent(side_n.at[:, :, pl.ds(0, 3 * toks)], sn_ss)
    sent(side_g.at[pl.ds(0, 3 * toks), :], sg_ss)
    sent(bn.at[:, pl.ds(0, 3 * toks), :], bn_ss)
    sent(bg.at[:, :, pl.ds(0, 3 * toks)], bg_ss)
    sent(rsn_s, rn_ss)
    sent(rsg_s, rg_ss)
    sent(vzr.at[pl.ds(1, N_MP - 1)], vz_ss)
    sent(vdr.at[pl.ds(1, GROUP - 1)], vd_ss)
    bs_copy.wait_send()

    @pl.when(end_of_line)
    def _():
        sent(zfar, zf_ss)
        sent(znear, zn_ss)
        for t in (0, 1):
            for g in range(Z_PARTS):
                z_done(t, g, beside).wait_recv()
                z_pass(t, g).wait_recv()
        cot_load.wait()

    @pl.when(middle)
    def _():
        sent(zmid, zm_ss)
        sent(zout, zo_ss)
        sent(zmid, zw_ss)


def write_kernel(n_qkv, n_att, bn, bg, rsn, rsg, zout, vec, mixed_h, gtok_h, gain_o, shift_o, gq_h, bq_o, gk_h, bk_o, gv_h, bv_o, go_h, gu_h, bu_o, gd_h, ob_o, stage, sems, zsem):
    n_chunks, n_g = bn.shape[0], bg.shape[0]
    toks = zout.shape[1]
    slots = stage.shape[0]
    z_outs = [
        pltpu.make_async_copy(zout.at[t], out, zsem.at[t]) for t, out in enumerate((mixed_h, gtok_h))
    ]
    for out in z_outs:
        out.start()
    places = []
    for s in range(n_chunks):
        if s < n_qkv:
            out, at = (gq_h, gk_h, gv_h)[s // n_att], s % n_att
        else:
            out, at = gu_h, s - n_qkv
        places.append((True, s, out.at[:, pl.ds(at * BLK, BLK)]))
    for s in range(n_g):
        out, at = (go_h, s) if s < n_att else (gd_h, s - n_att)
        places.append((False, s, out.at[pl.ds(at * BLK, BLK), :]))
    copies = []
    for number, (first, s, place) in enumerate(places):
        slot = number % slots
        if number >= slots:
            copies[number - slots].wait()
        if first:
            value = bn[s, 2 * toks : 3 * toks, :].astype(F32) + rsn[s].astype(F32)
        else:
            value = bg[s, :, 2 * toks : 3 * toks].astype(F32) + rsg[s].astype(F32)
        stage[slot] = value
        copies.append(pltpu.make_async_copy(stage.at[slot], place, sems.at[slot]))
        copies[number].start()
    for row, out in enumerate((gain_o, shift_o, ob_o)):
        out[...] = vec[row]
    row = 8
    for out in (bq_o, bk_o, bv_o, bu_o):
        for at in range(out.shape[0] // BLK):
            out[at * BLK : at * BLK + BLK] = vec[row]
            row += 1
    for copy in copies[-slots:]:
        copy.wait()
    for out in z_outs:
        out.wait()


def layer(tokens, lengths, ln_gain, ln_bias, w_query, b_query, w_key, b_key, w_value, b_value, w_out, w_up, b_up, w_down, out_bias, cotangent):
    toks, width = tokens.shape
    heads_w = w_query.shape[1]
    hidden = w_up.shape[1]
    n_chunks = (3 * heads_w + hidden) // BLK
    g_chunks = (heads_w + hidden) // BLK
    n_own = width // BLK
    n_vec = -(-n_chunks // 8) * 8
    half = toks // 2
    dma = pltpu.SemaphoreType.DMA
    vmem = pltpu.VMEM
    scratch = [
        vmem((toks, width), BF16),
        vmem((toks, width), BF16),
        vmem((toks, width), BF16),
        vmem((n_own, BLK, toks), BF16),
        vmem(w_query.shape, BF16),
        vmem(w_key.shape, BF16),
        vmem(w_value.shape, BF16),
        vmem(w_out.shape, BF16),
        vmem(w_up.shape, BF16),
        vmem(w_down.shape, BF16),
        vmem((2, BLK, 4 * toks), BF16),
        vmem((4 * toks, 2 * BLK), BF16),
        vmem((n_chunks, BLK, BLK), BF16),
        vmem((g_chunks, BLK, BLK), BF16),
        vmem((toks, hidden), BF16),
        vmem((toks, hidden), BF16),
        vmem((toks, 3 * heads_w), BF16),
        vmem((toks, heads_w), BF16),
        vmem((toks, heads_w), BF16),
        vmem((toks, heads_w), BF16),
        vmem((toks, heads_w), BF16),
        vmem((toks, heads_w), BF16),
        vmem((toks, toks), F32),
        vmem((toks, 128), F32),
        vmem((toks, 128), F32),
        vmem((toks, 128), F32),
        vmem((toks, 128), F32),
        vmem((toks, 128), F32),
        vmem((2, toks, width), BF16),
        vmem((2, half, width), BF16),
        vmem((2, half, width), BF16),
        vmem((2, half, width), BF16),
        vmem((n_own, 8, BLK), F32),
        vmem((N_MP, n_own, 8, BLK), F32),
        vmem((n_own, 8, BLK), F32),
        vmem((GROUP, 8, BLK), F32),
        vmem((8, width), F32),
        vmem((n_vec, BLK), F32),
        vmem((n_vec, BLK), F32),
        vmem((half, width), BF16),
        dma((7,)),
        dma((hidden // BLK,)),
        dma((hidden // BLK,)),
        dma,
        dma((3, 2)),
        dma,
        dma((3, 2)),
        dma,
        dma((n_chunks, 2)),
        dma,
        dma((g_chunks, 2)),
        dma,
        dma((n_chunks,)),
        dma,
        dma((g_chunks,)),
        dma,
        dma((2 * Z_PARTS,)),
        dma,
        dma((2 * Z_PARTS,)),
        dma,
        dma((2 * Z_PARTS,)),
        dma,
        dma((2 * Z_PARTS,)),
        dma,
        dma((2 * Z_PARTS,)),
        dma,
        dma((N_MP,)),
        dma,
        dma((GROUP,)),
        dma,
        dma,
    ]
    anyspace = pl.BlockSpec(memory_space=pl.ANY)
    local = pl.BlockSpec(memory_space=pltpu.VMEM)
    row = lambda value: value.reshape(1, -1)
    kept = pl.pallas_call(
        functools.partial(layer_kernel, n_chunks, g_chunks),
        out_shape=(
            vmem((n_chunks, 4 * toks, BLK), BF16),
            vmem((g_chunks, BLK, 4 * toks), BF16),
            vmem((n_chunks, BLK, BLK), BF16),
            vmem((g_chunks, BLK, BLK), BF16),
            vmem((2, toks, width), BF16),
            vmem((8 + n_vec, BLK), F32),
        ),
        in_specs=[pl.BlockSpec(memory_space=pltpu.SMEM), anyspace, anyspace]
        + [local] * 7
        + [anyspace] * 6,
        out_specs=(local,) * 6,
        scratch_shapes=scratch,
        compiler_params=pltpu.CompilerParams(
            collective_id=0, has_side_effects=True, vmem_limit_bytes=MAIN_VMEM
        ),
    )(
        lengths,
        tokens,
        cotangent,
        row(ln_gain),
        row(ln_bias),
        row(b_query),
        row(b_key),
        row(b_value),
        row(b_up),
        row(out_bias),
        w_query,
        w_key,
        w_value,
        w_out,
        w_up,
        w_down,
    )
    f32 = lambda *shape: jax.ShapeDtypeStruct(shape, F32)
    low = jax.ShapeDtypeStruct((toks, width), BF16)
    spec = lambda kind: anyspace if len(kind.shape) == 2 else local
    outs = (
        low,
        low,
        f32(BLK),
        f32(BLK),
        f32(BLK, heads_w),
        f32(heads_w),
        f32(BLK, heads_w),
        f32(heads_w),
        f32(BLK, heads_w),
        f32(heads_w),
        f32(heads_w, BLK),
        f32(BLK, hidden),
        f32(hidden),
        f32(hidden, BLK),
        f32(BLK),
    )
    slots = 6
    return pl.pallas_call(
        functools.partial(write_kernel, 3 * heads_w // BLK, heads_w // BLK),
        out_shape=outs,
        in_specs=[local] * 6,
        out_specs=tuple(spec(kind) for kind in outs),
        scratch_shapes=[vmem((slots, BLK, BLK), F32), dma((slots,)), dma((2,))],
        compiler_params=pltpu.CompilerParams(vmem_limit_bytes=4 * 2**20),
    )(*kept)


def make_body(n_dp, n_mp):
    outer = n_dp // GROUP

    def order(value, axis):
        if outer == 1:
            return value
        shape = value.shape
        split = shape[:axis] + (outer, GROUP, shape[axis] // n_dp) + shape[axis + 1 :]
        return jnp.swapaxes(value.reshape(split), axis, axis + 1).reshape(shape)

    def restore(value, axis):
        if outer == 1:
            return value
        shape = value.shape
        split = shape[:axis] + (GROUP, outer, shape[axis] // n_dp) + shape[axis + 1 :]
        return jnp.swapaxes(value.reshape(split), axis, axis + 1).reshape(shape)

    groups = [[o * GROUP + i for o in range(outer)] for i in range(GROUP)]

    def scatter(value, axis):
        if outer == 1:
            return value
        return lax.psum_scatter(
            value, "dp", scatter_dimension=axis, axis_index_groups=groups, tiled=True
        )

    def total(value):
        if outer == 1:
            return value
        return lax.psum(value, "dp", axis_index_groups=groups)

    def body(tokens, lengths, ln_gain, ln_bias, w_query, b_query, w_key, b_key, w_value, b_value, w_out, w_up, b_up, w_down, out_bias, cotangent):
        found = layer(
            order(tokens, 1),
            lengths,
            order(ln_gain, 0),
            order(ln_bias, 0),
            order(w_query, 0),
            b_query,
            order(w_key, 0),
            b_key,
            order(w_value, 0),
            b_value,
            order(w_out, 1),
            order(w_up, 0),
            b_up,
            order(w_down, 1),
            order(out_bias, 0),
            order(cotangent, 1),
        )
        (mixed, grad_tokens, gain, shift, g_q, b_q, g_k, b_k, g_v, b_v, g_out, g_up, b_u, g_down, b_out) = found
        return (
            restore(mixed, 1),
            restore(grad_tokens, 1),
            scatter(gain, 0),
            scatter(shift, 0),
            scatter(g_q, 0),
            total(b_q),
            scatter(g_k, 0),
            total(b_k),
            scatter(g_v, 0),
            total(b_v),
            scatter(g_out, 1),
            scatter(g_up, 0),
            total(b_u),
            scatter(g_down, 1),
            scatter(b_out, 0),
        )

    return body


def solution(mesh):
    in_specs = (
        P("dp", None),
        P("dp", None),
        P(),
        P(),
        P(None, "mp"),
        P("mp"),
        P(None, "mp"),
        P("mp"),
        P(None, "mp"),
        P("mp"),
        P("mp", None),
        P(None, "mp"),
        P("mp"),
        P("mp", None),
        P(),
        P("dp", None),
    )
    out_specs = (
        P("dp", None),
        P("dp", None),
        P("dp"),
        P("dp"),
        P("dp", "mp"),
        P("mp"),
        P("dp", "mp"),
        P("mp"),
        P("dp", "mp"),
        P("mp"),
        P("mp", "dp"),
        P("dp", "mp"),
        P("mp"),
        P("mp", "dp"),
        P("dp"),
    )
    body = make_body(mesh.shape["dp"], mesh.shape["mp"])
    return jax.shard_map(body, mesh=mesh, in_specs=in_specs, out_specs=out_specs, check_vma=False)
```

```python
import functools
import math

import jax
import jax.numpy as jnp
from jax import lax
from jax.experimental import pallas as pl
from jax.experimental.pallas import tpu as pltpu
from jax.sharding import PartitionSpec as P

HD = 64
ROT = 32
EPSILON = 1e-05
GROUP = 8
CORE, XBIT, YBIT = 1, 2, 4
BLK = 256
WIDE = 512
N_MP = 4
Z_PARTS = 8
Z_LAG = 2
Z_TICKS = ((0, 2), (3, 3), (6, 4), (7, 5), (8, 6), (9, 7), (10, 8), (11, 9), (12, 10), (13, 11))
F32 = jnp.float32
BF16 = jnp.bfloat16
MESH = pl.DeviceIdType.MESH
MAIN_VMEM = 46 * 2**20
GELU_A = math.sqrt(2.0 / math.pi)
GELU_B = 0.044715


def nn(left, right):
    return lax.dot_general(left, right, (((1,), (0,)), ((), ())), preferred_element_type=F32)


def nt(left, right):
    return lax.dot_general(left, right, (((1,), (1,)), ((), ())), preferred_element_type=F32)


def tn(left, right):
    return lax.dot_general(left, right, (((0,), (0,)), ((), ())), preferred_element_type=F32)


def flip(index, mask):
    for bit in (1, 2, 4):
        if mask & bit:
            index = index + bit * (1 - 2 * ((index // bit) % 2))
    return index


def mult(value, by):
    return pl.multiple_of(value, by)


N_JS = (0, XBIT, CORE, XBIT | CORE)
N_MS = (0, YBIT)
G_JS = (0, YBIT, CORE, YBIT | CORE)
G_MS = (0, XBIT)


def layer_kernel(
    n_chunks,
    g_chunks,
    lens,
    tok_h,
    cot_h,
    gain,
    shift,
    bq,
    bk,
    bv,
    bup,
    obias,
    wq_h,
    wk_h,
    wv_h,
    wo_h,
    wu_h,
    wd_h,
    bn,
    bg,
    rsn_r,
    rsg_r,
    zout,
    vec_o,
    tok,
    gout,
    normed,
    turned_n,
    wq,
    wk,
    wv,
    wo,
    wu,
    wd,
    side_n,
    side_g,
    rsn_s,
    rsg_s,
    act,
    dact,
    gqkv,
    att,
    q_s,
    k_s,
    v_s,
    ga_s,
    amask,
    rot_c,
    rot_a,
    rot_b,
    stat_m,
    stat_i,
    zpart,
    zfar,
    znear,
    zmid,
    vzl,
    vz,
    vzr,
    vd,
    vdr,
    gsum,
    bsum,
    bsum_r,
    cot_rows,
    in_sem,
    wu_sem,
    wd_sem,
    sn_ss,
    sn_rs,
    sg_ss,
    sg_rs,
    bn_ss,
    bn_rs,
    bg_ss,
    bg_rs,
    rn_ss,
    rn_rs,
    rg_ss,
    rg_rs,
    zf_ss,
    zf_rs,
    zn_ss,
    zn_rs,
    zm_ss,
    zm_rs,
    zo_ss,
    zo_rs,
    zw_ss,
    zw_rs,
    vz_ss,
    vz_rs,
    vd_ss,
    vd_rs,
    bs_ss,
    bs_rs,
):
    toks, width = tok.shape
    hidden = wu.shape[1]
    heads_w = wq.shape[1]
    n_qkv = 3 * heads_w // BLK
    n_att = heads_w // BLK
    n_hid = hidden // BLK
    n_own = width // BLK
    dp = lax.axis_index("dp")
    zed = lax.axis_index("mp")
    inner = lax.rem(dp, GROUP)
    outer = dp - inner
    half = toks // 2
    piece_cols = width // Z_PARTS
    piece_rows = half // Z_PARTS

    def peer(mask):
        return (outer + flip(inner, mask), zed)

    middle = (zed == 1) | (zed == 2)
    end_of_line = (zed == 0) | (zed == 3)
    side_of_line = zed // 2
    beside = (dp, zed + 1 - 2 * lax.rem(zed, 2))
    across = (dp, 3 - zed)
    near_rows = mult(side_of_line * half, half)
    far_rows = mult((1 - side_of_line) * half, half)

    def zpeer(step):
        return (dp, lax.rem(zed + step, N_MP))

    def remote(src, dst, ssem, rsem, where):
        return pltpu.make_async_remote_copy(
            src_ref=src,
            dst_ref=dst,
            send_sem=ssem,
            recv_sem=rsem,
            device_id=where,
            device_id_type=MESH,
        )

    loads = [
        pltpu.make_async_copy(src, dst, in_sem.at[i])
        for i, (src, dst) in enumerate(
            ((cot_h, gout), (tok_h, tok), (wq_h, wq), (wk_h, wk), (wv_h, wv), (wo_h, wo))
        )
    ]
    for load in loads:
        load.start()

    def wu_load(c):
        cols = pl.ds(mult(c * BLK, BLK), BLK)
        return pltpu.make_async_copy(wu_h.at[:, cols], wu.at[:, cols], wu_sem.at[c])

    def wd_load(c):
        rows = pl.ds(mult(c * BLK, BLK), BLK)
        return pltpu.make_async_copy(wd_h.at[rows, :], wd.at[rows, :], wd_sem.at[c])

    @pl.loop(0, n_hid)
    def _(c):
        wu_load(c).start()

    @pl.loop(0, n_hid)
    def _(c):
        wd_load(c).start()

    cot_load = pltpu.make_async_copy(cot_h.at[pl.ds(near_rows, half), :], cot_rows, in_sem.at[6])
    cot_load.start()

    barrier = pltpu.get_barrier_semaphore()
    for mask in range(1, GROUP):
        pl.semaphore_signal(barrier, inc=1, device_id=peer(mask), device_id_type=MESH)
    for step in range(1, N_MP):
        pl.semaphore_signal(barrier, inc=1, device_id=zpeer(step), device_id_type=MESH)

    ends = []
    total_len = 0
    for j in range(lens.shape[1]):
        total_len = total_len + lens[0, j]
        ends.append(total_len)

    def segment_of(place):
        number = jnp.zeros_like(place)
        start_of = jnp.zeros_like(place)
        for j, end in enumerate(ends):
            start = end - lens[0, j]
            inside = ((place >= start) & (place < end)).astype(jnp.int32)
            number = number + inside * (j + 1)
            start_of = start_of + inside * start
        return number, start_of

    place_r = lax.broadcasted_iota(jnp.int32, (toks, toks), 0)
    place_c = lax.broadcasted_iota(jnp.int32, (toks, toks), 1)
    seg_r, _ = segment_of(place_r)
    seg_c, _ = segment_of(place_c)
    allowed = (seg_r == seg_c) & (place_c <= place_r)
    amask[...] = jnp.where(allowed, 0.0, -1e30)

    loads[0].wait()
    gsum[...] = jnp.zeros_like(gsum)
    step_rows = 32

    @pl.loop(0, toks // step_rows)
    def _(r):
        first = r * step_rows
        rows = pl.ds(mult(first, step_rows), step_rows)
        place = first + lax.broadcasted_iota(jnp.int32, (step_rows, width), 0)
        value = jnp.where(place < total_len, gout[rows, :].astype(F32), 0.0)
        gout[rows, :] = value.astype(BF16)
        gsum[0:1, :] = gsum[0:1, :] + jnp.sum(value, axis=0, keepdims=True)

    parity = lax.rem(zed, 2)

    def cross_core(index, times):
        return index + times * (1 - 2 * lax.rem(index, 2))

    def side_copy(to_side, ssem, rsem, chip_bit, other_bit, source, kind, m):
        owner_bit = m * other_bit
        if kind == 0:
            target = flip(cross_core(inner, parity), chip_bit)
            where = (outer + target, zed)
            slot_at = 1 + 2 * parity
        elif kind == 1:
            target = flip(inner, CORE)
            where = (outer + target, zed)
            slot_at = 2
        else:
            slot_at = 1 + 2 * parity
            where = beside
        place = to_side(m, mult(slot_at * toks, toks))
        src = place if kind == 2 else source(flip(target, owner_bit))
        return remote(src, place, ssem, rsem.at[kind, m], where)

    def side_g_copy(kind, m):
        def source(owner):
            return gout.at[:, pl.ds(mult(owner * BLK, BLK), BLK)]

        def to_side(m, at):
            return side_g.at[pl.ds(at, toks), pl.ds(m * BLK, BLK)]

        return side_copy(to_side, sg_ss, sg_rs, YBIT, XBIT, source, kind, m)

    def side_n_copy(kind, m):
        def source(owner):
            return turned_n.at[owner]

        def to_side(m, at):
            return side_n.at[pl.ds(m * BLK, BLK), pl.ds(at, toks)]

        return side_copy(to_side, sn_ss, sn_rs, XBIT, YBIT, source, kind, m)

    loads[1].wait()

    @pl.loop(0, toks // step_rows)
    def _(r):
        rows = pl.ds(mult(r * step_rows, step_rows), step_rows)
        value = tok[rows, :].astype(F32)
        mean = jnp.sum(value, axis=1, keepdims=True) * (1.0 / width)
        center = value - mean
        spread = jnp.sum(center * center, axis=1, keepdims=True) * (1.0 / width)
        inv = lax.rsqrt(spread + EPSILON)
        normed[rows, :] = (center * inv * gain[...] + shift[...]).astype(BF16)
        stat_m[rows, :] = jnp.broadcast_to(mean, (step_rows, 128))
        stat_i[rows, :] = jnp.broadcast_to(inv, (step_rows, 128))

    pl.semaphore_wait(barrier, GROUP - 1 + N_MP - 1)
    for m in (0, 1):
        side_g_copy(0, m).start()
    first_at = flip(cross_core(inner, parity), XBIT)
    for m in (0, 1):
        owner = flip(first_at, N_MS[m])
        turned_n[owner] = normed[:, pl.ds(mult(owner * BLK, BLK), BLK)].T
        side_n_copy(0, m).start()

    @pl.loop(0, n_own)
    def _(o):
        @pl.when((o != first_at) & (o != flip(first_at, YBIT)))
        def _():
            turned_n[o] = normed[:, pl.ds(mult(o * BLK, BLK), BLK)].T

    for m in (0, 1):
        side_g_copy(1, m).start()
        side_n_copy(1, m).start()
    for m in (0, 1):
        owner_g = mult(flip(inner, G_MS[m]) * BLK, BLK)
        side_g[0:toks, m * BLK : m * BLK + BLK] = gout[:, pl.ds(owner_g, BLK)]
        side_n[m * BLK : m * BLK + BLK, 0:toks] = turned_n[flip(inner, N_MS[m])]

    lane = lax.broadcasted_iota(jnp.int32, (toks, 128), 1)
    slot = lax.broadcasted_iota(jnp.int32, (toks, 128), 0)
    _, start_of = segment_of(slot)
    in_head = lane % HD
    order = (in_head % (ROT // 2)).astype(F32)
    freq = jnp.exp(order * (-2.0 / ROT * math.log(10000.0)))
    angle = (slot - start_of).astype(F32) * freq
    cosine, sine = jnp.cos(angle), jnp.sin(angle)
    rot_c[...] = jnp.where(in_head < ROT, cosine, 1.0)
    rot_a[...] = jnp.where(in_head < ROT // 2, -sine, 0.0)
    rot_b[...] = jnp.where((in_head >= ROT // 2) & (in_head < ROT), sine, 0.0)

    def rotate(value, sign):
        left = pltpu.roll(value, 128 - ROT // 2, 1)
        right = pltpu.roll(value, ROT // 2, 1)
        return value * rot_c[...] + sign * (left * rot_a[...] + right * rot_b[...])

    for load in loads[2:6]:
        load.wait()

    @pl.loop(0, heads_w // BLK)
    def _(n):
        cols = pl.ds(mult(n * BLK, BLK), BLK)
        query = nn(normed[...], wq[:, cols]) + bq[:, cols]
        keys = nn(normed[...], wk[:, cols]) + bk[:, cols]
        for part in range(BLK // 128):
            at = pl.ds(mult(n * BLK + part * 128, 128), 128)
            lanes = slice(part * 128, part * 128 + 128)
            q_s[:, at] = (rotate(query[:, lanes], 1.0) * 0.125).astype(BF16)
            k_s[:, at] = rotate(keys[:, lanes], 1.0).astype(BF16)
        v_s[:, cols] = (nn(normed[...], wv[:, cols]) + bv[:, cols]).astype(BF16)
        ga_s[:, cols] = nt(gout[...], wo[cols, :]).astype(BF16)

    def bn_copy(s, k):
        src = bn.at[s, pl.ds(toks if k == 2 else 0, toks), :]
        slot_at = (1, 2, 3)[k]
        return remote(
            src,
            bn.at[s, pl.ds(slot_at * toks, toks), :],
            bn_ss,
            bn_rs.at[s, min(k, 1)],
            peer((XBIT, CORE, CORE)[k]),
        )

    def bg_copy(s, k):
        src = bg.at[s, :, pl.ds(toks if k == 2 else 0, toks)]
        slot_at = (1, 2, 3)[k]
        return remote(
            src,
            bg.at[s, :, pl.ds(slot_at * toks, toks)],
            bg_ss,
            bg_rs.at[s, min(k, 1)],
            peer((YBIT, CORE, CORE)[k]),
        )

    def side_pass(m):
        for copy_of in (side_g_copy, side_n_copy):
            copy_of(0, m).wait_recv()
            copy_of(2, m).start()

    side_pass(0)
    low_lane = lax.broadcasted_iota(jnp.int32, (1, 128), 1) < HD
    head_mask = (jnp.where(low_lane, 1.0, 0.0).astype(BF16), jnp.where(low_lane, 0.0, 1.0).astype(BF16))
    low_full = lax.broadcasted_iota(jnp.int32, (toks, 128), 1) < HD

    @pl.loop(0, n_att)
    def _(n):
        @pl.when(n == n_att - 1)
        def _():
            side_pass(1)

        for part in range(BLK // 128):
            at = pl.ds(mult(n * BLK + part * 128, 128), 128)
            lanes = slice(part * 128, part * 128 + 128)
            qp, kp, vp, gp = q_s[:, at], k_s[:, at], v_s[:, at], ga_s[:, at]
            results = []
            for h in range(2):
                scores = nt(qp * head_mask[h], kp) + amask[...]
                top = jnp.max(scores, axis=1, keepdims=True)
                expo = jnp.exp(scores - top)
                probs = expo * (1.0 / jnp.sum(expo, axis=1, keepdims=True))
                probs_low = probs.astype(BF16)
                out = nn(probs_low, vp)
                prob_grad = nt(gp * head_mask[h], vp)
                delta = jnp.sum(probs * prob_grad, axis=1, keepdims=True)
                score_grad = (probs * (prob_grad - delta)).astype(BF16)
                results.append(
                    (out, nn(score_grad, kp), tn(score_grad, qp), tn(probs_low, gp))
                )
            out, dq, dk, dv = (
                jnp.where(low_full, first, second) for first, second in zip(*results)
            )
            att[:, at] = out.astype(BF16)
            bg[n, lanes, 0:toks] = out.astype(BF16).T
            dq = rotate(dq * 0.125, -1.0).astype(BF16)
            dk = rotate(dk, -1.0).astype(BF16)
            dv = dv.astype(BF16)
            for kind, value in enumerate((dq, dk, dv)):
                bn[n + kind * n_att, 0:toks, lanes] = value
                gqkv[:, pl.ds(mult(kind * heads_w + n * BLK + part * 128, 128), 128)] = value
        for k in (0, 1):
            bg_copy(n, k).start()
            for kind in range(3):
                bn_copy(n + kind * n_att, k).start()

    per_wide = WIDE // BLK

    @pl.loop(0, hidden // WIDE)
    def _(w):
        cols = pl.ds(mult(w * WIDE, WIDE), WIDE)
        for part in range(per_wide):
            wu_load(w * per_wide + part).wait()
        up = nn(normed[...], wu[:, cols]) + bup[:, cols]
        square = up * up
        tanh = jnp.tanh(GELU_A * up * (1.0 + GELU_B * square))
        active = (0.5 * up * (1.0 + tanh)).astype(BF16)
        act[:, cols] = active
        dact[:, cols] = (
            0.5 * (1.0 + tanh)
            + 0.5 * up * (1.0 - tanh * tanh) * (GELU_A * (1.0 + 3.0 * GELU_B * square))
        ).astype(BF16)
        for part in range(per_wide):
            c = n_att + w * per_wide + part
            bg[c, :, 0:toks] = active[:, part * BLK : part * BLK + BLK].T
            for k in (0, 1):
                bg_copy(c, k).start()

    def piece(t, g, first_row):
        if t == 0:
            return pl.ds(first_row, half), pl.ds(mult(g * piece_cols, piece_cols), piece_cols)
        return pl.ds(mult(first_row + g * piece_rows, piece_rows), piece_rows), pl.ds(0, width)

    def z_far(t, g):
        rows, cols = piece(t, g, far_rows)
        to_rows, _ = piece(t, g, 0)
        return remote(
            zpart.at[t, rows, cols],
            zfar.at[t, to_rows, cols],
            zf_ss,
            zf_rs.at[t * Z_PARTS + g],
            beside,
        )

    def z_near(t, g):
        rows, cols = piece(t, g, near_rows)
        to_rows, _ = piece(t, g, 0)
        return remote(
            zpart.at[t, rows, cols],
            znear.at[t, to_rows, cols],
            zn_ss,
            zn_rs.at[t * Z_PARTS + g],
            beside,
        )

    def z_mid(t, g):
        rows, cols = piece(t, g, far_rows)
        to_rows, _ = piece(t, g, 0)
        return remote(
            zpart.at[t, rows, cols],
            zmid.at[t, to_rows, cols],
            zm_ss,
            zm_rs.at[t * Z_PARTS + g],
            across,
        )

    def z_done(t, g, where):
        rows, cols = piece(t, g, near_rows)
        return remote(
            zout.at[t, rows, cols], zout.at[t, rows, cols], zo_ss, zo_rs.at[t * Z_PARTS + g], where
        )

    def z_pass(t, g):
        rows, cols = piece(t, g, far_rows)
        return remote(
            zout.at[t, rows, cols], zout.at[t, rows, cols], zw_ss, zw_rs.at[t * Z_PARTS + g], beside
        )

    def z_send(copies):
        @pl.when(end_of_line)
        def _():
            for copy in copies:
                copy.start()

    def z_first(t, g):
        z_far(t, g).wait_recv()
        rows, cols = piece(t, g, far_rows)
        there, _ = piece(t, g, 0)
        zpart[t, rows, cols] = (
            zpart[t, rows, cols].astype(F32) + zfar[t, there, cols].astype(F32)
        ).astype(BF16)
        z_mid(t, g).start()

    def z_second(t, g):
        z_near(t, g).wait_recv()
        z_mid(t, g).wait_recv()
        rows, cols = piece(t, g, near_rows)
        there, _ = piece(t, g, 0)
        total = (
            zpart[t, rows, cols].astype(F32)
            + znear[t, there, cols].astype(F32)
            + zmid[t, there, cols].astype(F32)
        )
        base = tok[rows, cols].astype(F32)
        if t == 0:
            place = near_rows + lax.broadcasted_iota(jnp.int32, total.shape, 0)
            branch = jnp.where(place < total_len, total + obias[:, cols], 0.0)
            zout[t, rows, cols] = (base + branch).astype(BF16)
        else:
            @pl.when(g == 0)
            def _():
                cot_load.wait()

            inv = stat_i[rows, 0:1]
            standard = (base - stat_m[rows, 0:1]) * inv
            grad = total * gain[...]
            mean_g = jnp.sum(grad, axis=1, keepdims=True) * (1.0 / width)
            mean_x = jnp.sum(grad * standard, axis=1, keepdims=True) * (1.0 / width)
            back = inv * (grad - mean_g - standard * mean_x)
            zout[t, rows, cols] = (cot_rows[there, :].astype(F32) + back).astype(BF16)
        z_done(t, g, across).start()
        z_done(t, g, beside).start()

    def z_third(t, g):
        z_done(t, g, across).wait_recv()
        z_pass(t, g).start()

    def z_tick(number, kinds=(0, 1)):
        for step, lag in ((z_first, 0), (z_second, Z_LAG), (z_third, 2 * Z_LAG)):
            at = number - lag
            for t in kinds:
                low = t * Z_PARTS
                if isinstance(number, int):
                    if low <= at < low + Z_PARTS:
                        pl.when(middle)(functools.partial(step, t, at - low))
                else:
                    inside = (at >= low) & (at < low + Z_PARTS)
                    pl.when(middle & inside)(functools.partial(step, t, at - low))

    @pl.loop(0, n_hid)
    def _(c):
        wd_load(c).wait()

    @pl.loop(0, width // WIDE)
    def _(n):
        cols = pl.ds(mult(n * WIDE, WIDE), WIDE)
        zpart[0, :, cols] = (nn(act[...], wd[:, cols]) + nn(att[...], wo[:, cols])).astype(BF16)
        for part in range(WIDE // piece_cols):
            g = n * (WIDE // piece_cols) + part
            z_send([z_far(0, g), z_near(0, g)])

    @pl.loop(0, hidden // WIDE)
    def _(w):
        cols = pl.ds(mult(w * WIDE, WIDE), WIDE)
        grad = (nt(gout[...], wd[cols, :]) * dact[:, cols].astype(F32)).astype(BF16)
        dact[:, cols] = grad
        for part in range(per_wide):
            c = n_qkv + w * per_wide + part
            bn[c, 0:toks, :] = grad[:, part * BLK : part * BLK + BLK]
            for k in (0, 1):
                bn_copy(c, k).start()

    z_tick(0)


    @pl.loop(0, width // WIDE)
    def _(n):
        cols = pl.ds(mult(n * WIDE, WIDE), WIDE)
        grad = nt(dact[...], wu[cols, :])
        for kind, weight in enumerate((wq, wk, wv)):
            grad = grad + nt(gqkv[:, kind * heads_w : (kind + 1) * heads_w], weight[cols, :])
        zpart[1, :, cols] = grad.astype(BF16)

        @pl.when(n == 2)
        def _():
            z_tick(1)

        for part in range(WIDE // 128):
            lanes = slice(part * 128, part * 128 + 128)
            at = pl.ds(mult(n * WIDE + part * 128, 128), 128)
            owner = n * per_wide + part * 128 // BLK
            into = slice(part * 128 % BLK, part * 128 % BLK + 128)
            piece_of = grad[:, lanes]
            standard = (tok[:, at].astype(F32) - stat_m[...]) * stat_i[...]
            vzl[owner, 0:1, into] = jnp.sum(piece_of * standard, axis=0, keepdims=True)
            vzl[owner, 1:2, into] = jnp.sum(piece_of, axis=0, keepdims=True)

    def vz_copy(step):
        return remote(vz, vzr.at[step], vz_ss, vz_rs.at[step], zpeer(step))

    for owner in range(n_own):
        vz[owner : owner + 1, :] = vzl[owner, 0:1, :]
        vz[n_own + owner : n_own + owner + 1, :] = vzl[owner, 1:2, :]
    for step in range(1, N_MP):
        vz_copy(step).start()
    for g in range(Z_PARTS):
        z_send([z_far(1, g), z_near(1, g)])

    def vd_copy(mask):
        return remote(
            vd.at[flip(inner, mask)],
            vdr.at[mask],
            vd_ss,
            vd_rs.at[mask],
            peer(mask),
        )

    bs_copy = remote(bsum, bsum_r, bs_ss, bs_rs, peer(YBIT))

    def rn_copy(s):
        return remote(rsn_s.at[s], rsn_r.at[s], rn_ss, rn_rs.at[s], peer(YBIT))

    def rg_copy(s):
        return remote(rsg_s.at[s], rsg_r.at[s], rg_ss, rg_rs.at[s], peer(XBIT))

    for kind in (1, 2):
        for m in (0, 1):
            side_g_copy(kind, m).wait_recv()
            side_n_copy(kind, m).wait_recv()
    bsum[...] = jnp.zeros_like(bsum)

    def vec_spread():
        total = vz[...]
        for step in range(1, N_MP):
            vz_copy(step).wait_recv()
            total = total + vzr[step]
        vd[...] = jnp.zeros_like(vd)
        for owner in range(n_own):
            vd[owner, 0:1, :] = total[owner : owner + 1, :]
            vd[owner, 1:2, :] = total[n_own + owner : n_own + owner + 1, :]
            vd[owner, 2:3, :] = gsum[0:1, owner * BLK : owner * BLK + BLK]
        for mask in range(1, GROUP):
            vd_copy(mask).start()

    def pair_n(p):
        return bn.at[p, pl.ds(2 * toks, 2 * toks), :]

    def pair_g(p):
        return bg.at[p, :, pl.ds(2 * toks, 2 * toks)]

    side_n[2 * BLK :, :] = jnp.ones((16, 4 * toks), BF16)

    @pl.loop(0, n_chunks + 1)
    def _(s):
        @pl.when(s < n_chunks)
        def _():
            bn_copy(s, 0).wait_recv()
            bn_copy(s, 2).start()

        @pl.when(s < g_chunks)
        def _():
            bg_copy(s, 0).wait_recv()
            bg_copy(s, 2).start()

        @pl.when(s > 0)
        def _():
            p = s - 1
            pltpu.make_async_copy(pair_n(p), pair_n(p), bn_rs.at[p, 1]).wait()
            both = nn(side_n[...], bn[p])
            rsn_s[p] = both[BLK : 2 * BLK, :].astype(BF16)
            rn_copy(p).start()
            bsum[pl.ds(p, 1), :] = both[2 * BLK : 2 * BLK + 1, :]
            bn[p, 2 * toks : 3 * toks, :] = both[:BLK, :].astype(BF16)

        @pl.when((s > 0) & (s <= g_chunks))
        def _():
            p = s - 1
            pltpu.make_async_copy(pair_g(p), pair_g(p), bg_rs.at[p, 1]).wait()
            both = nn(bg[p], side_g[...])
            rsg_s[p] = both[:, BLK:].astype(BF16)
            rg_copy(p).start()
            bg[p, :, 2 * toks : 3 * toks] = both[:, :BLK].astype(BF16)

        tick = -1
        for turn, number in Z_TICKS:
            tick = jnp.where(s == turn, number, tick)
        z_tick(tick)

    bs_copy.start()
    vec_spread()
    @pl.loop(Z_TICKS[-1][1] + 1, 2 * Z_PARTS + 2 * Z_LAG)
    def _(number):
        z_tick(number)

    bs_copy.wait_recv()
    sums = vd[inner]
    for mask in range(1, GROUP):
        vd_copy(mask).wait_recv()
        sums = sums + vdr[mask]
    vec_o[0:8, :] = sums
    vec_o[8:, :] = bsum[...] + bsum_r[...]

    @pl.loop(0, n_chunks)
    def _(s):
        rn_copy(s).wait_recv()

    @pl.loop(0, g_chunks)
    def _(s):
        rg_copy(s).wait_recv()

    def sent(ref, sem):
        pltpu.make_async_copy(ref, ref, sem).wait()

    sent(side_n.at[pl.ds(0, 2 * BLK), pl.ds(0, 3 * toks)], sn_ss)
    sent(side_g.at[pl.ds(0, 3 * toks), :], sg_ss)
    sent(bn.at[:, pl.ds(0, 3 * toks), :], bn_ss)
    sent(bg.at[:, :, pl.ds(0, 3 * toks)], bg_ss)
    sent(rsn_s, rn_ss)
    sent(rsg_s, rg_ss)
    sent(vzr.at[pl.ds(1, N_MP - 1)], vz_ss)
    sent(vdr.at[pl.ds(1, GROUP - 1)], vd_ss)
    bs_copy.wait_send()

    @pl.when(end_of_line)
    def _():
        sent(zfar, zf_ss)
        sent(znear, zn_ss)
        for t in (0, 1):
            for g in range(Z_PARTS):
                z_done(t, g, beside).wait_recv()
                z_pass(t, g).wait_recv()
        cot_load.wait()

    @pl.when(middle)
    def _():
        sent(zmid, zm_ss)
        sent(zout, zo_ss)
        sent(zmid, zw_ss)


def write_kernel(n_qkv, n_att, bn, bg, rsn, rsg, zout, vec, mixed_h, gtok_h, gain_o, shift_o, gq_h, bq_o, gk_h, bk_o, gv_h, bv_o, go_h, gu_h, bu_o, gd_h, ob_o, stage, sems, zsem):
    n_chunks, n_g = bn.shape[0], bg.shape[0]
    toks = zout.shape[1]
    slots = stage.shape[0]
    z_outs = [
        pltpu.make_async_copy(zout.at[t], out, zsem.at[t]) for t, out in enumerate((mixed_h, gtok_h))
    ]
    for out in z_outs:
        out.start()
    places = []
    for s in range(n_chunks):
        if s < n_qkv:
            out, at = (gq_h, gk_h, gv_h)[s // n_att], s % n_att
        else:
            out, at = gu_h, s - n_qkv
        places.append((True, s, out.at[:, pl.ds(at * BLK, BLK)]))
    for s in range(n_g):
        out, at = (go_h, s) if s < n_att else (gd_h, s - n_att)
        places.append((False, s, out.at[pl.ds(at * BLK, BLK), :]))
    copies = []
    for number, (first, s, place) in enumerate(places):
        slot = number % slots
        if number >= slots:
            copies[number - slots].wait()
        if first:
            value = bn[s, 2 * toks : 3 * toks, :].astype(F32) + rsn[s].astype(F32)
        else:
            value = bg[s, :, 2 * toks : 3 * toks].astype(F32) + rsg[s].astype(F32)
        stage[slot] = value
        copies.append(pltpu.make_async_copy(stage.at[slot], place, sems.at[slot]))
        copies[number].start()
    for row, out in enumerate((gain_o, shift_o, ob_o)):
        out[...] = vec[row]
    row = 8
    for out in (bq_o, bk_o, bv_o, bu_o):
        for at in range(out.shape[0] // BLK):
            out[at * BLK : at * BLK + BLK] = vec[row]
            row += 1
    for copy in copies[-slots:]:
        copy.wait()
    for out in z_outs:
        out.wait()


def layer(tokens, lengths, ln_gain, ln_bias, w_query, b_query, w_key, b_key, w_value, b_value, w_out, w_up, b_up, w_down, out_bias, cotangent):
    toks, width = tokens.shape
    heads_w = w_query.shape[1]
    hidden = w_up.shape[1]
    n_chunks = (3 * heads_w + hidden) // BLK
    g_chunks = (heads_w + hidden) // BLK
    n_own = width // BLK
    n_vec = -(-n_chunks // 8) * 8
    half = toks // 2
    dma = pltpu.SemaphoreType.DMA
    vmem = pltpu.VMEM
    scratch = [
        vmem((toks, width), BF16),
        vmem((toks, width), BF16),
        vmem((toks, width), BF16),
        vmem((n_own, BLK, toks), BF16),
        vmem(w_query.shape, BF16),
        vmem(w_key.shape, BF16),
        vmem(w_value.shape, BF16),
        vmem(w_out.shape, BF16),
        vmem(w_up.shape, BF16),
        vmem(w_down.shape, BF16),
        vmem((2 * BLK + 16, 4 * toks), BF16),
        vmem((4 * toks, 2 * BLK), BF16),
        vmem((n_chunks, BLK, BLK), BF16),
        vmem((g_chunks, BLK, BLK), BF16),
        vmem((toks, hidden), BF16),
        vmem((toks, hidden), BF16),
        vmem((toks, 3 * heads_w), BF16),
        vmem((toks, heads_w), BF16),
        vmem((toks, heads_w), BF16),
        vmem((toks, heads_w), BF16),
        vmem((toks, heads_w), BF16),
        vmem((toks, heads_w), BF16),
        vmem((toks, toks), F32),
        vmem((toks, 128), F32),
        vmem((toks, 128), F32),
        vmem((toks, 128), F32),
        vmem((toks, 128), F32),
        vmem((toks, 128), F32),
        vmem((2, toks, width), BF16),
        vmem((2, half, width), BF16),
        vmem((2, half, width), BF16),
        vmem((2, half, width), BF16),
        vmem((n_own, 8, BLK), F32),
        vmem((2 * n_own, BLK), F32),
        vmem((N_MP, 2 * n_own, BLK), F32),
        vmem((n_own, 8, BLK), F32),
        vmem((GROUP, 8, BLK), F32),
        vmem((8, width), F32),
        vmem((n_vec, BLK), F32),
        vmem((n_vec, BLK), F32),
        vmem((half, width), BF16),
        dma((7,)),
        dma((hidden // BLK,)),
        dma((hidden // BLK,)),
        dma,
        dma((3, 2)),
        dma,
        dma((3, 2)),
        dma,
        dma((n_chunks, 2)),
        dma,
        dma((g_chunks, 2)),
        dma,
        dma((n_chunks,)),
        dma,
        dma((g_chunks,)),
        dma,
        dma((2 * Z_PARTS,)),
        dma,
        dma((2 * Z_PARTS,)),
        dma,
        dma((2 * Z_PARTS,)),
        dma,
        dma((2 * Z_PARTS,)),
        dma,
        dma((2 * Z_PARTS,)),
        dma,
        dma((N_MP,)),
        dma,
        dma((GROUP,)),
        dma,
        dma,
    ]
    anyspace = pl.BlockSpec(memory_space=pl.ANY)
    local = pl.BlockSpec(memory_space=pltpu.VMEM)
    row = lambda value: value.reshape(1, -1)
    kept = pl.pallas_call(
        functools.partial(layer_kernel, n_chunks, g_chunks),
        out_shape=(
            vmem((n_chunks, 4 * toks, BLK), BF16),
            vmem((g_chunks, BLK, 4 * toks), BF16),
            vmem((n_chunks, BLK, BLK), BF16),
            vmem((g_chunks, BLK, BLK), BF16),
            vmem((2, toks, width), BF16),
            vmem((8 + n_vec, BLK), F32),
        ),
        in_specs=[pl.BlockSpec(memory_space=pltpu.SMEM), anyspace, anyspace]
        + [local] * 7
        + [anyspace] * 6,
        out_specs=(local,) * 6,
        scratch_shapes=scratch,
        compiler_params=pltpu.CompilerParams(
            collective_id=0, has_side_effects=True, vmem_limit_bytes=MAIN_VMEM
        ),
    )(
        lengths,
        tokens,
        cotangent,
        row(ln_gain),
        row(ln_bias),
        row(b_query),
        row(b_key),
        row(b_value),
        row(b_up),
        row(out_bias),
        w_query,
        w_key,
        w_value,
        w_out,
        w_up,
        w_down,
    )
    f32 = lambda *shape: jax.ShapeDtypeStruct(shape, F32)
    low = jax.ShapeDtypeStruct((toks, width), BF16)
    spec = lambda kind: anyspace if len(kind.shape) == 2 else local
    outs = (
        low,
        low,
        f32(BLK),
        f32(BLK),
        f32(BLK, heads_w),
        f32(heads_w),
        f32(BLK, heads_w),
        f32(heads_w),
        f32(BLK, heads_w),
        f32(heads_w),
        f32(heads_w, BLK),
        f32(BLK, hidden),
        f32(hidden),
        f32(hidden, BLK),
        f32(BLK),
    )
    slots = n_chunks + g_chunks
    return pl.pallas_call(
        functools.partial(write_kernel, 3 * heads_w // BLK, heads_w // BLK),
        out_shape=outs,
        in_specs=[local] * 6,
        out_specs=tuple(spec(kind) for kind in outs),
        scratch_shapes=[vmem((slots, BLK, BLK), F32), dma((slots,)), dma((2,))],
        compiler_params=pltpu.CompilerParams(vmem_limit_bytes=12 * 2**20),
    )(*kept)


def make_body(n_dp, n_mp):
    outer = n_dp // GROUP

    def order(value, axis):
        if outer == 1:
            return value
        shape = value.shape
        split = shape[:axis] + (outer, GROUP, shape[axis] // n_dp) + shape[axis + 1 :]
        return jnp.swapaxes(value.reshape(split), axis, axis + 1).reshape(shape)

    def restore(value, axis):
        if outer == 1:
            return value
        shape = value.shape
        split = shape[:axis] + (GROUP, outer, shape[axis] // n_dp) + shape[axis + 1 :]
        return jnp.swapaxes(value.reshape(split), axis, axis + 1).reshape(shape)

    groups = [[o * GROUP + i for o in range(outer)] for i in range(GROUP)]

    def scatter(value, axis):
        if outer == 1:
            return value
        return lax.psum_scatter(
            value, "dp", scatter_dimension=axis, axis_index_groups=groups, tiled=True
        )

    def total(value):
        if outer == 1:
            return value
        return lax.psum(value, "dp", axis_index_groups=groups)

    def body(tokens, lengths, ln_gain, ln_bias, w_query, b_query, w_key, b_key, w_value, b_value, w_out, w_up, b_up, w_down, out_bias, cotangent):
        found = layer(
            order(tokens, 1),
            lengths,
            order(ln_gain, 0),
            order(ln_bias, 0),
            order(w_query, 0),
            b_query,
            order(w_key, 0),
            b_key,
            order(w_value, 0),
            b_value,
            order(w_out, 1),
            order(w_up, 0),
            b_up,
            order(w_down, 1),
            order(out_bias, 0),
            order(cotangent, 1),
        )
        (mixed, grad_tokens, gain, shift, g_q, b_q, g_k, b_k, g_v, b_v, g_out, g_up, b_u, g_down, b_out) = found
        return (
            restore(mixed, 1),
            restore(grad_tokens, 1),
            scatter(gain, 0),
            scatter(shift, 0),
            scatter(g_q, 0),
            total(b_q),
            scatter(g_k, 0),
            total(b_k),
            scatter(g_v, 0),
            total(b_v),
            scatter(g_out, 1),
            scatter(g_up, 0),
            total(b_u),
            scatter(g_down, 1),
            scatter(b_out, 0),
        )

    return body


def solution(mesh):
    in_specs = (
        P("dp", None),
        P("dp", None),
        P(),
        P(),
        P(None, "mp"),
        P("mp"),
        P(None, "mp"),
        P("mp"),
        P(None, "mp"),
        P("mp"),
        P("mp", None),
        P(None, "mp"),
        P("mp"),
        P("mp", None),
        P(),
        P("dp", None),
    )
    out_specs = (
        P("dp", None),
        P("dp", None),
        P("dp"),
        P("dp"),
        P("dp", "mp"),
        P("mp"),
        P("dp", "mp"),
        P("mp"),
        P("dp", "mp"),
        P("mp"),
        P("mp", "dp"),
        P("dp", "mp"),
        P("mp"),
        P("mp", "dp"),
        P("dp"),
    )
    body = make_body(mesh.shape["dp"], mesh.shape["mp"])
    return jax.shard_map(body, mesh=mesh, in_specs=in_specs, out_specs=out_specs, check_vma=False)
```

```python
import functools
import math

import jax
import jax.numpy as jnp
from jax import lax
from jax.experimental import pallas as pl
from jax.experimental.pallas import tpu as pltpu
from jax.sharding import PartitionSpec as P

HD = 64
ROT = 32
EPSILON = 1e-05
GROUP = 8
CORE, XBIT, YBIT = 1, 2, 4
BLK = 256
WIDE = 512
N_MP = 4
Z_PARTS = 8
Z_LAG = 2
Z_TICKS = ((1, 2), (4, 3), (7, 4), (8, 5), (9, 6), (10, 7), (11, 8), (12, 9), (13, 10))
F32 = jnp.float32
BF16 = jnp.bfloat16
MESH = pl.DeviceIdType.MESH
MAIN_VMEM = 93 * 2**19
GELU_A = math.sqrt(2.0 / math.pi)
GELU_B = 0.044715


def nn(left, right):
    return lax.dot_general(left, right, (((1,), (0,)), ((), ())), preferred_element_type=F32)


def nt(left, right):
    return lax.dot_general(left, right, (((1,), (1,)), ((), ())), preferred_element_type=F32)


def tn(left, right):
    return lax.dot_general(left, right, (((0,), (0,)), ((), ())), preferred_element_type=F32)


def flip(index, mask):
    for bit in (1, 2, 4):
        if mask & bit:
            index = index + bit * (1 - 2 * ((index // bit) % 2))
    return index


def mult(value, by):
    return pl.multiple_of(value, by)


N_JS = (0, XBIT, CORE, XBIT | CORE)
N_MS = (0, YBIT)
G_JS = (0, YBIT, CORE, YBIT | CORE)
G_MS = (0, XBIT)


def layer_kernel(
    n_chunks,
    g_chunks,
    lens_h,
    tok_h,
    cot_h,
    gain_h,
    shift_h,
    bq_h,
    bk_h,
    bv_h,
    bup_h,
    obias_h,
    wq_h,
    wk_h,
    wv_h,
    wo_h,
    wu_h,
    wd_h,
    bn,
    bg,
    rsn_r,
    rsg_r,
    zout,
    vec_o,
    lens,
    gain,
    shift,
    bq,
    bk,
    bv,
    bup,
    obias,
    tok,
    gout,
    normed,
    turned_n,
    wq,
    wk,
    wv,
    wo,
    wu,
    wd,
    side_n,
    side_g,
    rsn_s,
    rsg_s,
    act,
    dact,
    gqkv,
    att,
    q_s,
    k_s,
    v_s,
    ga_s,
    amask,
    rot_c,
    rot_a,
    rot_b,
    stat_m,
    stat_i,
    zpart,
    zfar,
    znear,
    zmid,
    vzl,
    vz,
    vzr,
    vdr,
    gsum,
    bsum,
    bsum_r,
    cot_rows,
    in_sem,
    sn_ss,
    sg_ss,
    side_rs,
    bn_ss,
    bg_ss,
    blk_rs,
    rn_ss,
    rn_rs,
    rg_ss,
    rg_rs,
    zf_ss,
    zf_rs,
    zn_ss,
    zm_ss,
    zm_rs,
    zo_ss,
    zo_rs,
    zw_ss,
    ze_rs,
    vz_ss,
    vz_rs,
    vd_ss,
    vd_rs,
    bs_ss,
    bs_rs,
):
    toks, width = tok.shape
    hidden = wu.shape[1]
    heads_w = wq.shape[1]
    n_att = heads_w // BLK
    n_hid = hidden // BLK
    n_own = width // BLK
    dp = lax.axis_index("dp")
    zed = lax.axis_index("mp")
    inner = lax.rem(dp, GROUP)
    outer = dp - inner
    half = toks // 2
    piece_cols = width // Z_PARTS
    piece_rows = half // Z_PARTS

    def peer(mask):
        return (outer + flip(inner, mask), zed)

    def came(ref, sem):
        pltpu.make_async_copy(ref, ref, sem).wait()

    middle = (zed == 1) | (zed == 2)
    end_of_line = (zed == 0) | (zed == 3)
    side_of_line = zed // 2
    beside = (dp, zed + 1 - 2 * lax.rem(zed, 2))
    across = (dp, 3 - zed)
    near_rows = mult(side_of_line * half, half)
    far_rows = mult((1 - side_of_line) * half, half)

    def zpeer(step):
        return (dp, lax.rem(zed + step, N_MP))

    def remote(src, dst, ssem, rsem, where):
        return pltpu.make_async_remote_copy(
            src_ref=src,
            dst_ref=dst,
            send_sem=ssem,
            recv_sem=rsem,
            device_id=where,
            device_id_type=MESH,
        )

    def load(src, dst, number):
        copy = pltpu.make_async_copy(src, dst, in_sem.at[number])
        copy.start()
        return copy

    tok_load = load(tok_h, tok, 0)
    gain_load = load(gain_h, gain, 1)
    shift_load = load(shift_h, shift, 2)
    lens_load = load(lens_h, lens, 3)

    barrier = pltpu.get_barrier_semaphore()
    for mask in range(1, GROUP):
        pl.semaphore_signal(barrier, inc=1, device_id=peer(mask), device_id_type=MESH)
    for step in range(1, N_MP):
        pl.semaphore_signal(barrier, inc=1, device_id=zpeer(step), device_id_type=MESH)

    gout_load = load(cot_h, gout, 4)
    bias_loads = [
        load(src, dst, 5 + i)
        for i, (src, dst) in enumerate(
            ((bup_h, bup), (bq_h, bq), (bk_h, bk), (bv_h, bv), (obias_h, obias))
        )
    ]
    wu_load = load(wu_h, wu, 10)
    wd_load = load(wd_h, wd, 11)
    for src, dst in ((wq_h, wq), (wk_h, wk), (wv_h, wv), (wo_h, wo)):
        load(src, dst, 12)
    attn_load = pltpu.make_async_copy(wu_h, wu, in_sem.at[12])
    cot_load = load(cot_h.at[pl.ds(near_rows, half), :], cot_rows, 13)

    def segment_of(place):
        number = jnp.zeros_like(place)
        start_of = jnp.zeros_like(place)
        for j, end in enumerate(ends):
            start = end - lens[0, j]
            inside = ((place >= start) & (place < end)).astype(jnp.int32)
            number = number + inside * (j + 1)
            start_of = start_of + inside * start
        return number, start_of

    parity = lax.rem(zed, 2)

    def cross_core(index, times):
        return index + times * (1 - 2 * lax.rem(index, 2))

    def side_copy(to_side, ssem, chip_bit, other_bit, source, kind, m):
        owner_bit = m * other_bit
        if kind == 0:
            target = flip(cross_core(inner, parity), chip_bit)
            where = (outer + target, zed)
            slot_at = 1 + 2 * parity
        elif kind == 1:
            target = flip(inner, CORE)
            where = (outer + target, zed)
            slot_at = 2
        else:
            slot_at = 1 + 2 * parity
            where = beside
        place = to_side(m, mult(slot_at * toks, toks))
        src = place if kind == 2 else source(flip(target, owner_bit))
        return remote(src, place, ssem, side_rs.at[m if kind == 0 else 2], where)

    def side_g_copy(kind, m):
        def source(owner):
            return cot_h.at[:, pl.ds(mult(owner * BLK, BLK), BLK)]

        def to_side(m, at):
            return side_g.at[pl.ds(at, toks), pl.ds(m * BLK, BLK)]

        return side_copy(to_side, sg_ss, YBIT, XBIT, source, kind, m)

    def side_n_copy(kind, m):
        def source(owner):
            return turned_n.at[owner]

        def to_side(m, at):
            return side_n.at[pl.ds(m * BLK, BLK), pl.ds(at, toks)]

        return side_copy(to_side, sn_ss, XBIT, YBIT, source, kind, m)

    for copy in (tok_load, gain_load, shift_load):
        copy.wait()
    step_rows = 32

    @pl.loop(0, toks // step_rows, unroll=2)
    def _(r):
        rows = pl.ds(mult(r * step_rows, step_rows), step_rows)
        value = tok[rows, :].astype(F32)
        mean = jnp.sum(value, axis=1, keepdims=True) * (1.0 / width)
        center = value - mean
        spread = jnp.sum(center * center, axis=1, keepdims=True) * (1.0 / width)
        inv = lax.rsqrt(spread + EPSILON)
        normed[rows, :] = (center * inv * gain[...] + shift[...]).astype(BF16)
        stat_m[rows, :] = jnp.broadcast_to(mean, (step_rows, 128))
        stat_i[rows, :] = jnp.broadcast_to(inv, (step_rows, 128))

    pl.semaphore_wait(barrier, GROUP - 1 + N_MP - 1)
    for m in (0, 1):
        side_g_copy(0, m).start()
    first_at = flip(cross_core(inner, parity), XBIT)
    for m in (0, 1):
        owner = flip(first_at, N_MS[m])
        turned_n[owner] = normed[:, pl.ds(mult(owner * BLK, BLK), BLK)].T
        side_n_copy(0, m).start()

    @pl.loop(0, n_own)
    def _(o):
        @pl.when((o != first_at) & (o != flip(first_at, YBIT)))
        def _():
            turned_n[o] = normed[:, pl.ds(mult(o * BLK, BLK), BLK)].T

    for m in (0, 1):
        side_g_copy(1, m).start()
        side_n_copy(1, m).start()
    for copy in (lens_load, gout_load, *bias_loads):
        copy.wait()

    ends = []
    total_len = 0
    for j in range(lens.shape[1]):
        total_len = total_len + lens[0, j]
        ends.append(total_len)

    gsum[...] = jnp.zeros_like(gsum)

    @pl.loop(0, toks // step_rows)
    def _(r):
        first = r * step_rows
        rows = pl.ds(mult(first, step_rows), step_rows)
        place = first + lax.broadcasted_iota(jnp.int32, (step_rows, width), 0)
        value = jnp.where(place < total_len, gout[rows, :].astype(F32), 0.0)
        gout[rows, :] = value.astype(BF16)
        gsum[0:1, :] = gsum[0:1, :] + jnp.sum(value, axis=0, keepdims=True)

    for m in (0, 1):
        owner_g = mult(flip(inner, G_MS[m]) * BLK, BLK)
        side_g[0:toks, m * BLK : m * BLK + BLK] = gout[:, pl.ds(owner_g, BLK)]
        side_n[m * BLK : m * BLK + BLK, 0:toks] = turned_n[flip(inner, N_MS[m])]

    def bn_copy(s, k):
        src = bn.at[s, pl.ds(toks if k == 2 else 0, toks), :]
        slot_at = (1, 2, 3)[k]
        return remote(
            src,
            bn.at[s, pl.ds(slot_at * toks, toks), :],
            bn_ss,
            blk_rs.at[s, min(k, 1)],
            peer((XBIT, CORE, CORE)[k]),
        )

    def bg_copy(s, k):
        src = bg.at[s, :, pl.ds(toks if k == 2 else 0, toks)]
        slot_at = (1, 2, 3)[k]
        return remote(
            src,
            bg.at[s, :, pl.ds(slot_at * toks, toks)],
            bg_ss,
            blk_rs.at[s, min(k, 1)],
            peer((YBIT, CORE, CORE)[k]),
        )

    def piece(t, g, first_row):
        if t == 0:
            return pl.ds(first_row, half), pl.ds(mult(g * piece_cols, piece_cols), piece_cols)
        return pl.ds(mult(first_row + g * piece_rows, piece_rows), piece_rows), pl.ds(0, width)

    def z_far(t, g):
        rows, cols = piece(t, g, far_rows)
        to_rows, _ = piece(t, g, 0)
        return remote(
            zpart.at[t, rows, cols],
            zfar.at[t, to_rows, cols],
            zf_ss,
            zf_rs.at[t * Z_PARTS + g],
            beside,
        )

    def z_near(t, g):
        rows, cols = piece(t, g, near_rows)
        to_rows, _ = piece(t, g, 0)
        return remote(
            zpart.at[t, rows, cols],
            znear.at[t, to_rows, cols],
            zn_ss,
            zm_rs.at[t * Z_PARTS + g],
            beside,
        )

    def z_mid(t, g):
        rows, cols = piece(t, g, far_rows)
        to_rows, _ = piece(t, g, 0)
        return remote(
            zpart.at[t, rows, cols],
            zmid.at[t, to_rows, cols],
            zm_ss,
            zm_rs.at[t * Z_PARTS + g],
            across,
        )

    def z_done(t, g, to_end):
        rows, cols = piece(t, g, near_rows)
        place = zout.at[t, rows, cols]
        if to_end:
            return remote(place, place, zo_ss, ze_rs, beside)
        return remote(place, place, zo_ss, zo_rs.at[t * Z_PARTS + g], across)

    def z_pass(t, g):
        rows, cols = piece(t, g, far_rows)
        return remote(zout.at[t, rows, cols], zout.at[t, rows, cols], zw_ss, ze_rs, beside)

    def z_send(copies):
        @pl.when(end_of_line)
        def _():
            for copy in copies:
                copy.start()

    def z_first(t, g):
        z_far(t, g).wait_recv()
        rows, cols = piece(t, g, far_rows)
        there, _ = piece(t, g, 0)
        zpart[t, rows, cols] = (
            zpart[t, rows, cols].astype(F32) + zfar[t, there, cols].astype(F32)
        ).astype(BF16)
        z_mid(t, g).start()

    def z_second(t, g):
        came(znear.at[0, :, pl.ds(0, 2 * piece_cols)], zm_rs.at[t * Z_PARTS + g])
        rows, cols = piece(t, g, near_rows)
        there, _ = piece(t, g, 0)
        total = (
            zpart[t, rows, cols].astype(F32)
            + znear[t, there, cols].astype(F32)
            + zmid[t, there, cols].astype(F32)
        )
        base = tok[rows, cols].astype(F32)
        if t == 0:
            place = near_rows + lax.broadcasted_iota(jnp.int32, total.shape, 0)
            branch = jnp.where(place < total_len, total + obias[:, cols], 0.0)
            zout[t, rows, cols] = (base + branch).astype(BF16)
        else:
            @pl.when(g == 0)
            def _():
                cot_load.wait()

            inv = stat_i[rows, 0:1]
            standard = (base - stat_m[rows, 0:1]) * inv
            grad = total * gain[...]
            mean_g = jnp.sum(grad, axis=1, keepdims=True) * (1.0 / width)
            mean_x = jnp.sum(grad * standard, axis=1, keepdims=True) * (1.0 / width)
            back = inv * (grad - mean_g - standard * mean_x)
            zout[t, rows, cols] = (cot_rows[there, :].astype(F32) + back).astype(BF16)
        z_done(t, g, False).start()
        z_done(t, g, True).start()

    def z_third(t, g):
        z_done(t, g, False).wait_recv()
        z_pass(t, g).start()

    def z_tick(number, kinds=(0, 1)):
        for step, lag in ((z_first, 0), (z_second, Z_LAG), (z_third, 2 * Z_LAG)):
            at = number - lag
            for t in kinds:
                low = t * Z_PARTS
                if isinstance(number, int):
                    if low <= at < low + Z_PARTS:
                        pl.when(middle)(functools.partial(step, t, at - low))
                else:
                    inside = (at >= low) & (at < low + Z_PARTS)
                    pl.when(middle & inside)(functools.partial(step, t, at - low))

    per_wide = WIDE // BLK

    wu_load.wait()

    @pl.loop(0, hidden // (2 * WIDE))
    def _(w):
        blocks = [pl.ds(mult((2 * w + side) * WIDE, WIDE), WIDE) for side in (0, 1)]
        ups = [nn(normed[...], wu[:, cols]) + bup[:, cols] for cols in blocks]
        for side, (up, cols) in enumerate(zip(ups, blocks)):
            square = up * up
            tanh = jnp.tanh(GELU_A * up * (1.0 + GELU_B * square))
            row = lax.broadcasted_iota(jnp.int32, up.shape, 0)
            active = jnp.where(row < total_len, 0.5 * up * (1.0 + tanh), 0.0).astype(BF16)
            act[:, cols] = active
            dact[:, cols] = (
                0.5 * (1.0 + tanh)
                + 0.5 * up * (1.0 - tanh * tanh) * (GELU_A * (1.0 + 3.0 * GELU_B * square))
            ).astype(BF16)
            for part in range(per_wide):
                c = (2 * w + side) * per_wide + part
                bg[c, :, 0:toks] = active[:, part * BLK : part * BLK + BLK].T
        for part in range(2 * per_wide):
            for k in (0, 1):
                bg_copy(2 * w * per_wide + part, k).start()

    def side_pass(m):
        came(bn.at[0, pl.ds(0, 2 * toks), :], side_rs.at[m])
        for copy_of in (side_g_copy, side_n_copy):
            copy_of(2, m).start()

    side_pass(0)

    def hidden_grad(first, past, shift):
        @pl.loop(first, past)
        def _(w):
            cols = pl.ds(mult(w * WIDE, WIDE), WIDE)
            grad = (nt(gout[...], wd[cols, :]) * dact[:, cols].astype(F32)).astype(BF16)
            dact[:, cols] = grad
            for part in range(per_wide):
                c = shift + w * per_wide + part
                bn[c, 0:toks, :] = grad[:, part * BLK : part * BLK + BLK]
                for k in (0, 1):
                    bn_copy(c, k).start()

    n_wide = hidden // WIDE
    wd_load.wait()
    hidden_grad(0, n_wide // 2, 0)
    side_pass(1)

    place_r = lax.broadcasted_iota(jnp.int32, (toks, toks), 0)
    place_c = lax.broadcasted_iota(jnp.int32, (toks, toks), 1)
    seg_r, _ = segment_of(place_r)
    seg_c, _ = segment_of(place_c)
    allowed = (seg_r == seg_c) & (place_c <= place_r)
    for h in (0, 1):
        amask[h * toks : h * toks + toks, :] = jnp.where(allowed, 0.0, -1e30)

    lane = lax.broadcasted_iota(jnp.int32, (toks, 128), 1)
    slot = lax.broadcasted_iota(jnp.int32, (toks, 128), 0)
    _, start_of = segment_of(slot)
    in_head = lane % HD
    order = (in_head % (ROT // 2)).astype(F32)
    freq = jnp.exp(order * (-2.0 / ROT * math.log(10000.0)))
    angle = (slot - start_of).astype(F32) * freq
    cosine, sine = jnp.cos(angle), jnp.sin(angle)
    rot_c[...] = jnp.where(in_head < ROT, cosine, 1.0)
    rot_a[...] = jnp.where(in_head < ROT // 2, -sine, 0.0)
    rot_b[...] = jnp.where((in_head >= ROT // 2) & (in_head < ROT), sine, 0.0)

    def rotate(value, sign):
        left = pltpu.roll(value, 128 - ROT // 2, 1)
        right = pltpu.roll(value, ROT // 2, 1)
        return value * rot_c[...] + sign * (left * rot_a[...] + right * rot_b[...])

    attn_load.wait()

    @pl.loop(0, heads_w // BLK)
    def _(n):
        cols = pl.ds(mult(n * BLK, BLK), BLK)
        query = nn(normed[...], wq[:, cols]) + bq[:, cols]
        keys = nn(normed[...], wk[:, cols]) + bk[:, cols]
        for part in range(BLK // 128):
            at = pl.ds(mult(n * BLK + part * 128, 128), 128)
            lanes = slice(part * 128, part * 128 + 128)
            q_s[:, at] = (rotate(query[:, lanes], 1.0) * 0.125).astype(BF16)
            k_s[:, at] = rotate(keys[:, lanes], 1.0).astype(BF16)
        v_s[:, cols] = (nn(normed[...], wv[:, cols]) + bv[:, cols]).astype(BF16)
        ga_s[:, cols] = nt(gout[...], wo[cols, :]).astype(BF16)

    low_lane = lax.broadcasted_iota(jnp.int32, (1, 128), 1) < HD
    first_head = jnp.where(low_lane, 1.0, 0.0).astype(BF16)
    second_head = jnp.where(low_lane, 0.0, 1.0).astype(BF16)
    low_full = lax.broadcasted_iota(jnp.int32, (toks, 128), 1) < HD

    def apart(value):
        return jnp.concatenate([value * first_head, value * second_head], axis=0)

    def together(value):
        return jnp.where(low_full, value[:toks], value[toks:])

    @pl.loop(0, n_att)
    def _(n):
        base_n = n_hid // 2 + 3 * n
        for part in range(BLK // 128):
            at = pl.ds(mult(n * BLK + part * 128, 128), 128)
            lanes = slice(part * 128, part * 128 + 128)
            kp, vp = k_s[:, at], v_s[:, at]
            q2, g2 = apart(q_s[:, at]), apart(ga_s[:, at])
            scores = nt(q2, kp) + amask[...]
            top = jnp.max(scores, axis=1, keepdims=True)
            expo = jnp.exp(scores - top)
            probs = expo * (1.0 / jnp.sum(expo, axis=1, keepdims=True))
            probs_low = probs.astype(BF16)
            prob_grad = nt(g2, vp)
            delta = jnp.sum(probs * prob_grad, axis=1, keepdims=True)
            score_grad = (probs * (prob_grad - delta)).astype(BF16)
            out = jnp.where(slot < total_len, together(nn(probs_low, vp)), 0.0).astype(BF16)
            att[:, at] = out
            bg[n_hid + n, lanes, 0:toks] = out.T
            dq = rotate(together(nn(score_grad, kp)) * 0.125, -1.0).astype(BF16)
            dk = rotate(tn(score_grad, q2), -1.0).astype(BF16)
            dv = tn(probs_low, g2).astype(BF16)
            for kind, value in enumerate((dq, dk, dv)):
                bn[base_n + kind, 0:toks, lanes] = value
                gqkv[:, pl.ds(mult(kind * heads_w + n * BLK + part * 128, 128), 128)] = value
        for k in (0, 1):
            bg_copy(n_hid + n, k).start()
            for kind in range(3):
                bn_copy(base_n + kind, k).start()

    @pl.loop(0, width // WIDE)
    def _(n):
        cols = pl.ds(mult(n * WIDE, WIDE), WIDE)
        zpart[0, :, cols] = (nn(act[...], wd[:, cols]) + nn(att[...], wo[:, cols])).astype(BF16)
        for part in range(WIDE // piece_cols):
            g = n * (WIDE // piece_cols) + part
            z_send([z_far(0, g), z_near(0, g)])

    hidden_grad(n_wide // 2, n_wide, 3 * n_att)

    vzl[...] = jnp.zeros_like(vzl)

    @pl.loop(0, width // WIDE)
    def _(n):
        cols = pl.ds(mult(n * WIDE, WIDE), WIDE)
        grad = nt(dact[...], wu[cols, :])
        for kind, weight in enumerate((wq, wk, wv)):
            grad = grad + nt(gqkv[:, kind * heads_w : (kind + 1) * heads_w], weight[cols, :])
        zpart[1, :, cols] = grad.astype(BF16)

        for turn, number in ((1, 0), (3, 1)):
            @pl.when(n == turn)
            def _(number=number):
                z_tick(number)

        for part in range(WIDE // 128):
            lanes = slice(part * 128, part * 128 + 128)
            at = pl.ds(mult(n * WIDE + part * 128, 128), 128)
            owner = n * per_wide + part * 128 // BLK
            into = slice(part * 128 % BLK, part * 128 % BLK + 128)
            piece_of = grad[:, lanes]
            standard = (tok[:, at].astype(F32) - stat_m[...]) * stat_i[...]
            vzl[owner, 0:1, into] = jnp.sum(piece_of * standard, axis=0, keepdims=True)
            vzl[owner, 1:2, into] = jnp.sum(piece_of, axis=0, keepdims=True)

    def vd_copy(mask):
        return remote(
            vzl.at[flip(inner, mask)], vdr.at[mask - 1], vd_ss, vd_rs, peer(mask)
        )

    for owner in range(n_own):
        vzl[owner, 2:3, :] = gsum[0:1, owner * BLK : owner * BLK + BLK]
    for mask in range(1, GROUP):
        vd_copy(mask).start()
    for g in range(Z_PARTS):
        z_send([z_far(1, g), z_near(1, g)])

    bs_copy = remote(bsum, bsum_r, bs_ss, bs_rs, peer(YBIT))

    def rn_copy(s):
        return remote(rsn_s.at[s], rsn_r.at[s], rn_ss, rn_rs, peer(YBIT))

    def rg_copy(s):
        return remote(rsg_s.at[s], rsg_r.at[s], rg_ss, rg_rs, peer(XBIT))

    came(bn.at[pl.ds(0, 2), :, :], side_rs.at[2])
    bsum[...] = jnp.zeros_like(bsum)

    def vz_copy(step):
        return remote(vz, vzr.at[step - 1], vz_ss, vz_rs, zpeer(step))

    def vec_spread():
        came(vdr, vd_rs)
        vz[...] = vzl[inner] + jnp.sum(vdr[...], axis=0)
        for step in range(1, N_MP):
            vz_copy(step).start()

    side_n[2 * BLK :, :] = jnp.ones((16, 4 * toks), BF16)

    @pl.loop(0, n_chunks + 1)
    def _(s):
        @pl.when(s < g_chunks)
        def _():
            came(bn.at[s, pl.ds(0, 2 * toks), :], blk_rs.at[s, 0])
            bn_copy(s, 2).start()
            bg_copy(s, 2).start()

        @pl.when((s >= g_chunks) & (s < n_chunks))
        def _():
            came(bn.at[s, pl.ds(0, toks), :], blk_rs.at[s, 0])
            bn_copy(s, 2).start()

        @pl.when((s > 0) & (s <= g_chunks))
        def _():
            came(bn.at[s - 1], blk_rs.at[s - 1, 1])

        @pl.when(s > g_chunks)
        def _():
            came(bn.at[s - 1, pl.ds(0, 2 * toks), :], blk_rs.at[s - 1, 1])

        @pl.when(s > 0)
        def _():
            p = s - 1
            both = nn(side_n[...], bn[p])
            rsn_s[p] = both[BLK : 2 * BLK, :].astype(BF16)
            rn_copy(p).start()
            bsum[pl.ds(p, 1), :] = both[2 * BLK : 2 * BLK + 1, :]
            bn[p, 2 * toks : 3 * toks, :] = both[:BLK, :].astype(BF16)

        @pl.when((s > 0) & (s <= g_chunks))
        def _():
            p = s - 1
            both = nn(bg[p], side_g[...])
            rsg_s[p] = both[:, BLK:].astype(BF16)
            rg_copy(p).start()
            bg[p, :, 2 * toks : 3 * toks] = both[:, :BLK].astype(BF16)

        tick = -1
        for turn, number in Z_TICKS:
            tick = jnp.where(s == turn, number, tick)
        z_tick(tick)

    bs_copy.start()
    vec_spread()
    @pl.loop(Z_TICKS[-1][1] + 1, 2 * Z_PARTS + 2 * Z_LAG)
    def _(number):
        z_tick(number)

    bs_copy.wait_recv()
    came(vzr, vz_rs)
    vec_o[0:8, :] = vz[...] + jnp.sum(vzr[...], axis=0)
    vec_o[2:3, :] = vz[2:3, :]
    vec_o[8:, :] = bsum[...] + bsum_r[...]

    came(rsn_r, rn_rs)
    came(rsg_r, rg_rs)

    came(side_n.at[pl.ds(0, 2 * BLK), pl.ds(0, 3 * toks)], sn_ss)
    came(side_g.at[pl.ds(0, 3 * toks), :], sg_ss)
    came(bn.at[:, pl.ds(0, 3 * toks), :], bn_ss)
    came(bg.at[:, :, pl.ds(0, 3 * toks)], bg_ss)
    came(rsn_s, rn_ss)
    came(rsg_s, rg_ss)
    came(vzr, vz_ss)
    came(vdr, vd_ss)
    bs_copy.wait_send()

    @pl.when(end_of_line)
    def _():
        came(zfar, zf_ss)
        came(znear, zn_ss)
        came(zout, ze_rs)
        cot_load.wait()

    @pl.when(middle)
    def _():
        came(zmid, zm_ss)
        came(zout, zo_ss)
        came(zmid, zw_ss)


def write_kernel(n_hid, n_att, bn, bg, rsn, rsg, zout, vec, mixed_h, gtok_h, gain_o, shift_o, gq_h, bq_o, gk_h, bk_o, gv_h, bv_o, go_h, gu_h, bu_o, gd_h, ob_o, stage, sem, zsem):
    n_chunks, n_g = bn.shape[0], bg.shape[0]
    toks = zout.shape[1]
    z_outs = [
        pltpu.make_async_copy(zout.at[t], out, zsem) for t, out in enumerate((mixed_h, gtok_h))
    ]
    for out in z_outs:
        out.start()
    places, biases = [], []
    for s in range(n_chunks):
        inside = s - n_hid // 2
        if 0 <= inside < 3 * n_att:
            (out, bias), at = ((gq_h, bq_o), (gk_h, bk_o), (gv_h, bv_o))[inside % 3], inside // 3
        else:
            (out, bias), at = (gu_h, bu_o), s if inside < 0 else s - 3 * n_att
        biases.append((bias, at))
        places.append((True, s, out.at[:, pl.ds(at * BLK, BLK)]))
    for s in range(n_g):
        out, at = (gd_h, s) if s < n_hid else (go_h, s - n_hid)
        places.append((False, s, out.at[pl.ds(at * BLK, BLK), :]))
    copies = []
    for number, (first, s, place) in enumerate(places):
        slot = number
        if first:
            value = bn[s, 2 * toks : 3 * toks, :].astype(F32) + rsn[s].astype(F32)
        else:
            value = bg[s, :, 2 * toks : 3 * toks].astype(F32) + rsg[s].astype(F32)
        stage[slot] = value
        copies.append(pltpu.make_async_copy(stage.at[slot], place, sem))
        copies[number].start()
    for row, out in enumerate((gain_o, shift_o, ob_o)):
        out[...] = vec[row]
    for s, (out, at) in enumerate(biases):
        out[at * BLK : at * BLK + BLK] = vec[8 + s]
    pltpu.make_async_copy(stage, stage, sem).wait()
    pltpu.make_async_copy(zout, zout, zsem).wait()


def layer(tokens, lengths, ln_gain, ln_bias, w_query, b_query, w_key, b_key, w_value, b_value, w_out, w_up, b_up, w_down, out_bias, cotangent):
    toks, width = tokens.shape
    heads_w = w_query.shape[1]
    hidden = w_up.shape[1]
    n_chunks = (3 * heads_w + hidden) // BLK
    g_chunks = (heads_w + hidden) // BLK
    n_own = width // BLK
    n_vec = -(-n_chunks // 8) * 8
    half = toks // 2
    dma = pltpu.SemaphoreType.DMA
    vmem = pltpu.VMEM
    scratch = [
        pltpu.SMEM(lengths.shape, jnp.int32),
        vmem((1, width), F32),
        vmem((1, width), F32),
        vmem((1, heads_w), F32),
        vmem((1, heads_w), F32),
        vmem((1, heads_w), F32),
        vmem((1, hidden), F32),
        vmem((1, width), F32),
        vmem((toks, width), BF16),
        vmem((toks, width), BF16),
        vmem((toks, width), BF16),
        vmem((n_own, BLK, toks), BF16),
        vmem(w_query.shape, BF16),
        vmem(w_key.shape, BF16),
        vmem(w_value.shape, BF16),
        vmem(w_out.shape, BF16),
        vmem(w_up.shape, BF16),
        vmem(w_down.shape, BF16),
        vmem((2 * BLK + 16, 4 * toks), BF16),
        vmem((4 * toks, 2 * BLK), BF16),
        vmem((n_chunks, BLK, BLK), BF16),
        vmem((g_chunks, BLK, BLK), BF16),
        vmem((toks, hidden), BF16),
        vmem((toks, hidden), BF16),
        vmem((toks, 3 * heads_w), BF16),
        vmem((toks, heads_w), BF16),
        vmem((toks, heads_w), BF16),
        vmem((toks, heads_w), BF16),
        vmem((toks, heads_w), BF16),
        vmem((toks, heads_w), BF16),
        vmem((2 * toks, toks), F32),
        vmem((toks, 128), F32),
        vmem((toks, 128), F32),
        vmem((toks, 128), F32),
        vmem((toks, 128), F32),
        vmem((toks, 128), F32),
        vmem((2, toks, width), BF16),
        vmem((2, half, width), BF16),
        vmem((2, half, width), BF16),
        vmem((2, half, width), BF16),
        vmem((n_own, 8, BLK), F32),
        vmem((8, BLK), F32),
        vmem((N_MP - 1, 8, BLK), F32),
        vmem((GROUP - 1, 8, BLK), F32),
        vmem((8, width), F32),
        vmem((n_vec, BLK), F32),
        vmem((n_vec, BLK), F32),
        vmem((half, width), BF16),
        dma((14,)),
        dma,
        dma,
        dma((3,)),
        dma,
        dma,
        dma((n_chunks, 2)),
        dma,
        dma,
        dma,
        dma,
        dma,
        dma((2 * Z_PARTS,)),
        dma,
        dma,
        dma((2 * Z_PARTS,)),
        dma,
        dma((2 * Z_PARTS,)),
        dma,
        dma,
        dma,
        dma,
        dma,
        dma,
        dma,
        dma,
    ]
    anyspace = pl.BlockSpec(memory_space=pl.ANY)
    local = pl.BlockSpec(memory_space=pltpu.VMEM)
    row = lambda value: value.reshape(1, -1)
    kept = pl.pallas_call(
        functools.partial(layer_kernel, n_chunks, g_chunks),
        out_shape=(
            vmem((n_chunks, 4 * toks, BLK), BF16),
            vmem((g_chunks, BLK, 4 * toks), BF16),
            vmem((n_chunks, BLK, BLK), BF16),
            vmem((g_chunks, BLK, BLK), BF16),
            vmem((2, toks, width), BF16),
            vmem((8 + n_vec, BLK), F32),
        ),
        in_specs=[anyspace] * 16,
        out_specs=(local,) * 6,
        scratch_shapes=scratch,
        compiler_params=pltpu.CompilerParams(
            collective_id=0, has_side_effects=True, vmem_limit_bytes=MAIN_VMEM
        ),
    )(
        lengths,
        tokens,
        cotangent,
        row(ln_gain),
        row(ln_bias),
        row(b_query),
        row(b_key),
        row(b_value),
        row(b_up),
        row(out_bias),
        w_query,
        w_key,
        w_value,
        w_out,
        w_up,
        w_down,
    )
    f32 = lambda *shape: jax.ShapeDtypeStruct(shape, F32)
    low = jax.ShapeDtypeStruct((toks, width), BF16)
    spec = lambda kind: anyspace if len(kind.shape) == 2 else local
    outs = (
        low,
        low,
        f32(BLK),
        f32(BLK),
        f32(BLK, heads_w),
        f32(heads_w),
        f32(BLK, heads_w),
        f32(heads_w),
        f32(BLK, heads_w),
        f32(heads_w),
        f32(heads_w, BLK),
        f32(BLK, hidden),
        f32(hidden),
        f32(hidden, BLK),
        f32(BLK),
    )
    slots = n_chunks + g_chunks
    return pl.pallas_call(
        functools.partial(write_kernel, hidden // BLK, heads_w // BLK),
        out_shape=outs,
        in_specs=[local] * 6,
        out_specs=tuple(spec(kind) for kind in outs),
        scratch_shapes=[vmem((slots, BLK, BLK), F32), dma, dma],
        compiler_params=pltpu.CompilerParams(vmem_limit_bytes=12 * 2**20),
    )(*kept)


def make_body(n_dp, n_mp):
    outer = n_dp // GROUP

    def order(value, axis):
        if outer == 1:
            return value
        shape = value.shape
        split = shape[:axis] + (outer, GROUP, shape[axis] // n_dp) + shape[axis + 1 :]
        return jnp.swapaxes(value.reshape(split), axis, axis + 1).reshape(shape)

    def restore(value, axis):
        if outer == 1:
            return value
        shape = value.shape
        split = shape[:axis] + (GROUP, outer, shape[axis] // n_dp) + shape[axis + 1 :]
        return jnp.swapaxes(value.reshape(split), axis, axis + 1).reshape(shape)

    groups = [[o * GROUP + i for o in range(outer)] for i in range(GROUP)]

    def scatter(value, axis):
        if outer == 1:
            return value
        return lax.psum_scatter(
            value, "dp", scatter_dimension=axis, axis_index_groups=groups, tiled=True
        )

    def total(value):
        if outer == 1:
            return value
        return lax.psum(value, "dp", axis_index_groups=groups)

    def body(tokens, lengths, ln_gain, ln_bias, w_query, b_query, w_key, b_key, w_value, b_value, w_out, w_up, b_up, w_down, out_bias, cotangent):
        found = layer(
            order(tokens, 1),
            lengths,
            order(ln_gain, 0),
            order(ln_bias, 0),
            order(w_query, 0),
            b_query,
            order(w_key, 0),
            b_key,
            order(w_value, 0),
            b_value,
            order(w_out, 1),
            order(w_up, 0),
            b_up,
            order(w_down, 1),
            order(out_bias, 0),
            order(cotangent, 1),
        )
        (mixed, grad_tokens, gain, shift, g_q, b_q, g_k, b_k, g_v, b_v, g_out, g_up, b_u, g_down, b_out) = found
        return (
            restore(mixed, 1),
            restore(grad_tokens, 1),
            scatter(gain, 0),
            scatter(shift, 0),
            scatter(g_q, 0),
            total(b_q),
            scatter(g_k, 0),
            total(b_k),
            scatter(g_v, 0),
            total(b_v),
            scatter(g_out, 1),
            scatter(g_up, 0),
            total(b_u),
            scatter(g_down, 1),
            scatter(b_out, 0),
        )

    return body


def solution(mesh):
    in_specs = (
        P("dp", None),
        P("dp", None),
        P(),
        P(),
        P(None, "mp"),
        P("mp"),
        P(None, "mp"),
        P("mp"),
        P(None, "mp"),
        P("mp"),
        P("mp", None),
        P(None, "mp"),
        P("mp"),
        P("mp", None),
        P(),
        P("dp", None),
    )
    out_specs = (
        P("dp", None),
        P("dp", None),
        P("dp"),
        P("dp"),
        P("dp", "mp"),
        P("mp"),
        P("dp", "mp"),
        P("mp"),
        P("dp", "mp"),
        P("mp"),
        P("mp", "dp"),
        P("dp", "mp"),
        P("mp"),
        P("mp", "dp"),
        P("dp"),
    )
    body = make_body(mesh.shape["dp"], mesh.shape["mp"])
    return jax.shard_map(body, mesh=mesh, in_specs=in_specs, out_specs=out_specs, check_vma=False)
```

```python
import functools
import math

import jax
import jax.numpy as jnp
from jax import lax
from jax.experimental import pallas as pl
from jax.experimental.pallas import tpu as pltpu
from jax.sharding import PartitionSpec as P

HD = 64
ROT = 32
EPSILON = 1e-05
GROUP = 8
CORE, XBIT, YBIT = 1, 2, 4
BLK = 256
WIDE = 512
N_MP = 4
Z_PARTS = 8
Z_LEAD = 2
Z_LAG = (0, 2, 4)
Z_TICKS = ((1, 4), (4, 5), (6, 6), (9, 7), (10, 8), (11, 9), (12, 10), (13, 11))
F32 = jnp.float32
BF16 = jnp.bfloat16
MESH = pl.DeviceIdType.MESH
MAIN_VMEM = 93 * 2**19
GELU_A = math.sqrt(2.0 / math.pi)
GELU_B = 0.044715


def nn(left, right):
    return lax.dot_general(left, right, (((1,), (0,)), ((), ())), preferred_element_type=F32)


def nt(left, right):
    return lax.dot_general(left, right, (((1,), (1,)), ((), ())), preferred_element_type=F32)


def tn(left, right):
    return lax.dot_general(left, right, (((0,), (0,)), ((), ())), preferred_element_type=F32)


def flip(index, mask):
    for bit in (1, 2, 4):
        if mask & bit:
            index = index + bit * (1 - 2 * ((index // bit) % 2))
    return index


def mult(value, by):
    return pl.multiple_of(value, by)


N_JS = (0, XBIT, CORE, XBIT | CORE)
N_MS = (0, YBIT)
G_JS = (0, YBIT, CORE, YBIT | CORE)
G_MS = (0, XBIT)


def layer_kernel(
    n_chunks,
    g_chunks,
    lens_h,
    tok_h,
    cot_h,
    gain_h,
    shift_h,
    bq_h,
    bk_h,
    bv_h,
    bup_h,
    obias_h,
    wq_h,
    wk_h,
    wv_h,
    wo_h,
    wu_h,
    wd_h,
    bn,
    bg,
    rsn_r,
    rsg_r,
    zout,
    vec_o,
    lens,
    gain,
    shift,
    bq,
    bk,
    bv,
    bup,
    obias,
    tok,
    gout,
    normed,
    turned_n,
    wq,
    wk,
    wv,
    wo,
    wu,
    wd,
    side_n,
    side_g,
    rsn_s,
    rsg_s,
    act,
    gup,
    gqkv,
    att,
    q_s,
    k_s,
    v_s,
    ga_s,
    amask,
    rot_c,
    rot_a,
    rot_b,
    stat_m,
    stat_i,
    zpart,
    zfar,
    znear,
    zmid,
    vzl,
    vz,
    vzr,
    vdr,
    gsum,
    bsum,
    bsum_r,
    cot_rows,
    in_sem,
    wide_sem,
    side_ss,
    side_rs,
    bn_ss,
    bg_ss,
    blk_rs,
    rn_ss,
    rn_rs,
    rg_ss,
    rg_rs,
    zf_ss,
    zf_rs,
    zn_ss,
    zm_ss,
    zm_rs,
    zo_ss,
    zo_rs,
    zw_ss,
    ze_rs,
    vz_ss,
    vz_rs,
    vd_ss,
    vd_rs,
    bs_ss,
    bs_rs,
):
    toks, width = tok.shape
    hidden = wu.shape[1]
    heads_w = wq.shape[1]
    n_att = heads_w // BLK
    n_hid = hidden // BLK
    n_own = width // BLK
    dp = lax.axis_index("dp")
    zed = lax.axis_index("mp")
    inner = lax.rem(dp, GROUP)
    outer = dp - inner
    half = toks // 2
    piece_cols = width // Z_PARTS
    piece_rows = half // Z_PARTS

    def peer(mask):
        return (outer + flip(inner, mask), zed)

    def came(ref, sem):
        pltpu.make_async_copy(ref, ref, sem).wait()

    middle = (zed == 1) | (zed == 2)
    end_of_line = (zed == 0) | (zed == 3)
    side_of_line = zed // 2
    beside = (dp, zed + 1 - 2 * lax.rem(zed, 2))
    across = (dp, 3 - zed)
    near_rows = mult(side_of_line * half, half)
    far_rows = mult((1 - side_of_line) * half, half)

    def zpeer(step):
        return (dp, lax.rem(zed + step, N_MP))

    def remote(src, dst, ssem, rsem, where):
        return pltpu.make_async_remote_copy(
            src_ref=src,
            dst_ref=dst,
            send_sem=ssem,
            recv_sem=rsem,
            device_id=where,
            device_id_type=MESH,
        )

    def load(src, dst, number):
        copy = pltpu.make_async_copy(src, dst, in_sem.at[number])
        copy.start()
        return copy

    tok_load = load(tok_h, tok, 0)
    gain_load = load(gain_h, gain, 1)
    shift_load = load(shift_h, shift, 2)
    lens_load = load(lens_h, lens, 3)

    barrier = pltpu.get_barrier_semaphore()
    for mask in range(1, GROUP):
        pl.semaphore_signal(barrier, inc=1, device_id=peer(mask), device_id_type=MESH)
    for step in range(1, N_MP):
        pl.semaphore_signal(barrier, inc=1, device_id=zpeer(step), device_id_type=MESH)

    gout_load = load(cot_h, gout, 4)
    bias_loads = [
        load(src, dst, 5 + i)
        for i, (src, dst) in enumerate(
            ((bup_h, bup), (bq_h, bq), (bk_h, bk), (bv_h, bv), (obias_h, obias))
        )
    ]
    def wide_loads(w):
        part = pl.ds(mult(w * WIDE, WIDE), WIDE)
        return (
            pltpu.make_async_copy(wu_h.at[:, part], wu.at[:, part], wide_sem.at[w, 0]),
            pltpu.make_async_copy(wd_h.at[part, :], wd.at[part, :], wide_sem.at[w, 1]),
        )

    @pl.loop(0, hidden // WIDE)
    def _(w):
        for copy in wide_loads(w):
            copy.start()

    for src, dst in ((wq_h, wq), (wk_h, wk), (wv_h, wv), (wo_h, wo)):
        load(src, dst, 12)
    attn_load = pltpu.make_async_copy(wu_h, wu, in_sem.at[12])
    cot_load = load(cot_h.at[pl.ds(near_rows, half), :], cot_rows, 13)

    def segment_of(place):
        number = jnp.zeros_like(place)
        start_of = jnp.zeros_like(place)
        for j, end in enumerate(ends):
            start = end - lens[0, j]
            inside = ((place >= start) & (place < end)).astype(jnp.int32)
            number = number + inside * (j + 1)
            start_of = start_of + inside * start
        return number, start_of

    def cross_core(index, times):
        return index + times * (1 - 2 * lax.rem(index, 2))

    def flip_by(index, bit, times):
        return index + times * (bit * (1 - 2 * ((index // bit) % 2)))

    own_part = lax.rem(zed, 2)
    own_slot = 1 + 2 * side_of_line
    other_slot = 3 - 2 * side_of_line

    def side_places(slot_at, m):
        at = pl.ds(mult(slot_at * toks, toks), toks)
        rows = pl.ds(mult(m * BLK, BLK), BLK)
        return side_n.at[rows, at], side_g.at[at, rows]

    def side_direct():
        at_n = flip(cross_core(inner, side_of_line), XBIT)
        at_g = flip(cross_core(inner, side_of_line), YBIT)
        owner_n = flip_by(at_n, YBIT, own_part)
        owner_g = flip_by(at_g, XBIT, own_part)
        place_n, place_g = side_places(own_slot, own_part)
        source_g = cot_h.at[:, pl.ds(mult(owner_g * BLK, BLK), BLK)]
        return (
            remote(turned_n.at[owner_n], place_n, side_ss, side_rs.at[0], (outer + at_n, zed)),
            remote(source_g, place_g, side_ss, side_rs.at[0], (outer + at_g, zed)),
            owner_n,
        )

    def side_core(m):
        place_n, place_g = side_places(2, m)
        owner_n = flip(inner, CORE ^ N_MS[m])
        owner_g = flip(inner, CORE ^ G_MS[m])
        source_g = cot_h.at[:, pl.ds(mult(owner_g * BLK, BLK), BLK)]
        return (
            remote(turned_n.at[owner_n], place_n, side_ss, side_rs.at[4], peer(CORE)),
            remote(source_g, place_g, side_ss, side_rs.at[4], peer(CORE)),
        )

    def side_send(slot_at, m, number, where):
        for place in side_places(slot_at, m):
            remote(place, place, side_ss, side_rs.at[number], where).start()

    def side_came(number, blocks=2):
        came(bn.at[0, pl.ds(0, blocks * toks), :], side_rs.at[number])

    def side_pass(stage):
        if stage == 0:
            side_came(0)
            side_send(own_slot, own_part, 1, beside)

            @pl.when(middle)
            def _():
                side_send(own_slot, own_part, 2, across)
        elif stage == 1:
            @pl.when(middle)
            def _():
                side_came(1)
                side_send(own_slot, 1 - own_part, 3, across)
                side_came(2)
                side_send(other_slot, 1 - own_part, 2, beside)
        else:
            @pl.when(middle)
            def _():
                side_came(3)
                side_send(other_slot, own_part, 3, beside)

    for copy in (tok_load, gain_load, shift_load):
        copy.wait()
    step_rows = 32

    @pl.loop(0, toks // step_rows, unroll=2)
    def _(r):
        rows = pl.ds(mult(r * step_rows, step_rows), step_rows)
        value = tok[rows, :].astype(F32)
        mean = jnp.sum(value, axis=1, keepdims=True) * (1.0 / width)
        center = value - mean
        spread = jnp.sum(center * center, axis=1, keepdims=True) * (1.0 / width)
        inv = lax.rsqrt(spread + EPSILON)
        normed[rows, :] = (center * inv * gain[...] + shift[...]).astype(BF16)
        stat_m[rows, :] = jnp.broadcast_to(mean, (step_rows, 128))
        stat_i[rows, :] = jnp.broadcast_to(inv, (step_rows, 128))

    pl.semaphore_wait(barrier, GROUP - 1 + N_MP - 1)
    direct_n, direct_g, first_owner = side_direct()
    direct_g.start()
    turned_n[first_owner] = normed[:, pl.ds(mult(first_owner * BLK, BLK), BLK)].T
    direct_n.start()

    for copy in (lens_load, gout_load, *bias_loads):
        copy.wait()

    ends = []
    total_len = 0
    for j in range(lens.shape[1]):
        total_len = total_len + lens[0, j]
        ends.append(total_len)

    gsum[...] = jnp.zeros_like(gsum)

    @pl.loop(0, toks // step_rows)
    def _(r):
        first = r * step_rows
        rows = pl.ds(mult(first, step_rows), step_rows)
        place = first + lax.broadcasted_iota(jnp.int32, (step_rows, width), 0)
        value = jnp.where(place < total_len, gout[rows, :].astype(F32), 0.0)
        gout[rows, :] = value.astype(BF16)
        gsum[0:1, :] = gsum[0:1, :] + jnp.sum(value, axis=0, keepdims=True)

    def bn_copy(s, k):
        src = bn.at[s, pl.ds(toks if k == 2 else 0, toks), :]
        slot_at = (1, 2, 3)[k]
        return remote(
            src,
            bn.at[s, pl.ds(slot_at * toks, toks), :],
            bn_ss,
            blk_rs.at[s, min(k, 1)],
            peer((XBIT, CORE, CORE)[k]),
        )

    def bg_copy(s, k):
        src = bg.at[s, :, pl.ds(toks if k == 2 else 0, toks)]
        slot_at = (1, 2, 3)[k]
        return remote(
            src,
            bg.at[s, :, pl.ds(slot_at * toks, toks)],
            bg_ss,
            blk_rs.at[s, min(k, 1)],
            peer((YBIT, CORE, CORE)[k]),
        )

    def piece(t, g, first_row):
        if t == 0:
            return pl.ds(first_row, half), pl.ds(mult(g * piece_cols, piece_cols), piece_cols)
        return pl.ds(mult(first_row + g * piece_rows, piece_rows), piece_rows), pl.ds(0, width)

    def z_far(t, g):
        rows, cols = piece(t, g, far_rows)
        to_rows, _ = piece(t, g, 0)
        return remote(
            zpart.at[t, rows, cols],
            zfar.at[t, to_rows, cols],
            zf_ss,
            zf_rs.at[t * Z_PARTS + g],
            beside,
        )

    def z_near(t, g):
        rows, cols = piece(t, g, near_rows)
        to_rows, _ = piece(t, g, 0)
        return remote(
            zpart.at[t, rows, cols],
            znear.at[t, to_rows, cols],
            zn_ss,
            zm_rs.at[t * Z_PARTS + g],
            beside,
        )

    def z_mid(t, g):
        rows, cols = piece(t, g, far_rows)
        to_rows, _ = piece(t, g, 0)
        return remote(
            zpart.at[t, rows, cols],
            zmid.at[t, to_rows, cols],
            zm_ss,
            zm_rs.at[t * Z_PARTS + g],
            across,
        )

    def z_done(t, g, to_end):
        rows, cols = piece(t, g, near_rows)
        place = zout.at[t, rows, cols]
        if to_end:
            return remote(place, place, zo_ss, ze_rs, beside)
        return remote(place, place, zo_ss, zo_rs.at[t * Z_PARTS + g], across)

    def z_pass(t, g):
        rows, cols = piece(t, g, far_rows)
        return remote(zout.at[t, rows, cols], zout.at[t, rows, cols], zw_ss, ze_rs, beside)

    def z_send(copies):
        @pl.when(end_of_line)
        def _():
            for copy in copies:
                copy.start()

    def z_first(t, g):
        z_far(t, g).wait_recv()
        rows, cols = piece(t, g, far_rows)
        there, _ = piece(t, g, 0)
        zpart[t, rows, cols] = (
            zpart[t, rows, cols].astype(F32) + zfar[t, there, cols].astype(F32)
        ).astype(BF16)
        z_mid(t, g).start()

    def z_second(t, g):
        came(znear.at[0, :, pl.ds(0, 2 * piece_cols)], zm_rs.at[t * Z_PARTS + g])
        rows, cols = piece(t, g, near_rows)
        there, _ = piece(t, g, 0)
        total = (
            zpart[t, rows, cols].astype(F32)
            + znear[t, there, cols].astype(F32)
            + zmid[t, there, cols].astype(F32)
        )
        base = tok[rows, cols].astype(F32)
        if t == 0:
            place = near_rows + lax.broadcasted_iota(jnp.int32, total.shape, 0)
            branch = jnp.where(place < total_len, total + obias[:, cols], 0.0)
            zout[t, rows, cols] = (base + branch).astype(BF16)
        else:
            @pl.when(g == 0)
            def _():
                cot_load.wait()

            inv = stat_i[rows, 0:1]
            standard = (base - stat_m[rows, 0:1]) * inv
            grad = total * gain[...]
            mean_g = jnp.sum(grad, axis=1, keepdims=True) * (1.0 / width)
            mean_x = jnp.sum(grad * standard, axis=1, keepdims=True) * (1.0 / width)
            back = inv * (grad - mean_g - standard * mean_x)
            zout[t, rows, cols] = (cot_rows[there, :].astype(F32) + back).astype(BF16)
        z_done(t, g, False).start()
        z_done(t, g, True).start()

    def z_third(t, g):
        z_done(t, g, False).wait_recv()
        z_pass(t, g).start()

    def z_move(step, number):
        for t in (0, 1):
            at = number - t * Z_PARTS
            if isinstance(number, int):
                if 0 <= at < Z_PARTS:
                    pl.when(middle)(functools.partial(step, t, at))
            else:
                pl.when(middle & (at >= 0) & (at < Z_PARTS))(functools.partial(step, t, at))

    def z_tick(number):
        for step, lag in zip((z_first, z_second, z_third), Z_LAG):
            z_move(step, number - lag)

    per_wide = WIDE // BLK
    n_wide = hidden // WIDE

    def hidden_block(w, with_grad):
        cols = pl.ds(mult(w * WIDE, WIDE), WIDE)
        for copy in wide_loads(w):
            copy.wait()
        up = nn(normed[...], wu[:, cols]) + bup[:, cols]
        square = up * up
        tanh = jnp.tanh(GELU_A * up * (1.0 + GELU_B * square))
        row = lax.broadcasted_iota(jnp.int32, up.shape, 0)
        active = jnp.where(row < total_len, 0.5 * up * (1.0 + tanh), 0.0).astype(BF16)
        act[:, cols] = active
        slope = 0.5 * (1.0 + tanh) + 0.5 * up * (1.0 - tanh * tanh) * (
            GELU_A * (1.0 + 3.0 * GELU_B * square)
        )
        if with_grad:
            grad = (nt(gout[...], wd[cols, :]) * slope).astype(BF16)
            gup[:, cols] = grad
        else:
            gup[:, cols] = slope.astype(BF16)
        for part in range(per_wide):
            c = w * per_wide + part
            inside = slice(part * BLK, part * BLK + BLK)
            bg[c, :, 0:toks] = active[:, inside].T
            if with_grad:
                bn[c, 0:toks, :] = grad[:, inside]
        for part in range(per_wide):
            c = w * per_wide + part
            for k in (0, 1):
                bg_copy(c, k).start()
                if with_grad:
                    bn_copy(c, k).start()

    @pl.loop(0, n_wide // 2)
    def _(w):
        hidden_block(w, True)

    @pl.loop(n_wide // 2, n_wide)
    def _(w):
        hidden_block(w, False)

        @pl.when(w == n_wide // 2)
        def _():
            side_pass(0)

    def hidden_grad(first, past, shift):
        @pl.loop(first, past)
        def _(w):
            z_tick(w - first)
            cols = pl.ds(mult(w * WIDE, WIDE), WIDE)
            grad = (nt(gout[...], wd[cols, :]) * gup[:, cols].astype(F32)).astype(BF16)
            gup[:, cols] = grad
            for part in range(per_wide):
                c = shift + w * per_wide + part
                bn[c, 0:toks, :] = grad[:, part * BLK : part * BLK + BLK]
                for k in (0, 1):
                    bn_copy(c, k).start()

    place_r = lax.broadcasted_iota(jnp.int32, (toks, toks), 0)
    place_c = lax.broadcasted_iota(jnp.int32, (toks, toks), 1)
    seg_r, _ = segment_of(place_r)
    seg_c, _ = segment_of(place_c)
    allowed = (seg_r == seg_c) & (place_c <= place_r)
    for h in (0, 1):
        amask[h * toks : h * toks + toks, :] = jnp.where(allowed, 0.0, -1e30)

    lane = lax.broadcasted_iota(jnp.int32, (toks, 128), 1)
    slot = lax.broadcasted_iota(jnp.int32, (toks, 128), 0)
    _, start_of = segment_of(slot)
    in_head = lane % HD
    order = (in_head % (ROT // 2)).astype(F32)
    freq = jnp.exp(order * (-2.0 / ROT * math.log(10000.0)))
    angle = (slot - start_of).astype(F32) * freq
    cosine, sine = jnp.cos(angle), jnp.sin(angle)
    rot_c[...] = jnp.where(in_head < ROT, cosine, 1.0)
    rot_a[...] = jnp.where(in_head < ROT // 2, -sine, 0.0)
    rot_b[...] = jnp.where((in_head >= ROT // 2) & (in_head < ROT), sine, 0.0)

    def rotate(value, sign):
        left = pltpu.roll(value, 128 - ROT // 2, 1)
        right = pltpu.roll(value, ROT // 2, 1)
        return value * rot_c[...] + sign * (left * rot_a[...] + right * rot_b[...])

    attn_load.wait()

    @pl.loop(0, heads_w // BLK)
    def _(n):
        cols = pl.ds(mult(n * BLK, BLK), BLK)
        query = nn(normed[...], wq[:, cols]) + bq[:, cols]
        keys = nn(normed[...], wk[:, cols]) + bk[:, cols]
        for part in range(BLK // 128):
            at = pl.ds(mult(n * BLK + part * 128, 128), 128)
            lanes = slice(part * 128, part * 128 + 128)
            q_s[:, at] = (rotate(query[:, lanes], 1.0) * 0.125).astype(BF16)
            k_s[:, at] = rotate(keys[:, lanes], 1.0).astype(BF16)
        v_s[:, cols] = (nn(normed[...], wv[:, cols]) + bv[:, cols]).astype(BF16)
        ga_s[:, cols] = nt(gout[...], wo[cols, :]).astype(BF16)

    low_lane = lax.broadcasted_iota(jnp.int32, (1, 128), 1) < HD
    first_head = jnp.where(low_lane, 1.0, 0.0).astype(BF16)
    second_head = jnp.where(low_lane, 0.0, 1.0).astype(BF16)
    low_full = lax.broadcasted_iota(jnp.int32, (toks, 128), 1) < HD

    def apart(value):
        return jnp.concatenate([value * first_head, value * second_head], axis=0)

    def together(value):
        return jnp.where(low_full, value[:toks], value[toks:])

    @pl.loop(0, n_att)
    def _(n):
        base_n = n_hid // 2 + 3 * n

        for part in range(BLK // 128):
            at = pl.ds(mult(n * BLK + part * 128, 128), 128)
            lanes = slice(part * 128, part * 128 + 128)
            kp, vp = k_s[:, at], v_s[:, at]
            q2, g2 = apart(q_s[:, at]), apart(ga_s[:, at])
            scores = nt(q2, kp) + amask[...]
            top = jnp.max(scores, axis=1, keepdims=True)
            expo = jnp.exp(scores - top)
            probs = expo * (1.0 / jnp.sum(expo, axis=1, keepdims=True))
            probs_low = probs.astype(BF16)
            prob_grad = nt(g2, vp)
            delta = jnp.sum(probs * prob_grad, axis=1, keepdims=True)
            score_grad = (probs * (prob_grad - delta)).astype(BF16)
            out = jnp.where(slot < total_len, together(nn(probs_low, vp)), 0.0).astype(BF16)
            att[:, at] = out
            bg[n_hid + n, lanes, 0:toks] = out.T
            dq = rotate(together(nn(score_grad, kp)) * 0.125, -1.0).astype(BF16)
            dk = rotate(tn(score_grad, q2), -1.0).astype(BF16)
            dv = tn(probs_low, g2).astype(BF16)
            for kind, value in enumerate((dq, dk, dv)):
                bn[base_n + kind, 0:toks, lanes] = value
                gqkv[:, pl.ds(mult(kind * heads_w + n * BLK + part * 128, 128), 128)] = value
        for k in (0, 1):
            bg_copy(n_hid + n, k).start()
            for kind in range(3):
                bn_copy(base_n + kind, k).start()

    side_pass(1)

    @pl.loop(0, width // WIDE)
    def _(n):
        cols = pl.ds(mult(n * WIDE, WIDE), WIDE)
        zpart[0, :, cols] = (nn(act[...], wd[:, cols]) + nn(att[...], wo[:, cols])).astype(BF16)
        for part in range(Z_LEAD):
            g = n * Z_LEAD + part
            z_send([z_far(0, g)])

            @pl.when(n > 0)
            def _(g=g):
                z_send([z_near(0, g - Z_LEAD)])

    for m in (0, 1):
        for owner in (flip(inner, CORE ^ N_MS[m]), flip(inner, N_MS[m])):
            turned_n[owner] = normed[:, pl.ds(mult(owner * BLK, BLK), BLK)].T
        for copy in side_core(m):
            copy.start()
        owner_g = mult(flip(inner, G_MS[m]) * BLK, BLK)
        side_g[0:toks, m * BLK : m * BLK + BLK] = gout[:, pl.ds(owner_g, BLK)]
        side_n[m * BLK : m * BLK + BLK, 0:toks] = turned_n[flip(inner, N_MS[m])]
    hidden_grad(n_wide // 2, n_wide, 3 * n_att)

    vzl[...] = jnp.zeros_like(vzl)

    @pl.loop(0, width // WIDE)
    def _(n):
        cols = pl.ds(mult(n * WIDE, WIDE), WIDE)
        grad = nt(gup[...], wu[cols, :])
        for kind, weight in enumerate((wq, wk, wv)):
            grad = grad + nt(gqkv[:, kind * heads_w : (kind + 1) * heads_w], weight[cols, :])
        zpart[1, :, cols] = grad.astype(BF16)

        @pl.when(n == 0)
        def _():
            side_pass(2)

        @pl.when(n == 1)
        def _():
            z_tick(2)

        @pl.when(n == 3)
        def _():
            z_tick(3)

        for part in range(WIDE // 128):
            lanes = slice(part * 128, part * 128 + 128)
            at = pl.ds(mult(n * WIDE + part * 128, 128), 128)
            owner = n * per_wide + part * 128 // BLK
            into = slice(part * 128 % BLK, part * 128 % BLK + 128)
            piece_of = grad[:, lanes]
            standard = (tok[:, at].astype(F32) - stat_m[...]) * stat_i[...]
            vzl[owner, 0:1, into] = jnp.sum(piece_of * standard, axis=0, keepdims=True)
            vzl[owner, 1:2, into] = jnp.sum(piece_of, axis=0, keepdims=True)

    def vd_copy(mask):
        return remote(
            vzl.at[flip(inner, mask)], vdr.at[mask - 1], vd_ss, vd_rs, peer(mask)
        )

    for owner in range(n_own):
        vzl[owner, 2:3, :] = gsum[0:1, owner * BLK : owner * BLK + BLK]
    for mask in range(1, GROUP):
        vd_copy(mask).start()
    for g in range(Z_PARTS):
        late = Z_PARTS - Z_LEAD + g
        z_send([z_far(1, g), z_near(late // Z_PARTS, late % Z_PARTS)])
    for g in range(Z_PARTS - Z_LEAD, Z_PARTS):
        z_send([z_near(1, g)])

    bs_copy = remote(bsum, bsum_r, bs_ss, bs_rs, peer(YBIT))

    def rn_copy(s):
        return remote(rsn_s.at[s], rsn_r.at[s], rn_ss, rn_rs, peer(YBIT))

    def rg_copy(s):
        return remote(rsg_s.at[s], rsg_r.at[s], rg_ss, rg_rs, peer(XBIT))

    side_came(4, 4)

    @pl.when(end_of_line)
    def _():
        for number in (1, 2, 3):
            side_came(number)

    bsum[...] = jnp.zeros_like(bsum)

    def vz_copy(step):
        return remote(vz, vzr.at[step - 1], vz_ss, vz_rs, zpeer(step))

    def vec_spread():
        came(vdr, vd_rs)
        vz[...] = vzl[inner] + jnp.sum(vdr[...], axis=0)
        for step in range(1, N_MP):
            vz_copy(step).start()

    side_n[2 * BLK :, :] = jnp.ones((16, 4 * toks), BF16)

    @pl.loop(0, n_chunks + 1)
    def _(s):
        @pl.when(s < g_chunks)
        def _():
            came(bn.at[s, pl.ds(0, 2 * toks), :], blk_rs.at[s, 0])
            bn_copy(s, 2).start()
            bg_copy(s, 2).start()

        @pl.when((s >= g_chunks) & (s < n_chunks))
        def _():
            came(bn.at[s, pl.ds(0, toks), :], blk_rs.at[s, 0])
            bn_copy(s, 2).start()

        @pl.when((s > 0) & (s <= g_chunks))
        def _():
            came(bn.at[s - 1], blk_rs.at[s - 1, 1])

        @pl.when(s > g_chunks)
        def _():
            came(bn.at[s - 1, pl.ds(0, 2 * toks), :], blk_rs.at[s - 1, 1])

        @pl.when(s > 0)
        def _():
            p = s - 1
            both = nn(side_n[...], bn[p])
            rsn_s[p] = both[BLK : 2 * BLK, :].astype(BF16)
            rn_copy(p).start()
            bsum[pl.ds(p, 1), :] = both[2 * BLK : 2 * BLK + 1, :]
            bn[p, 2 * toks : 3 * toks, :] = both[:BLK, :].astype(BF16)

        @pl.when((s > 0) & (s <= g_chunks))
        def _():
            p = s - 1
            both = nn(bg[p], side_g[...])
            rsg_s[p] = both[:, BLK:].astype(BF16)
            rg_copy(p).start()
            bg[p, :, 2 * toks : 3 * toks] = both[:, :BLK].astype(BF16)

        tick = -1
        for turn, number in Z_TICKS:
            tick = jnp.where(s == turn, number, tick)
        z_tick(tick)

    bs_copy.start()
    vec_spread()
    @pl.loop(Z_TICKS[-1][1] + 1, 2 * Z_PARTS + Z_LAG[-1])
    def _(number):
        z_tick(number)

    bs_copy.wait_recv()
    came(vzr, vz_rs)
    vec_o[0:8, :] = vz[...] + jnp.sum(vzr[...], axis=0)
    vec_o[2:3, :] = vz[2:3, :]
    vec_o[8:, :] = bsum[...] + bsum_r[...]

    came(rsn_r, rn_rs)
    came(rsg_r, rg_rs)

    came(bn.at[:, pl.ds(0, 3 * toks), :], bn_ss)
    came(bg.at[:, :, pl.ds(0, 3 * toks)], bg_ss)
    came(rsn_s, rn_ss)
    came(rsg_s, rg_ss)
    came(vzr, vz_ss)
    came(vdr, vd_ss)
    bs_copy.wait_send()

    @pl.when(end_of_line)
    def _():
        came(bn.at[pl.ds(0, 2)], side_ss)
        came(zfar, zf_ss)
        came(znear, zn_ss)
        came(zout, ze_rs)
        cot_load.wait()

    @pl.when(middle)
    def _():
        came(bn.at[pl.ds(0, 4)], side_ss)
        came(zmid, zm_ss)
        came(zout, zo_ss)
        came(zmid, zw_ss)


def write_kernel(n_hid, n_att, bn, bg, rsn, rsg, zout, vec, mixed_h, gtok_h, gain_o, shift_o, gq_h, bq_o, gk_h, bk_o, gv_h, bv_o, go_h, gu_h, bu_o, gd_h, ob_o, stage, sem, zsem):
    n_chunks, n_g = bn.shape[0], bg.shape[0]
    toks = zout.shape[1]
    z_outs = [
        pltpu.make_async_copy(zout.at[t], out, zsem) for t, out in enumerate((mixed_h, gtok_h))
    ]
    for out in z_outs:
        out.start()
    places, biases = [], []
    for s in range(n_chunks):
        inside = s - n_hid // 2
        if 0 <= inside < 3 * n_att:
            (out, bias), at = ((gq_h, bq_o), (gk_h, bk_o), (gv_h, bv_o))[inside % 3], inside // 3
        else:
            (out, bias), at = (gu_h, bu_o), s if inside < 0 else s - 3 * n_att
        biases.append((bias, at))
        places.append((True, s, out.at[:, pl.ds(at * BLK, BLK)]))
    for s in range(n_g):
        out, at = (gd_h, s) if s < n_hid else (go_h, s - n_hid)
        places.append((False, s, out.at[pl.ds(at * BLK, BLK), :]))
    copies = []
    for number, (first, s, place) in enumerate(places):
        slot = number
        if first:
            value = bn[s, 2 * toks : 3 * toks, :].astype(F32) + rsn[s].astype(F32)
        else:
            value = bg[s, :, 2 * toks : 3 * toks].astype(F32) + rsg[s].astype(F32)
        stage[slot] = value
        copies.append(pltpu.make_async_copy(stage.at[slot], place, sem))
        copies[number].start()
    for row, out in enumerate((gain_o, shift_o, ob_o)):
        out[...] = vec[row]
    for s, (out, at) in enumerate(biases):
        out[at * BLK : at * BLK + BLK] = vec[8 + s]
    pltpu.make_async_copy(stage, stage, sem).wait()
    pltpu.make_async_copy(zout, zout, zsem).wait()


def layer(tokens, lengths, ln_gain, ln_bias, w_query, b_query, w_key, b_key, w_value, b_value, w_out, w_up, b_up, w_down, out_bias, cotangent):
    toks, width = tokens.shape
    heads_w = w_query.shape[1]
    hidden = w_up.shape[1]
    n_chunks = (3 * heads_w + hidden) // BLK
    g_chunks = (heads_w + hidden) // BLK
    n_own = width // BLK
    n_vec = -(-n_chunks // 8) * 8
    half = toks // 2
    dma = pltpu.SemaphoreType.DMA
    vmem = pltpu.VMEM
    scratch = [
        pltpu.SMEM(lengths.shape, jnp.int32),
        vmem((1, width), F32),
        vmem((1, width), F32),
        vmem((1, heads_w), F32),
        vmem((1, heads_w), F32),
        vmem((1, heads_w), F32),
        vmem((1, hidden), F32),
        vmem((1, width), F32),
        vmem((toks, width), BF16),
        vmem((toks, width), BF16),
        vmem((toks, width), BF16),
        vmem((n_own, BLK, toks), BF16),
        vmem(w_query.shape, BF16),
        vmem(w_key.shape, BF16),
        vmem(w_value.shape, BF16),
        vmem(w_out.shape, BF16),
        vmem(w_up.shape, BF16),
        vmem(w_down.shape, BF16),
        vmem((2 * BLK + 16, 4 * toks), BF16),
        vmem((4 * toks, 2 * BLK), BF16),
        vmem((n_chunks, BLK, BLK), BF16),
        vmem((g_chunks, BLK, BLK), BF16),
        vmem((toks, hidden), BF16),
        vmem((toks, hidden), BF16),
        vmem((toks, 3 * heads_w), BF16),
        vmem((toks, heads_w), BF16),
        vmem((toks, heads_w), BF16),
        vmem((toks, heads_w), BF16),
        vmem((toks, heads_w), BF16),
        vmem((toks, heads_w), BF16),
        vmem((2 * toks, toks), F32),
        vmem((toks, 128), F32),
        vmem((toks, 128), F32),
        vmem((toks, 128), F32),
        vmem((toks, 128), F32),
        vmem((toks, 128), F32),
        vmem((2, toks, width), BF16),
        vmem((2, half, width), BF16),
        vmem((2, half, width), BF16),
        vmem((2, half, width), BF16),
        vmem((n_own, 8, BLK), F32),
        vmem((8, BLK), F32),
        vmem((N_MP - 1, 8, BLK), F32),
        vmem((GROUP - 1, 8, BLK), F32),
        vmem((8, width), F32),
        vmem((n_vec, BLK), F32),
        vmem((n_vec, BLK), F32),
        vmem((half, width), BF16),
        dma((14,)),
        dma((hidden // WIDE, 2)),
        dma,
        dma((5,)),
        dma,
        dma,
        dma((n_chunks, 2)),
        dma,
        dma,
        dma,
        dma,
        dma,
        dma((2 * Z_PARTS,)),
        dma,
        dma,
        dma((2 * Z_PARTS,)),
        dma,
        dma((2 * Z_PARTS,)),
        dma,
        dma,
        dma,
        dma,
        dma,
        dma,
        dma,
        dma,
    ]
    anyspace = pl.BlockSpec(memory_space=pl.ANY)
    local = pl.BlockSpec(memory_space=pltpu.VMEM)
    row = lambda value: value.reshape(1, -1)
    kept = pl.pallas_call(
        functools.partial(layer_kernel, n_chunks, g_chunks),
        out_shape=(
            vmem((n_chunks, 4 * toks, BLK), BF16),
            vmem((g_chunks, BLK, 4 * toks), BF16),
            vmem((n_chunks, BLK, BLK), BF16),
            vmem((g_chunks, BLK, BLK), BF16),
            vmem((2, toks, width), BF16),
            vmem((8 + n_vec, BLK), F32),
        ),
        in_specs=[anyspace] * 16,
        out_specs=(local,) * 6,
        scratch_shapes=scratch,
        compiler_params=pltpu.CompilerParams(
            collective_id=0, has_side_effects=True, vmem_limit_bytes=MAIN_VMEM
        ),
    )(
        lengths,
        tokens,
        cotangent,
        row(ln_gain),
        row(ln_bias),
        row(b_query),
        row(b_key),
        row(b_value),
        row(b_up),
        row(out_bias),
        w_query,
        w_key,
        w_value,
        w_out,
        w_up,
        w_down,
    )
    f32 = lambda *shape: jax.ShapeDtypeStruct(shape, F32)
    low = jax.ShapeDtypeStruct((toks, width), BF16)
    spec = lambda kind: anyspace if len(kind.shape) == 2 else local
    outs = (
        low,
        low,
        f32(BLK),
        f32(BLK),
        f32(BLK, heads_w),
        f32(heads_w),
        f32(BLK, heads_w),
        f32(heads_w),
        f32(BLK, heads_w),
        f32(heads_w),
        f32(heads_w, BLK),
        f32(BLK, hidden),
        f32(hidden),
        f32(hidden, BLK),
        f32(BLK),
    )
    slots = n_chunks + g_chunks
    return pl.pallas_call(
        functools.partial(write_kernel, hidden // BLK, heads_w // BLK),
        out_shape=outs,
        in_specs=[local] * 6,
        out_specs=tuple(spec(kind) for kind in outs),
        scratch_shapes=[vmem((slots, BLK, BLK), F32), dma, dma],
        compiler_params=pltpu.CompilerParams(vmem_limit_bytes=12 * 2**20),
    )(*kept)


def make_body(n_dp, n_mp):
    outer = n_dp // GROUP

    def order(value, axis):
        if outer == 1:
            return value
        shape = value.shape
        split = shape[:axis] + (outer, GROUP, shape[axis] // n_dp) + shape[axis + 1 :]
        return jnp.swapaxes(value.reshape(split), axis, axis + 1).reshape(shape)

    def restore(value, axis):
        if outer == 1:
            return value
        shape = value.shape
        split = shape[:axis] + (GROUP, outer, shape[axis] // n_dp) + shape[axis + 1 :]
        return jnp.swapaxes(value.reshape(split), axis, axis + 1).reshape(shape)

    groups = [[o * GROUP + i for o in range(outer)] for i in range(GROUP)]

    def scatter(value, axis):
        if outer == 1:
            return value
        return lax.psum_scatter(
            value, "dp", scatter_dimension=axis, axis_index_groups=groups, tiled=True
        )

    def total(value):
        if outer == 1:
            return value
        return lax.psum(value, "dp", axis_index_groups=groups)

    def body(tokens, lengths, ln_gain, ln_bias, w_query, b_query, w_key, b_key, w_value, b_value, w_out, w_up, b_up, w_down, out_bias, cotangent):
        found = layer(
            order(tokens, 1),
            lengths,
            order(ln_gain, 0),
            order(ln_bias, 0),
            order(w_query, 0),
            b_query,
            order(w_key, 0),
            b_key,
            order(w_value, 0),
            b_value,
            order(w_out, 1),
            order(w_up, 0),
            b_up,
            order(w_down, 1),
            order(out_bias, 0),
            order(cotangent, 1),
        )
        (mixed, grad_tokens, gain, shift, g_q, b_q, g_k, b_k, g_v, b_v, g_out, g_up, b_u, g_down, b_out) = found
        return (
            restore(mixed, 1),
            restore(grad_tokens, 1),
            scatter(gain, 0),
            scatter(shift, 0),
            scatter(g_q, 0),
            total(b_q),
            scatter(g_k, 0),
            total(b_k),
            scatter(g_v, 0),
            total(b_v),
            scatter(g_out, 1),
            scatter(g_up, 0),
            total(b_u),
            scatter(g_down, 1),
            scatter(b_out, 0),
        )

    return body


def solution(mesh):
    in_specs = (
        P("dp", None),
        P("dp", None),
        P(),
        P(),
        P(None, "mp"),
        P("mp"),
        P(None, "mp"),
        P("mp"),
        P(None, "mp"),
        P("mp"),
        P("mp", None),
        P(None, "mp"),
        P("mp"),
        P("mp", None),
        P(),
        P("dp", None),
    )
    out_specs = (
        P("dp", None),
        P("dp", None),
        P("dp"),
        P("dp"),
        P("dp", "mp"),
        P("mp"),
        P("dp", "mp"),
        P("mp"),
        P("dp", "mp"),
        P("mp"),
        P("mp", "dp"),
        P("dp", "mp"),
        P("mp"),
        P("mp", "dp"),
        P("dp"),
    )
    body = make_body(mesh.shape["dp"], mesh.shape["mp"])
    return jax.shard_map(body, mesh=mesh, in_specs=in_specs, out_specs=out_specs, check_vma=False)
```

```python
import functools
import math

import jax
import jax.numpy as jnp
from jax import lax
from jax.experimental import pallas as pl
from jax.experimental.pallas import tpu as pltpu
from jax.sharding import PartitionSpec as P

HD = 64
ROT = 32
EPSILON = 1e-05
GROUP = 8
CORE, XBIT, YBIT = 1, 2, 4
BLK = 256
WIDE = 512
N_MP = 4
Z_PARTS = 8
Z_LEAD = 2
Z_LAG = (0, 2, 4)
Z_TICKS = ((1, 4), (4, 5), (6, 6), (9, 7), (10, 8), (11, 9), (12, 10), (13, 11))
F32 = jnp.float32
BF16 = jnp.bfloat16
MESH = pl.DeviceIdType.MESH
MAIN_VMEM = 93 * 2**19
GELU_A = math.sqrt(2.0 / math.pi)
GELU_B = 0.044715


def nn(left, right):
    return lax.dot_general(left, right, (((1,), (0,)), ((), ())), preferred_element_type=F32)


def nt(left, right):
    return lax.dot_general(left, right, (((1,), (1,)), ((), ())), preferred_element_type=F32)


def tn(left, right):
    return lax.dot_general(left, right, (((0,), (0,)), ((), ())), preferred_element_type=F32)


def flip(index, mask):
    for bit in (1, 2, 4):
        if mask & bit:
            index = index + bit * (1 - 2 * ((index // bit) % 2))
    return index


def mult(value, by):
    return pl.multiple_of(value, by)


N_JS = (0, XBIT, CORE, XBIT | CORE)
N_MS = (0, YBIT)
G_JS = (0, YBIT, CORE, YBIT | CORE)
G_MS = (0, XBIT)


def layer_kernel(
    n_chunks,
    g_chunks,
    lens_h,
    tok_h,
    cot_h,
    gain_h,
    shift_h,
    bq_h,
    bk_h,
    bv_h,
    bup_h,
    obias_h,
    wq_h,
    wk_h,
    wv_h,
    wo_h,
    wu_h,
    wd_h,
    bn,
    bg,
    rsn_r,
    rsg_r,
    zout,
    vec_o,
    lens,
    norm_in,
    bias_in,
    tok,
    gout,
    normed,
    turned_n,
    wq,
    wk,
    wv,
    wo,
    wu,
    wd,
    side_n,
    side_g,
    rsn_s,
    rsg_s,
    act,
    gup,
    gqkv,
    att,
    q_s,
    k_s,
    v_s,
    ga_s,
    amask,
    rot_c,
    rot_a,
    rot_b,
    stat_m,
    stat_i,
    zpart,
    zfar,
    znear,
    zmid,
    vzl,
    vz,
    vzr,
    vdr,
    gsum,
    bsum,
    bsum_r,
    cot_rows,
    in_sem,
    tok_sem,
    wide_sem,
    side_ss,
    side_rs,
    bn_ss,
    bg_ss,
    blk_rs,
    rn_ss,
    rn_rs,
    rg_ss,
    rg_rs,
    zf_ss,
    zf_rs,
    zn_ss,
    zm_ss,
    zm_rs,
    zo_ss,
    zo_rs,
    zw_ss,
    ze_rs,
    vz_ss,
    vz_rs,
    vd_ss,
    vd_rs,
    bs_ss,
    bs_rs,
):
    toks, width = tok.shape
    hidden = wu.shape[1]
    heads_w = wq.shape[1]
    n_att = heads_w // BLK
    n_hid = hidden // BLK
    n_own = width // BLK
    dp = lax.axis_index("dp")
    zed = lax.axis_index("mp")
    inner = lax.rem(dp, GROUP)
    outer = dp - inner
    half = toks // 2
    piece_cols = width // Z_PARTS
    piece_rows = half // Z_PARTS

    def peer(mask):
        return (outer + flip(inner, mask), zed)

    def came(ref, sem):
        pltpu.make_async_copy(ref, ref, sem).wait()

    middle = (zed == 1) | (zed == 2)
    end_of_line = (zed == 0) | (zed == 3)
    side_of_line = zed // 2
    beside = (dp, zed + 1 - 2 * lax.rem(zed, 2))
    across = (dp, 3 - zed)
    near_rows = mult(side_of_line * half, half)
    far_rows = mult((1 - side_of_line) * half, half)

    def zpeer(step):
        return (dp, lax.rem(zed + step, N_MP))

    def remote(src, dst, ssem, rsem, where):
        return pltpu.make_async_remote_copy(
            src_ref=src,
            dst_ref=dst,
            send_sem=ssem,
            recv_sem=rsem,
            device_id=where,
            device_id_type=MESH,
        )

    def load(src, dst, number):
        copy = pltpu.make_async_copy(src, dst, in_sem.at[number])
        copy.start()
        return copy

    tok_parts = 4

    def tok_load(c):
        rows = pl.ds(mult(c * (toks // tok_parts), toks // tok_parts), toks // tok_parts)
        return pltpu.make_async_copy(tok_h.at[rows, :], tok.at[rows, :], tok_sem.at[c])

    for c in range(tok_parts):
        tok_load(c).start()
    for at, src in enumerate((gain_h, shift_h)):
        load(src, norm_in.at[:, pl.ds(at * width, width)], 0)
    lens_load = load(lens_h, lens, 1)

    barrier = pltpu.get_barrier_semaphore()
    for mask in range(1, GROUP):
        pl.semaphore_signal(barrier, inc=1, device_id=peer(mask), device_id_type=MESH)
    for step in range(1, N_MP):
        pl.semaphore_signal(barrier, inc=1, device_id=zpeer(step), device_id_type=MESH)

    gout_load = load(cot_h, gout, 2)
    at = 0
    biases = []
    for src in (bup_h, bq_h, bk_h, bv_h, obias_h):
        biases.append(bias_in.at[:, pl.ds(at, src.shape[1])])
        load(src, biases[-1], 3)
        at += src.shape[1]
    bup, bq, bk, bv, obias = biases
    gain, shift = norm_in.at[:, pl.ds(0, width)], norm_in.at[:, pl.ds(width, width)]

    def wide_loads(w):
        part = pl.ds(mult(w * WIDE, WIDE), WIDE)
        return (
            pltpu.make_async_copy(wu_h.at[:, part], wu.at[:, part], wide_sem.at[w]),
            pltpu.make_async_copy(wd_h.at[part, :], wd.at[part, :], wide_sem.at[w]),
        )

    @pl.loop(0, hidden // WIDE)
    def _(w):
        for copy in wide_loads(w):
            copy.start()

    for src, dst in ((wq_h, wq), (wk_h, wk), (wv_h, wv), (wo_h, wo)):
        load(src, dst, 4)
    attn_load = pltpu.make_async_copy(wu_h, wu, in_sem.at[4])
    cot_load = load(cot_h.at[pl.ds(near_rows, half), :], cot_rows, 5)

    def segment_of(place):
        number = jnp.zeros_like(place)
        start_of = jnp.zeros_like(place)
        for j, end in enumerate(ends):
            start = end - lens[0, j]
            inside = ((place >= start) & (place < end)).astype(jnp.int32)
            number = number + inside * (j + 1)
            start_of = start_of + inside * start
        return number, start_of

    def cross_core(index, times):
        return index + times * (1 - 2 * lax.rem(index, 2))

    def flip_by(index, bit, times):
        return index + times * (bit * (1 - 2 * ((index // bit) % 2)))

    own_part = lax.rem(zed, 2)
    own_slot = 1 + 2 * side_of_line
    other_slot = 3 - 2 * side_of_line

    def side_places(slot_at, m):
        at = pl.ds(mult(slot_at * toks, toks), toks)
        rows = pl.ds(mult(m * BLK, BLK), BLK)
        return side_n.at[rows, at], side_g.at[at, rows]

    def side_direct():
        at_n = flip(cross_core(inner, side_of_line), XBIT)
        at_g = flip(cross_core(inner, side_of_line), YBIT)
        owner_n = flip_by(at_n, YBIT, own_part)
        owner_g = flip_by(at_g, XBIT, own_part)
        place_n, place_g = side_places(own_slot, own_part)
        source_g = cot_h.at[:, pl.ds(mult(owner_g * BLK, BLK), BLK)]
        return (
            remote(turned_n.at[owner_n], place_n, side_ss, side_rs.at[0], (outer + at_n, zed)),
            remote(source_g, place_g, side_ss, side_rs.at[0], (outer + at_g, zed)),
            owner_n,
        )

    def side_core(m):
        place_n, place_g = side_places(2, m)
        owner_n = flip(inner, CORE ^ N_MS[m])
        owner_g = flip(inner, CORE ^ G_MS[m])
        source_g = cot_h.at[:, pl.ds(mult(owner_g * BLK, BLK), BLK)]
        return (
            remote(turned_n.at[owner_n], place_n, side_ss, side_rs.at[4], peer(CORE)),
            remote(source_g, place_g, side_ss, side_rs.at[4], peer(CORE)),
        )

    def side_send(slot_at, m, number, where):
        for place in side_places(slot_at, m):
            remote(place, place, side_ss, side_rs.at[number], where).start()

    def side_came(number, blocks=2):
        came(bn.at[0, pl.ds(0, blocks * toks), :], side_rs.at[number])

    def side_pass(stage):
        if stage == 0:
            side_came(0)
            side_send(own_slot, own_part, 1, beside)

            @pl.when(middle)
            def _():
                side_send(own_slot, own_part, 2, across)
        elif stage == 1:
            @pl.when(middle)
            def _():
                side_came(1)
                side_send(own_slot, 1 - own_part, 3, across)
                side_came(2)
                side_send(other_slot, 1 - own_part, 2, beside)
        else:
            @pl.when(middle)
            def _():
                side_came(3)
                side_send(other_slot, own_part, 3, beside)

    lane = lax.broadcasted_iota(jnp.int32, (toks, 128), 1)
    slot = lax.broadcasted_iota(jnp.int32, (toks, 128), 0)
    in_head = lane % HD
    order = (in_head % (ROT // 2)).astype(F32)
    freq = jnp.exp(order * (-2.0 / ROT * math.log(10000.0)))
    angle = slot.astype(F32) * freq
    rot_c[...] = jnp.cos(angle)
    rot_a[...] = jnp.sin(angle)

    came(norm_in, in_sem.at[0])
    step_rows = 32

    @pl.loop(0, tok_parts)
    def _(c):
        tok_load(c).wait()
        for part in range(toks // tok_parts // step_rows):
            rows = pl.ds(mult(c * (toks // tok_parts) + part * step_rows, step_rows), step_rows)
            value = tok[rows, :].astype(F32)
            mean = jnp.sum(value, axis=1, keepdims=True) * (1.0 / width)
            center = value - mean
            spread = jnp.sum(center * center, axis=1, keepdims=True) * (1.0 / width)
            inv = lax.rsqrt(spread + EPSILON)
            normed[rows, :] = (center * inv * gain[...] + shift[...]).astype(BF16)
            stat_m[rows, :] = jnp.broadcast_to(mean, (step_rows, 128))
            stat_i[rows, :] = jnp.broadcast_to(inv, (step_rows, 128))

    pl.semaphore_wait(barrier, GROUP - 1 + N_MP - 1)
    direct_n, direct_g, first_owner = side_direct()
    direct_g.start()
    turned_n[first_owner] = normed[:, pl.ds(mult(first_owner * BLK, BLK), BLK)].T
    direct_n.start()

    lens_load.wait()
    gout_load.wait()
    came(bias_in, in_sem.at[3])

    ends = []
    total_len = 0
    for j in range(lens.shape[1]):
        total_len = total_len + lens[0, j]
        ends.append(total_len)

    gsum[...] = jnp.zeros_like(gsum)

    @pl.loop(0, toks // step_rows)
    def _(r):
        first = r * step_rows
        rows = pl.ds(mult(first, step_rows), step_rows)
        place = first + lax.broadcasted_iota(jnp.int32, (step_rows, width), 0)
        value = jnp.where(place < total_len, gout[rows, :].astype(F32), 0.0)
        gout[rows, :] = value.astype(BF16)
        gsum[0:1, :] = gsum[0:1, :] + jnp.sum(value, axis=0, keepdims=True)

    for m in (0, 1):
        for owner in (flip(inner, CORE ^ N_MS[m]), flip(inner, N_MS[m])):
            turned_n[owner] = normed[:, pl.ds(mult(owner * BLK, BLK), BLK)].T
        for copy in side_core(m):
            copy.start()
        owner_g = mult(flip(inner, G_MS[m]) * BLK, BLK)
        side_g[0:toks, m * BLK : m * BLK + BLK] = gout[:, pl.ds(owner_g, BLK)]
        side_n[m * BLK : m * BLK + BLK, 0:toks] = turned_n[flip(inner, N_MS[m])]
    def bn_copy(s, k):
        src = bn.at[s, pl.ds(toks if k == 2 else 0, toks), :]
        slot_at = (1, 2, 3)[k]
        return remote(
            src,
            bn.at[s, pl.ds(slot_at * toks, toks), :],
            bn_ss,
            blk_rs.at[s, min(k, 1)],
            peer((XBIT, CORE, CORE)[k]),
        )

    def bg_copy(s, k):
        src = bg.at[s, :, pl.ds(toks if k == 2 else 0, toks)]
        slot_at = (1, 2, 3)[k]
        return remote(
            src,
            bg.at[s, :, pl.ds(slot_at * toks, toks)],
            bg_ss,
            blk_rs.at[s, min(k, 1)],
            peer((YBIT, CORE, CORE)[k]),
        )

    def piece(t, g, first_row):
        if t == 0:
            return pl.ds(first_row, half), pl.ds(mult(g * piece_cols, piece_cols), piece_cols)
        return pl.ds(mult(first_row + g * piece_rows, piece_rows), piece_rows), pl.ds(0, width)

    def z_far(t, g):
        rows, cols = piece(t, g, far_rows)
        to_rows, _ = piece(t, g, 0)
        return remote(
            zpart.at[t, rows, cols],
            zfar.at[t, to_rows, cols],
            zf_ss,
            zf_rs.at[t * Z_PARTS + g],
            beside,
        )

    def z_near(t, g):
        rows, cols = piece(t, g, near_rows)
        to_rows, _ = piece(t, g, 0)
        return remote(
            zpart.at[t, rows, cols],
            znear.at[t, to_rows, cols],
            zn_ss,
            zm_rs.at[t * Z_PARTS + g],
            beside,
        )

    def z_mid(t, g):
        rows, cols = piece(t, g, far_rows)
        to_rows, _ = piece(t, g, 0)
        return remote(
            zpart.at[t, rows, cols],
            zmid.at[t, to_rows, cols],
            zm_ss,
            zm_rs.at[t * Z_PARTS + g],
            across,
        )

    def z_done(t, g, to_end):
        rows, cols = piece(t, g, near_rows)
        place = zout.at[t, rows, cols]
        if to_end:
            return remote(place, place, zo_ss, ze_rs, beside)
        return remote(place, place, zo_ss, zo_rs.at[t * Z_PARTS + g], across)

    def z_pass(t, g):
        rows, cols = piece(t, g, far_rows)
        return remote(zout.at[t, rows, cols], zout.at[t, rows, cols], zw_ss, ze_rs, beside)

    def z_send(copies):
        @pl.when(end_of_line)
        def _():
            for copy in copies:
                copy.start()

    def z_first(t, g):
        z_far(t, g).wait_recv()
        rows, cols = piece(t, g, far_rows)
        there, _ = piece(t, g, 0)
        zpart[t, rows, cols] = (
            zpart[t, rows, cols].astype(F32) + zfar[t, there, cols].astype(F32)
        ).astype(BF16)
        z_mid(t, g).start()

    def z_second(t, g):
        came(znear.at[0, :, pl.ds(0, 2 * piece_cols)], zm_rs.at[t * Z_PARTS + g])
        rows, cols = piece(t, g, near_rows)
        there, _ = piece(t, g, 0)
        total = (
            zpart[t, rows, cols].astype(F32)
            + znear[t, there, cols].astype(F32)
            + zmid[t, there, cols].astype(F32)
        )
        base = tok[rows, cols].astype(F32)
        if t == 0:
            place = near_rows + lax.broadcasted_iota(jnp.int32, total.shape, 0)
            branch = jnp.where(place < total_len, total + obias[:, cols], 0.0)
            zout[t, rows, cols] = (base + branch).astype(BF16)
        else:
            @pl.when(g == 0)
            def _():
                cot_load.wait()

            inv = stat_i[rows, 0:1]
            standard = (base - stat_m[rows, 0:1]) * inv
            grad = total * gain[...]
            mean_g = jnp.sum(grad, axis=1, keepdims=True) * (1.0 / width)
            mean_x = jnp.sum(grad * standard, axis=1, keepdims=True) * (1.0 / width)
            back = inv * (grad - mean_g - standard * mean_x)
            zout[t, rows, cols] = (cot_rows[there, :].astype(F32) + back).astype(BF16)
        z_done(t, g, False).start()
        z_done(t, g, True).start()

    def z_third(t, g):
        z_done(t, g, False).wait_recv()
        z_pass(t, g).start()

    def z_move(step, number):
        for t in (0, 1):
            at = number - t * Z_PARTS
            if isinstance(number, int):
                if 0 <= at < Z_PARTS:
                    pl.when(middle)(functools.partial(step, t, at))
            else:
                pl.when(middle & (at >= 0) & (at < Z_PARTS))(functools.partial(step, t, at))

    def z_tick(number):
        for step, lag in zip((z_first, z_second, z_third), Z_LAG):
            z_move(step, number - lag)

    per_wide = WIDE // BLK
    n_wide = hidden // WIDE

    def hidden_block(w, with_grad):
        cols = pl.ds(mult(w * WIDE, WIDE), WIDE)
        came(wu.at[:, pl.ds(0, 2 * WIDE)], wide_sem.at[w])
        up = nn(normed[...], wu[:, cols]) + bup[:, cols]
        square = up * up
        tanh = jnp.tanh(GELU_A * up * (1.0 + GELU_B * square))
        row = lax.broadcasted_iota(jnp.int32, up.shape, 0)
        active = jnp.where(row < total_len, 0.5 * up * (1.0 + tanh), 0.0).astype(BF16)
        act[:, cols] = active
        slope = 0.5 * (1.0 + tanh) + 0.5 * up * (1.0 - tanh * tanh) * (
            GELU_A * (1.0 + 3.0 * GELU_B * square)
        )
        if with_grad:
            grad = (nt(gout[...], wd[cols, :]) * slope).astype(BF16)
            gup[:, cols] = grad
        else:
            gup[:, cols] = slope.astype(BF16)
        for part in range(per_wide):
            c = w * per_wide + part
            inside = slice(part * BLK, part * BLK + BLK)
            bg[c, :, 0:toks] = active[:, inside].T
            if with_grad:
                bn[c, 0:toks, :] = grad[:, inside]
        for part in range(per_wide):
            c = w * per_wide + part
            for k in (0, 1):
                bg_copy(c, k).start()
                if with_grad:
                    bn_copy(c, k).start()

    @pl.loop(0, n_wide // 2)
    def _(w):
        hidden_block(w, True)

    @pl.loop(n_wide // 2, n_wide)
    def _(w):
        hidden_block(w, False)

        @pl.when(w == n_wide // 2)
        def _():
            side_pass(0)

    def hidden_grad(first, past, shift):
        @pl.loop(first, past)
        def _(w):
            z_tick(w - first)
            cols = pl.ds(mult(w * WIDE, WIDE), WIDE)
            grad = (nt(gout[...], wd[cols, :]) * gup[:, cols].astype(F32)).astype(BF16)
            gup[:, cols] = grad
            for part in range(per_wide):
                c = shift + w * per_wide + part
                bn[c, 0:toks, :] = grad[:, part * BLK : part * BLK + BLK]
                for k in (0, 1):
                    bn_copy(c, k).start()

    seg_r, _ = segment_of(slot)
    seg_c, _ = segment_of(lax.broadcasted_iota(jnp.int32, (8, toks), 1))
    place_r = lax.broadcasted_iota(jnp.int32, (toks, toks), 0)
    place_c = lax.broadcasted_iota(jnp.int32, (toks, toks), 1)
    same = jnp.concatenate([seg_r] * (toks // 128), axis=1) == seg_c[0:1, :]
    mask = jnp.where(same & (place_c <= place_r), 0.0, -1e30)
    for h in (0, 1):
        amask[h * toks : h * toks + toks, :] = mask

    which = lax.broadcasted_iota(jnp.int32, (8, 128), 0)
    starts = jnp.zeros((8, 128), jnp.int32)
    for j, end in enumerate(ends):
        starts = jnp.where(which == j, end - lens[0, j], starts)
    turn = starts.astype(F32) * freq[0:8, :]
    turn_c, turn_s = jnp.cos(turn), jnp.sin(turn)
    back_c, back_s = jnp.ones((toks, 128), F32), jnp.zeros((toks, 128), F32)
    for j in range(len(ends)):
        inside = seg_r == j + 1
        back_c = jnp.where(inside, turn_c[j : j + 1, :], back_c)
        back_s = jnp.where(inside, turn_s[j : j + 1, :], back_s)
    slot_c, slot_s = rot_c[...], rot_a[...]
    cosine = slot_c * back_c + slot_s * back_s
    sine = slot_s * back_c - slot_c * back_s
    rot_c[...] = jnp.where(in_head < ROT, cosine, 1.0)
    rot_a[...] = jnp.where(in_head < ROT // 2, -sine, 0.0)
    rot_b[...] = jnp.where((in_head >= ROT // 2) & (in_head < ROT), sine, 0.0)

    def rotate(value, sign):
        left = pltpu.roll(value, 128 - ROT // 2, 1)
        right = pltpu.roll(value, ROT // 2, 1)
        return value * rot_c[...] + sign * (left * rot_a[...] + right * rot_b[...])

    attn_load.wait()

    @pl.loop(0, heads_w // BLK)
    def _(n):
        cols = pl.ds(mult(n * BLK, BLK), BLK)
        query = nn(normed[...], wq[:, cols]) + bq[:, cols]
        keys = nn(normed[...], wk[:, cols]) + bk[:, cols]
        for part in range(BLK // 128):
            at = pl.ds(mult(n * BLK + part * 128, 128), 128)
            lanes = slice(part * 128, part * 128 + 128)
            q_s[:, at] = (rotate(query[:, lanes], 1.0) * 0.125).astype(BF16)
            k_s[:, at] = rotate(keys[:, lanes], 1.0).astype(BF16)
        v_s[:, cols] = (nn(normed[...], wv[:, cols]) + bv[:, cols]).astype(BF16)
        ga_s[:, cols] = nt(gout[...], wo[cols, :]).astype(BF16)

    low_lane = lax.broadcasted_iota(jnp.int32, (1, 128), 1) < HD
    first_head = jnp.where(low_lane, 1.0, 0.0).astype(BF16)
    second_head = jnp.where(low_lane, 0.0, 1.0).astype(BF16)
    low_full = lax.broadcasted_iota(jnp.int32, (toks, 128), 1) < HD

    def apart(value):
        return jnp.concatenate([value * first_head, value * second_head], axis=0)

    def together(value):
        return jnp.where(low_full, value[:toks], value[toks:])

    @pl.loop(0, n_att)
    def _(n):
        base_n = n_hid // 2 + 3 * n

        for part in range(BLK // 128):
            at = pl.ds(mult(n * BLK + part * 128, 128), 128)
            lanes = slice(part * 128, part * 128 + 128)
            kp, vp = k_s[:, at], v_s[:, at]
            q2, g2 = apart(q_s[:, at]), apart(ga_s[:, at])
            scores = nt(q2, kp) + amask[...]
            top = jnp.max(scores, axis=1, keepdims=True)
            expo = jnp.exp(scores - top)
            probs = expo * (1.0 / jnp.sum(expo, axis=1, keepdims=True))
            probs_low = probs.astype(BF16)
            prob_grad = nt(g2, vp)
            delta = jnp.sum(probs * prob_grad, axis=1, keepdims=True)
            score_grad = (probs * (prob_grad - delta)).astype(BF16)
            out = jnp.where(slot < total_len, together(nn(probs_low, vp)), 0.0).astype(BF16)
            att[:, at] = out
            bg[n_hid + n, lanes, 0:toks] = out.T
            dq = rotate(together(nn(score_grad, kp)) * 0.125, -1.0).astype(BF16)
            dk = rotate(tn(score_grad, q2), -1.0).astype(BF16)
            dv = tn(probs_low, g2).astype(BF16)
            for kind, value in enumerate((dq, dk, dv)):
                bn[base_n + kind, 0:toks, lanes] = value
                gqkv[:, pl.ds(mult(kind * heads_w + n * BLK + part * 128, 128), 128)] = value
        for k in (0, 1):
            bg_copy(n_hid + n, k).start()
            for kind in range(3):
                bn_copy(base_n + kind, k).start()

    side_pass(1)

    @pl.loop(0, width // WIDE)
    def _(n):
        cols = pl.ds(mult(n * WIDE, WIDE), WIDE)
        zpart[0, :, cols] = (nn(act[...], wd[:, cols]) + nn(att[...], wo[:, cols])).astype(BF16)
        for part in range(Z_LEAD):
            g = n * Z_LEAD + part
            z_send([z_far(0, g)])

            @pl.when(n > 0)
            def _(g=g):
                z_send([z_near(0, g - Z_LEAD)])

    hidden_grad(n_wide // 2, n_wide, 3 * n_att)

    vzl[...] = jnp.zeros_like(vzl)

    @pl.loop(0, width // WIDE)
    def _(n):
        cols = pl.ds(mult(n * WIDE, WIDE), WIDE)
        grad = nt(gup[...], wu[cols, :])
        for kind, weight in enumerate((wq, wk, wv)):
            grad = grad + nt(gqkv[:, kind * heads_w : (kind + 1) * heads_w], weight[cols, :])
        zpart[1, :, cols] = grad.astype(BF16)

        @pl.when(n == 0)
        def _():
            side_pass(2)

        @pl.when(n == 1)
        def _():
            z_tick(2)

        @pl.when(n == 3)
        def _():
            z_tick(3)

        for part in range(WIDE // 128):
            lanes = slice(part * 128, part * 128 + 128)
            at = pl.ds(mult(n * WIDE + part * 128, 128), 128)
            owner = n * per_wide + part * 128 // BLK
            half_row = part * 128 % BLK // 128
            piece_of = grad[:, lanes]
            standard = (tok[:, at].astype(F32) - stat_m[...]) * stat_i[...]
            vzl[owner, half_row : half_row + 1, :] = jnp.sum(piece_of * standard, axis=0, keepdims=True)
            vzl[owner, 2 + half_row : 3 + half_row, :] = jnp.sum(piece_of, axis=0, keepdims=True)

    def vd_copy(mask):
        return remote(
            vzl.at[flip(inner, mask)], vdr.at[mask - 1], vd_ss, vd_rs, peer(mask)
        )

    for owner in range(n_own):
        for half_row in (0, 1):
            first = owner * BLK + half_row * 128
            vzl[owner, 4 + half_row : 5 + half_row, :] = gsum[0:1, first : first + 128]
    for mask in range(1, GROUP):
        vd_copy(mask).start()
    for g in range(Z_PARTS):
        late = Z_PARTS - Z_LEAD + g
        z_send([z_far(1, g), z_near(late // Z_PARTS, late % Z_PARTS)])
    for g in range(Z_PARTS - Z_LEAD, Z_PARTS):
        z_send([z_near(1, g)])

    bs_copy = remote(bsum, bsum_r, bs_ss, bs_rs, peer(YBIT))

    def rn_copy(s):
        return remote(rsn_s.at[s], rsn_r.at[s], rn_ss, rn_rs, peer(YBIT))

    def rg_copy(s):
        return remote(rsg_s.at[s], rsg_r.at[s], rg_ss, rg_rs, peer(XBIT))

    side_came(4, 4)

    @pl.when(end_of_line)
    def _():
        for number in (1, 2, 3):
            side_came(number)

    bsum[...] = jnp.zeros_like(bsum)

    def vz_copy(step):
        return remote(vz, vzr.at[step - 1], vz_ss, vz_rs, zpeer(step))

    def vec_spread():
        came(vdr, vd_rs)
        vz[...] = vzl[inner] + jnp.sum(vdr[...], axis=0)
        for step in range(1, N_MP):
            vz_copy(step).start()

    side_n[2 * BLK :, :] = jnp.ones((16, 4 * toks), BF16)

    @pl.loop(0, n_chunks + 1)
    def _(s):
        @pl.when(s < g_chunks)
        def _():
            came(bn.at[s, pl.ds(0, 2 * toks), :], blk_rs.at[s, 0])
            bn_copy(s, 2).start()
            bg_copy(s, 2).start()

        @pl.when((s >= g_chunks) & (s < n_chunks))
        def _():
            came(bn.at[s, pl.ds(0, toks), :], blk_rs.at[s, 0])
            bn_copy(s, 2).start()

        @pl.when((s > 0) & (s <= g_chunks))
        def _():
            came(bn.at[s - 1], blk_rs.at[s - 1, 1])

        @pl.when(s > g_chunks)
        def _():
            came(bn.at[s - 1, pl.ds(0, 2 * toks), :], blk_rs.at[s - 1, 1])

        @pl.when(s > 0)
        def _():
            p = s - 1
            both = nn(side_n[...], bn[p])
            rsn_s[p] = both[BLK : 2 * BLK, :].astype(BF16)
            rn_copy(p).start()
            bsum[pl.ds(p, 1), :] = both[2 * BLK : 2 * BLK + 1, :]
            bn[p, 2 * toks : 3 * toks, :] = both[:BLK, :].astype(BF16)

        @pl.when((s > 0) & (s <= g_chunks))
        def _():
            p = s - 1
            both = nn(bg[p], side_g[...])
            rsg_s[p] = both[:, BLK:].astype(BF16)
            rg_copy(p).start()
            bg[p, :, 2 * toks : 3 * toks] = both[:, :BLK].astype(BF16)

        tick = -1
        for turn, number in Z_TICKS:
            tick = jnp.where(s == turn, number, tick)
        z_tick(tick)

    bs_copy.start()
    vec_spread()
    @pl.loop(Z_TICKS[-1][1] + 1, 2 * Z_PARTS + Z_LAG[-1])
    def _(number):
        z_tick(number)

    bs_copy.wait_recv()
    came(vzr, vz_rs)
    norm_sums = vz[...] + jnp.sum(vzr[...], axis=0)
    for half_row in (0, 1):
        lanes = slice(half_row * 128, half_row * 128 + 128)
        vec_o[0:1, lanes] = norm_sums[half_row : half_row + 1, :]
        vec_o[1:2, lanes] = norm_sums[2 + half_row : 3 + half_row, :]
        vec_o[2:3, lanes] = vz[4 + half_row : 5 + half_row, :]
    vec_o[8:, :] = bsum[...] + bsum_r[...]

    came(rsn_r, rn_rs)
    came(rsg_r, rg_rs)

    came(bn.at[:, pl.ds(0, 3 * toks), :], bn_ss)
    came(bg.at[:, :, pl.ds(0, 3 * toks)], bg_ss)
    came(rsn_s, rn_ss)
    came(rsg_s, rg_ss)
    came(vzr, vz_ss)
    came(vdr, vd_ss)
    bs_copy.wait_send()

    @pl.when(end_of_line)
    def _():
        came(bn.at[pl.ds(0, 2)], side_ss)
        came(zfar, zf_ss)
        came(znear, zn_ss)
        came(zout, ze_rs)
        cot_load.wait()

    @pl.when(middle)
    def _():
        came(bn.at[pl.ds(0, 4)], side_ss)
        came(zmid, zm_ss)
        came(zout, zo_ss)
        came(zmid, zw_ss)


def write_kernel(n_hid, n_att, bn, bg, rsn, rsg, zout, vec, mixed_h, gtok_h, gain_o, shift_o, gq_h, bq_o, gk_h, bk_o, gv_h, bv_o, go_h, gu_h, bu_o, gd_h, ob_o, stage, small, sem, zsem, small_sem):
    n_chunks, n_g = bn.shape[0], bg.shape[0]
    toks = zout.shape[1]
    z_outs = [
        pltpu.make_async_copy(zout.at[t], out, zsem) for t, out in enumerate((mixed_h, gtok_h))
    ]
    for out in z_outs:
        out.start()
    places, biases = [], []
    for s in range(n_chunks):
        inside = s - n_hid // 2
        if 0 <= inside < 3 * n_att:
            (out, bias), at = ((gq_h, bq_o), (gk_h, bk_o), (gv_h, bv_o))[inside % 3], inside // 3
        else:
            (out, bias), at = (gu_h, bu_o), s if inside < 0 else s - 3 * n_att
        biases.append((bias, at))
        places.append((True, s, out.at[:, pl.ds(at * BLK, BLK)]))
    for s in range(n_g):
        out, at = (gd_h, s) if s < n_hid else (go_h, s - n_hid)
        places.append((False, s, out.at[pl.ds(at * BLK, BLK), :]))
    smalls = [(gain_o, (0,)), (shift_o, (1,)), (ob_o, (2,))]
    for bias in (bq_o, bk_o, bv_o, bu_o):
        smalls.append((bias, tuple(8 + s for at, s in sorted((at, s) for s, (b, at) in enumerate(biases) if b is bias))))
    at = 0
    for out, rows in smalls:
        for part, row in enumerate(rows):
            small[at + part * BLK : at + part * BLK + BLK] = vec[row]
        pltpu.make_async_copy(small.at[pl.ds(at, len(rows) * BLK)], out, small_sem).start()
        at += len(rows) * BLK
    copies = []
    for number, (first, s, place) in enumerate(places):
        slot = number
        if first:
            value = bn[s, 2 * toks : 3 * toks, :].astype(F32) + rsn[s].astype(F32)
        else:
            value = bg[s, :, 2 * toks : 3 * toks].astype(F32) + rsg[s].astype(F32)
        stage[slot] = value
        copies.append(pltpu.make_async_copy(stage.at[slot], place, sem))
        copies[number].start()
    pltpu.make_async_copy(stage, stage, sem).wait()
    pltpu.make_async_copy(zout, zout, zsem).wait()
    pltpu.make_async_copy(small, small, small_sem).wait()


def layer(tokens, lengths, ln_gain, ln_bias, w_query, b_query, w_key, b_key, w_value, b_value, w_out, w_up, b_up, w_down, out_bias, cotangent):
    toks, width = tokens.shape
    heads_w = w_query.shape[1]
    hidden = w_up.shape[1]
    n_chunks = (3 * heads_w + hidden) // BLK
    g_chunks = (heads_w + hidden) // BLK
    n_own = width // BLK
    n_vec = -(-n_chunks // 8) * 8
    half = toks // 2
    dma = pltpu.SemaphoreType.DMA
    vmem = pltpu.VMEM
    scratch = [
        pltpu.SMEM(lengths.shape, jnp.int32),
        vmem((1, 2 * width), F32),
        vmem((1, hidden + 3 * heads_w + width), F32),
        vmem((toks, width), BF16),
        vmem((toks, width), BF16),
        vmem((toks, width), BF16),
        vmem((n_own, BLK, toks), BF16),
        vmem(w_query.shape, BF16),
        vmem(w_key.shape, BF16),
        vmem(w_value.shape, BF16),
        vmem(w_out.shape, BF16),
        vmem(w_up.shape, BF16),
        vmem(w_down.shape, BF16),
        vmem((2 * BLK + 16, 4 * toks), BF16),
        vmem((4 * toks, 2 * BLK), BF16),
        vmem((n_chunks, BLK, BLK), BF16),
        vmem((g_chunks, BLK, BLK), BF16),
        vmem((toks, hidden), BF16),
        vmem((toks, hidden), BF16),
        vmem((toks, 3 * heads_w), BF16),
        vmem((toks, heads_w), BF16),
        vmem((toks, heads_w), BF16),
        vmem((toks, heads_w), BF16),
        vmem((toks, heads_w), BF16),
        vmem((toks, heads_w), BF16),
        vmem((2 * toks, toks), F32),
        vmem((toks, 128), F32),
        vmem((toks, 128), F32),
        vmem((toks, 128), F32),
        vmem((toks, 128), F32),
        vmem((toks, 128), F32),
        vmem((2, toks, width), BF16),
        vmem((2, half, width), BF16),
        vmem((2, half, width), BF16),
        vmem((2, half, width), BF16),
        vmem((n_own, 8, 128), F32),
        vmem((8, 128), F32),
        vmem((N_MP - 1, 8, 128), F32),
        vmem((GROUP - 1, 8, 128), F32),
        vmem((8, width), F32),
        vmem((n_vec, BLK), F32),
        vmem((n_vec, BLK), F32),
        vmem((half, width), BF16),
        dma((6,)),
        dma((4,)),
        dma((hidden // WIDE,)),
        dma,
        dma((5,)),
        dma,
        dma,
        dma((n_chunks, 2)),
        dma,
        dma,
        dma,
        dma,
        dma,
        dma((2 * Z_PARTS,)),
        dma,
        dma,
        dma((2 * Z_PARTS,)),
        dma,
        dma((2 * Z_PARTS,)),
        dma,
        dma,
        dma,
        dma,
        dma,
        dma,
        dma,
        dma,
    ]
    anyspace = pl.BlockSpec(memory_space=pl.ANY)
    local = pl.BlockSpec(memory_space=pltpu.VMEM)
    row = lambda value: value.reshape(1, -1)
    kept = pl.pallas_call(
        functools.partial(layer_kernel, n_chunks, g_chunks),
        out_shape=(
            vmem((n_chunks, 4 * toks, BLK), BF16),
            vmem((g_chunks, BLK, 4 * toks), BF16),
            vmem((n_chunks, BLK, BLK), BF16),
            vmem((g_chunks, BLK, BLK), BF16),
            vmem((2, toks, width), BF16),
            vmem((8 + n_vec, BLK), F32),
        ),
        in_specs=[anyspace] * 16,
        out_specs=(local,) * 6,
        scratch_shapes=scratch,
        compiler_params=pltpu.CompilerParams(
            collective_id=0, has_side_effects=True, vmem_limit_bytes=MAIN_VMEM
        ),
    )(
        lengths,
        tokens,
        cotangent,
        row(ln_gain),
        row(ln_bias),
        row(b_query),
        row(b_key),
        row(b_value),
        row(b_up),
        row(out_bias),
        w_query,
        w_key,
        w_value,
        w_out,
        w_up,
        w_down,
    )
    f32 = lambda *shape: jax.ShapeDtypeStruct(shape, F32)
    low = jax.ShapeDtypeStruct((toks, width), BF16)
    outs = (
        low,
        low,
        f32(BLK),
        f32(BLK),
        f32(BLK, heads_w),
        f32(heads_w),
        f32(BLK, heads_w),
        f32(heads_w),
        f32(BLK, heads_w),
        f32(heads_w),
        f32(heads_w, BLK),
        f32(BLK, hidden),
        f32(hidden),
        f32(hidden, BLK),
        f32(BLK),
    )
    slots = n_chunks + g_chunks
    return pl.pallas_call(
        functools.partial(write_kernel, hidden // BLK, heads_w // BLK),
        out_shape=outs,
        in_specs=[local] * 6,
        out_specs=(anyspace,) * len(outs),
        scratch_shapes=[
            vmem((slots, BLK, BLK), F32),
            vmem((3 * BLK + 3 * heads_w + hidden,), F32),
            dma,
            dma,
            dma,
        ],
        compiler_params=pltpu.CompilerParams(vmem_limit_bytes=12 * 2**20),
    )(*kept)


def make_body(n_dp, n_mp):
    outer = n_dp // GROUP

    def order(value, axis):
        if outer == 1:
            return value
        shape = value.shape
        split = shape[:axis] + (outer, GROUP, shape[axis] // n_dp) + shape[axis + 1 :]
        return jnp.swapaxes(value.reshape(split), axis, axis + 1).reshape(shape)

    def restore(value, axis):
        if outer == 1:
            return value
        shape = value.shape
        split = shape[:axis] + (GROUP, outer, shape[axis] // n_dp) + shape[axis + 1 :]
        return jnp.swapaxes(value.reshape(split), axis, axis + 1).reshape(shape)

    groups = [[o * GROUP + i for o in range(outer)] for i in range(GROUP)]

    def scatter(value, axis):
        if outer == 1:
            return value
        return lax.psum_scatter(
            value, "dp", scatter_dimension=axis, axis_index_groups=groups, tiled=True
        )

    def total(value):
        if outer == 1:
            return value
        return lax.psum(value, "dp", axis_index_groups=groups)

    def body(tokens, lengths, ln_gain, ln_bias, w_query, b_query, w_key, b_key, w_value, b_value, w_out, w_up, b_up, w_down, out_bias, cotangent):
        found = layer(
            order(tokens, 1),
            lengths,
            order(ln_gain, 0),
            order(ln_bias, 0),
            order(w_query, 0),
            b_query,
            order(w_key, 0),
            b_key,
            order(w_value, 0),
            b_value,
            order(w_out, 1),
            order(w_up, 0),
            b_up,
            order(w_down, 1),
            order(out_bias, 0),
            order(cotangent, 1),
        )
        (mixed, grad_tokens, gain, shift, g_q, b_q, g_k, b_k, g_v, b_v, g_out, g_up, b_u, g_down, b_out) = found
        return (
            restore(mixed, 1),
            restore(grad_tokens, 1),
            scatter(gain, 0),
            scatter(shift, 0),
            scatter(g_q, 0),
            total(b_q),
            scatter(g_k, 0),
            total(b_k),
            scatter(g_v, 0),
            total(b_v),
            scatter(g_out, 1),
            scatter(g_up, 0),
            total(b_u),
            scatter(g_down, 1),
            scatter(b_out, 0),
        )

    return body


def solution(mesh):
    in_specs = (
        P("dp", None),
        P("dp", None),
        P(),
        P(),
        P(None, "mp"),
        P("mp"),
        P(None, "mp"),
        P("mp"),
        P(None, "mp"),
        P("mp"),
        P("mp", None),
        P(None, "mp"),
        P("mp"),
        P("mp", None),
        P(),
        P("dp", None),
    )
    out_specs = (
        P("dp", None),
        P("dp", None),
        P("dp"),
        P("dp"),
        P("dp", "mp"),
        P("mp"),
        P("dp", "mp"),
        P("mp"),
        P("dp", "mp"),
        P("mp"),
        P("mp", "dp"),
        P("dp", "mp"),
        P("mp"),
        P("mp", "dp"),
        P("dp"),
    )
    body = make_body(mesh.shape["dp"], mesh.shape["mp"])
    return jax.shard_map(body, mesh=mesh, in_specs=in_specs, out_specs=out_specs, check_vma=False)
```

```python
import functools
import math

import jax
import jax.numpy as jnp
from jax import lax
from jax.experimental import pallas as pl
from jax.experimental.pallas import tpu as pltpu
from jax.sharding import PartitionSpec as P

HD = 64
ROT = 32
EPSILON = 1e-05
GROUP = 8
CORE, XBIT, YBIT = 1, 2, 4
BLK = 256
WIDE = 512
N_MP = 4
Z_PARTS = 8
Z_LEAD = 2
Z_LAG = (0, 2, 4)
Z_TICKS = ((1, 4), (3, 5), (6, 6), (8, 7), (9, 8), (10, 9), (11, 10), (12, 11), (13, 12))
F32 = jnp.float32
BF16 = jnp.bfloat16
MESH = pl.DeviceIdType.MESH
MAIN_VMEM = 93 * 2**19
GELU_A = math.sqrt(2.0 / math.pi)
GELU_B = 0.044715


def nn(left, right):
    return lax.dot_general(left, right, (((1,), (0,)), ((), ())), preferred_element_type=F32)


def nt(left, right):
    return lax.dot_general(left, right, (((1,), (1,)), ((), ())), preferred_element_type=F32)


def tn(left, right):
    return lax.dot_general(left, right, (((0,), (0,)), ((), ())), preferred_element_type=F32)


def flip(index, mask):
    for bit in (1, 2, 4):
        if mask & bit:
            index = index + bit * (1 - 2 * ((index // bit) % 2))
    return index


def mult(value, by):
    return pl.multiple_of(value, by)


N_JS = (0, XBIT, CORE, XBIT | CORE)
N_MS = (0, YBIT)
G_JS = (0, YBIT, CORE, YBIT | CORE)
G_MS = (0, XBIT)


def layer_kernel(
    n_chunks,
    g_chunks,
    lens_h,
    tok_h,
    cot_h,
    gain_h,
    shift_h,
    bq_h,
    bk_h,
    bv_h,
    bup_h,
    obias_h,
    wq_h,
    wk_h,
    wv_h,
    wo_h,
    wu_h,
    wd_h,
    bn,
    bg,
    rsn_r,
    rsg_r,
    zout,
    vec_o,
    lens,
    norm_in,
    bias_in,
    tok,
    gout,
    normed,
    turned_n,
    wq,
    wk,
    wv,
    wo,
    wu,
    wd,
    side_n,
    side_g,
    rsn_s,
    rsg_s,
    act,
    gup,
    gqkv,
    att,
    q_s,
    k_s,
    v_s,
    ga_s,
    amask,
    rot_c,
    rot_a,
    rot_b,
    stat_m,
    stat_i,
    zpart,
    zfar,
    znear,
    zmid,
    vzl,
    vz,
    vzr,
    vdr,
    gsum,
    bsum,
    bsum_s,
    bsum_r,
    cot_rows,
    in_sem,
    tok_sem,
    wide_sem,
    side_ss,
    side_rs,
    bn_ss,
    bg_ss,
    blk_rs,
    rn_ss,
    rn_rs,
    rg_ss,
    rg_rs,
    zf_ss,
    zf_rs,
    zn_ss,
    zm_ss,
    zm_rs,
    zo_ss,
    zo_rs,
    zw_ss,
    ze_rs,
    vz_ss,
    vz_rs,
    vd_ss,
    vd_rs,
    bs_ss,
    bs_rs,
):
    toks, width = tok.shape
    hidden = wu.shape[1]
    heads_w = wq.shape[1]
    n_att = heads_w // BLK
    n_hid = hidden // BLK
    n_own = width // BLK
    dp = lax.axis_index("dp")
    zed = lax.axis_index("mp")
    inner = lax.rem(dp, GROUP)
    outer = dp - inner
    half = toks // 2
    piece_cols = width // Z_PARTS
    piece_rows = half // Z_PARTS

    def peer(mask):
        return (outer + flip(inner, mask), zed)

    def came(ref, sem):
        pltpu.make_async_copy(ref, ref, sem).wait()

    middle = (zed == 1) | (zed == 2)
    end_of_line = (zed == 0) | (zed == 3)
    side_of_line = zed // 2
    beside = (dp, zed + 1 - 2 * lax.rem(zed, 2))
    across = (dp, 3 - zed)
    near_rows = mult(side_of_line * half, half)
    far_rows = mult((1 - side_of_line) * half, half)

    def zpeer(step):
        return (dp, lax.rem(zed + step, N_MP))

    def remote(src, dst, ssem, rsem, where):
        return pltpu.make_async_remote_copy(
            src_ref=src,
            dst_ref=dst,
            send_sem=ssem,
            recv_sem=rsem,
            device_id=where,
            device_id_type=MESH,
        )

    def load(src, dst, number):
        copy = pltpu.make_async_copy(src, dst, in_sem.at[number])
        copy.start()
        return copy

    tok_parts = 4

    def tok_load(c):
        rows = pl.ds(mult(c * (toks // tok_parts), toks // tok_parts), toks // tok_parts)
        return pltpu.make_async_copy(tok_h.at[rows, :], tok.at[rows, :], tok_sem.at[c])

    for c in range(tok_parts):
        tok_load(c).start()
    for at, src in enumerate((gain_h, shift_h)):
        load(src, norm_in.at[:, pl.ds(at * width, width)], 0)
    lens_load = load(lens_h, lens, 1)

    barrier = pltpu.get_barrier_semaphore()
    for mask in range(1, GROUP):
        pl.semaphore_signal(barrier, inc=1, device_id=peer(mask), device_id_type=MESH)
    for step in range(1, N_MP):
        pl.semaphore_signal(barrier, inc=1, device_id=zpeer(step), device_id_type=MESH)

    gout_load = load(cot_h, gout, 2)
    at = 0
    biases = []
    for src in (bup_h, bq_h, bk_h, bv_h, obias_h):
        biases.append(bias_in.at[:, pl.ds(at, src.shape[1])])
        load(src, biases[-1], 3)
        at += src.shape[1]
    bup, bq, bk, bv, obias = biases
    gain, shift = norm_in.at[:, pl.ds(0, width)], norm_in.at[:, pl.ds(width, width)]

    def wide_loads(w):
        part = pl.ds(mult(w * WIDE, WIDE), WIDE)
        return (
            pltpu.make_async_copy(wu_h.at[:, part], wu.at[:, part], wide_sem.at[w]),
            pltpu.make_async_copy(wd_h.at[part, :], wd.at[part, :], wide_sem.at[w]),
        )

    @pl.loop(0, hidden // WIDE)
    def _(w):
        for copy in wide_loads(w):
            copy.start()

    for src, dst in ((wq_h, wq), (wk_h, wk), (wv_h, wv), (wo_h, wo)):
        load(src, dst, 4)
    attn_load = pltpu.make_async_copy(wu_h, wu, in_sem.at[4])
    cot_load = load(cot_h.at[pl.ds(near_rows, half), :], cot_rows, 5)

    def segment_of(place):
        number = jnp.zeros_like(place)
        start_of = jnp.zeros_like(place)
        for j, end in enumerate(ends):
            start = end - lens[0, j]
            inside = ((place >= start) & (place < end)).astype(jnp.int32)
            number = number + inside * (j + 1)
            start_of = start_of + inside * start
        return number, start_of

    def cross_core(index, times):
        return index + times * (1 - 2 * lax.rem(index, 2))

    def flip_by(index, bit, times):
        return index + times * (bit * (1 - 2 * ((index // bit) % 2)))

    own_part = lax.rem(zed, 2)
    own_slot = 1 + 2 * side_of_line
    other_slot = 3 - 2 * side_of_line

    def side_places(slot_at, m):
        at = pl.ds(mult(slot_at * toks, toks), toks)
        rows = pl.ds(mult(m * BLK, BLK), BLK)
        return side_n.at[rows, at], side_g.at[at, rows]

    def side_direct():
        at_n = flip(cross_core(inner, side_of_line), XBIT)
        at_g = flip(cross_core(inner, side_of_line), YBIT)
        owner_n = flip_by(at_n, YBIT, own_part)
        owner_g = flip_by(at_g, XBIT, own_part)
        place_n, place_g = side_places(own_slot, own_part)
        source_g = cot_h.at[:, pl.ds(mult(owner_g * BLK, BLK), BLK)]
        return (
            remote(turned_n.at[owner_n], place_n, side_ss, side_rs.at[0], (outer + at_n, zed)),
            remote(source_g, place_g, side_ss, side_rs.at[0], (outer + at_g, zed)),
            owner_n,
        )

    def side_core(m):
        place_n, place_g = side_places(2, m)
        owner_n = flip(inner, CORE ^ N_MS[m])
        owner_g = flip(inner, CORE ^ G_MS[m])
        source_g = cot_h.at[:, pl.ds(mult(owner_g * BLK, BLK), BLK)]
        return (
            remote(turned_n.at[owner_n], place_n, side_ss, side_rs.at[1], peer(CORE)),
            remote(source_g, place_g, side_ss, side_rs.at[1], peer(CORE)),
        )

    def side_send(kind, slot_at, m, number, where):
        place = side_places(slot_at, m)[kind]
        remote(place, place, side_ss, side_rs.at[2 * number + kind], where).start()

    def side_came(kind, number):
        came(bn.at[0, pl.ds(0, toks), :], side_rs.at[2 * number + kind])

    def side_first():
        came(bn.at[0, pl.ds(0, 2 * toks), :], side_rs.at[0])
        for kind in (0, 1):
            side_send(kind, own_slot, own_part, 1, beside)

            @pl.when(middle)
            def _():
                side_send(kind, own_slot, own_part, 2, across)

    def side_relay(kind):
        @pl.when(middle)
        def _():
            side_came(kind, 1)
            side_send(kind, own_slot, 1 - own_part, 3, across)
            side_came(kind, 2)
            side_send(kind, other_slot, 1 - own_part, 2, beside)

    def side_out(kind):
        @pl.when(middle)
        def _():
            side_came(kind, 3)
            side_send(kind, other_slot, own_part, 3, beside)

    lane = lax.broadcasted_iota(jnp.int32, (toks, 128), 1)
    slot = lax.broadcasted_iota(jnp.int32, (toks, 128), 0)
    in_head = lane % HD
    order = (in_head % (ROT // 2)).astype(F32)
    freq = jnp.exp(order * (-2.0 / ROT * math.log(10000.0)))
    angle = slot.astype(F32) * freq
    rot_c[...] = jnp.cos(angle)
    rot_a[...] = jnp.sin(angle)

    came(norm_in, in_sem.at[0])
    step_rows = 32

    @pl.loop(0, tok_parts)
    def _(c):
        tok_load(c).wait()
        for part in range(toks // tok_parts // step_rows):
            rows = pl.ds(mult(c * (toks // tok_parts) + part * step_rows, step_rows), step_rows)
            value = tok[rows, :].astype(F32)
            mean = jnp.sum(value, axis=1, keepdims=True) * (1.0 / width)
            center = value - mean
            spread = jnp.sum(center * center, axis=1, keepdims=True) * (1.0 / width)
            inv = lax.rsqrt(spread + EPSILON)
            normed[rows, :] = (center * inv * gain[...] + shift[...]).astype(BF16)
            stat_m[rows, :] = jnp.broadcast_to(mean, (step_rows, 128))
            stat_i[rows, :] = jnp.broadcast_to(inv, (step_rows, 128))

    pl.semaphore_wait(barrier, GROUP - 1 + N_MP - 1)
    direct_n, direct_g, first_owner = side_direct()
    direct_g.start()
    turned_n[first_owner] = normed[:, pl.ds(mult(first_owner * BLK, BLK), BLK)].T
    direct_n.start()

    lens_load.wait()
    gout_load.wait()
    came(bias_in, in_sem.at[3])

    ends = []
    total_len = 0
    for j in range(lens.shape[1]):
        total_len = total_len + lens[0, j]
        ends.append(total_len)

    gsum[...] = jnp.zeros_like(gsum)

    @pl.loop(0, toks // step_rows)
    def _(r):
        first = r * step_rows
        rows = pl.ds(mult(first, step_rows), step_rows)
        place = first + lax.broadcasted_iota(jnp.int32, (step_rows, width), 0)
        value = jnp.where(place < total_len, gout[rows, :].astype(F32), 0.0)
        gout[rows, :] = value.astype(BF16)
        gsum[0:1, :] = gsum[0:1, :] + jnp.sum(value, axis=0, keepdims=True)

    for m in (0, 1):
        for owner in (flip(inner, CORE ^ N_MS[m]), flip(inner, N_MS[m])):
            turned_n[owner] = normed[:, pl.ds(mult(owner * BLK, BLK), BLK)].T
        for copy in side_core(m):
            copy.start()
        owner_g = mult(flip(inner, G_MS[m]) * BLK, BLK)
        side_g[0:toks, m * BLK : m * BLK + BLK] = gout[:, pl.ds(owner_g, BLK)]
        side_n[m * BLK : m * BLK + BLK, 0:toks] = turned_n[flip(inner, N_MS[m])]
    def bn_copy(s, k):
        src = bn.at[s, pl.ds(toks if k == 2 else 0, toks), :]
        slot_at = (1, 2, 3)[k]
        return remote(
            src,
            bn.at[s, pl.ds(slot_at * toks, toks), :],
            bn_ss,
            blk_rs.at[s, min(k, 1)],
            peer((XBIT, CORE, CORE)[k]),
        )

    def bg_copy(s, k):
        src = bg.at[s, :, pl.ds(toks if k == 2 else 0, toks)]
        slot_at = (1, 2, 3)[k]
        return remote(
            src,
            bg.at[s, :, pl.ds(slot_at * toks, toks)],
            bg_ss,
            blk_rs.at[s, min(k, 1)],
            peer((YBIT, CORE, CORE)[k]),
        )

    def piece(t, g, first_row):
        if t == 0:
            return pl.ds(first_row, half), pl.ds(mult(g * piece_cols, piece_cols), piece_cols)
        return pl.ds(mult(first_row + g * piece_rows, piece_rows), piece_rows), pl.ds(0, width)

    def z_far(t, g):
        rows, cols = piece(t, g, far_rows)
        to_rows, _ = piece(t, g, 0)
        return remote(
            zpart.at[t, rows, cols],
            zfar.at[t, to_rows, cols],
            zf_ss,
            zf_rs.at[t * Z_PARTS + g],
            beside,
        )

    def z_near(t, g):
        rows, cols = piece(t, g, near_rows)
        to_rows, _ = piece(t, g, 0)
        return remote(
            zpart.at[t, rows, cols],
            znear.at[t, to_rows, cols],
            zn_ss,
            zm_rs.at[t * Z_PARTS + g],
            beside,
        )

    def z_mid(t, g):
        rows, cols = piece(t, g, far_rows)
        to_rows, _ = piece(t, g, 0)
        return remote(
            zpart.at[t, rows, cols],
            zmid.at[t, to_rows, cols],
            zm_ss,
            zm_rs.at[t * Z_PARTS + g],
            across,
        )

    def z_done(t, g, to_end):
        rows, cols = piece(t, g, near_rows)
        place = zout.at[t, rows, cols]
        if to_end:
            return remote(place, place, zo_ss, ze_rs, beside)
        return remote(place, place, zo_ss, zo_rs.at[t * Z_PARTS + g], across)

    def z_pass(t, g):
        rows, cols = piece(t, g, far_rows)
        return remote(zout.at[t, rows, cols], zout.at[t, rows, cols], zw_ss, ze_rs, beside)

    def z_send(copies):
        @pl.when(end_of_line)
        def _():
            for copy in copies:
                copy.start()

    def z_first(t, g):
        z_far(t, g).wait_recv()
        rows, cols = piece(t, g, far_rows)
        there, _ = piece(t, g, 0)
        zpart[t, rows, cols] = (
            zpart[t, rows, cols].astype(F32) + zfar[t, there, cols].astype(F32)
        ).astype(BF16)
        z_mid(t, g).start()

    def z_second(t, g):
        came(znear.at[0, :, pl.ds(0, 2 * piece_cols)], zm_rs.at[t * Z_PARTS + g])
        rows, cols = piece(t, g, near_rows)
        there, _ = piece(t, g, 0)
        total = (
            zpart[t, rows, cols].astype(F32)
            + znear[t, there, cols].astype(F32)
            + zmid[t, there, cols].astype(F32)
        )
        base = tok[rows, cols].astype(F32)
        if t == 0:
            place = near_rows + lax.broadcasted_iota(jnp.int32, total.shape, 0)
            branch = jnp.where(place < total_len, total + obias[:, cols], 0.0)
            zout[t, rows, cols] = (base + branch).astype(BF16)
        else:
            @pl.when(g == 0)
            def _():
                cot_load.wait()

            inv = stat_i[rows, 0:1]
            standard = (base - stat_m[rows, 0:1]) * inv
            grad = total * gain[...]
            mean_g = jnp.sum(grad, axis=1, keepdims=True) * (1.0 / width)
            mean_x = jnp.sum(grad * standard, axis=1, keepdims=True) * (1.0 / width)
            back = inv * (grad - mean_g - standard * mean_x)
            zout[t, rows, cols] = (cot_rows[there, :].astype(F32) + back).astype(BF16)
        z_done(t, g, False).start()
        z_done(t, g, True).start()

    def z_third(t, g):
        z_done(t, g, False).wait_recv()
        z_pass(t, g).start()

    def z_move(step, number):
        for t in (0, 1):
            at = number - t * Z_PARTS
            if isinstance(number, int):
                if 0 <= at < Z_PARTS:
                    pl.when(middle)(functools.partial(step, t, at))
            else:
                pl.when(middle & (at >= 0) & (at < Z_PARTS))(functools.partial(step, t, at))

    def z_tick(number):
        for step, lag in zip((z_first, z_second, z_third), Z_LAG):
            z_move(step, number - lag)

    per_wide = WIDE // BLK
    n_wide = hidden // WIDE

    def hidden_block(w, with_grad):
        cols = pl.ds(mult(w * WIDE, WIDE), WIDE)
        came(wu.at[:, pl.ds(0, 2 * WIDE)], wide_sem.at[w])
        up = nn(normed[...], wu[:, cols]) + bup[:, cols]
        square = up * up
        tanh = jnp.tanh(GELU_A * up * (1.0 + GELU_B * square))
        row = lax.broadcasted_iota(jnp.int32, up.shape, 0)
        active = jnp.where(row < total_len, 0.5 * up * (1.0 + tanh), 0.0).astype(BF16)
        act[:, cols] = active
        slope = 0.5 * (1.0 + tanh) + 0.5 * up * (1.0 - tanh * tanh) * (
            GELU_A * (1.0 + 3.0 * GELU_B * square)
        )
        if with_grad:
            grad = (nt(gout[...], wd[cols, :]) * slope).astype(BF16)
            gup[:, cols] = grad
        else:
            gup[:, cols] = slope.astype(BF16)
        for part in range(per_wide):
            c = w * per_wide + part
            inside = slice(part * BLK, part * BLK + BLK)
            bg[c, :, 0:toks] = active[:, inside].T
            if with_grad:
                bn[c, 0:toks, :] = grad[:, inside]
        for part in range(per_wide):
            c = w * per_wide + part
            for k in (0, 1):
                bg_copy(c, k).start()
                if with_grad:
                    bn_copy(c, k).start()

    @pl.loop(0, n_wide // 2)
    def _(w):
        hidden_block(w, True)

    @pl.loop(n_wide // 2, n_wide)
    def _(w):
        hidden_block(w, False)

        @pl.when(w == n_wide // 2)
        def _():
            side_first()

    def hidden_grad(first, past, shift):
        @pl.loop(first, past)
        def _(w):
            @pl.when(w == first)
            def _():
                side_out(0)

            @pl.when(w == first + 1)
            def _():
                side_out(1)

            z_tick(w - first)
            cols = pl.ds(mult(w * WIDE, WIDE), WIDE)
            grad = (nt(gout[...], wd[cols, :]) * gup[:, cols].astype(F32)).astype(BF16)
            gup[:, cols] = grad
            for part in range(per_wide):
                c = shift + w * per_wide + part
                bn[c, 0:toks, :] = grad[:, part * BLK : part * BLK + BLK]
                for k in (0, 1):
                    bn_copy(c, k).start()

    seg_r, _ = segment_of(slot)
    seg_c, _ = segment_of(lax.broadcasted_iota(jnp.int32, (8, toks), 1))
    place_r = lax.broadcasted_iota(jnp.int32, (toks, toks), 0)
    place_c = lax.broadcasted_iota(jnp.int32, (toks, toks), 1)
    same = jnp.concatenate([seg_r] * (toks // 128), axis=1) == seg_c[0:1, :]
    mask = jnp.where(same & (place_c <= place_r), 0.0, -1e30)
    for h in (0, 1):
        amask[h * toks : h * toks + toks, :] = mask

    which = lax.broadcasted_iota(jnp.int32, (8, 128), 0)
    starts = jnp.zeros((8, 128), jnp.int32)
    for j, end in enumerate(ends):
        starts = jnp.where(which == j, end - lens[0, j], starts)
    turn = starts.astype(F32) * freq[0:8, :]
    turn_c, turn_s = jnp.cos(turn), jnp.sin(turn)
    back_c, back_s = jnp.ones((toks, 128), F32), jnp.zeros((toks, 128), F32)
    for j in range(len(ends)):
        inside = seg_r == j + 1
        back_c = jnp.where(inside, turn_c[j : j + 1, :], back_c)
        back_s = jnp.where(inside, turn_s[j : j + 1, :], back_s)
    slot_c, slot_s = rot_c[...], rot_a[...]
    cosine = slot_c * back_c + slot_s * back_s
    sine = slot_s * back_c - slot_c * back_s
    rot_c[...] = jnp.where(in_head < ROT, cosine, 1.0)
    rot_a[...] = jnp.where(in_head < ROT // 2, -sine, 0.0)
    rot_b[...] = jnp.where((in_head >= ROT // 2) & (in_head < ROT), sine, 0.0)

    def rotate(value, sign):
        left = pltpu.roll(value, 128 - ROT // 2, 1)
        right = pltpu.roll(value, ROT // 2, 1)
        return value * rot_c[...] + sign * (left * rot_a[...] + right * rot_b[...])

    attn_load.wait()

    @pl.loop(0, heads_w // BLK)
    def _(n):
        cols = pl.ds(mult(n * BLK, BLK), BLK)
        query = nn(normed[...], wq[:, cols]) + bq[:, cols]
        keys = nn(normed[...], wk[:, cols]) + bk[:, cols]
        for part in range(BLK // 128):
            at = pl.ds(mult(n * BLK + part * 128, 128), 128)
            lanes = slice(part * 128, part * 128 + 128)
            q_s[:, at] = (rotate(query[:, lanes], 1.0) * 0.125).astype(BF16)
            k_s[:, at] = rotate(keys[:, lanes], 1.0).astype(BF16)
        v_s[:, cols] = (nn(normed[...], wv[:, cols]) + bv[:, cols]).astype(BF16)
        ga_s[:, cols] = nt(gout[...], wo[cols, :]).astype(BF16)

    low_lane = lax.broadcasted_iota(jnp.int32, (1, 128), 1) < HD
    first_head = jnp.where(low_lane, 1.0, 0.0).astype(BF16)
    second_head = jnp.where(low_lane, 0.0, 1.0).astype(BF16)
    low_full = lax.broadcasted_iota(jnp.int32, (toks, 128), 1) < HD

    def apart(value):
        return jnp.concatenate([value * first_head, value * second_head], axis=0)

    def together(value):
        return jnp.where(low_full, value[:toks], value[toks:])

    @pl.loop(0, n_att)
    def _(n):
        base_n = n_hid // 2 + 3 * n

        @pl.when(n == n_att - 1)
        def _():
            side_relay(0)

        for part in range(BLK // 128):
            at = pl.ds(mult(n * BLK + part * 128, 128), 128)
            lanes = slice(part * 128, part * 128 + 128)
            kp, vp = k_s[:, at], v_s[:, at]
            q2, g2 = apart(q_s[:, at]), apart(ga_s[:, at])
            scores = nt(q2, kp) + amask[...]
            top = jnp.max(scores, axis=1, keepdims=True)
            expo = jnp.exp(scores - top)
            probs = expo * (1.0 / jnp.sum(expo, axis=1, keepdims=True))
            probs_low = probs.astype(BF16)
            prob_grad = nt(g2, vp)
            delta = jnp.sum(probs * prob_grad, axis=1, keepdims=True)
            score_grad = (probs * (prob_grad - delta)).astype(BF16)
            out = jnp.where(slot < total_len, together(nn(probs_low, vp)), 0.0).astype(BF16)
            att[:, at] = out
            bg[n_hid + n, lanes, 0:toks] = out.T
            dq = rotate(together(nn(score_grad, kp)) * 0.125, -1.0).astype(BF16)
            dk = rotate(tn(score_grad, q2), -1.0).astype(BF16)
            dv = tn(probs_low, g2).astype(BF16)
            for kind, value in enumerate((dq, dk, dv)):
                bn[base_n + kind, 0:toks, lanes] = value
                gqkv[:, pl.ds(mult(kind * heads_w + n * BLK + part * 128, 128), 128)] = value
        for k in (0, 1):
            bg_copy(n_hid + n, k).start()
            for kind in range(3):
                bn_copy(base_n + kind, k).start()

    side_relay(1)

    @pl.loop(0, width // WIDE)
    def _(n):
        cols = pl.ds(mult(n * WIDE, WIDE), WIDE)
        zpart[0, :, cols] = (nn(act[...], wd[:, cols]) + nn(att[...], wo[:, cols])).astype(BF16)
        for part in range(Z_LEAD):
            g = n * Z_LEAD + part
            z_send([z_far(0, g)])

            @pl.when(n > 0)
            def _(g=g):
                z_send([z_near(0, g - Z_LEAD)])

    hidden_grad(n_wide // 2, n_wide, 3 * n_att)

    vzl[...] = jnp.zeros_like(vzl)

    @pl.loop(0, width // WIDE)
    def _(n):
        cols = pl.ds(mult(n * WIDE, WIDE), WIDE)
        grad = nt(gup[...], wu[cols, :])
        for kind, weight in enumerate((wq, wk, wv)):
            grad = grad + nt(gqkv[:, kind * heads_w : (kind + 1) * heads_w], weight[cols, :])
        zpart[1, :, cols] = grad.astype(BF16)

        @pl.when(n == 1)
        def _():
            z_tick(2)

        @pl.when(n == 3)
        def _():
            z_tick(3)

        for part in range(WIDE // 128):
            lanes = slice(part * 128, part * 128 + 128)
            at = pl.ds(mult(n * WIDE + part * 128, 128), 128)
            owner = n * per_wide + part * 128 // BLK
            half_row = part * 128 % BLK // 128
            piece_of = grad[:, lanes]
            standard = (tok[:, at].astype(F32) - stat_m[...]) * stat_i[...]
            vzl[owner, half_row : half_row + 1, :] = jnp.sum(piece_of * standard, axis=0, keepdims=True)
            vzl[owner, 2 + half_row : 3 + half_row, :] = jnp.sum(piece_of, axis=0, keepdims=True)

    def vd_copy(mask):
        return remote(
            vzl.at[flip(inner, mask)], vdr.at[mask - 1], vd_ss, vd_rs, peer(mask)
        )

    for owner in range(n_own):
        for half_row in (0, 1):
            first = owner * BLK + half_row * 128
            vzl[owner, 4 + half_row : 5 + half_row, :] = gsum[0:1, first : first + 128]
    for mask in range(1, GROUP):
        vd_copy(mask).start()
    for g in range(Z_PARTS):
        late = Z_PARTS - Z_LEAD + g
        z_send([z_far(1, g), z_near(late // Z_PARTS, late % Z_PARTS)])
    for g in range(Z_PARTS - Z_LEAD, Z_PARTS):
        z_send([z_near(1, g)])

    bs_copy = remote(bsum_s, bsum_r, bs_ss, bs_rs, peer(YBIT))

    def rn_copy(s):
        return remote(rsn_s.at[s], rsn_r.at[s], rn_ss, rn_rs, peer(YBIT))

    def rg_copy(s):
        return remote(rsg_s.at[s], rsg_r.at[s], rg_ss, rg_rs, peer(XBIT))

    came(bn.at[0], side_rs.at[1])

    @pl.when(end_of_line)
    def _():
        for number in (1, 2, 3):
            for kind in (0, 1):
                side_came(kind, number)

    bsum[...] = jnp.zeros_like(bsum)

    def vz_copy(step):
        return remote(vz, vzr.at[step - 1], vz_ss, vz_rs, zpeer(step))

    def vec_spread():
        came(vdr, vd_rs)
        vz[...] = vzl[inner] + jnp.sum(vdr[...], axis=0)
        for step in range(1, N_MP):
            vz_copy(step).start()

    side_n[2 * BLK :, :] = jnp.ones((16, 4 * toks), BF16)

    @pl.loop(0, n_chunks + 1)
    def _(s):
        @pl.when(s < g_chunks)
        def _():
            came(bn.at[s, pl.ds(0, 2 * toks), :], blk_rs.at[s, 0])
            bn_copy(s, 2).start()
            bg_copy(s, 2).start()

        @pl.when((s >= g_chunks) & (s < n_chunks))
        def _():
            came(bn.at[s, pl.ds(0, toks), :], blk_rs.at[s, 0])
            bn_copy(s, 2).start()

        @pl.when((s > 0) & (s <= g_chunks))
        def _():
            came(bn.at[s - 1], blk_rs.at[s - 1, 1])

        @pl.when(s > g_chunks)
        def _():
            came(bn.at[s - 1, pl.ds(0, 2 * toks), :], blk_rs.at[s - 1, 1])

        @pl.when(s > 0)
        def _():
            p = s - 1
            both = nn(side_n[...], bn[p])
            rsn_s[p] = both[BLK : 2 * BLK, :].astype(BF16)
            rn_copy(p).start()
            bsum[pl.ds(p, 1), :] = both[2 * BLK : 2 * BLK + 1, :]
            bn[p, 2 * toks : 3 * toks, :] = both[:BLK, :].astype(BF16)

        @pl.when((s > 0) & (s <= g_chunks))
        def _():
            p = s - 1
            both = nn(bg[p], side_g[...])
            rsg_s[p] = both[:, BLK:].astype(BF16)
            rg_copy(p).start()
            bg[p, :, 2 * toks : 3 * toks] = both[:, :BLK].astype(BF16)

        tick = -1
        for turn, number in Z_TICKS:
            tick = jnp.where(s == turn, number, tick)
        z_tick(tick)

    bsum_s[...] = bsum[...].astype(BF16)
    bs_copy.start()
    vec_spread()
    @pl.loop(Z_TICKS[-1][1] + 1, 2 * Z_PARTS + Z_LAG[-1])
    def _(number):
        z_tick(number)

    bs_copy.wait_recv()
    came(vzr, vz_rs)
    norm_sums = vz[...] + jnp.sum(vzr[...], axis=0)
    for half_row in (0, 1):
        lanes = slice(half_row * 128, half_row * 128 + 128)
        vec_o[0:1, lanes] = norm_sums[half_row : half_row + 1, :]
        vec_o[1:2, lanes] = norm_sums[2 + half_row : 3 + half_row, :]
        vec_o[2:3, lanes] = vz[4 + half_row : 5 + half_row, :]
    vec_o[8:, :] = bsum[...] + bsum_r[...].astype(F32)

    came(rsn_r, rn_rs)
    came(rsg_r, rg_rs)

    came(bn.at[:, pl.ds(0, 3 * toks), :], bn_ss)
    came(bg.at[:, :, pl.ds(0, 3 * toks)], bg_ss)
    came(rsn_s, rn_ss)
    came(rsg_s, rg_ss)
    came(vzr, vz_ss)
    came(vdr, vd_ss)
    bs_copy.wait_send()

    @pl.when(end_of_line)
    def _():
        came(bn.at[pl.ds(0, 2)], side_ss)
        came(zfar, zf_ss)
        came(znear, zn_ss)
        came(zout, ze_rs)
        cot_load.wait()

    @pl.when(middle)
    def _():
        came(bn.at[pl.ds(0, 4)], side_ss)
        came(zmid, zm_ss)
        came(zout, zo_ss)
        came(zmid, zw_ss)


def write_kernel(n_hid, n_att, bn, bg, rsn, rsg, zout, vec, mixed_h, gtok_h, gain_o, shift_o, gq_h, bq_o, gk_h, bk_o, gv_h, bv_o, go_h, gu_h, bu_o, gd_h, ob_o, stage, small, sem, zsem, small_sem):
    n_chunks, n_g = bn.shape[0], bg.shape[0]
    toks = zout.shape[1]
    z_outs = [
        pltpu.make_async_copy(zout.at[t], out, zsem) for t, out in enumerate((mixed_h, gtok_h))
    ]
    for out in z_outs:
        out.start()
    places, biases = [], []
    for s in range(n_chunks):
        inside = s - n_hid // 2
        if 0 <= inside < 3 * n_att:
            (out, bias), at = ((gq_h, bq_o), (gk_h, bk_o), (gv_h, bv_o))[inside % 3], inside // 3
        else:
            (out, bias), at = (gu_h, bu_o), s if inside < 0 else s - 3 * n_att
        biases.append((bias, at))
        places.append((True, s, out.at[:, pl.ds(at * BLK, BLK)]))
    for s in range(n_g):
        out, at = (gd_h, s) if s < n_hid else (go_h, s - n_hid)
        places.append((False, s, out.at[pl.ds(at * BLK, BLK), :]))
    smalls = [(gain_o, (0,)), (shift_o, (1,)), (ob_o, (2,))]
    for bias in (bq_o, bk_o, bv_o, bu_o):
        smalls.append((bias, tuple(8 + s for at, s in sorted((at, s) for s, (b, at) in enumerate(biases) if b is bias))))
    at = 0
    for out, rows in smalls:
        for part, row in enumerate(rows):
            small[at + part * BLK : at + part * BLK + BLK] = vec[row]
        pltpu.make_async_copy(small.at[pl.ds(at, len(rows) * BLK)], out, small_sem).start()
        at += len(rows) * BLK
    copies = []
    for number, (first, s, place) in enumerate(places):
        slot = number
        if first:
            value = bn[s, 2 * toks : 3 * toks, :].astype(F32) + rsn[s].astype(F32)
        else:
            value = bg[s, :, 2 * toks : 3 * toks].astype(F32) + rsg[s].astype(F32)
        stage[slot] = value
        copies.append(pltpu.make_async_copy(stage.at[slot], place, sem))
        copies[number].start()
    pltpu.make_async_copy(stage, stage, sem).wait()
    pltpu.make_async_copy(zout, zout, zsem).wait()
    pltpu.make_async_copy(small, small, small_sem).wait()


def layer(tokens, lengths, ln_gain, ln_bias, w_query, b_query, w_key, b_key, w_value, b_value, w_out, w_up, b_up, w_down, out_bias, cotangent):
    toks, width = tokens.shape
    heads_w = w_query.shape[1]
    hidden = w_up.shape[1]
    n_chunks = (3 * heads_w + hidden) // BLK
    g_chunks = (heads_w + hidden) // BLK
    n_own = width // BLK
    n_vec = -(-n_chunks // 8) * 8
    half = toks // 2
    dma = pltpu.SemaphoreType.DMA
    vmem = pltpu.VMEM
    scratch = [
        pltpu.SMEM(lengths.shape, jnp.int32),
        vmem((1, 2 * width), F32),
        vmem((1, hidden + 3 * heads_w + width), F32),
        vmem((toks, width), BF16),
        vmem((toks, width), BF16),
        vmem((toks, width), BF16),
        vmem((n_own, BLK, toks), BF16),
        vmem(w_query.shape, BF16),
        vmem(w_key.shape, BF16),
        vmem(w_value.shape, BF16),
        vmem(w_out.shape, BF16),
        vmem(w_up.shape, BF16),
        vmem(w_down.shape, BF16),
        vmem((2 * BLK + 16, 4 * toks), BF16),
        vmem((4 * toks, 2 * BLK), BF16),
        vmem((n_chunks, BLK, BLK), BF16),
        vmem((g_chunks, BLK, BLK), BF16),
        vmem((toks, hidden), BF16),
        vmem((toks, hidden), BF16),
        vmem((toks, 3 * heads_w), BF16),
        vmem((toks, heads_w), BF16),
        vmem((toks, heads_w), BF16),
        vmem((toks, heads_w), BF16),
        vmem((toks, heads_w), BF16),
        vmem((toks, heads_w), BF16),
        vmem((2 * toks, toks), F32),
        vmem((toks, 128), F32),
        vmem((toks, 128), F32),
        vmem((toks, 128), F32),
        vmem((toks, 128), F32),
        vmem((toks, 128), F32),
        vmem((2, toks, width), BF16),
        vmem((2, half, width), BF16),
        vmem((2, half, width), BF16),
        vmem((2, half, width), BF16),
        vmem((n_own, 8, 128), F32),
        vmem((8, 128), F32),
        vmem((N_MP - 1, 8, 128), F32),
        vmem((GROUP - 1, 8, 128), F32),
        vmem((8, width), F32),
        vmem((n_vec, BLK), F32),
        vmem((n_vec, BLK), BF16),
        vmem((n_vec, BLK), BF16),
        vmem((half, width), BF16),
        dma((6,)),
        dma((4,)),
        dma((hidden // WIDE,)),
        dma,
        dma((8,)),
        dma,
        dma,
        dma((n_chunks, 2)),
        dma,
        dma,
        dma,
        dma,
        dma,
        dma((2 * Z_PARTS,)),
        dma,
        dma,
        dma((2 * Z_PARTS,)),
        dma,
        dma((2 * Z_PARTS,)),
        dma,
        dma,
        dma,
        dma,
        dma,
        dma,
        dma,
        dma,
    ]
    anyspace = pl.BlockSpec(memory_space=pl.ANY)
    local = pl.BlockSpec(memory_space=pltpu.VMEM)
    row = lambda value: value.reshape(1, -1)
    kept = pl.pallas_call(
        functools.partial(layer_kernel, n_chunks, g_chunks),
        out_shape=(
            vmem((n_chunks, 4 * toks, BLK), BF16),
            vmem((g_chunks, BLK, 4 * toks), BF16),
            vmem((n_chunks, BLK, BLK), BF16),
            vmem((g_chunks, BLK, BLK), BF16),
            vmem((2, toks, width), BF16),
            vmem((8 + n_vec, BLK), F32),
        ),
        in_specs=[anyspace] * 16,
        out_specs=(local,) * 6,
        scratch_shapes=scratch,
        compiler_params=pltpu.CompilerParams(
            collective_id=0, has_side_effects=True, vmem_limit_bytes=MAIN_VMEM
        ),
    )(
        lengths,
        tokens,
        cotangent,
        row(ln_gain),
        row(ln_bias),
        row(b_query),
        row(b_key),
        row(b_value),
        row(b_up),
        row(out_bias),
        w_query,
        w_key,
        w_value,
        w_out,
        w_up,
        w_down,
    )
    f32 = lambda *shape: jax.ShapeDtypeStruct(shape, F32)
    low = jax.ShapeDtypeStruct((toks, width), BF16)
    outs = (
        low,
        low,
        f32(BLK),
        f32(BLK),
        f32(BLK, heads_w),
        f32(heads_w),
        f32(BLK, heads_w),
        f32(heads_w),
        f32(BLK, heads_w),
        f32(heads_w),
        f32(heads_w, BLK),
        f32(BLK, hidden),
        f32(hidden),
        f32(hidden, BLK),
        f32(BLK),
    )
    slots = n_chunks + g_chunks
    return pl.pallas_call(
        functools.partial(write_kernel, hidden // BLK, heads_w // BLK),
        out_shape=outs,
        in_specs=[local] * 6,
        out_specs=(anyspace,) * len(outs),
        scratch_shapes=[
            vmem((slots, BLK, BLK), F32),
            vmem((3 * BLK + 3 * heads_w + hidden,), F32),
            dma,
            dma,
            dma,
        ],
        compiler_params=pltpu.CompilerParams(vmem_limit_bytes=12 * 2**20),
    )(*kept)


def make_body(n_dp, n_mp):
    outer = n_dp // GROUP

    def order(value, axis):
        if outer == 1:
            return value
        shape = value.shape
        split = shape[:axis] + (outer, GROUP, shape[axis] // n_dp) + shape[axis + 1 :]
        return jnp.swapaxes(value.reshape(split), axis, axis + 1).reshape(shape)

    def restore(value, axis):
        if outer == 1:
            return value
        shape = value.shape
        split = shape[:axis] + (GROUP, outer, shape[axis] // n_dp) + shape[axis + 1 :]
        return jnp.swapaxes(value.reshape(split), axis, axis + 1).reshape(shape)

    groups = [[o * GROUP + i for o in range(outer)] for i in range(GROUP)]

    def scatter(value, axis):
        if outer == 1:
            return value
        return lax.psum_scatter(
            value, "dp", scatter_dimension=axis, axis_index_groups=groups, tiled=True
        )

    def total(value):
        if outer == 1:
            return value
        return lax.psum(value, "dp", axis_index_groups=groups)

    def body(tokens, lengths, ln_gain, ln_bias, w_query, b_query, w_key, b_key, w_value, b_value, w_out, w_up, b_up, w_down, out_bias, cotangent):
        found = layer(
            order(tokens, 1),
            lengths,
            order(ln_gain, 0),
            order(ln_bias, 0),
            order(w_query, 0),
            b_query,
            order(w_key, 0),
            b_key,
            order(w_value, 0),
            b_value,
            order(w_out, 1),
            order(w_up, 0),
            b_up,
            order(w_down, 1),
            order(out_bias, 0),
            order(cotangent, 1),
        )
        (mixed, grad_tokens, gain, shift, g_q, b_q, g_k, b_k, g_v, b_v, g_out, g_up, b_u, g_down, b_out) = found
        return (
            restore(mixed, 1),
            restore(grad_tokens, 1),
            scatter(gain, 0),
            scatter(shift, 0),
            scatter(g_q, 0),
            total(b_q),
            scatter(g_k, 0),
            total(b_k),
            scatter(g_v, 0),
            total(b_v),
            scatter(g_out, 1),
            scatter(g_up, 0),
            total(b_u),
            scatter(g_down, 1),
            scatter(b_out, 0),
        )

    return body


def solution(mesh):
    in_specs = (
        P("dp", None),
        P("dp", None),
        P(),
        P(),
        P(None, "mp"),
        P("mp"),
        P(None, "mp"),
        P("mp"),
        P(None, "mp"),
        P("mp"),
        P("mp", None),
        P(None, "mp"),
        P("mp"),
        P("mp", None),
        P(),
        P("dp", None),
    )
    out_specs = (
        P("dp", None),
        P("dp", None),
        P("dp"),
        P("dp"),
        P("dp", "mp"),
        P("mp"),
        P("dp", "mp"),
        P("mp"),
        P("dp", "mp"),
        P("mp"),
        P("mp", "dp"),
        P("dp", "mp"),
        P("mp"),
        P("mp", "dp"),
        P("dp"),
    )
    body = make_body(mesh.shape["dp"], mesh.shape["mp"])
    return jax.shard_map(body, mesh=mesh, in_specs=in_specs, out_specs=out_specs, check_vma=False)
```

```python
import functools
import math

import jax
import jax.numpy as jnp
from jax import lax
from jax.experimental import pallas as pl
from jax.experimental.pallas import tpu as pltpu
from jax.sharding import PartitionSpec as P

HD = 64
ROT = 32
EPSILON = 1e-05
GROUP = 8
CORE, XBIT, YBIT = 1, 2, 4
BLK = 256
WIDE = 512
Z_PARTS = 8
Z_LEAD = 2
Z_LAG = (0, 2, 4)
Z_TICKS = ((1, 4), (3, 5), (6, 6), (8, 7), (9, 8), (10, 9), (11, 10), (12, 11), (13, 12))
F32 = jnp.float32
BF16 = jnp.bfloat16
MESH = pl.DeviceIdType.MESH
MAIN_VMEM = 93 * 2**19
GELU_A = math.sqrt(2.0 / math.pi)
GELU_B = 0.044715


def nn(left, right):
    return lax.dot_general(left, right, (((1,), (0,)), ((), ())), preferred_element_type=F32)


def nt(left, right):
    return lax.dot_general(left, right, (((1,), (1,)), ((), ())), preferred_element_type=F32)


def tn(left, right):
    return lax.dot_general(left, right, (((0,), (0,)), ((), ())), preferred_element_type=F32)


def flip(index, mask):
    for bit in (1, 2, 4):
        if mask & bit:
            index = index + bit * (1 - 2 * ((index // bit) % 2))
    return index


def mult(value, by):
    return pl.multiple_of(value, by)


N_JS = (0, XBIT, CORE, XBIT | CORE)
N_MS = (0, YBIT)
G_JS = (0, YBIT, CORE, YBIT | CORE)
G_MS = (0, XBIT)


def layer_kernel(
    n_chunks,
    g_chunks,
    lens_h,
    tok_h,
    cot_h,
    gain_h,
    shift_h,
    bq_h,
    bk_h,
    bv_h,
    bup_h,
    obias_h,
    wq_h,
    wk_h,
    wv_h,
    wo_h,
    wu_h,
    wd_h,
    bn,
    bg,
    rsn_r,
    rsg_r,
    zout,
    vec_o,
    lens,
    norm_in,
    bias_in,
    tok,
    gout,
    normed,
    turned_n,
    wq,
    wk,
    wv,
    wo,
    wu,
    wd,
    side_n,
    side_g,
    rsn_s,
    rsg_s,
    act,
    gup,
    gqkv,
    att,
    q_s,
    k_s,
    v_s,
    ga_s,
    amask,
    rot_c,
    rot_a,
    rot_b,
    stat_m,
    stat_i,
    zpart,
    zfar,
    znear,
    zmid,
    vzl,
    vz,
    vz_pair,
    norm_sums,
    vzr,
    vdr,
    gsum,
    bsum,
    bsum_s,
    bsum_r,
    cot_rows,
    in_sem,
    tok_sem,
    wide_sem,
    side_ss,
    side_rs,
    bn_ss,
    bg_ss,
    blk_rs,
    rn_ss,
    rn_rs,
    rg_ss,
    rg_rs,
    zf_ss,
    zf_rs,
    zn_ss,
    zm_ss,
    zm_rs,
    zo_ss,
    zo_rs,
    zw_ss,
    ze_rs,
    vz_ss,
    vz_rs,
    vd_ss,
    vd_rs,
    bs_ss,
    bs_rs,
):
    toks, width = tok.shape
    hidden = wu.shape[1]
    heads_w = wq.shape[1]
    n_att = heads_w // BLK
    n_hid = hidden // BLK
    n_own = width // BLK
    dp = lax.axis_index("dp")
    zed = lax.axis_index("mp")
    inner = lax.rem(dp, GROUP)
    outer = dp - inner
    half = toks // 2
    piece_cols = width // Z_PARTS
    piece_rows = half // Z_PARTS

    def peer(mask):
        return (outer + flip(inner, mask), zed)

    def came(ref, sem):
        pltpu.make_async_copy(ref, ref, sem).wait()

    middle = (zed == 1) | (zed == 2)
    end_of_line = (zed == 0) | (zed == 3)
    side_of_line = zed // 2
    beside = (dp, zed + 1 - 2 * lax.rem(zed, 2))
    across = (dp, 3 - zed)
    near_rows = mult(side_of_line * half, half)
    far_rows = mult((1 - side_of_line) * half, half)

    def remote(src, dst, ssem, rsem, where):
        return pltpu.make_async_remote_copy(
            src_ref=src,
            dst_ref=dst,
            send_sem=ssem,
            recv_sem=rsem,
            device_id=where,
            device_id_type=MESH,
        )

    def load(src, dst, number):
        copy = pltpu.make_async_copy(src, dst, in_sem.at[number])
        copy.start()
        return copy

    tok_parts = 4

    def tok_load(c):
        rows = pl.ds(mult(c * (toks // tok_parts), toks // tok_parts), toks // tok_parts)
        return pltpu.make_async_copy(tok_h.at[rows, :], tok.at[rows, :], tok_sem.at[c])

    for c in range(tok_parts):
        tok_load(c).start()
    for at, src in enumerate((gain_h, shift_h)):
        load(src, norm_in.at[:, pl.ds(at * width, width)], 0)
    lens_load = load(lens_h, lens, 1)

    barrier = pltpu.get_barrier_semaphore()
    for mask in range(1, GROUP):
        pl.semaphore_signal(barrier, inc=1, device_id=peer(mask), device_id_type=MESH)
    pl.semaphore_signal(barrier, inc=1, device_id=beside, device_id_type=MESH)

    @pl.when(middle)
    def _():
        pl.semaphore_signal(barrier, inc=1, device_id=across, device_id_type=MESH)

    gout_load = load(cot_h, gout, 2)
    at = 0
    biases = []
    for src in (bup_h, bq_h, bk_h, bv_h, obias_h):
        biases.append(bias_in.at[:, pl.ds(at, src.shape[1])])
        load(src, biases[-1], 3)
        at += src.shape[1]
    bup, bq, bk, bv, obias = biases
    gain, shift = norm_in.at[:, pl.ds(0, width)], norm_in.at[:, pl.ds(width, width)]

    def wide_loads(w):
        part = pl.ds(mult(w * WIDE, WIDE), WIDE)
        return (
            pltpu.make_async_copy(wu_h.at[:, part], wu.at[:, part], wide_sem.at[w]),
            pltpu.make_async_copy(wd_h.at[part, :], wd.at[part, :], wide_sem.at[w]),
        )

    @pl.loop(0, hidden // WIDE)
    def _(w):
        for copy in wide_loads(w):
            copy.start()

    for src, dst in ((wq_h, wq), (wk_h, wk), (wv_h, wv), (wo_h, wo)):
        load(src, dst, 4)
    attn_load = pltpu.make_async_copy(wu_h, wu, in_sem.at[4])
    cot_load = load(cot_h.at[pl.ds(near_rows, half), :], cot_rows, 5)

    def segment_of(place):
        number = jnp.zeros_like(place)
        start_of = jnp.zeros_like(place)
        for j, end in enumerate(ends):
            start = end - lens[0, j]
            inside = ((place >= start) & (place < end)).astype(jnp.int32)
            number = number + inside * (j + 1)
            start_of = start_of + inside * start
        return number, start_of

    def cross_core(index, times):
        return index + times * (1 - 2 * lax.rem(index, 2))

    def flip_by(index, bit, times):
        return index + times * (bit * (1 - 2 * ((index // bit) % 2)))

    own_part = lax.rem(zed, 2)
    own_slot = 1 + 2 * side_of_line
    other_slot = 3 - 2 * side_of_line

    def side_places(slot_at, m):
        at = pl.ds(mult(slot_at * toks, toks), toks)
        rows = pl.ds(mult(m * BLK, BLK), BLK)
        return side_n.at[rows, at], side_g.at[at, rows]

    def side_direct():
        at_n = flip(cross_core(inner, side_of_line), XBIT)
        at_g = flip(cross_core(inner, side_of_line), YBIT)
        owner_n = flip_by(at_n, YBIT, own_part)
        owner_g = flip_by(at_g, XBIT, own_part)
        place_n, place_g = side_places(own_slot, own_part)
        source_g = cot_h.at[:, pl.ds(mult(owner_g * BLK, BLK), BLK)]
        return (
            remote(turned_n.at[owner_n], place_n, side_ss, side_rs.at[0], (outer + at_n, zed)),
            remote(source_g, place_g, side_ss, side_rs.at[0], (outer + at_g, zed)),
            owner_n,
        )

    def side_core(m):
        place_n, place_g = side_places(2, m)
        owner_n = flip(inner, CORE ^ N_MS[m])
        owner_g = flip(inner, CORE ^ G_MS[m])
        source_g = cot_h.at[:, pl.ds(mult(owner_g * BLK, BLK), BLK)]
        return (
            remote(turned_n.at[owner_n], place_n, side_ss, side_rs.at[1], peer(CORE)),
            remote(source_g, place_g, side_ss, side_rs.at[1], peer(CORE)),
        )

    def side_send(kind, slot_at, m, number, where):
        place = side_places(slot_at, m)[kind]
        remote(place, place, side_ss, side_rs.at[2 * number + kind], where).start()

    def side_came(kind, number):
        came(bn.at[0, pl.ds(0, toks), :], side_rs.at[2 * number + kind])

    def side_first():
        came(bn.at[0, pl.ds(0, 2 * toks), :], side_rs.at[0])
        for kind in (0, 1):
            side_send(kind, own_slot, own_part, 1, beside)

            @pl.when(middle)
            def _():
                side_send(kind, own_slot, own_part, 2, across)

    def side_relay(kind):
        @pl.when(middle)
        def _():
            side_came(kind, 1)
            side_send(kind, own_slot, 1 - own_part, 3, across)
            side_came(kind, 2)
            side_send(kind, other_slot, 1 - own_part, 2, beside)

    def side_out(kind):
        @pl.when(middle)
        def _():
            side_came(kind, 3)
            side_send(kind, other_slot, own_part, 3, beside)

    lane = lax.broadcasted_iota(jnp.int32, (toks, 128), 1)
    slot = lax.broadcasted_iota(jnp.int32, (toks, 128), 0)
    in_head = lane % HD
    order = (in_head % (ROT // 2)).astype(F32)
    freq = jnp.exp(order * (-2.0 / ROT * math.log(10000.0)))
    angle = slot.astype(F32) * freq
    rot_c[...] = jnp.cos(angle)
    rot_a[...] = jnp.sin(angle)

    came(norm_in, in_sem.at[0])
    step_rows = 32

    @pl.loop(0, tok_parts)
    def _(c):
        tok_load(c).wait()
        for part in range(toks // tok_parts // step_rows):
            rows = pl.ds(mult(c * (toks // tok_parts) + part * step_rows, step_rows), step_rows)
            value = tok[rows, :].astype(F32)
            mean = jnp.sum(value, axis=1, keepdims=True) * (1.0 / width)
            center = value - mean
            spread = jnp.sum(center * center, axis=1, keepdims=True) * (1.0 / width)
            inv = lax.rsqrt(spread + EPSILON)
            normed[rows, :] = (center * inv * gain[...] + shift[...]).astype(BF16)
            stat_m[rows, :] = jnp.broadcast_to(mean, (step_rows, 128))
            stat_i[rows, :] = jnp.broadcast_to(inv, (step_rows, 128))

    @pl.when(end_of_line)
    def _():
        pl.semaphore_wait(barrier, GROUP)

    @pl.when(middle)
    def _():
        pl.semaphore_wait(barrier, GROUP + 1)

    direct_n, direct_g, first_owner = side_direct()
    direct_g.start()
    turned_n[first_owner] = normed[:, pl.ds(mult(first_owner * BLK, BLK), BLK)].T
    direct_n.start()

    lens_load.wait()
    gout_load.wait()
    came(bias_in, in_sem.at[3])

    ends = []
    total_len = 0
    for j in range(lens.shape[1]):
        total_len = total_len + lens[0, j]
        ends.append(total_len)

    gsum[...] = jnp.zeros_like(gsum)

    @pl.loop(0, toks // step_rows)
    def _(r):
        first = r * step_rows
        rows = pl.ds(mult(first, step_rows), step_rows)
        place = first + lax.broadcasted_iota(jnp.int32, (step_rows, width), 0)
        value = jnp.where(place < total_len, gout[rows, :].astype(F32), 0.0)
        gout[rows, :] = value.astype(BF16)
        gsum[0:1, :] = gsum[0:1, :] + jnp.sum(value, axis=0, keepdims=True)

    for m in (0, 1):
        for owner in (flip(inner, CORE ^ N_MS[m]), flip(inner, N_MS[m])):
            turned_n[owner] = normed[:, pl.ds(mult(owner * BLK, BLK), BLK)].T
        for copy in side_core(m):
            copy.start()
        owner_g = mult(flip(inner, G_MS[m]) * BLK, BLK)
        side_g[0:toks, m * BLK : m * BLK + BLK] = gout[:, pl.ds(owner_g, BLK)]
        side_n[m * BLK : m * BLK + BLK, 0:toks] = turned_n[flip(inner, N_MS[m])]
    def bn_copy(s, k):
        src = bn.at[s, pl.ds(toks if k == 2 else 0, toks), :]
        slot_at = (1, 2, 3)[k]
        return remote(
            src,
            bn.at[s, pl.ds(slot_at * toks, toks), :],
            bn_ss,
            blk_rs.at[s, min(k, 1)],
            peer((XBIT, CORE, CORE)[k]),
        )

    def bg_copy(s, k):
        src = bg.at[s, :, pl.ds(toks if k == 2 else 0, toks)]
        slot_at = (1, 2, 3)[k]
        return remote(
            src,
            bg.at[s, :, pl.ds(slot_at * toks, toks)],
            bg_ss,
            blk_rs.at[s, min(k, 1)],
            peer((YBIT, CORE, CORE)[k]),
        )

    def piece(t, g, first_row):
        if t == 0:
            return pl.ds(first_row, half), pl.ds(mult(g * piece_cols, piece_cols), piece_cols)
        return pl.ds(mult(first_row + g * piece_rows, piece_rows), piece_rows), pl.ds(0, width)

    def z_far(t, g):
        rows, cols = piece(t, g, far_rows)
        to_rows, _ = piece(t, g, 0)
        return remote(
            zpart.at[t, rows, cols],
            zfar.at[t, to_rows, cols],
            zf_ss,
            zf_rs.at[t * Z_PARTS + g],
            beside,
        )

    def z_near(t, g):
        rows, cols = piece(t, g, near_rows)
        to_rows, _ = piece(t, g, 0)
        return remote(
            zpart.at[t, rows, cols],
            znear.at[t, to_rows, cols],
            zn_ss,
            zm_rs.at[t * Z_PARTS + g],
            beside,
        )

    def z_mid(t, g):
        rows, cols = piece(t, g, far_rows)
        to_rows, _ = piece(t, g, 0)
        return remote(
            zpart.at[t, rows, cols],
            zmid.at[t, to_rows, cols],
            zm_ss,
            zm_rs.at[t * Z_PARTS + g],
            across,
        )

    def z_done(t, g, to_end):
        rows, cols = piece(t, g, near_rows)
        place = zout.at[t, rows, cols]
        if to_end:
            return remote(place, place, zo_ss, ze_rs, beside)
        return remote(place, place, zo_ss, zo_rs.at[t * Z_PARTS + g], across)

    def z_pass(t, g):
        rows, cols = piece(t, g, far_rows)
        return remote(zout.at[t, rows, cols], zout.at[t, rows, cols], zw_ss, ze_rs, beside)

    def z_send(copies):
        @pl.when(end_of_line)
        def _():
            for copy in copies:
                copy.start()

    def z_first(t, g):
        z_far(t, g).wait_recv()
        rows, cols = piece(t, g, far_rows)
        there, _ = piece(t, g, 0)
        zpart[t, rows, cols] = (
            zpart[t, rows, cols].astype(F32) + zfar[t, there, cols].astype(F32)
        ).astype(BF16)
        z_mid(t, g).start()

    def z_second(t, g):
        came(znear.at[0, :, pl.ds(0, 2 * piece_cols)], zm_rs.at[t * Z_PARTS + g])
        rows, cols = piece(t, g, near_rows)
        there, _ = piece(t, g, 0)
        total = (
            zpart[t, rows, cols].astype(F32)
            + znear[t, there, cols].astype(F32)
            + zmid[t, there, cols].astype(F32)
        )
        base = tok[rows, cols].astype(F32)
        if t == 0:
            place = near_rows + lax.broadcasted_iota(jnp.int32, total.shape, 0)
            branch = jnp.where(place < total_len, total + obias[:, cols], 0.0)
            zout[t, rows, cols] = (base + branch).astype(BF16)
        else:
            @pl.when(g == 0)
            def _():
                cot_load.wait()

            inv = stat_i[rows, 0:1]
            standard = (base - stat_m[rows, 0:1]) * inv
            grad = total * gain[...]
            mean_g = jnp.sum(grad, axis=1, keepdims=True) * (1.0 / width)
            mean_x = jnp.sum(grad * standard, axis=1, keepdims=True) * (1.0 / width)
            back = inv * (grad - mean_g - standard * mean_x)
            zout[t, rows, cols] = (cot_rows[there, :].astype(F32) + back).astype(BF16)
        z_done(t, g, False).start()
        z_done(t, g, True).start()

    def z_third(t, g):
        z_done(t, g, False).wait_recv()
        z_pass(t, g).start()

    def z_move(step, number):
        for t in (0, 1):
            at = number - t * Z_PARTS
            if isinstance(number, int):
                if 0 <= at < Z_PARTS:
                    pl.when(middle)(functools.partial(step, t, at))
            else:
                pl.when(middle & (at >= 0) & (at < Z_PARTS))(functools.partial(step, t, at))

    def z_tick(number):
        for step, lag in zip((z_first, z_second, z_third), Z_LAG):
            z_move(step, number - lag)

    per_wide = WIDE // BLK
    n_wide = hidden // WIDE

    def hidden_block(w, with_grad):
        cols = pl.ds(mult(w * WIDE, WIDE), WIDE)
        came(wu.at[:, pl.ds(0, 2 * WIDE)], wide_sem.at[w])
        up = nn(normed[...], wu[:, cols]) + bup[:, cols]
        square = up * up
        tanh = jnp.tanh(GELU_A * up * (1.0 + GELU_B * square))
        row = lax.broadcasted_iota(jnp.int32, up.shape, 0)
        active = jnp.where(row < total_len, 0.5 * up * (1.0 + tanh), 0.0).astype(BF16)
        act[:, cols] = active
        slope = 0.5 * (1.0 + tanh) + 0.5 * up * (1.0 - tanh * tanh) * (
            GELU_A * (1.0 + 3.0 * GELU_B * square)
        )
        if with_grad:
            grad = (nt(gout[...], wd[cols, :]) * slope).astype(BF16)
            gup[:, cols] = grad
        else:
            gup[:, cols] = slope.astype(BF16)
        for part in range(per_wide):
            c = w * per_wide + part
            inside = slice(part * BLK, part * BLK + BLK)
            bg[c, :, 0:toks] = active[:, inside].T
            if with_grad:
                bn[c, 0:toks, :] = grad[:, inside]
        for part in range(per_wide):
            c = w * per_wide + part
            for k in (0, 1):
                bg_copy(c, k).start()
                if with_grad:
                    bn_copy(c, k).start()

    @pl.loop(0, n_wide // 2)
    def _(w):
        hidden_block(w, True)

    @pl.loop(n_wide // 2, n_wide)
    def _(w):
        hidden_block(w, False)

        @pl.when(w == n_wide // 2)
        def _():
            side_first()

    def hidden_grad(first, past, shift):
        @pl.loop(first, past)
        def _(w):
            @pl.when(w == first)
            def _():
                side_out(0)

            @pl.when(w == first + 1)
            def _():
                side_out(1)

            z_tick(w - first)
            cols = pl.ds(mult(w * WIDE, WIDE), WIDE)
            grad = (nt(gout[...], wd[cols, :]) * gup[:, cols].astype(F32)).astype(BF16)
            gup[:, cols] = grad
            for part in range(per_wide):
                c = shift + w * per_wide + part
                bn[c, 0:toks, :] = grad[:, part * BLK : part * BLK + BLK]
                for k in (0, 1):
                    bn_copy(c, k).start()

    seg_r, _ = segment_of(slot)
    seg_c, _ = segment_of(lax.broadcasted_iota(jnp.int32, (8, toks), 1))
    place_r = lax.broadcasted_iota(jnp.int32, (toks, toks), 0)
    place_c = lax.broadcasted_iota(jnp.int32, (toks, toks), 1)
    same = jnp.concatenate([seg_r] * (toks // 128), axis=1) == seg_c[0:1, :]
    mask = jnp.where(same & (place_c <= place_r), 0.0, -1e30)
    for h in (0, 1):
        amask[h * toks : h * toks + toks, :] = mask

    which = lax.broadcasted_iota(jnp.int32, (8, 128), 0)
    starts = jnp.zeros((8, 128), jnp.int32)
    for j, end in enumerate(ends):
        starts = jnp.where(which == j, end - lens[0, j], starts)
    turn = starts.astype(F32) * freq[0:8, :]
    turn_c, turn_s = jnp.cos(turn), jnp.sin(turn)
    back_c, back_s = jnp.ones((toks, 128), F32), jnp.zeros((toks, 128), F32)
    for j in range(len(ends)):
        inside = seg_r == j + 1
        back_c = jnp.where(inside, turn_c[j : j + 1, :], back_c)
        back_s = jnp.where(inside, turn_s[j : j + 1, :], back_s)
    slot_c, slot_s = rot_c[...], rot_a[...]
    cosine = slot_c * back_c + slot_s * back_s
    sine = slot_s * back_c - slot_c * back_s
    rot_c[...] = jnp.where(in_head < ROT, cosine, 1.0)
    rot_a[...] = jnp.where(in_head < ROT // 2, -sine, 0.0)
    rot_b[...] = jnp.where((in_head >= ROT // 2) & (in_head < ROT), sine, 0.0)

    def rotate(value, sign):
        left = pltpu.roll(value, 128 - ROT // 2, 1)
        right = pltpu.roll(value, ROT // 2, 1)
        return value * rot_c[...] + sign * (left * rot_a[...] + right * rot_b[...])

    attn_load.wait()

    @pl.loop(0, heads_w // BLK)
    def _(n):
        cols = pl.ds(mult(n * BLK, BLK), BLK)
        query = nn(normed[...], wq[:, cols]) + bq[:, cols]
        keys = nn(normed[...], wk[:, cols]) + bk[:, cols]
        for part in range(BLK // 128):
            at = pl.ds(mult(n * BLK + part * 128, 128), 128)
            lanes = slice(part * 128, part * 128 + 128)
            q_s[:, at] = (rotate(query[:, lanes], 1.0) * 0.125).astype(BF16)
            k_s[:, at] = rotate(keys[:, lanes], 1.0).astype(BF16)
        v_s[:, cols] = (nn(normed[...], wv[:, cols]) + bv[:, cols]).astype(BF16)
        ga_s[:, cols] = nt(gout[...], wo[cols, :]).astype(BF16)

    low_lane = lax.broadcasted_iota(jnp.int32, (1, 128), 1) < HD
    first_head = jnp.where(low_lane, 1.0, 0.0).astype(BF16)
    second_head = jnp.where(low_lane, 0.0, 1.0).astype(BF16)
    low_full = lax.broadcasted_iota(jnp.int32, (toks, 128), 1) < HD

    def apart(value):
        return jnp.concatenate([value * first_head, value * second_head], axis=0)

    def together(value):
        return jnp.where(low_full, value[:toks], value[toks:])

    @pl.loop(0, n_att)
    def _(n):
        base_n = n_hid // 2 + 3 * n

        @pl.when(n == n_att - 1)
        def _():
            side_relay(0)

        for part in range(BLK // 128):
            at = pl.ds(mult(n * BLK + part * 128, 128), 128)
            lanes = slice(part * 128, part * 128 + 128)
            kp, vp = k_s[:, at], v_s[:, at]
            q2, g2 = apart(q_s[:, at]), apart(ga_s[:, at])
            scores = nt(q2, kp) + amask[...]
            top = jnp.max(scores, axis=1, keepdims=True)
            expo = jnp.exp(scores - top)
            probs = expo * (1.0 / jnp.sum(expo, axis=1, keepdims=True))
            probs_low = probs.astype(BF16)
            prob_grad = nt(g2, vp)
            delta = jnp.sum(probs * prob_grad, axis=1, keepdims=True)
            score_grad = (probs * (prob_grad - delta)).astype(BF16)
            out = jnp.where(slot < total_len, together(nn(probs_low, vp)), 0.0).astype(BF16)
            att[:, at] = out
            bg[n_hid + n, lanes, 0:toks] = out.T
            dq = rotate(together(nn(score_grad, kp)) * 0.125, -1.0).astype(BF16)
            dk = rotate(tn(score_grad, q2), -1.0).astype(BF16)
            dv = tn(probs_low, g2).astype(BF16)
            for kind, value in enumerate((dq, dk, dv)):
                bn[base_n + kind, 0:toks, lanes] = value
                gqkv[:, pl.ds(mult(kind * heads_w + n * BLK + part * 128, 128), 128)] = value
        for k in (0, 1):
            bg_copy(n_hid + n, k).start()
            for kind in range(3):
                bn_copy(base_n + kind, k).start()

    side_relay(1)

    def branches(cols):
        zpart[0, :, cols] = (nn(act[...], wd[:, cols]) + nn(att[...], wo[:, cols])).astype(BF16)

    for g in range(Z_LEAD):
        branches(pl.ds(g * piece_cols, piece_cols))
        z_send([z_far(0, g)])

    @pl.loop(1, width // WIDE)
    def _(n):
        branches(pl.ds(mult(n * WIDE, WIDE), WIDE))
        for part in range(Z_LEAD):
            g = n * Z_LEAD + part
            z_send([z_far(0, g), z_near(0, g - Z_LEAD)])

    hidden_grad(n_wide // 2, n_wide, 3 * n_att)

    vzl[...] = jnp.zeros_like(vzl)

    @pl.loop(0, width // WIDE)
    def _(n):
        cols = pl.ds(mult(n * WIDE, WIDE), WIDE)
        grad = nt(gup[...], wu[cols, :])
        for kind, weight in enumerate((wq, wk, wv)):
            grad = grad + nt(gqkv[:, kind * heads_w : (kind + 1) * heads_w], weight[cols, :])
        zpart[1, :, cols] = grad.astype(BF16)

        @pl.when(n == 1)
        def _():
            z_tick(2)

        @pl.when(n == 3)
        def _():
            z_tick(3)

        for part in range(WIDE // 128):
            lanes = slice(part * 128, part * 128 + 128)
            at = pl.ds(mult(n * WIDE + part * 128, 128), 128)
            owner = n * per_wide + part * 128 // BLK
            half_row = part * 128 % BLK // 128
            piece_of = grad[:, lanes]
            standard = (tok[:, at].astype(F32) - stat_m[...]) * stat_i[...]
            vzl[owner, half_row : half_row + 1, :] = jnp.sum(piece_of * standard, axis=0, keepdims=True)
            vzl[owner, 2 + half_row : 3 + half_row, :] = jnp.sum(piece_of, axis=0, keepdims=True)

    def vd_copy(mask):
        return remote(
            vzl.at[flip(inner, mask)], vdr.at[mask - 1], vd_ss, vd_rs, peer(mask)
        )

    for owner in range(n_own):
        for half_row in (0, 1):
            first = owner * BLK + half_row * 128
            vzl[owner, 4 + half_row : 5 + half_row, :] = gsum[0:1, first : first + 128]
    for mask in range(1, GROUP):
        vd_copy(mask).start()
    for g in range(Z_PARTS):
        late = Z_PARTS - Z_LEAD + g
        z_send([z_far(1, g), z_near(late // Z_PARTS, late % Z_PARTS)])
    for g in range(Z_PARTS - Z_LEAD, Z_PARTS):
        z_send([z_near(1, g)])

    bs_copy = remote(bsum_s, bsum_r, bs_ss, bs_rs, peer(YBIT))

    def rn_copy(s):
        return remote(rsn_s.at[s], rsn_r.at[s], rn_ss, rn_rs, peer(YBIT))

    def rg_copy(s):
        return remote(rsg_s.at[s], rsg_r.at[s], rg_ss, rg_rs, peer(XBIT))

    came(bn.at[0], side_rs.at[1])

    @pl.when(end_of_line)
    def _():
        for number in (1, 2, 3):
            for kind in (0, 1):
                side_came(kind, number)

    bsum[...] = jnp.zeros_like(bsum)

    def vz_copy(src, i, where):
        return remote(src, vzr.at[i], vz_ss, vz_rs.at[i], where)

    def vec_spread():
        came(vdr, vd_rs)
        vz[...] = vzl[inner] + jnp.sum(vdr[...], axis=0)

        @pl.when(end_of_line)
        def _():
            vz_copy(vz, 0, beside).start()

    def vec_pair():
        @pl.when(middle)
        def _():
            came(vz, vz_rs.at[0])
            vz_pair[...] = vz[...] + vzr[0]
            vz_copy(vz_pair, 1, across).start()

    def vec_back():
        @pl.when(middle)
        def _():
            came(vz, vz_rs.at[1])
            norm_sums[...] = vz_pair[...] + vzr[1]
            vz_copy(norm_sums, 0, beside).start()

    side_n[2 * BLK :, :] = jnp.ones((16, 4 * toks), BF16)

    @pl.loop(0, n_chunks + 1)
    def _(s):
        @pl.when(s < g_chunks)
        def _():
            came(bn.at[s, pl.ds(0, 2 * toks), :], blk_rs.at[s, 0])
            bn_copy(s, 2).start()
            bg_copy(s, 2).start()

        @pl.when((s >= g_chunks) & (s < n_chunks))
        def _():
            came(bn.at[s, pl.ds(0, toks), :], blk_rs.at[s, 0])
            bn_copy(s, 2).start()

        @pl.when((s > 0) & (s <= g_chunks))
        def _():
            came(bn.at[s - 1], blk_rs.at[s - 1, 1])

        @pl.when(s > g_chunks)
        def _():
            came(bn.at[s - 1, pl.ds(0, 2 * toks), :], blk_rs.at[s - 1, 1])

        @pl.when(s > 0)
        def _():
            p = s - 1
            both = nn(side_n[...], bn[p])
            rsn_s[p] = both[BLK : 2 * BLK, :].astype(BF16)
            rn_copy(p).start()
            bsum[pl.ds(p, 1), :] = both[2 * BLK : 2 * BLK + 1, :]
            bn[p, 2 * toks : 3 * toks, :] = both[:BLK, :].astype(BF16)

        @pl.when((s > 0) & (s <= g_chunks))
        def _():
            p = s - 1
            both = nn(bg[p], side_g[...])
            rsg_s[p] = both[:, BLK:].astype(BF16)
            rg_copy(p).start()
            bg[p, :, 2 * toks : 3 * toks] = both[:, :BLK].astype(BF16)

        tick = -1
        for turn, number in Z_TICKS:
            tick = jnp.where(s == turn, number, tick)
        z_tick(tick)

    bsum_s[...] = bsum[...].astype(BF16)
    bs_copy.start()
    vec_spread()
    @pl.loop(Z_TICKS[-1][1] + 1, 2 * Z_PARTS + Z_LAG[-1])
    def _(number):
        @pl.when(number == 2 * Z_PARTS)
        def _():
            vec_pair()

        z_tick(number)

    vec_back()

    bs_copy.wait_recv()

    @pl.when(end_of_line)
    def _():
        came(vz, vz_rs.at[0])
        norm_sums[...] = vzr[0]

    for half_row in (0, 1):
        lanes = slice(half_row * 128, half_row * 128 + 128)
        vec_o[0:1, lanes] = norm_sums[half_row : half_row + 1, :]
        vec_o[1:2, lanes] = norm_sums[2 + half_row : 3 + half_row, :]
        vec_o[2:3, lanes] = vz[4 + half_row : 5 + half_row, :]
    vec_o[8:, :] = bsum[...] + bsum_r[...].astype(F32)

    came(rsn_r, rn_rs)
    came(rsg_r, rg_rs)

    came(bn.at[:, pl.ds(0, 3 * toks), :], bn_ss)
    came(bg.at[:, :, pl.ds(0, 3 * toks)], bg_ss)
    came(rsn_s, rn_ss)
    came(rsg_s, rg_ss)
    came(vdr, vd_ss)
    bs_copy.wait_send()

    @pl.when(end_of_line)
    def _():
        came(bn.at[pl.ds(0, 2)], side_ss)
        came(vz, vz_ss)
        came(zfar, zf_ss)
        came(znear, zn_ss)
        came(zout, ze_rs)
        cot_load.wait()

    @pl.when(middle)
    def _():
        came(bn.at[pl.ds(0, 4)], side_ss)
        came(vzr, vz_ss)
        came(zmid, zm_ss)
        came(zout, zo_ss)
        came(zmid, zw_ss)


def write_kernel(n_hid, n_att, bn, bg, rsn, rsg, zout, vec, mixed_h, gtok_h, gain_o, shift_o, gq_h, bq_o, gk_h, bk_o, gv_h, bv_o, go_h, gu_h, bu_o, gd_h, ob_o, stage, small, sem, zsem, small_sem):
    n_chunks, n_g = bn.shape[0], bg.shape[0]
    toks = zout.shape[1]
    z_outs = [
        pltpu.make_async_copy(zout.at[t], out, zsem) for t, out in enumerate((mixed_h, gtok_h))
    ]
    for out in z_outs:
        out.start()
    places, biases = [], []
    for s in range(n_chunks):
        inside = s - n_hid // 2
        if 0 <= inside < 3 * n_att:
            (out, bias), at = ((gq_h, bq_o), (gk_h, bk_o), (gv_h, bv_o))[inside % 3], inside // 3
        else:
            (out, bias), at = (gu_h, bu_o), s if inside < 0 else s - 3 * n_att
        biases.append((bias, at))
        places.append((True, s, out.at[:, pl.ds(at * BLK, BLK)]))
    for s in range(n_g):
        out, at = (gd_h, s) if s < n_hid else (go_h, s - n_hid)
        places.append((False, s, out.at[pl.ds(at * BLK, BLK), :]))
    smalls = [(gain_o, (0,)), (shift_o, (1,)), (ob_o, (2,))]
    for bias in (bq_o, bk_o, bv_o, bu_o):
        smalls.append((bias, tuple(8 + s for at, s in sorted((at, s) for s, (b, at) in enumerate(biases) if b is bias))))
    at = 0
    for out, rows in smalls:
        for part, row in enumerate(rows):
            small[at + part * BLK : at + part * BLK + BLK] = vec[row]
        pltpu.make_async_copy(small.at[pl.ds(at, len(rows) * BLK)], out, small_sem).start()
        at += len(rows) * BLK
    copies = []
    for number, (first, s, place) in enumerate(places):
        slot = number
        if first:
            value = bn[s, 2 * toks : 3 * toks, :].astype(F32) + rsn[s].astype(F32)
        else:
            value = bg[s, :, 2 * toks : 3 * toks].astype(F32) + rsg[s].astype(F32)
        stage[slot] = value
        copies.append(pltpu.make_async_copy(stage.at[slot], place, sem))
        copies[number].start()
    pltpu.make_async_copy(stage, stage, sem).wait()
    pltpu.make_async_copy(zout, zout, zsem).wait()
    pltpu.make_async_copy(small, small, small_sem).wait()


def layer(tokens, lengths, ln_gain, ln_bias, w_query, b_query, w_key, b_key, w_value, b_value, w_out, w_up, b_up, w_down, out_bias, cotangent):
    toks, width = tokens.shape
    heads_w = w_query.shape[1]
    hidden = w_up.shape[1]
    n_chunks = (3 * heads_w + hidden) // BLK
    g_chunks = (heads_w + hidden) // BLK
    n_own = width // BLK
    n_vec = -(-n_chunks // 8) * 8
    half = toks // 2
    dma = pltpu.SemaphoreType.DMA
    vmem = pltpu.VMEM
    scratch = [
        pltpu.SMEM(lengths.shape, jnp.int32),
        vmem((1, 2 * width), F32),
        vmem((1, hidden + 3 * heads_w + width), F32),
        vmem((toks, width), BF16),
        vmem((toks, width), BF16),
        vmem((toks, width), BF16),
        vmem((n_own, BLK, toks), BF16),
        vmem(w_query.shape, BF16),
        vmem(w_key.shape, BF16),
        vmem(w_value.shape, BF16),
        vmem(w_out.shape, BF16),
        vmem(w_up.shape, BF16),
        vmem(w_down.shape, BF16),
        vmem((2 * BLK + 16, 4 * toks), BF16),
        vmem((4 * toks, 2 * BLK), BF16),
        vmem((n_chunks, BLK, BLK), BF16),
        vmem((g_chunks, BLK, BLK), BF16),
        vmem((toks, hidden), BF16),
        vmem((toks, hidden), BF16),
        vmem((toks, 3 * heads_w), BF16),
        vmem((toks, heads_w), BF16),
        vmem((toks, heads_w), BF16),
        vmem((toks, heads_w), BF16),
        vmem((toks, heads_w), BF16),
        vmem((toks, heads_w), BF16),
        vmem((2 * toks, toks), F32),
        vmem((toks, 128), F32),
        vmem((toks, 128), F32),
        vmem((toks, 128), F32),
        vmem((toks, 128), F32),
        vmem((toks, 128), F32),
        vmem((2, toks, width), BF16),
        vmem((2, half, width), BF16),
        vmem((2, half, width), BF16),
        vmem((2, half, width), BF16),
        vmem((n_own, 8, 128), F32),
        vmem((8, 128), F32),
        vmem((8, 128), F32),
        vmem((8, 128), F32),
        vmem((2, 8, 128), F32),
        vmem((GROUP - 1, 8, 128), F32),
        vmem((8, width), F32),
        vmem((n_vec, BLK), F32),
        vmem((n_vec, BLK), BF16),
        vmem((n_vec, BLK), BF16),
        vmem((half, width), BF16),
        dma((6,)),
        dma((4,)),
        dma((hidden // WIDE,)),
        dma,
        dma((8,)),
        dma,
        dma,
        dma((n_chunks, 2)),
        dma,
        dma,
        dma,
        dma,
        dma,
        dma((2 * Z_PARTS,)),
        dma,
        dma,
        dma((2 * Z_PARTS,)),
        dma,
        dma((2 * Z_PARTS,)),
        dma,
        dma,
        dma,
        dma((2,)),
        dma,
        dma,
        dma,
        dma,
    ]
    anyspace = pl.BlockSpec(memory_space=pl.ANY)
    local = pl.BlockSpec(memory_space=pltpu.VMEM)
    row = lambda value: value.reshape(1, -1)
    kept = pl.pallas_call(
        functools.partial(layer_kernel, n_chunks, g_chunks),
        out_shape=(
            vmem((n_chunks, 4 * toks, BLK), BF16),
            vmem((g_chunks, BLK, 4 * toks), BF16),
            vmem((n_chunks, BLK, BLK), BF16),
            vmem((g_chunks, BLK, BLK), BF16),
            vmem((2, toks, width), BF16),
            vmem((8 + n_vec, BLK), F32),
        ),
        in_specs=[anyspace] * 16,
        out_specs=(local,) * 6,
        scratch_shapes=scratch,
        compiler_params=pltpu.CompilerParams(
            collective_id=0, has_side_effects=True, vmem_limit_bytes=MAIN_VMEM
        ),
    )(
        lengths,
        tokens,
        cotangent,
        row(ln_gain),
        row(ln_bias),
        row(b_query),
        row(b_key),
        row(b_value),
        row(b_up),
        row(out_bias),
        w_query,
        w_key,
        w_value,
        w_out,
        w_up,
        w_down,
    )
    f32 = lambda *shape: jax.ShapeDtypeStruct(shape, F32)
    low = jax.ShapeDtypeStruct((toks, width), BF16)
    outs = (
        low,
        low,
        f32(BLK),
        f32(BLK),
        f32(BLK, heads_w),
        f32(heads_w),
        f32(BLK, heads_w),
        f32(heads_w),
        f32(BLK, heads_w),
        f32(heads_w),
        f32(heads_w, BLK),
        f32(BLK, hidden),
        f32(hidden),
        f32(hidden, BLK),
        f32(BLK),
    )
    slots = n_chunks + g_chunks
    return pl.pallas_call(
        functools.partial(write_kernel, hidden // BLK, heads_w // BLK),
        out_shape=outs,
        in_specs=[local] * 6,
        out_specs=(anyspace,) * len(outs),
        scratch_shapes=[
            vmem((slots, BLK, BLK), F32),
            vmem((3 * BLK + 3 * heads_w + hidden,), F32),
            dma,
            dma,
            dma,
        ],
        compiler_params=pltpu.CompilerParams(vmem_limit_bytes=12 * 2**20),
    )(*kept)


def make_body(n_dp, n_mp):
    outer = n_dp // GROUP

    def order(value, axis):
        if outer == 1:
            return value
        shape = value.shape
        split = shape[:axis] + (outer, GROUP, shape[axis] // n_dp) + shape[axis + 1 :]
        return jnp.swapaxes(value.reshape(split), axis, axis + 1).reshape(shape)

    def restore(value, axis):
        if outer == 1:
            return value
        shape = value.shape
        split = shape[:axis] + (GROUP, outer, shape[axis] // n_dp) + shape[axis + 1 :]
        return jnp.swapaxes(value.reshape(split), axis, axis + 1).reshape(shape)

    groups = [[o * GROUP + i for o in range(outer)] for i in range(GROUP)]

    def scatter(value, axis):
        if outer == 1:
            return value
        return lax.psum_scatter(
            value, "dp", scatter_dimension=axis, axis_index_groups=groups, tiled=True
        )

    def total(value):
        if outer == 1:
            return value
        return lax.psum(value, "dp", axis_index_groups=groups)

    def body(tokens, lengths, ln_gain, ln_bias, w_query, b_query, w_key, b_key, w_value, b_value, w_out, w_up, b_up, w_down, out_bias, cotangent):
        found = layer(
            order(tokens, 1),
            lengths,
            order(ln_gain, 0),
            order(ln_bias, 0),
            order(w_query, 0),
            b_query,
            order(w_key, 0),
            b_key,
            order(w_value, 0),
            b_value,
            order(w_out, 1),
            order(w_up, 0),
            b_up,
            order(w_down, 1),
            order(out_bias, 0),
            order(cotangent, 1),
        )
        (mixed, grad_tokens, gain, shift, g_q, b_q, g_k, b_k, g_v, b_v, g_out, g_up, b_u, g_down, b_out) = found
        return (
            restore(mixed, 1),
            restore(grad_tokens, 1),
            scatter(gain, 0),
            scatter(shift, 0),
            scatter(g_q, 0),
            total(b_q),
            scatter(g_k, 0),
            total(b_k),
            scatter(g_v, 0),
            total(b_v),
            scatter(g_out, 1),
            scatter(g_up, 0),
            total(b_u),
            scatter(g_down, 1),
            scatter(b_out, 0),
        )

    return body


def solution(mesh):
    in_specs = (
        P("dp", None),
        P("dp", None),
        P(),
        P(),
        P(None, "mp"),
        P("mp"),
        P(None, "mp"),
        P("mp"),
        P(None, "mp"),
        P("mp"),
        P("mp", None),
        P(None, "mp"),
        P("mp"),
        P("mp", None),
        P(),
        P("dp", None),
    )
    out_specs = (
        P("dp", None),
        P("dp", None),
        P("dp"),
        P("dp"),
        P("dp", "mp"),
        P("mp"),
        P("dp", "mp"),
        P("mp"),
        P("dp", "mp"),
        P("mp"),
        P("mp", "dp"),
        P("dp", "mp"),
        P("mp"),
        P("mp", "dp"),
        P("dp"),
    )
    body = make_body(mesh.shape["dp"], mesh.shape["mp"])
    return jax.shard_map(body, mesh=mesh, in_specs=in_specs, out_specs=out_specs, check_vma=False)
```

```python
import functools
import math

import jax
import jax.numpy as jnp
from jax import lax
from jax.experimental import pallas as pl
from jax.experimental.pallas import tpu as pltpu
from jax.sharding import PartitionSpec as P

HD = 64
ROT = 32
EPSILON = 1e-05
GROUP = 8
CORE, XBIT, YBIT = 1, 2, 4
BLK = 256
WIDE = 512
Z_PARTS = 8
Z_LEAD = 2
Z_LAG = (0, 2, 4)
Z_TICKS = ((1, 4), (3, 5), (5, 6), (7, 7), (8, 8), (9, 9), (10, 10), (11, 11), (12, 12), (13, 13))
F32 = jnp.float32
BF16 = jnp.bfloat16
MESH = pl.DeviceIdType.MESH
MAIN_VMEM = 93 * 2**19
GELU_A = math.sqrt(2.0 / math.pi)
GELU_B = 0.044715


def nn(left, right):
    return lax.dot_general(left, right, (((1,), (0,)), ((), ())), preferred_element_type=F32)


def nt(left, right):
    return lax.dot_general(left, right, (((1,), (1,)), ((), ())), preferred_element_type=F32)


def tn(left, right):
    return lax.dot_general(left, right, (((0,), (0,)), ((), ())), preferred_element_type=F32)


def flip(index, mask):
    for bit in (1, 2, 4):
        if mask & bit:
            index = index + bit * (1 - 2 * ((index // bit) % 2))
    return index


def mult(value, by):
    return pl.multiple_of(value, by)


N_JS = (0, XBIT, CORE, XBIT | CORE)
N_MS = (0, YBIT)
G_JS = (0, YBIT, CORE, YBIT | CORE)
G_MS = (0, XBIT)


def layer_kernel(
    n_chunks,
    g_chunks,
    lens_h,
    tok_h,
    cot_h,
    gain_h,
    shift_h,
    bq_h,
    bk_h,
    bv_h,
    bup_h,
    obias_h,
    wq_h,
    wk_h,
    wv_h,
    wo_h,
    wu_h,
    wd_h,
    bn,
    bg,
    rsn_r,
    rsg_r,
    zout,
    vec_o,
    lens,
    norm_in,
    bias_in,
    tok,
    gout,
    normed,
    turned_n,
    wq,
    wk,
    wv,
    wo,
    wu,
    wd,
    side_n,
    side_g,
    rsn_s,
    rsg_s,
    act,
    gup,
    gqkv,
    att,
    q_s,
    k_s,
    v_s,
    ga_s,
    amask,
    rot_c,
    rot_a,
    rot_b,
    stat_m,
    stat_i,
    zpart,
    zfar,
    znear,
    zmid,
    vzl,
    vz,
    vz_pair,
    norm_sums,
    vzr,
    vdr,
    gsum,
    bsum,
    bsum_s,
    bsum_r,
    cot_rows,
    in_sem,
    tok_sem,
    wide_sem,
    side_ss,
    side_rs,
    bn_ss,
    bg_ss,
    blk_rs,
    rn_ss,
    rn_rs,
    rg_ss,
    rg_rs,
    zf_ss,
    zf_rs,
    zn_ss,
    zm_ss,
    zm_rs,
    zo_ss,
    zo_rs,
    zw_ss,
    ze_rs,
    vz_ss,
    vz_rs,
    vd_ss,
    vd_rs,
    bs_ss,
    bs_rs,
):
    toks, width = tok.shape
    hidden = wu.shape[1]
    heads_w = wq.shape[1]
    n_att = heads_w // BLK
    n_hid = hidden // BLK
    n_own = width // BLK
    dp = lax.axis_index("dp")
    zed = lax.axis_index("mp")
    inner = lax.rem(dp, GROUP)
    outer = dp - inner
    half = toks // 2
    piece_cols = width // Z_PARTS
    piece_rows = half // Z_PARTS

    def peer(mask):
        return (outer + flip(inner, mask), zed)

    def came(ref, sem):
        pltpu.make_async_copy(ref, ref, sem).wait()

    middle = (zed == 1) | (zed == 2)
    end_of_line = (zed == 0) | (zed == 3)
    side_of_line = zed // 2
    beside = (dp, zed + 1 - 2 * lax.rem(zed, 2))
    across = (dp, 3 - zed)
    near_rows = mult(side_of_line * half, half)
    far_rows = mult((1 - side_of_line) * half, half)

    def remote(src, dst, ssem, rsem, where):
        return pltpu.make_async_remote_copy(
            src_ref=src,
            dst_ref=dst,
            send_sem=ssem,
            recv_sem=rsem,
            device_id=where,
            device_id_type=MESH,
        )

    def load(src, dst, number):
        copy = pltpu.make_async_copy(src, dst, in_sem.at[number])
        copy.start()
        return copy

    tok_parts = 4

    def tok_load(c):
        rows = pl.ds(mult(c * (toks // tok_parts), toks // tok_parts), toks // tok_parts)
        return pltpu.make_async_copy(tok_h.at[rows, :], tok.at[rows, :], tok_sem.at[c])

    for c in range(tok_parts):
        tok_load(c).start()
    for at, src in enumerate((gain_h, shift_h)):
        load(src, norm_in.at[:, pl.ds(at * width, width)], 0)
    lens_load = load(lens_h, lens, 1)

    barrier = pltpu.get_barrier_semaphore()
    for mask in range(1, GROUP):
        pl.semaphore_signal(barrier, inc=1, device_id=peer(mask), device_id_type=MESH)
    pl.semaphore_signal(barrier, inc=1, device_id=beside, device_id_type=MESH)

    @pl.when(middle)
    def _():
        pl.semaphore_signal(barrier, inc=1, device_id=across, device_id_type=MESH)

    gout_load = load(cot_h, gout, 2)
    at = 0
    biases = []
    for src in (bup_h, bq_h, bk_h, bv_h, obias_h):
        biases.append(bias_in.at[:, pl.ds(at, src.shape[1])])
        load(src, biases[-1], 3)
        at += src.shape[1]
    bup, bq, bk, bv, obias = biases
    gain, shift = norm_in.at[:, pl.ds(0, width)], norm_in.at[:, pl.ds(width, width)]

    def wide_loads(w):
        part = pl.ds(mult(w * WIDE, WIDE), WIDE)
        return (
            pltpu.make_async_copy(wu_h.at[:, part], wu.at[:, part], wide_sem.at[w]),
            pltpu.make_async_copy(wd_h.at[part, :], wd.at[part, :], wide_sem.at[w]),
        )

    @pl.loop(0, hidden // WIDE)
    def _(w):
        for copy in wide_loads(w):
            copy.start()

    for src, dst in ((wq_h, wq), (wk_h, wk), (wv_h, wv), (wo_h, wo)):
        load(src, dst, 4)
    attn_load = pltpu.make_async_copy(wu_h, wu, in_sem.at[4])
    cot_load = load(cot_h.at[pl.ds(near_rows, half), :], cot_rows, 5)

    def segment_of(place):
        number = jnp.zeros_like(place)
        start_of = jnp.zeros_like(place)
        for j, end in enumerate(ends):
            start = end - lens[0, j]
            inside = ((place >= start) & (place < end)).astype(jnp.int32)
            number = number + inside * (j + 1)
            start_of = start_of + inside * start
        return number, start_of

    def cross_core(index, times):
        return index + times * (1 - 2 * lax.rem(index, 2))

    def flip_by(index, bit, times):
        return index + times * (bit * (1 - 2 * ((index // bit) % 2)))

    own_part = lax.rem(zed, 2)
    own_slot = 1 + 2 * side_of_line
    other_slot = 3 - 2 * side_of_line

    def side_places(slot_at, m):
        at = pl.ds(mult(slot_at * toks, toks), toks)
        rows = pl.ds(mult(m * BLK, BLK), BLK)
        return side_n.at[rows, at], side_g.at[at, rows]

    def side_direct():
        at_n = flip(cross_core(inner, side_of_line), XBIT)
        at_g = flip(cross_core(inner, side_of_line), YBIT)
        owner_n = flip_by(at_n, YBIT, own_part)
        owner_g = flip_by(at_g, XBIT, own_part)
        place_n, place_g = side_places(own_slot, own_part)
        source_g = cot_h.at[:, pl.ds(mult(owner_g * BLK, BLK), BLK)]
        return (
            remote(turned_n.at[owner_n], place_n, side_ss, side_rs.at[0], (outer + at_n, zed)),
            remote(source_g, place_g, side_ss, side_rs.at[0], (outer + at_g, zed)),
            owner_n,
        )

    def side_core(m):
        place_n, place_g = side_places(2, m)
        owner_n = flip(inner, CORE ^ N_MS[m])
        owner_g = flip(inner, CORE ^ G_MS[m])
        source_g = cot_h.at[:, pl.ds(mult(owner_g * BLK, BLK), BLK)]
        return (
            remote(turned_n.at[owner_n], place_n, side_ss, side_rs.at[1], peer(CORE)),
            remote(source_g, place_g, side_ss, side_rs.at[1], peer(CORE)),
        )

    def side_send(kind, slot_at, m, number, where):
        place = side_places(slot_at, m)[kind]
        remote(place, place, side_ss, side_rs.at[2 * number + kind], where).start()

    def side_came(kind, number):
        came(bn.at[0, pl.ds(0, toks), :], side_rs.at[2 * number + kind])

    def side_first():
        came(bn.at[0, pl.ds(0, 2 * toks), :], side_rs.at[0])
        for kind in (0, 1):
            side_send(kind, own_slot, own_part, 1, beside)

            @pl.when(middle)
            def _():
                side_send(kind, own_slot, own_part, 2, across)

    def side_relay(kind):
        @pl.when(middle)
        def _():
            side_came(kind, 1)
            side_send(kind, own_slot, 1 - own_part, 3, across)
            side_came(kind, 2)
            side_send(kind, other_slot, 1 - own_part, 2, beside)

    def side_out(kind):
        @pl.when(middle)
        def _():
            side_came(kind, 3)
            side_send(kind, other_slot, own_part, 3, beside)

    lane = lax.broadcasted_iota(jnp.int32, (toks, 128), 1)
    slot = lax.broadcasted_iota(jnp.int32, (toks, 128), 0)
    in_head = lane % HD
    order = (in_head % (ROT // 2)).astype(F32)
    freq = jnp.exp(order * (-2.0 / ROT * math.log(10000.0)))
    angle = slot.astype(F32) * freq
    rot_c[...] = jnp.cos(angle)
    rot_a[...] = jnp.sin(angle)

    came(norm_in, in_sem.at[0])
    step_rows = 32

    @pl.loop(0, tok_parts)
    def _(c):
        tok_load(c).wait()
        for part in range(toks // tok_parts // step_rows):
            rows = pl.ds(mult(c * (toks // tok_parts) + part * step_rows, step_rows), step_rows)
            value = tok[rows, :].astype(F32)
            mean = jnp.sum(value, axis=1, keepdims=True) * (1.0 / width)
            center = value - mean
            spread = jnp.sum(center * center, axis=1, keepdims=True) * (1.0 / width)
            inv = lax.rsqrt(spread + EPSILON)
            normed[rows, :] = (center * inv * gain[...] + shift[...]).astype(BF16)
            stat_m[rows, :] = jnp.broadcast_to(mean, (step_rows, 128))
            stat_i[rows, :] = jnp.broadcast_to(inv, (step_rows, 128))

    @pl.when(end_of_line)
    def _():
        pl.semaphore_wait(barrier, GROUP)

    @pl.when(middle)
    def _():
        pl.semaphore_wait(barrier, GROUP + 1)

    direct_n, direct_g, first_owner = side_direct()
    direct_g.start()
    turned_n[first_owner] = normed[:, pl.ds(mult(first_owner * BLK, BLK), BLK)].T
    direct_n.start()

    lens_load.wait()
    gout_load.wait()
    came(bias_in, in_sem.at[3])

    ends = []
    total_len = 0
    for j in range(lens.shape[1]):
        total_len = total_len + lens[0, j]
        ends.append(total_len)

    gsum[...] = jnp.zeros_like(gsum)

    @pl.loop(0, toks // step_rows)
    def _(r):
        first = r * step_rows
        rows = pl.ds(mult(first, step_rows), step_rows)
        place = first + lax.broadcasted_iota(jnp.int32, (step_rows, width), 0)
        value = jnp.where(place < total_len, gout[rows, :].astype(F32), 0.0)
        gout[rows, :] = value.astype(BF16)
        gsum[0:1, :] = gsum[0:1, :] + jnp.sum(value, axis=0, keepdims=True)

    for m in (0, 1):
        for owner in (flip(inner, CORE ^ N_MS[m]), flip(inner, N_MS[m])):
            turned_n[owner] = normed[:, pl.ds(mult(owner * BLK, BLK), BLK)].T
        for copy in side_core(m):
            copy.start()
        owner_g = mult(flip(inner, G_MS[m]) * BLK, BLK)
        side_g[0:toks, m * BLK : m * BLK + BLK] = gout[:, pl.ds(owner_g, BLK)]
        side_n[m * BLK : m * BLK + BLK, 0:toks] = turned_n[flip(inner, N_MS[m])]
    def bn_copy(s, k):
        src = bn.at[s, pl.ds(toks if k == 2 else 0, toks), :]
        slot_at = (1, 2, 3)[k]
        return remote(
            src,
            bn.at[s, pl.ds(slot_at * toks, toks), :],
            bn_ss,
            blk_rs.at[s, min(k, 1)],
            peer((XBIT, CORE, CORE)[k]),
        )

    def bg_copy(s, k):
        src = bg.at[s, :, pl.ds(toks if k == 2 else 0, toks)]
        slot_at = (1, 2, 3)[k]
        return remote(
            src,
            bg.at[s, :, pl.ds(slot_at * toks, toks)],
            bg_ss,
            blk_rs.at[s, min(k, 1)],
            peer((YBIT, CORE, CORE)[k]),
        )

    def piece(t, g, first_row):
        if t == 0:
            return pl.ds(first_row, half), pl.ds(mult(g * piece_cols, piece_cols), piece_cols)
        return pl.ds(mult(first_row + g * piece_rows, piece_rows), piece_rows), pl.ds(0, width)

    def z_far(t, g):
        rows, cols = piece(t, g, far_rows)
        to_rows, _ = piece(t, g, 0)
        return remote(
            zpart.at[t, rows, cols],
            zfar.at[t, to_rows, cols],
            zf_ss,
            zf_rs.at[t * Z_PARTS + g],
            beside,
        )

    def z_near(t, g):
        rows, cols = piece(t, g, near_rows)
        to_rows, _ = piece(t, g, 0)
        return remote(
            zpart.at[t, rows, cols],
            znear.at[t, to_rows, cols],
            zn_ss,
            zm_rs.at[t * Z_PARTS + g],
            beside,
        )

    def z_mid(t, g):
        rows, cols = piece(t, g, far_rows)
        to_rows, _ = piece(t, g, 0)
        return remote(
            zpart.at[t, rows, cols],
            zmid.at[t, to_rows, cols],
            zm_ss,
            zm_rs.at[t * Z_PARTS + g],
            across,
        )

    def z_done(t, g, to_end):
        rows, cols = piece(t, g, near_rows)
        place = zout.at[t, rows, cols]
        if to_end:
            return remote(place, place, zo_ss, ze_rs, beside)
        return remote(place, place, zo_ss, zo_rs.at[t * Z_PARTS + g], across)

    def z_pass(t, g):
        rows, cols = piece(t, g, far_rows)
        return remote(zout.at[t, rows, cols], zout.at[t, rows, cols], zw_ss, ze_rs, beside)

    def z_send(copies):
        @pl.when(end_of_line)
        def _():
            for copy in copies:
                copy.start()

    def z_first(t, g):
        z_far(t, g).wait_recv()
        rows, cols = piece(t, g, far_rows)
        there, _ = piece(t, g, 0)
        zpart[t, rows, cols] = (
            zpart[t, rows, cols].astype(F32) + zfar[t, there, cols].astype(F32)
        ).astype(BF16)
        z_mid(t, g).start()

    def z_second(t, g):
        came(znear.at[0, :, pl.ds(0, 2 * piece_cols)], zm_rs.at[t * Z_PARTS + g])
        rows, cols = piece(t, g, near_rows)
        there, _ = piece(t, g, 0)
        total = (
            zpart[t, rows, cols].astype(F32)
            + znear[t, there, cols].astype(F32)
            + zmid[t, there, cols].astype(F32)
        )
        base = tok[rows, cols].astype(F32)
        if t == 0:
            place = near_rows + lax.broadcasted_iota(jnp.int32, total.shape, 0)
            branch = jnp.where(place < total_len, total + obias[:, cols], 0.0)
            zout[t, rows, cols] = (base + branch).astype(BF16)
        else:
            @pl.when(g == 0)
            def _():
                cot_load.wait()

            inv = stat_i[rows, 0:1]
            standard = (base - stat_m[rows, 0:1]) * inv
            grad = total * gain[...]
            mean_g = jnp.sum(grad, axis=1, keepdims=True) * (1.0 / width)
            mean_x = jnp.sum(grad * standard, axis=1, keepdims=True) * (1.0 / width)
            back = inv * (grad - mean_g - standard * mean_x)
            zout[t, rows, cols] = (cot_rows[there, :].astype(F32) + back).astype(BF16)
        z_done(t, g, False).start()
        z_done(t, g, True).start()

    def z_third(t, g):
        z_done(t, g, False).wait_recv()
        z_pass(t, g).start()

    def z_move(step, number):
        for t in (0, 1):
            at = number - t * Z_PARTS
            if isinstance(number, int):
                if 0 <= at < Z_PARTS:
                    pl.when(middle)(functools.partial(step, t, at))
            else:
                pl.when(middle & (at >= 0) & (at < Z_PARTS))(functools.partial(step, t, at))

    def z_tick(number):
        for step, lag in zip((z_first, z_second, z_third), Z_LAG):
            z_move(step, number - lag)

    per_wide = WIDE // BLK
    n_wide = hidden // WIDE

    def hidden_block(w, with_grad):
        cols = pl.ds(mult(w * WIDE, WIDE), WIDE)
        came(wu.at[:, pl.ds(0, 2 * WIDE)], wide_sem.at[w])
        up = nn(normed[...], wu[:, cols]) + bup[:, cols]
        square = up * up
        tanh = jnp.tanh(GELU_A * up * (1.0 + GELU_B * square))
        row = lax.broadcasted_iota(jnp.int32, up.shape, 0)
        active = jnp.where(row < total_len, 0.5 * up * (1.0 + tanh), 0.0).astype(BF16)
        act[:, cols] = active
        slope = 0.5 * (1.0 + tanh) + 0.5 * up * (1.0 - tanh * tanh) * (
            GELU_A * (1.0 + 3.0 * GELU_B * square)
        )
        if with_grad:
            grad = (nt(gout[...], wd[cols, :]) * slope).astype(BF16)
            gup[:, cols] = grad
        else:
            gup[:, cols] = slope.astype(BF16)
        for part in range(per_wide):
            c = w * per_wide + part
            inside = slice(part * BLK, part * BLK + BLK)
            bg[c, :, 0:toks] = active[:, inside].T
            if with_grad:
                bn[c, 0:toks, :] = grad[:, inside]
        for part in range(per_wide):
            c = w * per_wide + part
            for k in (0, 1):
                bg_copy(c, k).start()
                if with_grad:
                    bn_copy(c, k).start()

    @pl.loop(0, n_wide // 2)
    def _(w):
        hidden_block(w, True)

    @pl.loop(n_wide // 2, n_wide)
    def _(w):
        hidden_block(w, False)

        @pl.when(w == n_wide // 2)
        def _():
            side_first()

    def hidden_grad(first, past, shift):
        @pl.loop(first, past)
        def _(w):
            @pl.when(w == first)
            def _():
                side_out(0)

            @pl.when(w == first + 1)
            def _():
                side_out(1)

            z_tick(w - first)
            cols = pl.ds(mult(w * WIDE, WIDE), WIDE)
            grad = (nt(gout[...], wd[cols, :]) * gup[:, cols].astype(F32)).astype(BF16)
            gup[:, cols] = grad
            for part in range(per_wide):
                c = shift + w * per_wide + part
                bn[c, 0:toks, :] = grad[:, part * BLK : part * BLK + BLK]
                for k in (0, 1):
                    bn_copy(c, k).start()

    seg_r, _ = segment_of(slot)
    seg_c, _ = segment_of(lax.broadcasted_iota(jnp.int32, (8, toks), 1))
    place_r = lax.broadcasted_iota(jnp.int32, (toks, toks), 0)
    place_c = lax.broadcasted_iota(jnp.int32, (toks, toks), 1)
    same = jnp.concatenate([seg_r] * (toks // 128), axis=1) == seg_c[0:1, :]
    mask = jnp.where(same & (place_c <= place_r), 0.0, -1e30)
    for h in (0, 1):
        amask[h * toks : h * toks + toks, :] = mask

    which = lax.broadcasted_iota(jnp.int32, (8, 128), 0)
    starts = jnp.zeros((8, 128), jnp.int32)
    for j, end in enumerate(ends):
        starts = jnp.where(which == j, end - lens[0, j], starts)
    turn = starts.astype(F32) * freq[0:8, :]
    turn_c, turn_s = jnp.cos(turn), jnp.sin(turn)
    back_c, back_s = jnp.ones((toks, 128), F32), jnp.zeros((toks, 128), F32)
    for j in range(len(ends)):
        inside = seg_r == j + 1
        back_c = jnp.where(inside, turn_c[j : j + 1, :], back_c)
        back_s = jnp.where(inside, turn_s[j : j + 1, :], back_s)
    slot_c, slot_s = rot_c[...], rot_a[...]
    cosine = slot_c * back_c + slot_s * back_s
    sine = slot_s * back_c - slot_c * back_s
    rot_c[...] = jnp.where(in_head < ROT, cosine, 1.0)
    rot_a[...] = jnp.where(in_head < ROT // 2, -sine, 0.0)
    rot_b[...] = jnp.where((in_head >= ROT // 2) & (in_head < ROT), sine, 0.0)

    def rotate(value, sign):
        left = pltpu.roll(value, 128 - ROT // 2, 1)
        right = pltpu.roll(value, ROT // 2, 1)
        return value * rot_c[...] + sign * (left * rot_a[...] + right * rot_b[...])

    attn_load.wait()

    @pl.loop(0, heads_w // BLK)
    def _(n):
        cols = pl.ds(mult(n * BLK, BLK), BLK)
        query = nn(normed[...], wq[:, cols]) + bq[:, cols]
        keys = nn(normed[...], wk[:, cols]) + bk[:, cols]
        for part in range(BLK // 128):
            at = pl.ds(mult(n * BLK + part * 128, 128), 128)
            lanes = slice(part * 128, part * 128 + 128)
            q_s[:, at] = (rotate(query[:, lanes], 1.0) * 0.125).astype(BF16)
            k_s[:, at] = rotate(keys[:, lanes], 1.0).astype(BF16)
        v_s[:, cols] = (nn(normed[...], wv[:, cols]) + bv[:, cols]).astype(BF16)
        ga_s[:, cols] = nt(gout[...], wo[cols, :]).astype(BF16)

    low_lane = lax.broadcasted_iota(jnp.int32, (1, 128), 1) < HD
    first_head = jnp.where(low_lane, 1.0, 0.0).astype(BF16)
    second_head = jnp.where(low_lane, 0.0, 1.0).astype(BF16)
    low_full = lax.broadcasted_iota(jnp.int32, (toks, 128), 1) < HD

    def apart(value):
        return jnp.concatenate([value * first_head, value * second_head], axis=0)

    def together(value):
        return jnp.where(low_full, value[:toks], value[toks:])

    @pl.loop(0, n_att)
    def _(n):
        base_n = n_hid // 2 + 3 * n

        @pl.when(n == n_att - 1)
        def _():
            side_relay(0)

        for part in range(BLK // 128):
            at = pl.ds(mult(n * BLK + part * 128, 128), 128)
            lanes = slice(part * 128, part * 128 + 128)
            kp, vp = k_s[:, at], v_s[:, at]
            q2, g2 = apart(q_s[:, at]), apart(ga_s[:, at])
            scores = nt(q2, kp) + amask[...]
            top = jnp.max(scores, axis=1, keepdims=True)
            expo = jnp.exp(scores - top)
            probs = expo * (1.0 / jnp.sum(expo, axis=1, keepdims=True))
            probs_low = probs.astype(BF16)
            prob_grad = nt(g2, vp)
            delta = jnp.sum(probs * prob_grad, axis=1, keepdims=True)
            score_grad = (probs * (prob_grad - delta)).astype(BF16)
            out = jnp.where(slot < total_len, together(nn(probs_low, vp)), 0.0).astype(BF16)
            att[:, at] = out
            bg[n_hid + n, lanes, 0:toks] = out.T
            dq = rotate(together(nn(score_grad, kp)) * 0.125, -1.0).astype(BF16)
            dk = rotate(tn(score_grad, q2), -1.0).astype(BF16)
            dv = tn(probs_low, g2).astype(BF16)
            for kind, value in enumerate((dq, dk, dv)):
                bn[base_n + kind, 0:toks, lanes] = value
                gqkv[:, pl.ds(mult(kind * heads_w + n * BLK + part * 128, 128), 128)] = value
        for k in (0, 1):
            bg_copy(n_hid + n, k).start()
            for kind in range(3):
                bn_copy(base_n + kind, k).start()

    side_relay(1)

    def branches(cols):
        zpart[0, :, cols] = (nn(act[...], wd[:, cols]) + nn(att[...], wo[:, cols])).astype(BF16)

    for g in range(Z_LEAD):
        branches(pl.ds(g * piece_cols, piece_cols))
        z_send([z_far(0, g)])

    @pl.loop(1, width // WIDE)
    def _(n):
        branches(pl.ds(mult(n * WIDE, WIDE), WIDE))
        for part in range(Z_LEAD):
            g = n * Z_LEAD + part
            z_send([z_far(0, g), z_near(0, g - Z_LEAD)])

    hidden_grad(n_wide // 2, n_wide, 3 * n_att)

    vzl[...] = jnp.zeros_like(vzl)

    @pl.loop(0, width // WIDE)
    def _(n):
        cols = pl.ds(mult(n * WIDE, WIDE), WIDE)
        grad = nt(gup[...], wu[cols, :])
        for kind, weight in enumerate((wq, wk, wv)):
            grad = grad + nt(gqkv[:, kind * heads_w : (kind + 1) * heads_w], weight[cols, :])
        zpart[1, :, cols] = grad.astype(BF16)

        @pl.when(n == 1)
        def _():
            z_tick(2)

        @pl.when(n == 3)
        def _():
            z_tick(3)

        for part in range(WIDE // 128):
            lanes = slice(part * 128, part * 128 + 128)
            at = pl.ds(mult(n * WIDE + part * 128, 128), 128)
            owner = n * per_wide + part * 128 // BLK
            half_row = part * 128 % BLK // 128
            piece_of = grad[:, lanes]
            standard = (tok[:, at].astype(F32) - stat_m[...]) * stat_i[...]
            vzl[owner, half_row : half_row + 1, :] = jnp.sum(piece_of * standard, axis=0, keepdims=True)
            vzl[owner, 2 + half_row : 3 + half_row, :] = jnp.sum(piece_of, axis=0, keepdims=True)

    def vd_copy(mask):
        return remote(
            vzl.at[flip(inner, mask)], vdr.at[mask - 1], vd_ss, vd_rs, peer(mask)
        )

    for owner in range(n_own):
        for half_row in (0, 1):
            first = owner * BLK + half_row * 128
            vzl[owner, 4 + half_row : 5 + half_row, :] = gsum[0:1, first : first + 128]
    for mask in range(1, GROUP):
        vd_copy(mask).start()
    for g in range(Z_PARTS):
        late = Z_PARTS - Z_LEAD + g
        z_send([z_far(1, g), z_near(late // Z_PARTS, late % Z_PARTS)])
    for g in range(Z_PARTS - Z_LEAD, Z_PARTS):
        z_send([z_near(1, g)])

    bs_copy = remote(bsum_s, bsum_r, bs_ss, bs_rs, peer(YBIT))

    def rn_copy(s):
        return remote(rsn_s.at[s], rsn_r.at[s], rn_ss, rn_rs, peer(YBIT))

    def rg_copy(s):
        return remote(rsg_s.at[s], rsg_r.at[s], rg_ss, rg_rs, peer(XBIT))

    came(bn.at[0], side_rs.at[1])

    @pl.when(end_of_line)
    def _():
        for number in (1, 2, 3):
            for kind in (0, 1):
                side_came(kind, number)

    bsum[...] = jnp.zeros_like(bsum)

    def vz_copy(src, i, where):
        return remote(src, vzr.at[i], vz_ss, vz_rs.at[i], where)

    def vec_spread():
        came(vdr, vd_rs)
        vz[...] = vzl[inner] + jnp.sum(vdr[...], axis=0)

        @pl.when(end_of_line)
        def _():
            vz_copy(vz, 0, beside).start()

    def vec_pair():
        @pl.when(middle)
        def _():
            came(vz, vz_rs.at[0])
            vz_pair[...] = vz[...] + vzr[0]
            vz_copy(vz_pair, 1, across).start()

    def vec_back():
        @pl.when(middle)
        def _():
            came(vz, vz_rs.at[1])
            norm_sums[...] = vz_pair[...] + vzr[1]
            vz_copy(norm_sums, 0, beside).start()

    side_n[2 * BLK :, :] = jnp.ones((16, 4 * toks), BF16)

    @pl.loop(0, n_chunks + 1)
    def _(s):
        @pl.when(s < g_chunks)
        def _():
            came(bn.at[s, pl.ds(0, 2 * toks), :], blk_rs.at[s, 0])
            bn_copy(s, 2).start()
            bg_copy(s, 2).start()

        @pl.when((s >= g_chunks) & (s < n_chunks))
        def _():
            came(bn.at[s, pl.ds(0, toks), :], blk_rs.at[s, 0])
            bn_copy(s, 2).start()

        @pl.when((s > 0) & (s <= g_chunks))
        def _():
            came(bn.at[s - 1], blk_rs.at[s - 1, 1])

        @pl.when(s > g_chunks)
        def _():
            came(bn.at[s - 1, pl.ds(0, 2 * toks), :], blk_rs.at[s - 1, 1])

        @pl.when(s > 0)
        def _():
            p = s - 1
            both = nn(side_n[...], bn[p])
            rsn_s[p] = both[BLK : 2 * BLK, :].astype(BF16)
            rn_copy(p).start()
            bsum[pl.ds(p, 1), :] = both[2 * BLK : 2 * BLK + 1, :]
            bn[p, 2 * toks : 3 * toks, :] = both[:BLK, :].astype(BF16)

        @pl.when((s > 0) & (s <= g_chunks))
        def _():
            p = s - 1
            both = nn(bg[p], side_g[...])
            rsg_s[p] = both[:, BLK:].astype(BF16)
            rg_copy(p).start()
            bg[p, :, 2 * toks : 3 * toks] = both[:, :BLK].astype(BF16)

        tick = -1
        for turn, number in Z_TICKS:
            tick = jnp.where(s == turn, number, tick)
        z_tick(tick)

    bsum_s[...] = bsum[...].astype(BF16)
    bs_copy.start()
    vec_spread()
    @pl.loop(Z_TICKS[-1][1] + 1, 2 * Z_PARTS + Z_LAG[-1])
    def _(number):
        @pl.when(number == 2 * Z_PARTS)
        def _():
            vec_pair()

        z_tick(number)

    vec_back()

    bs_copy.wait_recv()

    @pl.when(end_of_line)
    def _():
        came(vz, vz_rs.at[0])
        norm_sums[...] = vzr[0]

    for half_row in (0, 1):
        lanes = slice(half_row * 128, half_row * 128 + 128)
        vec_o[0:1, lanes] = norm_sums[half_row : half_row + 1, :]
        vec_o[1:2, lanes] = norm_sums[2 + half_row : 3 + half_row, :]
        vec_o[2:3, lanes] = vz[4 + half_row : 5 + half_row, :]
    vec_o[8:, :] = bsum[...] + bsum_r[...].astype(F32)

    came(rsn_r, rn_rs)
    came(rsg_r, rg_rs)

    came(bn.at[:, pl.ds(0, 3 * toks), :], bn_ss)
    came(bg.at[:, :, pl.ds(0, 3 * toks)], bg_ss)
    came(rsn_s, rn_ss)
    came(rsg_s, rg_ss)
    came(vdr, vd_ss)
    bs_copy.wait_send()

    @pl.when(end_of_line)
    def _():
        came(bn.at[pl.ds(0, 2)], side_ss)
        came(vz, vz_ss)
        came(zfar, zf_ss)
        came(znear, zn_ss)
        came(zout, ze_rs)
        cot_load.wait()

    @pl.when(middle)
    def _():
        came(bn.at[pl.ds(0, 4)], side_ss)
        came(vzr, vz_ss)
        came(zmid, zm_ss)
        came(zout, zo_ss)
        came(zmid, zw_ss)


def write_kernel(n_hid, n_att, bn, bg, rsn, rsg, zout, vec, mixed_h, gtok_h, gain_o, shift_o, gq_h, bq_o, gk_h, bk_o, gv_h, bv_o, go_h, gu_h, bu_o, gd_h, ob_o, stage, small, sem, zsem, small_sem):
    n_chunks, n_g = bn.shape[0], bg.shape[0]
    toks = zout.shape[1]
    z_outs = [
        pltpu.make_async_copy(zout.at[t], out, zsem) for t, out in enumerate((mixed_h, gtok_h))
    ]
    for out in z_outs:
        out.start()
    places, biases = [], []
    for s in range(n_chunks):
        inside = s - n_hid // 2
        if 0 <= inside < 3 * n_att:
            (out, bias), at = ((gq_h, bq_o), (gk_h, bk_o), (gv_h, bv_o))[inside % 3], inside // 3
        else:
            (out, bias), at = (gu_h, bu_o), s if inside < 0 else s - 3 * n_att
        biases.append((bias, at))
        places.append((True, s, out.at[:, pl.ds(at * BLK, BLK)]))
    for s in range(n_g):
        out, at = (gd_h, s) if s < n_hid else (go_h, s - n_hid)
        places.append((False, s, out.at[pl.ds(at * BLK, BLK), :]))
    smalls = [(gain_o, (0,)), (shift_o, (1,)), (ob_o, (2,))]
    for bias in (bq_o, bk_o, bv_o, bu_o):
        smalls.append((bias, tuple(8 + s for at, s in sorted((at, s) for s, (b, at) in enumerate(biases) if b is bias))))
    at = 0
    for out, rows in smalls:
        for part, row in enumerate(rows):
            small[at + part * BLK : at + part * BLK + BLK] = vec[row]
        pltpu.make_async_copy(small.at[pl.ds(at, len(rows) * BLK)], out, small_sem).start()
        at += len(rows) * BLK
    copies = []
    for number, (first, s, place) in enumerate(places):
        slot = number
        if first:
            value = bn[s, 2 * toks : 3 * toks, :].astype(F32) + rsn[s].astype(F32)
        else:
            value = bg[s, :, 2 * toks : 3 * toks].astype(F32) + rsg[s].astype(F32)
        stage[slot] = value
        copies.append(pltpu.make_async_copy(stage.at[slot], place, sem))
        copies[number].start()
    pltpu.make_async_copy(stage, stage, sem).wait()
    pltpu.make_async_copy(zout, zout, zsem).wait()
    pltpu.make_async_copy(small, small, small_sem).wait()


def layer(tokens, lengths, ln_gain, ln_bias, w_query, b_query, w_key, b_key, w_value, b_value, w_out, w_up, b_up, w_down, out_bias, cotangent):
    toks, width = tokens.shape
    heads_w = w_query.shape[1]
    hidden = w_up.shape[1]
    n_chunks = (3 * heads_w + hidden) // BLK
    g_chunks = (heads_w + hidden) // BLK
    n_own = width // BLK
    n_vec = -(-n_chunks // 8) * 8
    half = toks // 2
    dma = pltpu.SemaphoreType.DMA
    vmem = pltpu.VMEM
    scratch = [
        pltpu.SMEM(lengths.shape, jnp.int32),
        vmem((1, 2 * width), F32),
        vmem((1, hidden + 3 * heads_w + width), F32),
        vmem((toks, width), BF16),
        vmem((toks, width), BF16),
        vmem((toks, width), BF16),
        vmem((n_own, BLK, toks), BF16),
        vmem(w_query.shape, BF16),
        vmem(w_key.shape, BF16),
        vmem(w_value.shape, BF16),
        vmem(w_out.shape, BF16),
        vmem(w_up.shape, BF16),
        vmem(w_down.shape, BF16),
        vmem((2 * BLK + 16, 4 * toks), BF16),
        vmem((4 * toks, 2 * BLK), BF16),
        vmem((n_chunks, BLK, BLK), BF16),
        vmem((g_chunks, BLK, BLK), BF16),
        vmem((toks, hidden), BF16),
        vmem((toks, hidden), BF16),
        vmem((toks, 3 * heads_w), BF16),
        vmem((toks, heads_w), BF16),
        vmem((toks, heads_w), BF16),
        vmem((toks, heads_w), BF16),
        vmem((toks, heads_w), BF16),
        vmem((toks, heads_w), BF16),
        vmem((2 * toks, toks), F32),
        vmem((toks, 128), F32),
        vmem((toks, 128), F32),
        vmem((toks, 128), F32),
        vmem((toks, 128), F32),
        vmem((toks, 128), F32),
        vmem((2, toks, width), BF16),
        vmem((2, half, width), BF16),
        vmem((2, half, width), BF16),
        vmem((2, half, width), BF16),
        vmem((n_own, 8, 128), F32),
        vmem((8, 128), F32),
        vmem((8, 128), F32),
        vmem((8, 128), F32),
        vmem((2, 8, 128), F32),
        vmem((GROUP - 1, 8, 128), F32),
        vmem((8, width), F32),
        vmem((n_vec, BLK), F32),
        vmem((n_vec, BLK), BF16),
        vmem((n_vec, BLK), BF16),
        vmem((half, width), BF16),
        dma((6,)),
        dma((4,)),
        dma((hidden // WIDE,)),
        dma,
        dma((8,)),
        dma,
        dma,
        dma((n_chunks, 2)),
        dma,
        dma,
        dma,
        dma,
        dma,
        dma((2 * Z_PARTS,)),
        dma,
        dma,
        dma((2 * Z_PARTS,)),
        dma,
        dma((2 * Z_PARTS,)),
        dma,
        dma,
        dma,
        dma((2,)),
        dma,
        dma,
        dma,
        dma,
    ]
    anyspace = pl.BlockSpec(memory_space=pl.ANY)
    local = pl.BlockSpec(memory_space=pltpu.VMEM)
    row = lambda value: value.reshape(1, -1)
    kept = pl.pallas_call(
        functools.partial(layer_kernel, n_chunks, g_chunks),
        out_shape=(
            vmem((n_chunks, 4 * toks, BLK), BF16),
            vmem((g_chunks, BLK, 4 * toks), BF16),
            vmem((n_chunks, BLK, BLK), BF16),
            vmem((g_chunks, BLK, BLK), BF16),
            vmem((2, toks, width), BF16),
            vmem((8 + n_vec, BLK), F32),
        ),
        in_specs=[anyspace] * 16,
        out_specs=(local,) * 6,
        scratch_shapes=scratch,
        compiler_params=pltpu.CompilerParams(
            collective_id=0, has_side_effects=True, vmem_limit_bytes=MAIN_VMEM
        ),
    )(
        lengths,
        tokens,
        cotangent,
        row(ln_gain),
        row(ln_bias),
        row(b_query),
        row(b_key),
        row(b_value),
        row(b_up),
        row(out_bias),
        w_query,
        w_key,
        w_value,
        w_out,
        w_up,
        w_down,
    )
    f32 = lambda *shape: jax.ShapeDtypeStruct(shape, F32)
    low = jax.ShapeDtypeStruct((toks, width), BF16)
    outs = (
        low,
        low,
        f32(BLK),
        f32(BLK),
        f32(BLK, heads_w),
        f32(heads_w),
        f32(BLK, heads_w),
        f32(heads_w),
        f32(BLK, heads_w),
        f32(heads_w),
        f32(heads_w, BLK),
        f32(BLK, hidden),
        f32(hidden),
        f32(hidden, BLK),
        f32(BLK),
    )
    slots = n_chunks + g_chunks
    return pl.pallas_call(
        functools.partial(write_kernel, hidden // BLK, heads_w // BLK),
        out_shape=outs,
        in_specs=[local] * 6,
        out_specs=(anyspace,) * len(outs),
        scratch_shapes=[
            vmem((slots, BLK, BLK), F32),
            vmem((3 * BLK + 3 * heads_w + hidden,), F32),
            dma,
            dma,
            dma,
        ],
        compiler_params=pltpu.CompilerParams(vmem_limit_bytes=12 * 2**20),
    )(*kept)


def make_body(n_dp, n_mp):
    outer = n_dp // GROUP

    def order(value, axis):
        if outer == 1:
            return value
        shape = value.shape
        split = shape[:axis] + (outer, GROUP, shape[axis] // n_dp) + shape[axis + 1 :]
        return jnp.swapaxes(value.reshape(split), axis, axis + 1).reshape(shape)

    def restore(value, axis):
        if outer == 1:
            return value
        shape = value.shape
        split = shape[:axis] + (GROUP, outer, shape[axis] // n_dp) + shape[axis + 1 :]
        return jnp.swapaxes(value.reshape(split), axis, axis + 1).reshape(shape)

    groups = [[o * GROUP + i for o in range(outer)] for i in range(GROUP)]

    def scatter(value, axis):
        if outer == 1:
            return value
        return lax.psum_scatter(
            value, "dp", scatter_dimension=axis, axis_index_groups=groups, tiled=True
        )

    def total(value):
        if outer == 1:
            return value
        return lax.psum(value, "dp", axis_index_groups=groups)

    def body(tokens, lengths, ln_gain, ln_bias, w_query, b_query, w_key, b_key, w_value, b_value, w_out, w_up, b_up, w_down, out_bias, cotangent):
        found = layer(
            order(tokens, 1),
            lengths,
            order(ln_gain, 0),
            order(ln_bias, 0),
            order(w_query, 0),
            b_query,
            order(w_key, 0),
            b_key,
            order(w_value, 0),
            b_value,
            order(w_out, 1),
            order(w_up, 0),
            b_up,
            order(w_down, 1),
            order(out_bias, 0),
            order(cotangent, 1),
        )
        (mixed, grad_tokens, gain, shift, g_q, b_q, g_k, b_k, g_v, b_v, g_out, g_up, b_u, g_down, b_out) = found
        return (
            restore(mixed, 1),
            restore(grad_tokens, 1),
            scatter(gain, 0),
            scatter(shift, 0),
            scatter(g_q, 0),
            total(b_q),
            scatter(g_k, 0),
            total(b_k),
            scatter(g_v, 0),
            total(b_v),
            scatter(g_out, 1),
            scatter(g_up, 0),
            total(b_u),
            scatter(g_down, 1),
            scatter(b_out, 0),
        )

    return body


def solution(mesh):
    in_specs = (
        P("dp", None),
        P("dp", None),
        P(),
        P(),
        P(None, "mp"),
        P("mp"),
        P(None, "mp"),
        P("mp"),
        P(None, "mp"),
        P("mp"),
        P("mp", None),
        P(None, "mp"),
        P("mp"),
        P("mp", None),
        P(),
        P("dp", None),
    )
    out_specs = (
        P("dp", None),
        P("dp", None),
        P("dp"),
        P("dp"),
        P("dp", "mp"),
        P("mp"),
        P("dp", "mp"),
        P("mp"),
        P("dp", "mp"),
        P("mp"),
        P("mp", "dp"),
        P("dp", "mp"),
        P("mp"),
        P("mp", "dp"),
        P("dp"),
    )
    body = make_body(mesh.shape["dp"], mesh.shape["mp"])
    return jax.shard_map(body, mesh=mesh, in_specs=in_specs, out_specs=out_specs, check_vma=False)
```

```python
import functools
import math

import jax
import jax.numpy as jnp
from jax import lax
from jax.experimental import pallas as pl
from jax.experimental.pallas import tpu as pltpu
from jax.sharding import PartitionSpec as P

HD = 64
ROT = 32
EPSILON = 1e-05
GROUP = 8
CORE, XBIT, YBIT = 1, 2, 4
BLK = 256
WIDE = 512
Z_PARTS = 8
Z_LEAD = 2
Z_LAG = (0, 2, 4)
Z_TICKS = ((1, 4), (3, 5), (5, 6), (7, 7), (8, 8), (9, 9), (10, 10), (11, 11), (12, 12), (13, 13))
F32 = jnp.float32
BF16 = jnp.bfloat16
MESH = pl.DeviceIdType.MESH
MAIN_VMEM = 93 * 2**19
GELU_A = math.sqrt(2.0 / math.pi)
GELU_B = 0.044715


def nn(left, right):
    return lax.dot_general(left, right, (((1,), (0,)), ((), ())), preferred_element_type=F32)


def nt(left, right):
    return lax.dot_general(left, right, (((1,), (1,)), ((), ())), preferred_element_type=F32)


def tn(left, right):
    return lax.dot_general(left, right, (((0,), (0,)), ((), ())), preferred_element_type=F32)


def flip(index, mask):
    for bit in (1, 2, 4):
        if mask & bit:
            index = index + bit * (1 - 2 * ((index // bit) % 2))
    return index


def mult(value, by):
    return pl.multiple_of(value, by)


N_JS = (0, XBIT, CORE, XBIT | CORE)
N_MS = (0, YBIT)
G_JS = (0, YBIT, CORE, YBIT | CORE)
G_MS = (0, XBIT)


def layer_kernel(
    n_chunks,
    g_chunks,
    lens_h,
    tok_h,
    cot_h,
    gain_h,
    shift_h,
    bq_h,
    bk_h,
    bv_h,
    bup_h,
    obias_h,
    wq_h,
    wk_h,
    wv_h,
    wo_h,
    wu_h,
    wd_h,
    bn,
    bg,
    rsn_r,
    rsg_r,
    zout,
    vec_o,
    lens,
    norm_in,
    bias_in,
    tok,
    gout,
    normed,
    turned_n,
    wq,
    wk,
    wv,
    wo,
    wu,
    wd,
    side_n,
    side_g,
    rsn_s,
    rsg_s,
    act,
    gup,
    gqkv,
    att,
    q_s,
    k_s,
    v_s,
    ga_s,
    amask,
    rot_c,
    rot_a,
    rot_b,
    stat_m,
    stat_i,
    zpart,
    zfar,
    znear,
    zmid,
    vzl,
    vz,
    vz_pair,
    norm_sums,
    vzr,
    vdr,
    gsum,
    bsum,
    bsum_s,
    bsum_r,
    cot_rows,
    in_sem,
    tok_sem,
    wide_sem,
    side_ss,
    side_rs,
    bn_ss,
    bg_ss,
    blk_rs,
    rn_ss,
    rn_rs,
    rg_ss,
    rg_rs,
    zf_ss,
    zf_rs,
    zn_ss,
    zm_ss,
    zm_rs,
    zo_ss,
    zo_rs,
    zw_ss,
    ze_rs,
    vz_ss,
    vz_rs,
    vd_ss,
    vd_rs,
    bs_ss,
    bs_rs,
):
    toks, width = tok.shape
    hidden = wu.shape[1]
    heads_w = wq.shape[1]
    n_att = heads_w // BLK
    n_hid = hidden // BLK
    n_own = width // BLK
    dp = lax.axis_index("dp")
    zed = lax.axis_index("mp")
    inner = lax.rem(dp, GROUP)
    outer = dp - inner
    half = toks // 2
    piece_cols = width // Z_PARTS
    piece_rows = half // Z_PARTS

    def peer(mask):
        return (outer + flip(inner, mask), zed)

    def came(ref, sem):
        pltpu.make_async_copy(ref, ref, sem).wait()

    middle = (zed == 1) | (zed == 2)
    end_of_line = (zed == 0) | (zed == 3)
    side_of_line = zed // 2
    beside = (dp, zed + 1 - 2 * lax.rem(zed, 2))
    across = (dp, 3 - zed)
    near_rows = mult(side_of_line * half, half)
    far_rows = mult((1 - side_of_line) * half, half)

    def remote(src, dst, ssem, rsem, where):
        return pltpu.make_async_remote_copy(
            src_ref=src,
            dst_ref=dst,
            send_sem=ssem,
            recv_sem=rsem,
            device_id=where,
            device_id_type=MESH,
        )

    def load(src, dst, number):
        copy = pltpu.make_async_copy(src, dst, in_sem.at[number])
        copy.start()
        return copy

    tok_parts = 4

    def tok_load(c):
        rows = pl.ds(mult(c * (toks // tok_parts), toks // tok_parts), toks // tok_parts)
        return pltpu.make_async_copy(tok_h.at[rows, :], tok.at[rows, :], tok_sem.at[c])

    for c in range(tok_parts):
        tok_load(c).start()
    for at, src in enumerate((gain_h, shift_h)):
        load(src, norm_in.at[:, pl.ds(at * width, width)], 0)
    lens_load = load(lens_h, lens, 1)

    barrier = pltpu.get_barrier_semaphore()
    for mask in range(1, GROUP):
        pl.semaphore_signal(barrier, inc=1, device_id=peer(mask), device_id_type=MESH)
    pl.semaphore_signal(barrier, inc=1, device_id=beside, device_id_type=MESH)

    @pl.when(middle)
    def _():
        pl.semaphore_signal(barrier, inc=1, device_id=across, device_id_type=MESH)

    gout_load = load(cot_h, gout, 2)
    at = 0
    biases = []
    for src in (bup_h, bq_h, bk_h, bv_h, obias_h):
        biases.append(bias_in.at[:, pl.ds(at, src.shape[1])])
        load(src, biases[-1], 3)
        at += src.shape[1]
    bup, bq, bk, bv, obias = biases
    gain, shift = norm_in.at[:, pl.ds(0, width)], norm_in.at[:, pl.ds(width, width)]

    def wide_loads(w):
        part = pl.ds(mult(w * WIDE, WIDE), WIDE)
        return (
            pltpu.make_async_copy(wu_h.at[:, part], wu.at[:, part], wide_sem.at[w]),
            pltpu.make_async_copy(wd_h.at[part, :], wd.at[part, :], wide_sem.at[w]),
        )

    @pl.loop(0, hidden // WIDE)
    def _(w):
        for copy in wide_loads(w):
            copy.start()

    for src, dst in ((wq_h, wq), (wk_h, wk), (wv_h, wv), (wo_h, wo)):
        load(src, dst, 4)
    attn_load = pltpu.make_async_copy(wu_h, wu, in_sem.at[4])
    cot_load = load(cot_h.at[pl.ds(near_rows, half), :], cot_rows, 5)

    def segment_of(place):
        number = jnp.zeros_like(place)
        start_of = jnp.zeros_like(place)
        for j, end in enumerate(ends):
            start = end - lens[0, j]
            inside = ((place >= start) & (place < end)).astype(jnp.int32)
            number = number + inside * (j + 1)
            start_of = start_of + inside * start
        return number, start_of

    def cross_core(index, times):
        return index + times * (1 - 2 * lax.rem(index, 2))

    def flip_by(index, bit, times):
        return index + times * (bit * (1 - 2 * ((index // bit) % 2)))

    own_part = lax.rem(zed, 2)
    own_slot = 1 + 2 * side_of_line
    other_slot = 3 - 2 * side_of_line

    def side_places(slot_at, m):
        at = pl.ds(mult(slot_at * toks, toks), toks)
        rows = pl.ds(mult(m * BLK, BLK), BLK)
        return side_n.at[rows, at], side_g.at[at, rows]

    def side_direct():
        at_n = flip(cross_core(inner, side_of_line), XBIT)
        at_g = flip(cross_core(inner, side_of_line), YBIT)
        owner_n = flip_by(at_n, YBIT, own_part)
        owner_g = flip_by(at_g, XBIT, own_part)
        place_n, place_g = side_places(own_slot, own_part)
        source_g = cot_h.at[:, pl.ds(mult(owner_g * BLK, BLK), BLK)]
        return (
            remote(turned_n.at[owner_n], place_n, side_ss, side_rs.at[0], (outer + at_n, zed)),
            remote(source_g, place_g, side_ss, side_rs.at[0], (outer + at_g, zed)),
            owner_n,
        )

    def side_core(m):
        place_n, place_g = side_places(2, m)
        owner_n = flip(inner, CORE ^ N_MS[m])
        owner_g = flip(inner, CORE ^ G_MS[m])
        source_g = cot_h.at[:, pl.ds(mult(owner_g * BLK, BLK), BLK)]
        return (
            remote(turned_n.at[owner_n], place_n, side_ss, side_rs.at[1], peer(CORE)),
            remote(source_g, place_g, side_ss, side_rs.at[1], peer(CORE)),
        )

    def side_send(kind, slot_at, m, number, where):
        place = side_places(slot_at, m)[kind]
        remote(place, place, side_ss, side_rs.at[2 * number + kind], where).start()

    def side_came(kind, number):
        came(bn.at[0, pl.ds(0, toks), :], side_rs.at[2 * number + kind])

    def side_first():
        came(bn.at[0, pl.ds(0, 2 * toks), :], side_rs.at[0])
        for kind in (0, 1):
            side_send(kind, own_slot, own_part, 1, beside)

            @pl.when(middle)
            def _():
                side_send(kind, own_slot, own_part, 2, across)

    def side_relay(kind):
        @pl.when(middle)
        def _():
            side_came(kind, 1)
            side_send(kind, own_slot, 1 - own_part, 3, across)
            side_came(kind, 2)
            side_send(kind, other_slot, 1 - own_part, 2, beside)

    def side_out(kind):
        @pl.when(middle)
        def _():
            side_came(kind, 3)
            side_send(kind, other_slot, own_part, 3, beside)

    lane = lax.broadcasted_iota(jnp.int32, (toks, 128), 1)
    slot = lax.broadcasted_iota(jnp.int32, (toks, 128), 0)
    in_head = lane % HD
    order = (in_head % (ROT // 2)).astype(F32)
    freq = jnp.exp(order * (-2.0 / ROT * math.log(10000.0)))
    angle = slot.astype(F32) * freq
    rot_c[...] = jnp.cos(angle)
    rot_a[...] = jnp.sin(angle)

    came(norm_in, in_sem.at[0])
    step_rows = 32

    @pl.loop(0, tok_parts)
    def _(c):
        tok_load(c).wait()
        for part in range(toks // tok_parts // step_rows):
            rows = pl.ds(mult(c * (toks // tok_parts) + part * step_rows, step_rows), step_rows)
            value = tok[rows, :].astype(F32)
            mean = jnp.sum(value, axis=1, keepdims=True) * (1.0 / width)
            center = value - mean
            spread = jnp.sum(center * center, axis=1, keepdims=True) * (1.0 / width)
            inv = lax.rsqrt(spread + EPSILON)
            normed[rows, :] = (center * inv * gain[...] + shift[...]).astype(BF16)
            stat_m[rows, :] = jnp.broadcast_to(mean, (step_rows, 128))
            stat_i[rows, :] = jnp.broadcast_to(inv, (step_rows, 128))

    @pl.when(end_of_line)
    def _():
        pl.semaphore_wait(barrier, GROUP)

    @pl.when(middle)
    def _():
        pl.semaphore_wait(barrier, GROUP + 1)

    direct_n, direct_g, first_owner = side_direct()
    direct_g.start()
    turned_n[first_owner] = normed[:, pl.ds(mult(first_owner * BLK, BLK), BLK)].T
    direct_n.start()

    lens_load.wait()
    gout_load.wait()
    came(bias_in, in_sem.at[3])

    ends = []
    total_len = 0
    for j in range(lens.shape[1]):
        total_len = total_len + lens[0, j]
        ends.append(total_len)

    gsum[...] = jnp.zeros_like(gsum)

    @pl.loop(0, toks // step_rows, unroll=2)
    def _(r):
        first = r * step_rows
        rows = pl.ds(mult(first, step_rows), step_rows)
        place = first + lax.broadcasted_iota(jnp.int32, (step_rows, width), 0)
        value = jnp.where(place < total_len, gout[rows, :].astype(F32), 0.0)
        gout[rows, :] = value.astype(BF16)
        gsum[0:1, :] = gsum[0:1, :] + jnp.sum(value, axis=0, keepdims=True)

    for m in (0, 1):
        for owner in (flip(inner, CORE ^ N_MS[m]), flip(inner, N_MS[m])):
            turned_n[owner] = normed[:, pl.ds(mult(owner * BLK, BLK), BLK)].T
        for copy in side_core(m):
            copy.start()
        owner_g = mult(flip(inner, G_MS[m]) * BLK, BLK)
        side_g[0:toks, m * BLK : m * BLK + BLK] = gout[:, pl.ds(owner_g, BLK)]
        side_n[m * BLK : m * BLK + BLK, 0:toks] = turned_n[flip(inner, N_MS[m])]
    def bn_copy(s, k):
        src = bn.at[s, pl.ds(toks if k == 2 else 0, toks), :]
        slot_at = (1, 2, 3)[k]
        return remote(
            src,
            bn.at[s, pl.ds(slot_at * toks, toks), :],
            bn_ss,
            blk_rs.at[s, min(k, 1)],
            peer((XBIT, CORE, CORE)[k]),
        )

    def bg_copy(s, k):
        src = bg.at[s, :, pl.ds(toks if k == 2 else 0, toks)]
        slot_at = (1, 2, 3)[k]
        return remote(
            src,
            bg.at[s, :, pl.ds(slot_at * toks, toks)],
            bg_ss,
            blk_rs.at[s, min(k, 1)],
            peer((YBIT, CORE, CORE)[k]),
        )

    def piece(t, g, first_row):
        if t == 0:
            return pl.ds(first_row, half), pl.ds(mult(g * piece_cols, piece_cols), piece_cols)
        return pl.ds(mult(first_row + g * piece_rows, piece_rows), piece_rows), pl.ds(0, width)

    def z_far(t, g):
        rows, cols = piece(t, g, far_rows)
        to_rows, _ = piece(t, g, 0)
        return remote(
            zpart.at[t, rows, cols],
            zfar.at[t, to_rows, cols],
            zf_ss,
            zf_rs.at[t * Z_PARTS + g],
            beside,
        )

    def z_near(t, g):
        rows, cols = piece(t, g, near_rows)
        to_rows, _ = piece(t, g, 0)
        return remote(
            zpart.at[t, rows, cols],
            znear.at[t, to_rows, cols],
            zn_ss,
            zm_rs.at[t * Z_PARTS + g],
            beside,
        )

    def z_mid(t, g):
        rows, cols = piece(t, g, far_rows)
        to_rows, _ = piece(t, g, 0)
        return remote(
            zpart.at[t, rows, cols],
            zmid.at[t, to_rows, cols],
            zm_ss,
            zm_rs.at[t * Z_PARTS + g],
            across,
        )

    def z_done(t, g, to_end):
        rows, cols = piece(t, g, near_rows)
        place = zout.at[t, rows, cols]
        if to_end:
            return remote(place, place, zo_ss, ze_rs, beside)
        return remote(place, place, zo_ss, zo_rs.at[t * Z_PARTS + g], across)

    def z_pass(t, g):
        rows, cols = piece(t, g, far_rows)
        return remote(zout.at[t, rows, cols], zout.at[t, rows, cols], zw_ss, ze_rs, beside)

    def z_send(copies):
        @pl.when(end_of_line)
        def _():
            for copy in copies:
                copy.start()

    def z_first(t, g):
        z_far(t, g).wait_recv()
        rows, cols = piece(t, g, far_rows)
        there, _ = piece(t, g, 0)
        zpart[t, rows, cols] = (
            zpart[t, rows, cols].astype(F32) + zfar[t, there, cols].astype(F32)
        ).astype(BF16)
        z_mid(t, g).start()

    def z_second(t, g):
        came(znear.at[0, :, pl.ds(0, 2 * piece_cols)], zm_rs.at[t * Z_PARTS + g])
        rows, cols = piece(t, g, near_rows)
        there, _ = piece(t, g, 0)
        total = (
            zpart[t, rows, cols].astype(F32)
            + znear[t, there, cols].astype(F32)
            + zmid[t, there, cols].astype(F32)
        )
        base = tok[rows, cols].astype(F32)
        if t == 0:
            place = near_rows + lax.broadcasted_iota(jnp.int32, total.shape, 0)
            branch = jnp.where(place < total_len, total + obias[:, cols], 0.0)
            zout[t, rows, cols] = (base + branch).astype(BF16)
        else:
            @pl.when(g == 0)
            def _():
                cot_load.wait()

            inv = stat_i[rows, 0:1]
            standard = (base - stat_m[rows, 0:1]) * inv
            grad = total * gain[...]
            mean_g = jnp.sum(grad, axis=1, keepdims=True) * (1.0 / width)
            mean_x = jnp.sum(grad * standard, axis=1, keepdims=True) * (1.0 / width)
            back = inv * (grad - mean_g - standard * mean_x)
            zout[t, rows, cols] = (cot_rows[there, :].astype(F32) + back).astype(BF16)
        z_done(t, g, False).start()
        z_done(t, g, True).start()

    def z_third(t, g):
        z_done(t, g, False).wait_recv()
        z_pass(t, g).start()

    def z_move(step, number):
        for t in (0, 1):
            at = number - t * Z_PARTS
            if isinstance(number, int):
                if 0 <= at < Z_PARTS:
                    pl.when(middle)(functools.partial(step, t, at))
            else:
                pl.when(middle & (at >= 0) & (at < Z_PARTS))(functools.partial(step, t, at))

    def z_tick(number):
        for step, lag in zip((z_first, z_second, z_third), Z_LAG):
            z_move(step, number - lag)

    per_wide = WIDE // BLK
    n_wide = hidden // WIDE

    def hidden_block(w, with_grad):
        cols = pl.ds(mult(w * WIDE, WIDE), WIDE)
        came(wu.at[:, pl.ds(0, 2 * WIDE)], wide_sem.at[w])
        up = nn(normed[...], wu[:, cols]) + bup[:, cols]
        square = up * up
        tanh = jnp.tanh(GELU_A * up * (1.0 + GELU_B * square))
        row = lax.broadcasted_iota(jnp.int32, up.shape, 0)
        active = jnp.where(row < total_len, 0.5 * up * (1.0 + tanh), 0.0).astype(BF16)
        act[:, cols] = active
        slope = 0.5 * (1.0 + tanh) + 0.5 * up * (1.0 - tanh * tanh) * (
            GELU_A * (1.0 + 3.0 * GELU_B * square)
        )
        if with_grad:
            grad = (nt(gout[...], wd[cols, :]) * slope).astype(BF16)
            gup[:, cols] = grad
        else:
            gup[:, cols] = slope.astype(BF16)
        for part in range(per_wide):
            c = w * per_wide + part
            inside = slice(part * BLK, part * BLK + BLK)
            bg[c, :, 0:toks] = active[:, inside].T
            if with_grad:
                bn[c, 0:toks, :] = grad[:, inside]
        for part in range(per_wide):
            c = w * per_wide + part
            for k in (0, 1):
                bg_copy(c, k).start()
                if with_grad:
                    bn_copy(c, k).start()

    @pl.loop(0, n_wide // 2)
    def _(w):
        hidden_block(w, True)

    @pl.loop(n_wide // 2, n_wide)
    def _(w):
        hidden_block(w, False)

        @pl.when(w == n_wide // 2)
        def _():
            side_first()

    def hidden_grad(first, past, shift):
        @pl.loop(first, past)
        def _(w):
            @pl.when(w == first)
            def _():
                side_out(0)

            @pl.when(w == first + 1)
            def _():
                side_out(1)

            z_tick(w - first)
            cols = pl.ds(mult(w * WIDE, WIDE), WIDE)
            grad = (nt(gout[...], wd[cols, :]) * gup[:, cols].astype(F32)).astype(BF16)
            gup[:, cols] = grad
            for part in range(per_wide):
                c = shift + w * per_wide + part
                bn[c, 0:toks, :] = grad[:, part * BLK : part * BLK + BLK]
                for k in (0, 1):
                    bn_copy(c, k).start()

    seg_r, _ = segment_of(slot)
    seg_c, _ = segment_of(lax.broadcasted_iota(jnp.int32, (8, toks), 1))
    place_r = lax.broadcasted_iota(jnp.int32, (toks, toks), 0)
    place_c = lax.broadcasted_iota(jnp.int32, (toks, toks), 1)
    same = jnp.concatenate([seg_r] * (toks // 128), axis=1) == seg_c[0:1, :]
    mask = jnp.where(same & (place_c <= place_r), 0.0, -1e30)
    for h in (0, 1):
        amask[h * toks : h * toks + toks, :] = mask

    which = lax.broadcasted_iota(jnp.int32, (8, 128), 0)
    starts = jnp.zeros((8, 128), jnp.int32)
    for j, end in enumerate(ends):
        starts = jnp.where(which == j, end - lens[0, j], starts)
    turn = starts.astype(F32) * freq[0:8, :]
    turn_c, turn_s = jnp.cos(turn), jnp.sin(turn)
    back_c, back_s = jnp.ones((toks, 128), F32), jnp.zeros((toks, 128), F32)
    for j in range(len(ends)):
        inside = seg_r == j + 1
        back_c = jnp.where(inside, turn_c[j : j + 1, :], back_c)
        back_s = jnp.where(inside, turn_s[j : j + 1, :], back_s)
    slot_c, slot_s = rot_c[...], rot_a[...]
    cosine = slot_c * back_c + slot_s * back_s
    sine = slot_s * back_c - slot_c * back_s
    rot_c[...] = jnp.where(in_head < ROT, cosine, 1.0)
    rot_a[...] = jnp.where(in_head < ROT // 2, -sine, 0.0)
    rot_b[...] = jnp.where((in_head >= ROT // 2) & (in_head < ROT), sine, 0.0)

    def rotate(value, sign):
        left = pltpu.roll(value, 128 - ROT // 2, 1)
        right = pltpu.roll(value, ROT // 2, 1)
        return value * rot_c[...] + sign * (left * rot_a[...] + right * rot_b[...])

    attn_load.wait()

    @pl.loop(0, heads_w // BLK)
    def _(n):
        cols = pl.ds(mult(n * BLK, BLK), BLK)
        query = nn(normed[...], wq[:, cols]) + bq[:, cols]
        keys = nn(normed[...], wk[:, cols]) + bk[:, cols]
        for part in range(BLK // 128):
            at = pl.ds(mult(n * BLK + part * 128, 128), 128)
            lanes = slice(part * 128, part * 128 + 128)
            q_s[:, at] = (rotate(query[:, lanes], 1.0) * 0.125).astype(BF16)
            k_s[:, at] = rotate(keys[:, lanes], 1.0).astype(BF16)
        v_s[:, cols] = (nn(normed[...], wv[:, cols]) + bv[:, cols]).astype(BF16)
        ga_s[:, cols] = nt(gout[...], wo[cols, :]).astype(BF16)

    low_lane = lax.broadcasted_iota(jnp.int32, (1, 128), 1) < HD
    first_head = jnp.where(low_lane, 1.0, 0.0).astype(BF16)
    second_head = jnp.where(low_lane, 0.0, 1.0).astype(BF16)
    low_full = lax.broadcasted_iota(jnp.int32, (toks, 128), 1) < HD

    def apart(value):
        return jnp.concatenate([value * first_head, value * second_head], axis=0)

    def together(value):
        return jnp.where(low_full, value[:toks], value[toks:])

    @pl.loop(0, n_att)
    def _(n):
        base_n = n_hid // 2 + 3 * n

        @pl.when(n == n_att - 1)
        def _():
            side_relay(0)

        for part in range(BLK // 128):
            at = pl.ds(mult(n * BLK + part * 128, 128), 128)
            lanes = slice(part * 128, part * 128 + 128)
            kp, vp = k_s[:, at], v_s[:, at]
            q2, g2 = apart(q_s[:, at]), apart(ga_s[:, at])
            scores = nt(q2, kp) + amask[...]
            top = jnp.max(scores, axis=1, keepdims=True)
            expo = jnp.exp(scores - top)
            probs = expo * (1.0 / jnp.sum(expo, axis=1, keepdims=True))
            probs_low = probs.astype(BF16)
            prob_grad = nt(g2, vp)
            delta = jnp.sum(probs * prob_grad, axis=1, keepdims=True)
            score_grad = (probs * (prob_grad - delta)).astype(BF16)
            out = jnp.where(slot < total_len, together(nn(probs_low, vp)), 0.0).astype(BF16)
            att[:, at] = out
            bg[n_hid + n, lanes, 0:toks] = out.T
            dq = rotate(together(nn(score_grad, kp)) * 0.125, -1.0).astype(BF16)
            dk = rotate(tn(score_grad, q2), -1.0).astype(BF16)
            dv = tn(probs_low, g2).astype(BF16)
            for kind, value in enumerate((dq, dk, dv)):
                bn[base_n + kind, 0:toks, lanes] = value
                gqkv[:, pl.ds(mult(kind * heads_w + n * BLK + part * 128, 128), 128)] = value
        for k in (0, 1):
            bg_copy(n_hid + n, k).start()
            for kind in range(3):
                bn_copy(base_n + kind, k).start()

    side_relay(1)

    def branches(cols):
        zpart[0, :, cols] = (nn(act[...], wd[:, cols]) + nn(att[...], wo[:, cols])).astype(BF16)

    for g in range(Z_LEAD):
        branches(pl.ds(g * piece_cols, piece_cols))
        z_send([z_far(0, g)])

    @pl.loop(1, width // WIDE)
    def _(n):
        branches(pl.ds(mult(n * WIDE, WIDE), WIDE))
        for part in range(Z_LEAD):
            g = n * Z_LEAD + part
            z_send([z_far(0, g), z_near(0, g - Z_LEAD)])

    hidden_grad(n_wide // 2, n_wide, 3 * n_att)

    vzl[...] = jnp.zeros_like(vzl)

    @pl.loop(0, width // WIDE)
    def _(n):
        cols = pl.ds(mult(n * WIDE, WIDE), WIDE)
        grad = nt(gup[...], wu[cols, :])
        for kind, weight in enumerate((wq, wk, wv)):
            grad = grad + nt(gqkv[:, kind * heads_w : (kind + 1) * heads_w], weight[cols, :])
        zpart[1, :, cols] = grad.astype(BF16)

        @pl.when(n == 1)
        def _():
            z_tick(2)

        @pl.when(n == 3)
        def _():
            z_tick(3)

        for part in range(WIDE // 128):
            lanes = slice(part * 128, part * 128 + 128)
            at = pl.ds(mult(n * WIDE + part * 128, 128), 128)
            owner = n * per_wide + part * 128 // BLK
            half_row = part * 128 % BLK // 128
            piece_of = grad[:, lanes]
            standard = (tok[:, at].astype(F32) - stat_m[...]) * stat_i[...]
            vzl[owner, half_row : half_row + 1, :] = jnp.sum(piece_of * standard, axis=0, keepdims=True)
            vzl[owner, 2 + half_row : 3 + half_row, :] = jnp.sum(piece_of, axis=0, keepdims=True)

    def vd_copy(mask):
        return remote(
            vzl.at[flip(inner, mask)], vdr.at[mask - 1], vd_ss, vd_rs, peer(mask)
        )

    for owner in range(n_own):
        for half_row in (0, 1):
            first = owner * BLK + half_row * 128
            vzl[owner, 4 + half_row : 5 + half_row, :] = gsum[0:1, first : first + 128]
    for mask in range(1, GROUP):
        vd_copy(mask).start()
    for g in range(Z_PARTS):
        late = Z_PARTS - Z_LEAD + g
        z_send([z_far(1, g), z_near(late // Z_PARTS, late % Z_PARTS)])
    for g in range(Z_PARTS - Z_LEAD, Z_PARTS):
        z_send([z_near(1, g)])

    bs_copy = remote(bsum_s, bsum_r, bs_ss, bs_rs, peer(YBIT))

    def rn_copy(s):
        return remote(rsn_s.at[s], rsn_r.at[s], rn_ss, rn_rs, peer(YBIT))

    def rg_copy(s):
        return remote(rsg_s.at[s], rsg_r.at[s], rg_ss, rg_rs, peer(XBIT))

    came(bn.at[0], side_rs.at[1])

    @pl.when(end_of_line)
    def _():
        for number in (1, 2, 3):
            for kind in (0, 1):
                side_came(kind, number)

    bsum[...] = jnp.zeros_like(bsum)

    def vz_copy(src, i, where):
        return remote(src, vzr.at[i], vz_ss, vz_rs.at[i], where)

    def vec_spread():
        came(vdr, vd_rs)
        vz[...] = vzl[inner] + jnp.sum(vdr[...], axis=0)

        @pl.when(end_of_line)
        def _():
            vz_copy(vz, 0, beside).start()

    def vec_pair():
        @pl.when(middle)
        def _():
            came(vz, vz_rs.at[0])
            vz_pair[...] = vz[...] + vzr[0]
            vz_copy(vz_pair, 1, across).start()

    def vec_back():
        @pl.when(middle)
        def _():
            came(vz, vz_rs.at[1])
            norm_sums[...] = vz_pair[...] + vzr[1]
            vz_copy(norm_sums, 0, beside).start()

    side_n[2 * BLK :, :] = jnp.ones((16, 4 * toks), BF16)

    @pl.loop(0, n_chunks + 1)
    def _(s):
        @pl.when(s < g_chunks)
        def _():
            came(bn.at[s, pl.ds(0, 2 * toks), :], blk_rs.at[s, 0])
            bn_copy(s, 2).start()
            bg_copy(s, 2).start()

        @pl.when((s >= g_chunks) & (s < n_chunks))
        def _():
            came(bn.at[s, pl.ds(0, toks), :], blk_rs.at[s, 0])
            bn_copy(s, 2).start()

        @pl.when((s > 0) & (s <= g_chunks))
        def _():
            came(bn.at[s - 1], blk_rs.at[s - 1, 1])

        @pl.when(s > g_chunks)
        def _():
            came(bn.at[s - 1, pl.ds(0, 2 * toks), :], blk_rs.at[s - 1, 1])

        @pl.when(s > 0)
        def _():
            p = s - 1
            both = nn(side_n[...], bn[p])
            rsn_s[p] = both[BLK : 2 * BLK, :].astype(BF16)
            rn_copy(p).start()
            bsum[pl.ds(p, 1), :] = both[2 * BLK : 2 * BLK + 1, :]
            bn[p, 2 * toks : 3 * toks, :] = both[:BLK, :].astype(BF16)

        @pl.when((s > 0) & (s <= g_chunks))
        def _():
            p = s - 1
            both = nn(bg[p], side_g[...])
            rsg_s[p] = both[:, BLK:].astype(BF16)
            rg_copy(p).start()
            bg[p, :, 2 * toks : 3 * toks] = both[:, :BLK].astype(BF16)

        tick = -1
        for turn, number in Z_TICKS:
            tick = jnp.where(s == turn, number, tick)
        z_tick(tick)

    bsum_s[...] = bsum[...].astype(BF16)
    bs_copy.start()
    vec_spread()
    @pl.loop(Z_TICKS[-1][1] + 1, 2 * Z_PARTS + Z_LAG[-1])
    def _(number):
        @pl.when(number == 2 * Z_PARTS)
        def _():
            vec_pair()

        z_tick(number)

    vec_back()

    bs_copy.wait_recv()

    @pl.when(end_of_line)
    def _():
        came(vz, vz_rs.at[0])
        norm_sums[...] = vzr[0]

    for half_row in (0, 1):
        lanes = slice(half_row * 128, half_row * 128 + 128)
        vec_o[0:1, lanes] = norm_sums[half_row : half_row + 1, :]
        vec_o[1:2, lanes] = norm_sums[2 + half_row : 3 + half_row, :]
        vec_o[2:3, lanes] = vz[4 + half_row : 5 + half_row, :]
    vec_o[8:, :] = bsum[...] + bsum_r[...].astype(F32)

    came(rsn_r, rn_rs)
    came(rsg_r, rg_rs)

    came(bn.at[:, pl.ds(0, 3 * toks), :], bn_ss)
    came(bg.at[:, :, pl.ds(0, 3 * toks)], bg_ss)
    came(rsn_s, rn_ss)
    came(rsg_s, rg_ss)
    came(vdr, vd_ss)
    bs_copy.wait_send()

    @pl.when(end_of_line)
    def _():
        came(bn.at[pl.ds(0, 2)], side_ss)
        came(vz, vz_ss)
        came(zfar, zf_ss)
        came(znear, zn_ss)
        came(zout, ze_rs)
        cot_load.wait()

    @pl.when(middle)
    def _():
        came(bn.at[pl.ds(0, 4)], side_ss)
        came(vzr, vz_ss)
        came(zmid, zm_ss)
        came(zout, zo_ss)
        came(zmid, zw_ss)


def write_kernel(n_hid, n_att, bn, bg, rsn, rsg, zout, vec, mixed_h, gtok_h, gain_o, shift_o, gq_h, bq_o, gk_h, bk_o, gv_h, bv_o, go_h, gu_h, bu_o, gd_h, ob_o, stage, small, sem, zsem, small_sem):
    n_chunks, n_g = bn.shape[0], bg.shape[0]
    toks = zout.shape[1]
    z_outs = [
        pltpu.make_async_copy(zout.at[t], out, zsem) for t, out in enumerate((mixed_h, gtok_h))
    ]
    for out in z_outs:
        out.start()
    places, biases = [], []
    for s in range(n_chunks):
        inside = s - n_hid // 2
        if 0 <= inside < 3 * n_att:
            (out, bias), at = ((gq_h, bq_o), (gk_h, bk_o), (gv_h, bv_o))[inside % 3], inside // 3
        else:
            (out, bias), at = (gu_h, bu_o), s if inside < 0 else s - 3 * n_att
        biases.append((bias, at))
        places.append((True, s, out.at[:, pl.ds(at * BLK, BLK)]))
    for s in range(n_g):
        out, at = (gd_h, s) if s < n_hid else (go_h, s - n_hid)
        places.append((False, s, out.at[pl.ds(at * BLK, BLK), :]))
    smalls = [(gain_o, (0,)), (shift_o, (1,)), (ob_o, (2,))]
    for bias in (bq_o, bk_o, bv_o, bu_o):
        smalls.append((bias, tuple(8 + s for at, s in sorted((at, s) for s, (b, at) in enumerate(biases) if b is bias))))
    at = 0
    for out, rows in smalls:
        for part, row in enumerate(rows):
            small[at + part * BLK : at + part * BLK + BLK] = vec[row]
        pltpu.make_async_copy(small.at[pl.ds(at, len(rows) * BLK)], out, small_sem).start()
        at += len(rows) * BLK
    copies = []
    for number, (first, s, place) in enumerate(places):
        slot = number
        if first:
            value = bn[s, 2 * toks : 3 * toks, :].astype(F32) + rsn[s].astype(F32)
        else:
            value = bg[s, :, 2 * toks : 3 * toks].astype(F32) + rsg[s].astype(F32)
        stage[slot] = value
        copies.append(pltpu.make_async_copy(stage.at[slot], place, sem))
        copies[number].start()
    pltpu.make_async_copy(stage, stage, sem).wait()
    pltpu.make_async_copy(zout, zout, zsem).wait()
    pltpu.make_async_copy(small, small, small_sem).wait()


def layer(tokens, lengths, ln_gain, ln_bias, w_query, b_query, w_key, b_key, w_value, b_value, w_out, w_up, b_up, w_down, out_bias, cotangent):
    toks, width = tokens.shape
    heads_w = w_query.shape[1]
    hidden = w_up.shape[1]
    n_chunks = (3 * heads_w + hidden) // BLK
    g_chunks = (heads_w + hidden) // BLK
    n_own = width // BLK
    n_vec = -(-n_chunks // 8) * 8
    half = toks // 2
    dma = pltpu.SemaphoreType.DMA
    vmem = pltpu.VMEM
    scratch = [
        pltpu.SMEM(lengths.shape, jnp.int32),
        vmem((1, 2 * width), F32),
        vmem((1, hidden + 3 * heads_w + width), F32),
        vmem((toks, width), BF16),
        vmem((toks, width), BF16),
        vmem((toks, width), BF16),
        vmem((n_own, BLK, toks), BF16),
        vmem(w_query.shape, BF16),
        vmem(w_key.shape, BF16),
        vmem(w_value.shape, BF16),
        vmem(w_out.shape, BF16),
        vmem(w_up.shape, BF16),
        vmem(w_down.shape, BF16),
        vmem((2 * BLK + 16, 4 * toks), BF16),
        vmem((4 * toks, 2 * BLK), BF16),
        vmem((n_chunks, BLK, BLK), BF16),
        vmem((g_chunks, BLK, BLK), BF16),
        vmem((toks, hidden), BF16),
        vmem((toks, hidden), BF16),
        vmem((toks, 3 * heads_w), BF16),
        vmem((toks, heads_w), BF16),
        vmem((toks, heads_w), BF16),
        vmem((toks, heads_w), BF16),
        vmem((toks, heads_w), BF16),
        vmem((toks, heads_w), BF16),
        vmem((2 * toks, toks), F32),
        vmem((toks, 128), F32),
        vmem((toks, 128), F32),
        vmem((toks, 128), F32),
        vmem((toks, 128), F32),
        vmem((toks, 128), F32),
        vmem((2, toks, width), BF16),
        vmem((2, half, width), BF16),
        vmem((2, half, width), BF16),
        vmem((2, half, width), BF16),
        vmem((n_own, 8, 128), F32),
        vmem((8, 128), F32),
        vmem((8, 128), F32),
        vmem((8, 128), F32),
        vmem((2, 8, 128), F32),
        vmem((GROUP - 1, 8, 128), F32),
        vmem((8, width), F32),
        vmem((n_vec, BLK), F32),
        vmem((n_vec, BLK), BF16),
        vmem((n_vec, BLK), BF16),
        vmem((half, width), BF16),
        dma((6,)),
        dma((4,)),
        dma((hidden // WIDE,)),
        dma,
        dma((8,)),
        dma,
        dma,
        dma((n_chunks, 2)),
        dma,
        dma,
        dma,
        dma,
        dma,
        dma((2 * Z_PARTS,)),
        dma,
        dma,
        dma((2 * Z_PARTS,)),
        dma,
        dma((2 * Z_PARTS,)),
        dma,
        dma,
        dma,
        dma((2,)),
        dma,
        dma,
        dma,
        dma,
    ]
    anyspace = pl.BlockSpec(memory_space=pl.ANY)
    local = pl.BlockSpec(memory_space=pltpu.VMEM)
    row = lambda value: value.reshape(1, -1)
    kept = pl.pallas_call(
        functools.partial(layer_kernel, n_chunks, g_chunks),
        out_shape=(
            vmem((n_chunks, 4 * toks, BLK), BF16),
            vmem((g_chunks, BLK, 4 * toks), BF16),
            vmem((n_chunks, BLK, BLK), BF16),
            vmem((g_chunks, BLK, BLK), BF16),
            vmem((2, toks, width), BF16),
            vmem((8 + n_vec, BLK), F32),
        ),
        in_specs=[anyspace] * 16,
        out_specs=(local,) * 6,
        scratch_shapes=scratch,
        compiler_params=pltpu.CompilerParams(
            collective_id=0, has_side_effects=True, vmem_limit_bytes=MAIN_VMEM
        ),
    )(
        lengths,
        tokens,
        cotangent,
        row(ln_gain),
        row(ln_bias),
        row(b_query),
        row(b_key),
        row(b_value),
        row(b_up),
        row(out_bias),
        w_query,
        w_key,
        w_value,
        w_out,
        w_up,
        w_down,
    )
    f32 = lambda *shape: jax.ShapeDtypeStruct(shape, F32)
    low = jax.ShapeDtypeStruct((toks, width), BF16)
    outs = (
        low,
        low,
        f32(BLK),
        f32(BLK),
        f32(BLK, heads_w),
        f32(heads_w),
        f32(BLK, heads_w),
        f32(heads_w),
        f32(BLK, heads_w),
        f32(heads_w),
        f32(heads_w, BLK),
        f32(BLK, hidden),
        f32(hidden),
        f32(hidden, BLK),
        f32(BLK),
    )
    slots = n_chunks + g_chunks
    return pl.pallas_call(
        functools.partial(write_kernel, hidden // BLK, heads_w // BLK),
        out_shape=outs,
        in_specs=[local] * 6,
        out_specs=(anyspace,) * len(outs),
        scratch_shapes=[
            vmem((slots, BLK, BLK), F32),
            vmem((3 * BLK + 3 * heads_w + hidden,), F32),
            dma,
            dma,
            dma,
        ],
        compiler_params=pltpu.CompilerParams(vmem_limit_bytes=12 * 2**20),
    )(*kept)


def make_body(n_dp, n_mp):
    outer = n_dp // GROUP

    def order(value, axis):
        if outer == 1:
            return value
        shape = value.shape
        split = shape[:axis] + (outer, GROUP, shape[axis] // n_dp) + shape[axis + 1 :]
        return jnp.swapaxes(value.reshape(split), axis, axis + 1).reshape(shape)

    def restore(value, axis):
        if outer == 1:
            return value
        shape = value.shape
        split = shape[:axis] + (GROUP, outer, shape[axis] // n_dp) + shape[axis + 1 :]
        return jnp.swapaxes(value.reshape(split), axis, axis + 1).reshape(shape)

    groups = [[o * GROUP + i for o in range(outer)] for i in range(GROUP)]

    def scatter(value, axis):
        if outer == 1:
            return value
        return lax.psum_scatter(
            value, "dp", scatter_dimension=axis, axis_index_groups=groups, tiled=True
        )

    def total(value):
        if outer == 1:
            return value
        return lax.psum(value, "dp", axis_index_groups=groups)

    def body(tokens, lengths, ln_gain, ln_bias, w_query, b_query, w_key, b_key, w_value, b_value, w_out, w_up, b_up, w_down, out_bias, cotangent):
        found = layer(
            order(tokens, 1),
            lengths,
            order(ln_gain, 0),
            order(ln_bias, 0),
            order(w_query, 0),
            b_query,
            order(w_key, 0),
            b_key,
            order(w_value, 0),
            b_value,
            order(w_out, 1),
            order(w_up, 0),
            b_up,
            order(w_down, 1),
            order(out_bias, 0),
            order(cotangent, 1),
        )
        (mixed, grad_tokens, gain, shift, g_q, b_q, g_k, b_k, g_v, b_v, g_out, g_up, b_u, g_down, b_out) = found
        return (
            restore(mixed, 1),
            restore(grad_tokens, 1),
            scatter(gain, 0),
            scatter(shift, 0),
            scatter(g_q, 0),
            total(b_q),
            scatter(g_k, 0),
            total(b_k),
            scatter(g_v, 0),
            total(b_v),
            scatter(g_out, 1),
            scatter(g_up, 0),
            total(b_u),
            scatter(g_down, 1),
            scatter(b_out, 0),
        )

    return body


def solution(mesh):
    in_specs = (
        P("dp", None),
        P("dp", None),
        P(),
        P(),
        P(None, "mp"),
        P("mp"),
        P(None, "mp"),
        P("mp"),
        P(None, "mp"),
        P("mp"),
        P("mp", None),
        P(None, "mp"),
        P("mp"),
        P("mp", None),
        P(),
        P("dp", None),
    )
    out_specs = (
        P("dp", None),
        P("dp", None),
        P("dp"),
        P("dp"),
        P("dp", "mp"),
        P("mp"),
        P("dp", "mp"),
        P("mp"),
        P("dp", "mp"),
        P("mp"),
        P("mp", "dp"),
        P("dp", "mp"),
        P("mp"),
        P("mp", "dp"),
        P("dp"),
    )
    body = make_body(mesh.shape["dp"], mesh.shape["mp"])
    return jax.shard_map(body, mesh=mesh, in_specs=in_specs, out_specs=out_specs, check_vma=False)
```
